32 devices in a mesh: fsdp: 16 (over z, x, core), seq: 2 (over y).
Axes of the slice: x: 2, y: 2, z: 4, core: 2. Of those that a mesh axis runs over, the one named last changes fastest.
Arguments:
- tokens: bfloat16 [24576, 1536], P(('fsdp', 'seq')), may hold values from -6 to 6
- segments: int32 [24576], replicated, may hold values from 0 to 16, as said below
- text: bfloat16 [32, 64, 1536], P('fsdp'), may hold values from -6 to 6
- qkv_weight: bfloat16 [1536, 4608], P('fsdp'), may hold values from -0.15625 to 0.15625
- out_weight: bfloat16 [1536, 1536], P('fsdp'), may hold values from -3 to 3
- cross_query_weight: bfloat16 [1536, 1536], P('fsdp'), may hold values from -0.15625 to 0.15625
- cross_kv_weight: bfloat16 [1536, 3072], P('fsdp'), may hold values from -0.15625 to 0.15625
- cross_out_weight: bfloat16 [1536, 1536], P('fsdp'), may hold values from -0.625 to 0.625
- up_weight: bfloat16 [1536, 6144], P('fsdp'), may hold values from -0.15625 to 0.15625
- down_weight: bfloat16 [6144, 1536], P('fsdp'), may hold values from -0.078125 to 0.078125
- norm_gain: bfloat16 [3, 1536], P(None, 'fsdp'), may hold values from 0.5 to 1.5
- norm_bias: bfloat16 [3, 1536], P(None, 'fsdp'), may hold values from -3 to 3
- cotangent: bfloat16 [24576, 1536], P(('fsdp', 'seq')), may hold values from -6 to 6
Outputs:
- layer_out: bfloat16 [24576, 1536], P(('fsdp', 'seq'))
- grad_tokens: bfloat16 [24576, 1536], P(('fsdp', 'seq'))
- grad_text: float32 [32, 64, 1536], P('fsdp')
- grad_qkv: float32 [1536, 4608], P('fsdp')
- grad_out: float32 [1536, 1536], P('fsdp')
- grad_cross_query: float32 [1536, 1536], P('fsdp')
- grad_cross_kv: float32 [1536, 3072], P('fsdp')
- grad_cross_out: float32 [1536, 1536], P('fsdp')
- grad_up: float32 [1536, 6144], P('fsdp')
- grad_down: float32 [6144, 1536], P('fsdp')
- grad_gain: float32 [3, 1536], P(None, 'fsdp')
- grad_bias: float32 [3, 1536], P(None, 'fsdp')
The draws below stay inside these ranges and needn't reach their ends.
Inputs may be any that keep to these rules, and one draw needn't show every extreme that they name: `segments`: segment numbers never decrease, and grow by exactly one at each first token of a clip; token 0 has segment 0, and each aligned block of 1536 tokens holds exactly one other first token, never at the block's own first token.
All inputs are finite; a program needn't handle non-finite values.
Results may differ from the reference program's by a relative error of at most 0.023.
Values may be sent and summed in bfloat16 or wider, within the bound.
No kernel may reach another device: no remote copies, remote signals or barrier semaphores. Data moves between devices by JAX's collectives and lax.ppermute only.
A program may use at most 704 MiB of HBM per device.

```python
import jax
import jax.numpy as jnp
from jax import lax

D = 1536
HEADS = 24
HEAD = 64
FF = 6144
TXT = 64
SPAN = 1536
QB = 512
TOKENS = 24576
GROUP = 1536
REACH = 3072
SLOTS = 2
TEXTS = 32
N_FSDP = 16


def draw_segments(key, part):
    offsets = jax.random.randint(key, (TOKENS // SPAN,), 1, SPAN, dtype=jnp.int32)
    position = jnp.arange(TOKENS, dtype=jnp.int32)
    blocks = position // SPAN
    inside = position - blocks * SPAN
    return blocks + (inside >= offsets[blocks]).astype(jnp.int32)


def steps_of(own_key, shape, split, low, high):
    def one(dim, parts):
        heights = jax.random.uniform(jax.random.fold_in(jax.random.fold_in(own_key, 6), dim), (parts,), jnp.float32, low / len(split), high / len(split))
        return jnp.repeat(jnp.exp(heights), shape[dim] // parts).reshape((-1,) + (1,) * (len(shape) - dim - 1))

    loudness = one(*split[0])
    for cut in split[1:]:
        loudness = loudness * one(*cut)
    return loudness


def gaussian(key, shape, deviation, bound, pieces=(), kind=jnp.bfloat16):
    drawn = deviation * jax.random.normal(key, shape, jnp.float32)
    if pieces:
        drawn = drawn * steps_of(key, shape, pieces, -0.22, 0.18)
    return jnp.clip(drawn, -bound, bound).astype(kind)


def setup_inputs(seed: int = 0) -> dict:
    arg_keys = jax.random.split(jax.random.key(seed), 14)
    return {
        "tokens": gaussian(arg_keys[0], (TOKENS, D), 1.0, 6.0, ((0, 32),)),
        "segments": draw_segments(jax.random.fold_in(arg_keys[13], 71), 0),
        "text": gaussian(arg_keys[2], (TEXTS, TXT, D), 1.0, 6.0, ((0, 16),)),
        "qkv_weight": gaussian(arg_keys[3], (D, 3 * D), D ** -0.5, 0.15625, ((0, 16),)),
        "out_weight": gaussian(arg_keys[4], (D, D), (4 * D // SPAN) ** -0.5, 3.0, ((0, 16),)),
        "cross_query_weight": gaussian(arg_keys[5], (D, D), D ** -0.5, 0.15625, ((0, 16),)),
        "cross_kv_weight": gaussian(arg_keys[6], (D, 2 * D), D ** -0.5, 0.15625, ((0, 16),)),
        "cross_out_weight": gaussian(arg_keys[7], (D, D), (D // 16) ** -0.5, 0.625, ((0, 16),)),
        "up_weight": gaussian(arg_keys[8], (D, FF), D ** -0.5, 0.15625, ((0, 16),)),
        "down_weight": gaussian(arg_keys[9], (FF, D), FF ** -0.5, 0.078125, ((0, 16),)),
        "norm_gain": jnp.clip(1.0 + 0.1 * jax.random.normal(arg_keys[10], (3, D), jnp.float32), 0.5, 1.5).astype(jnp.bfloat16),
        "norm_bias": gaussian(arg_keys[11], (3, D), 0.5, 3.0, ((1, 16),)),
        "cotangent": gaussian(arg_keys[12], (TOKENS, D), 1.0, 6.0, ((0, 32),)),
    }


@jax.custom_vjp
def low(v):
    return lax.optimization_barrier(v.astype(jnp.bfloat16)).astype(jnp.float32)

@jax.custom_vjp
def low_back(v):
    return v

def low_keep(v):
    return (low(v), None)

def low_pass(kept, grad):
    return (grad,)

def back_keep(v):
    return (v, None)

def back_low(kept, grad):
    return (low(grad),)
low.defvjp(low_keep, low_pass)
low_back.defvjp(back_keep, back_low)
EPS = 1e-05
NEG = -1e+30
HIGH = lax.Precision.HIGHEST

def layer_norm(values, gain, bias):
    average = lax.optimization_barrier(jnp.mean(values, axis=-1, keepdims=True))
    centred = values - average
    spread = lax.optimization_barrier(jnp.mean(centred * centred, axis=-1, keepdims=True))
    return centred * lax.rsqrt(spread + EPS) * gain + bias

def matmul(left_side, right_side):
    return jnp.dot(left_side, right_side, precision=HIGH, preferred_element_type=jnp.float32)

def softmax_rows(scores):
    row_top = lax.optimization_barrier(jnp.max(scores, axis=-1, keepdims=True))
    weights = jnp.exp(scores - row_top)
    return weights / lax.optimization_barrier(jnp.sum(weights, axis=-1, keepdims=True))

def self_attention(qkv, segments):
    score_scale = HEAD ** (-0.5)
    queries = qkv[:, 0].reshape(TOKENS, HEADS, HEAD)
    front_pad = jnp.zeros((REACH, HEADS, HEAD), jnp.float32)
    keys_all = jnp.concatenate([front_pad, qkv[:, 1].reshape(TOKENS, HEADS, HEAD)], axis=0)
    values_all = jnp.concatenate([front_pad, qkv[:, 2].reshape(TOKENS, HEADS, HEAD)], axis=0)
    seg_all = jnp.concatenate([jnp.full((REACH,), -1, jnp.int32), segments.astype(jnp.int32)])

    def block(block_index):
        row_start = (block_index * QB).astype(jnp.int32)
        query_block = lax.dynamic_slice_in_dim(queries, row_start, QB, 0)
        key_block = lax.dynamic_slice_in_dim(keys_all, row_start, REACH + QB, 0)
        value_block = lax.dynamic_slice_in_dim(values_all, row_start, REACH + QB, 0)
        seg_rows = lax.dynamic_slice_in_dim(segments.astype(jnp.int32), row_start, QB)
        seg_cols = lax.dynamic_slice_in_dim(seg_all, row_start, REACH + QB)
        rows_at = jnp.arange(QB)[:, None]
        cols_at = jnp.arange(REACH + QB)[None, :]
        allowed = (seg_rows[:, None] == seg_cols[None, :]) & (cols_at <= rows_at + REACH)
        scores = jnp.einsum('qhd,khd->hqk', query_block, key_block, precision=HIGH) * score_scale
        scores = low_back(scores)
        scores = jnp.where(allowed[None], scores, NEG)
        shares = low(softmax_rows(scores))
        return jnp.einsum('hqk,khd->qhd', shares, value_block, precision=HIGH)
    blocks = lax.map(jax.checkpoint(block), jnp.arange(TOKENS // QB, dtype=jnp.int32))
    return blocks.reshape(TOKENS, D)

def cross_attention(cross_query, cross_kv, segments):
    score_scale = HEAD ** (-0.5)

    def one_group(group_index):
        query_rows = lax.dynamic_slice_in_dim(cross_query, group_index * GROUP, GROUP, 0).reshape(GROUP, HEADS, HEAD)
        text_rows = lax.dynamic_slice_in_dim(cross_kv, group_index * (SLOTS * TXT), SLOTS * TXT, 0)
        keys = text_rows[:, :D].reshape(SLOTS * TXT, HEADS, HEAD)
        values = text_rows[:, D:].reshape(SLOTS * TXT, HEADS, HEAD)
        seg_rows = lax.dynamic_slice_in_dim(segments.astype(jnp.int32), group_index * GROUP, GROUP)
        slot_rows = seg_rows - group_index * (GROUP // SPAN)
        key_slot = jnp.arange(SLOTS * TXT, dtype=jnp.int32) // TXT
        allowed = slot_rows[:, None] == key_slot[None, :]
        scores = jnp.einsum('qhd,khd->hqk', query_rows, keys, precision=HIGH) * score_scale
        scores = low_back(scores)
        scores = jnp.where(allowed[None], scores, NEG)
        shares = low(softmax_rows(scores))
        return jnp.einsum('hqk,khd->qhd', shares, values, precision=HIGH).reshape(GROUP, D)
    groups = lax.map(jax.checkpoint(one_group), jnp.arange(N_FSDP, dtype=jnp.int32))
    return groups.reshape(TOKENS, D)

def forward(tokens, text, qkv_weight, out_weight, cross_query_weight, cross_kv_weight, cross_out_weight, up_weight, down_weight, norm_gain, norm_bias, segments):
    normed_one = low(layer_norm(tokens, norm_gain[0], norm_bias[0]))
    qkv = low_back(low(matmul(normed_one, qkv_weight)))
    attended = low_back(low(self_attention(qkv.reshape(TOKENS, 3, D), segments)))
    hidden_one = tokens + low_back(matmul(attended, out_weight))
    normed_two = low(layer_norm(hidden_one, norm_gain[1], norm_bias[1]))
    cross_query = low_back(low(matmul(normed_two, cross_query_weight)))
    cross_kv = low_back(low(matmul(text.reshape(TEXTS * TXT, D), cross_kv_weight)))
    cross_result = low_back(low(cross_attention(cross_query, cross_kv, segments)))
    hidden_two = hidden_one + low_back(matmul(cross_result, cross_out_weight))
    normed_three = low(layer_norm(hidden_two, norm_gain[2], norm_bias[2]))
    upward = low_back(matmul(normed_three, up_weight))
    active = low(jax.nn.gelu(upward, approximate=False))
    return hidden_two + low_back(matmul(active, down_weight))

def reference(tokens, segments, text, qkv_weight, out_weight, cross_query_weight, cross_kv_weight, cross_out_weight, up_weight, down_weight, norm_gain, norm_bias, cotangent):
    floats = tuple((arr.astype(jnp.float32) for arr in (tokens, text, qkv_weight, out_weight, cross_query_weight, cross_kv_weight, cross_out_weight, up_weight, down_weight, norm_gain, norm_bias)))

    def run_layer(*inputs_all):
        return forward(*inputs_all, segments)
    output, pullback = jax.vjp(run_layer, *floats)
    grads = pullback(cotangent.astype(jnp.float32))
    return (output.astype(jnp.bfloat16), grads[0].astype(jnp.bfloat16), grads[1], grads[2], grads[3], grads[4], grads[5], grads[6], grads[7], grads[8], grads[9], grads[10])
```

```python
import functools

import jax
import jax.numpy as jnp
from jax import lax
from jax.experimental import pallas as pl
from jax.experimental.pallas import tpu as pltpu
from jax.sharding import PartitionSpec as P

HEADS = 24
HEAD = 64
PAIR = 2 * HEAD
TXT = 64
SPAN = 1536
EPS = 1e-05
NEG = -1e30
SCALE = HEAD**-0.5
VMEM_BYTES = 48 * 2**20


def matmul(left_side, right_side):
    return jnp.dot(left_side, right_side, preferred_element_type=jnp.float32)


def contract_rows(left_side, right_side):
    return lax.dot_general(
        left_side, right_side, (((0,), (0,)), ((), ())), preferred_element_type=jnp.float32
    )


def contract_cols(left_side, right_side):
    return lax.dot_general(
        left_side, right_side, (((1,), (1,)), ((), ())), preferred_element_type=jnp.float32
    )


def block_bounds(starts, reach, tq, tk):
    rows = starts.shape[0]
    first = starts[::tq]
    last = starts[tq - 1 :: tq]
    row0 = reach + jnp.arange(rows // tq, dtype=jnp.int32) * tq
    low = first // tk
    high = (row0 + tq - 1) // tk + 1
    free_low = jnp.minimum(jnp.maximum((last + tk - 1) // tk, low), high)
    free_high = jnp.clip((row0 + 1) // tk, free_low, high)
    return jnp.stack([low, free_low, free_high, high], axis=1)


def attend_kernel(bounds, q_ref, kp_ref, vp_ref, ko_ref, vo_ref, start_ref, o_ref, lse_ref, k_all, v_first, v_second, *, reach, tq, tk):
    i = pl.program_id(1)
    lane = lax.broadcasted_iota(jnp.int32, (1, PAIR), 1)
    lower = lane < HEAD

    @pl.when(i == 0)
    def _():
        one = jnp.ones((1, 1), jnp.bfloat16)
        k_all[:reach] = kp_ref[...]
        k_all[reach:] = ko_ref[...]
        v_first[:reach] = jnp.where(lower, vp_ref[...], one)
        v_first[reach:] = jnp.where(lower, vo_ref[...], one)
        v_second[:reach] = jnp.where(lower, one, vp_ref[...])
        v_second[reach:] = jnp.where(lower, one, vo_ref[...])

    scaled = q_ref[...] * jnp.bfloat16(SCALE)
    zero = jnp.zeros((1, 1), jnp.bfloat16)
    halves = (jnp.where(lower, scaled, zero), jnp.where(lower, zero, scaled))
    values = (v_first, v_second)
    reps = tk // PAIR

    def wide(x):
        return jnp.concatenate([x] * reps, axis=1)

    def step(masked, j, carried):
        rows = pl.ds(pl.multiple_of(j * tk, tk), tk)
        keys = k_all[rows, :]
        if masked:
            at = j * tk + lax.broadcasted_iota(jnp.int32, (tq, tk), 1)
            row = reach + i * tq + lax.broadcasted_iota(jnp.int32, (tq, tk), 0)
            allowed = (at >= wide(start_ref[...])) & (at <= row)
        out = []
        scores = []
        for half in halves:
            s = lax.dot_general(half, keys, (((1,), (1,)), ((), ())), preferred_element_type=jnp.float32)
            if masked:
                s = jnp.where(allowed, s, NEG)
            scores.append(s)
        for s, value, (top, total) in zip(scores, values, carried):
            new_top = jnp.maximum(top, jnp.max(s, axis=1, keepdims=True))
            weights = jnp.exp(s - wide(new_top)).astype(jnp.bfloat16)
            keep = jnp.exp(top - new_top)
            total = total * keep + jnp.dot(weights, value[rows, :], preferred_element_type=jnp.float32)
            out.append((new_top, total))
        return tuple(out)

    one_state = (jnp.full((tq, PAIR), NEG, jnp.float32), jnp.zeros((tq, PAIR), jnp.float32))
    state = (one_state, one_state)
    low, free_low, free_high, high = (bounds[i, n] for n in range(4))
    state = lax.fori_loop(low, free_low, functools.partial(step, True), state)
    state = lax.fori_loop(free_low, free_high, functools.partial(step, False), state)
    state = lax.fori_loop(free_high, high, functools.partial(step, True), state)
    outs, logs = [], []
    for top, total in state:
        count = pltpu.roll(total, HEAD, 1)
        outs.append(total / count)
        logs.append(top + jnp.log(count))
    o_ref[...] = jnp.where(lower, outs[0], outs[1]).astype(o_ref.dtype)
    lse_ref[...] = jnp.where(lower, logs[0], logs[1])


def self_attend(q, kv_before, kv_own, starts, *, tq=384, tk=384):
    rows, width = q.shape
    reach = kv_before.shape[0]
    pairs = width // PAIR
    bounds = block_bounds(starts, reach, tq, tk)
    starts_wide = jnp.broadcast_to(starts[:, None], (rows, PAIR))
    spec = pltpu.PrefetchScalarGridSpec(
        num_scalar_prefetch=1,
        grid=(pairs, rows // tq),
        in_specs=[
            pl.BlockSpec((tq, PAIR), lambda p, i, b: (i, p)),
            pl.BlockSpec((reach, PAIR), lambda p, i, b: (0, p)),
            pl.BlockSpec((reach, PAIR), lambda p, i, b: (0, pairs + p)),
            pl.BlockSpec((rows, PAIR), lambda p, i, b: (0, p)),
            pl.BlockSpec((rows, PAIR), lambda p, i, b: (0, pairs + p)),
            pl.BlockSpec((tq, PAIR), lambda p, i, b: (i, 0)),
        ],
        out_specs=[
            pl.BlockSpec((tq, PAIR), lambda p, i, b: (i, p)),
            pl.BlockSpec((tq, PAIR), lambda p, i, b: (i, p)),
        ],
        scratch_shapes=[pltpu.VMEM((reach + rows, PAIR), jnp.bfloat16)] * 3,
    )
    return pl.pallas_call(
        functools.partial(attend_kernel, reach=reach, tq=tq, tk=tk),
        grid_spec=spec,
        out_shape=[
            jax.ShapeDtypeStruct((rows, width), jnp.bfloat16),
            jax.ShapeDtypeStruct((rows, width), jnp.float32),
        ],
        compiler_params=pltpu.CompilerParams(
            dimension_semantics=("arbitrary", "arbitrary"), vmem_limit_bytes=VMEM_BYTES
        ),
        cost_estimate=pl.CostEstimate(flops=16 * rows * rows * width, bytes_accessed=12 * rows * width, transcendentals=rows * rows * width // HEAD),
        name="self_attend",
    )(bounds, q, kv_before, kv_before, kv_own, kv_own, starts_wide)


def attend_back_kernel(bounds, q_ref, do_ref, o_ref, lse_ref, kp_ref, vp_ref, ko_ref, vo_ref, start_ref, dq_ref, dkp_ref, dvp_ref, dko_ref, dvo_ref, k_all, v_all, dk_sum, dv_sum, *, reach, tq, tk):
    i = pl.program_id(1)
    lane = lax.broadcasted_iota(jnp.int32, (1, PAIR), 1)
    lower = lane < HEAD

    @pl.when(i == 0)
    def _():
        k_all[:reach] = kp_ref[...]
        k_all[reach:] = ko_ref[...]
        v_all[:reach] = vp_ref[...]
        v_all[reach:] = vo_ref[...]
        dk_sum[...] = jnp.zeros_like(dk_sum)
        dv_sum[...] = jnp.zeros_like(dv_sum)

    zero = jnp.zeros((1, 1), jnp.bfloat16)
    scaled = q_ref[...] * jnp.bfloat16(SCALE)
    grad = do_ref[...]
    q_halves = (jnp.where(lower, scaled, zero), jnp.where(lower, zero, scaled))
    do_halves = (jnp.where(lower, grad, zero), jnp.where(lower, zero, grad))
    product = (grad.astype(jnp.float32) * o_ref[...].astype(jnp.float32)).T
    inner = (
        jnp.sum(product[:HEAD], axis=0, keepdims=True),
        jnp.sum(product[HEAD:], axis=0, keepdims=True),
    )
    lse_t = lse_ref[...].T
    lse = (lse_t[:1], lse_t[HEAD : HEAD + 1])
    starts = start_ref[0]

    def step(masked, j, dq):
        rows = pl.ds(pl.multiple_of(j * tk, tk), tk)
        keys = k_all[rows, :]
        values = v_all[rows, :]
        if masked:
            at = j * tk + lax.broadcasted_iota(jnp.int32, (tk, tq), 0)
            row = reach + i * tq + lax.broadcasted_iota(jnp.int32, (tk, tq), 1)
            allowed = (at >= starts) & (at <= row)
        dks, dvs = [], []
        for h in range(2):
            s = lax.dot_general(keys, q_halves[h], (((1,), (1,)), ((), ())), preferred_element_type=jnp.float32)
            d = lax.dot_general(values, do_halves[h], (((1,), (1,)), ((), ())), preferred_element_type=jnp.float32)
            if masked:
                s = jnp.where(allowed, s, NEG)
            p = jnp.exp(s - lse[h])
            ds = (p * (d - inner[h])).astype(jnp.bfloat16)
            dvs.append(jnp.dot(p.astype(jnp.bfloat16), do_halves[h], preferred_element_type=jnp.float32))
            dks.append(jnp.dot(ds, q_halves[h], preferred_element_type=jnp.float32))
            k_half = jnp.where(lower, keys, zero) if h == 0 else jnp.where(lower, zero, keys)
            dq = dq + lax.dot_general(ds, k_half, (((0,), (0,)), ((), ())), preferred_element_type=jnp.float32)
        dv_sum[rows, :] += dvs[0] + dvs[1]
        dk_sum[rows, :] += dks[0] + dks[1]
        return dq

    low, free_low, free_high, high = (bounds[i, n] for n in range(4))
    dq = jnp.zeros((tq, PAIR), jnp.float32)
    dq = lax.fori_loop(low, free_low, functools.partial(step, True), dq)
    dq = lax.fori_loop(free_low, free_high, functools.partial(step, False), dq)
    dq = lax.fori_loop(free_high, high, functools.partial(step, True), dq)
    dq_ref[...] = (dq * SCALE).astype(dq_ref.dtype)

    @pl.when(i == pl.num_programs(1) - 1)
    def _():
        dkp_ref[...] = dk_sum[:reach].astype(dkp_ref.dtype)
        dvp_ref[...] = dv_sum[:reach].astype(dvp_ref.dtype)
        dko_ref[...] = dk_sum[reach:].astype(dko_ref.dtype)
        dvo_ref[...] = dv_sum[reach:].astype(dvo_ref.dtype)


def self_attend_back(q, do, o, lse, kv_before, kv_own, starts, *, tq=384, tk=384):
    rows, width = q.shape
    reach = kv_before.shape[0]
    pairs = width // PAIR
    bounds = block_bounds(starts, reach, tq, tk)
    starts_row = starts.reshape(rows // tq, 1, tq)
    spec = pltpu.PrefetchScalarGridSpec(
        num_scalar_prefetch=1,
        grid=(pairs, rows // tq),
        in_specs=[
            pl.BlockSpec((tq, PAIR), lambda p, i, b: (i, p)),
            pl.BlockSpec((tq, PAIR), lambda p, i, b: (i, p)),
            pl.BlockSpec((tq, PAIR), lambda p, i, b: (i, p)),
            pl.BlockSpec((tq, PAIR), lambda p, i, b: (i, p)),
            pl.BlockSpec((reach, PAIR), lambda p, i, b: (0, p)),
            pl.BlockSpec((reach, PAIR), lambda p, i, b: (0, pairs + p)),
            pl.BlockSpec((rows, PAIR), lambda p, i, b: (0, p)),
            pl.BlockSpec((rows, PAIR), lambda p, i, b: (0, pairs + p)),
            pl.BlockSpec((1, 1, tq), lambda p, i, b: (i, 0, 0)),
        ],
        out_specs=[
            pl.BlockSpec((tq, PAIR), lambda p, i, b: (i, p)),
            pl.BlockSpec((reach, PAIR), lambda p, i, b: (0, p)),
            pl.BlockSpec((reach, PAIR), lambda p, i, b: (0, p)),
            pl.BlockSpec((rows, PAIR), lambda p, i, b: (0, p)),
            pl.BlockSpec((rows, PAIR), lambda p, i, b: (0, p)),
        ],
        scratch_shapes=[pltpu.VMEM((reach + rows, PAIR), jnp.bfloat16)] * 2
        + [pltpu.VMEM((reach + rows, PAIR), jnp.float32)] * 2,
    )
    return pl.pallas_call(
        functools.partial(attend_back_kernel, reach=reach, tq=tq, tk=tk),
        grid_spec=spec,
        out_shape=[
            jax.ShapeDtypeStruct((rows, width), jnp.bfloat16),
            jax.ShapeDtypeStruct((reach, width), jnp.bfloat16),
            jax.ShapeDtypeStruct((reach, width), jnp.bfloat16),
            jax.ShapeDtypeStruct((rows, width), jnp.bfloat16),
            jax.ShapeDtypeStruct((rows, width), jnp.bfloat16),
        ],
        compiler_params=pltpu.CompilerParams(
            dimension_semantics=("arbitrary", "arbitrary"), vmem_limit_bytes=VMEM_BYTES
        ),
        cost_estimate=pl.CostEstimate(flops=40 * rows * rows * width, bytes_accessed=20 * rows * width, transcendentals=rows * rows * width // HEAD),
        name="self_attend_back",
    )(bounds, q, do, o, lse, kv_before, kv_before, kv_own, kv_own, starts_row)


def cross_kernel(q_ref, k_ref, v_ref, slot_ref, o_ref):
    lower = lax.broadcasted_iota(jnp.int32, (1, PAIR), 1) < HEAD
    zero = jnp.zeros((1, 1), jnp.bfloat16)
    scaled = q_ref[...] * jnp.bfloat16(SCALE)
    tokens, texts = q_ref.shape[0], k_ref.shape[0]
    allowed = slot_ref[:, :1] == lax.broadcasted_iota(jnp.int32, (tokens, texts), 1) // TXT
    results = []
    for h in range(2):
        half = jnp.where(lower, scaled, zero) if h == 0 else jnp.where(lower, zero, scaled)
        scores = jnp.where(allowed, contract_cols(half, k_ref[...]), NEG)
        weights = jnp.exp(scores - jnp.max(scores, axis=1, keepdims=True))
        shares = weights / jnp.sum(weights, axis=1, keepdims=True)
        results.append(matmul(shares.astype(jnp.bfloat16), v_ref[...]))
    o_ref[...] = jnp.where(lower, results[0], results[1]).astype(o_ref.dtype)


def cross_attend(q, k, v, slots_wide):
    tokens, width = q.shape
    texts = k.shape[0]
    column = lambda p: (0, p)
    return pl.pallas_call(
        cross_kernel,
        grid=(width // PAIR,),
        in_specs=[
            pl.BlockSpec((tokens, PAIR), column),
            pl.BlockSpec((texts, PAIR), column),
            pl.BlockSpec((texts, PAIR), column),
            pl.BlockSpec((tokens, PAIR), lambda p: (0, 0)),
        ],
        out_specs=pl.BlockSpec((tokens, PAIR), column),
        out_shape=jax.ShapeDtypeStruct(q.shape, jnp.bfloat16),
        compiler_params=pltpu.CompilerParams(vmem_limit_bytes=VMEM_BYTES),
        cost_estimate=pl.CostEstimate(
            flops=8 * tokens * texts * width,
            bytes_accessed=4 * tokens * width,
            transcendentals=tokens * texts * width // HEAD,
        ),
        name="cross_attend",
    )(q, k, v, slots_wide)


def cross_back_kernel(q_ref, g_ref, k_ref, v_ref, slot_ref, dq_ref, dk_ref, dv_ref):
    lower = lax.broadcasted_iota(jnp.int32, (1, PAIR), 1) < HEAD
    zero = jnp.zeros((1, 1), jnp.bfloat16)
    scaled = q_ref[...] * jnp.bfloat16(SCALE)
    grad = g_ref[...]
    keys = k_ref[...]
    tokens, texts = q_ref.shape[0], k_ref.shape[0]
    allowed = slot_ref[:, :1] == lax.broadcasted_iota(jnp.int32, (tokens, texts), 1) // TXT
    dqs, dks, dvs = [], [], []
    for h in range(2):
        q_half = jnp.where(lower, scaled, zero) if h == 0 else jnp.where(lower, zero, scaled)
        g_half = jnp.where(lower, grad, zero) if h == 0 else jnp.where(lower, zero, grad)
        scores = jnp.where(allowed, contract_cols(q_half, keys), NEG)
        weights = jnp.exp(scores - jnp.max(scores, axis=1, keepdims=True))
        shares = weights / jnp.sum(weights, axis=1, keepdims=True)
        grad_shares = contract_cols(g_half, v_ref[...])
        inner = jnp.sum(shares * grad_shares, axis=1, keepdims=True)
        grad_scores = (shares * (grad_shares - inner)).astype(jnp.bfloat16)
        dqs.append(matmul(grad_scores, keys))
        dks.append(contract_rows(grad_scores, q_half))
        dvs.append(contract_rows(shares.astype(jnp.bfloat16), g_half))
    dq_ref[...] = (jnp.where(lower, dqs[0], dqs[1]) * SCALE).astype(dq_ref.dtype)
    dk_ref[...] = dks[0] + dks[1]
    dv_ref[...] = dvs[0] + dvs[1]


def cross_attend_back(q, grad, k, v, slots_wide):
    tokens, width = q.shape
    texts = k.shape[0]
    column = lambda p: (0, p)
    return pl.pallas_call(
        cross_back_kernel,
        grid=(width // PAIR,),
        in_specs=[
            pl.BlockSpec((tokens, PAIR), column),
            pl.BlockSpec((tokens, PAIR), column),
            pl.BlockSpec((texts, PAIR), column),
            pl.BlockSpec((texts, PAIR), column),
            pl.BlockSpec((tokens, PAIR), lambda p: (0, 0)),
        ],
        out_specs=[
            pl.BlockSpec((tokens, PAIR), column),
            pl.BlockSpec((texts, PAIR), column),
            pl.BlockSpec((texts, PAIR), column),
        ],
        out_shape=[
            jax.ShapeDtypeStruct(q.shape, jnp.bfloat16),
            jax.ShapeDtypeStruct((texts, width), jnp.float32),
            jax.ShapeDtypeStruct((texts, width), jnp.float32),
        ],
        compiler_params=pltpu.CompilerParams(vmem_limit_bytes=VMEM_BYTES),
        cost_estimate=pl.CostEstimate(
            flops=20 * tokens * texts * width,
            bytes_accessed=6 * tokens * width,
            transcendentals=tokens * texts * width // HEAD,
        ),
        name="cross_attend_back",
    )(q, grad, k, v, slots_wide)


def swap(value, axis, bit):
    count = lax.axis_size(axis)
    return lax.ppermute(value, axis, [(i, i ^ bit) for i in range(count)])


def passed_along(value, axis, steps):
    count = lax.axis_size(axis)
    initial, last = (max(0, -steps), min(count, count - steps))
    return lax.ppermute(value, axis, [(source, source + steps) for source in range(initial, last)])


def in_order(mine, other, dim):
    second = lax.axis_index("seq") == 1
    return jnp.concatenate([jnp.where(second, other, mine), jnp.where(second, mine, other)], axis=dim)


def gathered(value, dim):
    if lax.axis_size("seq") == 2:
        return in_order(value, swap(value, "seq", 1), dim)
    return lax.all_gather(value, "seq", axis=dim, tiled=True)


def own_block(value, dim):
    size = value.shape[dim] // lax.axis_size("seq")
    return lax.dynamic_slice_in_dim(value, lax.axis_index("seq") * size, size, dim)


def other_block(value, dim):
    size = value.shape[dim] // 2
    return lax.dynamic_slice_in_dim(value, (1 - lax.axis_index("seq")) * size, size, dim)


def exchanged(value, split, concat):
    if lax.axis_size("seq") == 2:
        return in_order(own_block(value, split), swap(other_block(value, split), "seq", 1), concat)
    return lax.all_to_all(value, "seq", split_axis=split, concat_axis=concat, tiled=True)


def summed_block(value, dim):
    if lax.axis_size("seq") == 2:
        received = swap(other_block(value, dim).astype(jnp.bfloat16), "seq", 1)
        return own_block(value, dim) + received.astype(jnp.float32)
    return lax.psum_scatter(
        value.astype(jnp.bfloat16), "seq", scatter_dimension=dim, tiled=True
    ).astype(jnp.float32)


def paired(value):
    short = -value.shape[-1] % PAIR
    return jnp.pad(value, ((0, 0), (0, short))) if short else value


def normed(values):
    average = jnp.mean(values, axis=-1, keepdims=True)
    centred = values - average
    spread = jnp.mean(centred * centred, axis=-1, keepdims=True)
    root = lax.rsqrt(spread + EPS)
    return centred * root, root


def norm_back(grad, n, root, gain):
    a = grad * gain
    back = (a - jnp.mean(a, axis=-1, keepdims=True) - n * jnp.mean(a * n, axis=-1, keepdims=True)) * root
    return back, jnp.sum(grad * n, axis=0), jnp.sum(grad, axis=0)


def scattered(grad):
    return lax.psum_scatter(grad.astype(jnp.bfloat16), "fsdp", scatter_dimension=0, tiled=True)


def clip_starts(segments, group_index, group_rows):
    padded = jnp.concatenate([jnp.full((SPAN,), -1, jnp.int32), segments])
    spans = lax.dynamic_slice_in_dim(padded, group_index * group_rows, SPAN + group_rows)
    spans = spans.reshape(-1, SPAN)
    ahead = jnp.sum((spans == spans[:, :1]).astype(jnp.int32), axis=1)
    firsts = ahead + jnp.arange(spans.shape[0], dtype=jnp.int32) * SPAN
    late = spans[1:] != spans[1:, :1]
    return jnp.where(late, firsts[1:, None], firsts[:-1, None]).reshape(group_rows), spans[1:].reshape(group_rows)


def shards(
    tokens,
    segments,
    text,
    qkv_weight,
    out_weight,
    cross_query_weight,
    cross_kv_weight,
    cross_out_weight,
    up_weight,
    down_weight,
    norm_gain,
    norm_bias,
    cotangent,
):
    group_index = lax.axis_index("fsdp")
    seq_index = lax.axis_index("seq")
    seq_count = lax.axis_size("seq")
    tok_rows, width = tokens.shape
    group_rows = tok_rows * seq_count
    head_cols = width // seq_count
    shard_rows = qkv_weight.shape[0]
    row_block = lambda value: lax.all_gather(value, "fsdp", axis=0, tiled=True)

    norms = jnp.pad(jnp.concatenate([norm_gain, norm_bias]).T, ((0, 0), (0, PAIR - 6)))
    qkv_mine = own_block(qkv_weight.reshape(shard_rows, 3, width), 2).reshape(shard_rows, 3 * head_cols)
    first = row_block(jnp.concatenate([qkv_mine, norms], axis=1))
    w_q, w_kv, w_qkv = first[:, :head_cols], first[:, head_cols : 3 * head_cols], first[:, : 3 * head_cols]
    norm_rows = first[:, 3 * head_cols : 3 * head_cols + 6].astype(jnp.float32).T
    gains, biases = norm_rows[:3], norm_rows[3:]

    starts, seg_group = clip_starts(segments, group_index, group_rows)
    slots = own_block(seg_group, 0) - group_index * (group_rows // SPAN)
    slots_wide = jnp.broadcast_to(slots[:, None], (tok_rows, PAIR))

    inputs = tokens.astype(jnp.float32)
    n_group, _ = normed(gathered(tokens, 0).astype(jnp.float32))
    normed_one = (n_group * gains[0] + biases[0]).astype(jnp.bfloat16)
    kv_own = matmul(normed_one, w_kv).astype(jnp.bfloat16)
    kv_before = passed_along(kv_own[group_rows - SPAN :], "fsdp", 1)
    queries = matmul(normed_one, w_q).astype(jnp.bfloat16)
    if head_cols % PAIR:
        pad_kv = lambda kv: jnp.concatenate([paired(kv[:, :head_cols]), paired(kv[:, head_cols:])], axis=1)
        queries, kv_own, kv_before = paired(queries), pad_kv(kv_own), pad_kv(kv_before)
    heads_out, log_totals = self_attend(queries, kv_before, kv_own, starts)
    attended = exchanged(heads_out[:, :head_cols], 0, 1)
    full_out = row_block(out_weight)
    hidden_one = inputs + matmul(attended, full_out)

    ckv_mine = own_block(cross_kv_weight.reshape(shard_rows, 2, width), 2).reshape(shard_rows, 2 * head_cols)
    w_ckv = row_block(ckv_mine)
    text_rows = text.reshape(-1, width)
    text_count = text_rows.shape[0]
    ckv_part = matmul(text_rows, w_ckv).astype(jnp.bfloat16).reshape(text_count, 2, head_cols)
    cross_kv = gathered(ckv_part, 2)
    cross_k, cross_v = cross_kv[:, 0], cross_kv[:, 1]
    full_cq = row_block(cross_query_weight)
    n_two, root_two = normed(hidden_one)
    normed_two = (n_two * gains[1] + biases[1]).astype(jnp.bfloat16)
    cross_query = matmul(normed_two, full_cq).astype(jnp.bfloat16)
    cross_result = cross_attend(cross_query, cross_k, cross_v, slots_wide)
    full_cout = row_block(cross_out_weight)
    hidden_two = hidden_one + matmul(cross_result, full_cout)

    full_up, full_down = row_block(up_weight), row_block(down_weight)
    n_three, root_three = normed(hidden_two)
    normed_three = (n_three * gains[2] + biases[2]).astype(jnp.bfloat16)
    upward = matmul(normed_three, full_up)
    below = 0.5 * (1.0 + lax.erf(upward * (0.5**0.5)))
    active = (upward * below).astype(jnp.bfloat16)
    slope = below + upward * (jnp.exp(-0.5 * upward * upward) * 0.3989422804014327)
    layer_out = (hidden_two + matmul(active, full_down)).astype(jnp.bfloat16)

    grad_down = scattered(contract_rows(active, cotangent))
    grad_upward = (contract_cols(cotangent, full_down) * slope).astype(jnp.bfloat16)
    grad_up = scattered(contract_rows(normed_three, grad_upward))
    back_h2, gain_three, bias_three = norm_back(contract_cols(grad_upward, full_up), n_three, root_three, gains[2])
    grad_two = cotangent.astype(jnp.float32) + back_h2
    grad_two_low = grad_two.astype(jnp.bfloat16)
    grad_cout = scattered(contract_rows(cross_result, grad_two_low))
    grad_result = contract_cols(grad_two_low, full_cout).astype(jnp.bfloat16)
    grad_query_c, grad_text_k, grad_text_v = cross_attend_back(cross_query, grad_result, cross_k, cross_v, slots_wide)
    grad_cq = scattered(contract_rows(normed_two, grad_query_c))
    grad_text_kv = summed_block(jnp.stack([grad_text_k, grad_text_v], axis=1), 2)
    grad_text_kv = grad_text_kv.astype(jnp.bfloat16).reshape(text_count, 2 * head_cols)
    grad_text = contract_cols(grad_text_kv, w_ckv)
    grad_ckv = scattered(contract_rows(text_rows, grad_text_kv))
    back_h1, gain_two, bias_two = norm_back(contract_cols(grad_query_c, full_cq), n_two, root_two, gains[1])
    grad_one = grad_two + back_h1

    grad_one_low = grad_one.astype(jnp.bfloat16)
    grad_attended = contract_cols(grad_one_low, full_out).astype(jnp.bfloat16)
    grad_heads = paired(exchanged(grad_attended, 1, 0))
    grad_wout = scattered(contract_rows(attended, grad_one_low))
    grad_q, grad_k_before, grad_v_before, grad_k, grad_v = self_attend_back(
        queries, grad_heads, heads_out, log_totals, kv_before, kv_own, starts
    )
    late = group_rows - SPAN
    owned = [grad_q[:, :head_cols]]
    for part, before in ((grad_k, grad_k_before), (grad_v, grad_v_before)):
        returned = passed_along(before[:, :head_cols], "fsdp", -1).astype(jnp.float32)
        part = part[:, :head_cols].astype(jnp.float32)
        part = jnp.concatenate([part[:late], part[late:] + returned]) if late else part + returned
        owned.append(part.astype(jnp.bfloat16))
    grad_proj = jnp.concatenate(owned, axis=1)
    grad_wqkv = scattered(contract_rows(normed_one, grad_proj))
    grad_normed_one = summed_block(contract_cols(grad_proj, w_qkv), 0)
    n_one, root_one = normed(inputs)
    back_x, gain_one, bias_one = norm_back(grad_normed_one, n_one, root_one, gains[0])
    grad_tokens = (grad_one + back_x).astype(jnp.bfloat16)

    def whole(part):
        return lax.psum(part, "seq").astype(jnp.float32)

    def columns(part, blocks):
        return gathered(part.reshape(shard_rows, blocks, head_cols), 2).reshape(shard_rows, -1).astype(jnp.float32)

    norm_grads = lax.psum(
        jnp.stack([gain_one, gain_two, gain_three, bias_one, bias_two, bias_three]), ("fsdp", "seq")
    )
    norm_grads = lax.dynamic_slice_in_dim(norm_grads, group_index * shard_rows, shard_rows, 1)
    return (
        layer_out,
        grad_tokens,
        lax.psum(grad_text.astype(jnp.bfloat16), "seq").astype(jnp.float32).reshape(text.shape),
        columns(grad_wqkv, 3),
        whole(grad_wout),
        whole(grad_cq),
        columns(grad_ckv, 2),
        whole(grad_cout),
        whole(grad_up),
        whole(grad_down),
        norm_grads[:3],
        norm_grads[3:],
    )


def solution(mesh):
    rows, shard, copied = P(("fsdp", "seq"), None), P("fsdp", None), P(None, "fsdp")
    groups = P("fsdp", None, None)
    in_specs = (rows, P(), groups, *[shard] * 7, copied, copied, rows)
    out_specs = (rows, rows, groups, *[shard] * 7, copied, copied)
    return jax.shard_map(shards, mesh=mesh, in_specs=in_specs, out_specs=out_specs, check_vma=False)
```

```python
import functools

import jax
import jax.numpy as jnp
from jax import lax
from jax.experimental import pallas as pl
from jax.experimental.pallas import tpu as pltpu
from jax.sharding import PartitionSpec as P

HEADS = 24
HEAD = 64
PAIR = 2 * HEAD
TXT = 64
SPAN = 1536
EPS = 1e-05
NEG = -1e30
SCALE = HEAD**-0.5
VMEM_BYTES = 56 * 2**20


def matmul(left_side, right_side):
    return jnp.dot(left_side, right_side, preferred_element_type=jnp.float32)


def contract_rows(left_side, right_side):
    return lax.dot_general(
        left_side, right_side, (((0,), (0,)), ((), ())), preferred_element_type=jnp.float32
    )


def contract_cols(left_side, right_side):
    return lax.dot_general(
        left_side, right_side, (((1,), (1,)), ((), ())), preferred_element_type=jnp.float32
    )


TILE = 384


def block_bounds(starts, reach):
    rows = starts.shape[0]
    first = starts[::TILE]
    last = starts[TILE - 1 :: TILE]
    row0 = reach + jnp.arange(rows // TILE, dtype=jnp.int32) * TILE
    low = first // TILE
    high = (row0 + TILE - 1) // TILE + 1
    free_low = jnp.minimum(jnp.maximum((last + TILE - 1) // TILE, low), high)
    free_high = jnp.clip((row0 + 1) // TILE, free_low, high)
    return jnp.stack([low, free_low, free_high, high], axis=1)


def pairs_a_step(width):
    return 3 if width % (3 * PAIR) == 0 else 1


def split_heads(block):
    lower = lax.broadcasted_iota(jnp.int32, (1, PAIR), 1) < HEAD
    zero = jnp.zeros((1, 1), block.dtype)
    return [jnp.where(lower, block, zero), jnp.where(lower, zero, block)]


def lanes(p):
    return slice(p * PAIR, (p + 1) * PAIR)


def tile_allowed(j, row0, starts):
    at = j * TILE + lax.broadcasted_iota(jnp.int32, (TILE, TILE), 0)
    row = row0 + lax.broadcasted_iota(jnp.int32, (TILE, TILE), 1)
    return (at >= starts) & (at <= row)


def over_tiles(bounds, i, step, state):
    low, free_low, free_high, high = (bounds[i, n] for n in range(4))
    state = lax.fori_loop(low, free_low, functools.partial(step, True), state)
    state = lax.fori_loop(free_low, free_high, functools.partial(step, False), state)
    return lax.fori_loop(free_high, high, functools.partial(step, True), state)


def attend_kernel(
    bounds, q_ref, kp_ref, vp_ref, ko_ref, vo_ref, start_ref, o_ref, lse_ref, k_all, v_t, *, reach, pairs
):
    i = pl.program_id(1)

    @pl.when(i == 0)
    def _():
        k_all[:reach] = kp_ref[...]
        k_all[reach:] = ko_ref[...]
        for p in range(pairs):
            for ref, begin in ((vp_ref, 0), (vo_ref, reach)):
                end = begin + ref.shape[0]
                turned = ref[:, lanes(p)].T
                for h in range(2):
                    v_t[2 * p + h, :HEAD, begin:end] = turned[h * HEAD : (h + 1) * HEAD]
                    v_t[2 * p + h, HEAD:, begin:end] = jnp.ones((16, end - begin), jnp.bfloat16)

    halves = []
    for p in range(pairs):
        halves += split_heads(q_ref[:, lanes(p)] * jnp.bfloat16(SCALE))
    starts = start_ref[0]

    def step(masked, j, carried):
        rows = pl.ds(pl.multiple_of(j * TILE, TILE), TILE)
        if masked:
            allowed = tile_allowed(j, reach + i * TILE, starts)
        scores = []
        for n in range(2 * pairs):
            s = contract_cols(k_all[rows, lanes(n // 2)], halves[n])
            scores.append(jnp.where(allowed, s, NEG) if masked else s)
        out = []
        for n, (top, total) in enumerate(carried):
            new_top = jnp.maximum(top, jnp.max(scores[n], axis=0, keepdims=True))
            weights = jnp.exp(scores[n] - new_top).astype(jnp.bfloat16)
            total = total * jnp.exp(top - new_top) + matmul(v_t[n, :, rows], weights)
            out.append((new_top, total))
        return tuple(out)

    nothing = (jnp.full((1, TILE), NEG, jnp.float32), jnp.zeros((HEAD + 16, TILE), jnp.float32))
    state = over_tiles(bounds, i, step, (nothing,) * (2 * pairs))
    for p in range(pairs):
        outs = []
        for n in (2 * p, 2 * p + 1):
            top, total = state[n]
            count = total[HEAD : HEAD + 1]
            outs.append(total[:HEAD] / count)
            lse_ref[0, 0, n : n + 1, :] = top + jnp.log(count)
        o_ref[:, lanes(p)] = jnp.concatenate(outs, axis=0).T.astype(o_ref.dtype)


def attend_specs(rows, reach, width):
    pairs = pairs_a_step(width)
    wide = pairs * PAIR
    steps = width // wide
    block = pl.BlockSpec((TILE, wide), lambda p, i, b: (i, p))
    kv = [
        pl.BlockSpec((reach, wide), lambda p, i, b: (0, p)),
        pl.BlockSpec((reach, wide), lambda p, i, b: (0, steps + p)),
        pl.BlockSpec((rows, wide), lambda p, i, b: (0, p)),
        pl.BlockSpec((rows, wide), lambda p, i, b: (0, steps + p)),
    ]
    logs = pl.BlockSpec((1, 1, 8, TILE), lambda p, i, b: (p, i, 0, 0))
    starts = pl.BlockSpec((1, 1, TILE), lambda p, i, b: (i, 0, 0))
    return pairs, wide, (steps, rows // TILE), block, kv, logs, starts


def self_attend(q, kv_before, kv_own, starts):
    rows, width = q.shape
    reach = kv_before.shape[0]
    pairs, wide, grid, block, kv, logs, start_block = attend_specs(rows, reach, width)
    spec = pltpu.PrefetchScalarGridSpec(
        num_scalar_prefetch=1,
        grid=grid,
        in_specs=[block, *kv, start_block],
        out_specs=[block, logs],
        scratch_shapes=[
            pltpu.VMEM((reach + rows, wide), jnp.bfloat16),
            pltpu.VMEM((2 * pairs, HEAD + 16, reach + rows), jnp.bfloat16),
        ],
    )
    return pl.pallas_call(
        functools.partial(attend_kernel, reach=reach, pairs=pairs),
        grid_spec=spec,
        out_shape=[
            jax.ShapeDtypeStruct((rows, width), jnp.bfloat16),
            jax.ShapeDtypeStruct((*grid, 8, TILE), jnp.float32),
        ],
        compiler_params=pltpu.CompilerParams(vmem_limit_bytes=VMEM_BYTES),
        cost_estimate=pl.CostEstimate(
            flops=20 * rows * rows * width,
            bytes_accessed=12 * rows * width,
            transcendentals=rows * rows * width // HEAD,
        ),
        name="self_attend",
    )(block_bounds(starts, reach), q, kv_before, kv_before, kv_own, kv_own, starts.reshape(-1, 1, TILE))


def attend_back_kernel(
    bounds, q_ref, g_ref, o_ref, lse_ref, kp_ref, vp_ref, ko_ref, vo_ref, start_ref,
    dq_ref, dkp_ref, dvp_ref, dko_ref, dvo_ref, k_all, v_all, dk_sum, dv_sum, k_t, *, reach, pairs
):
    i = pl.program_id(1)

    @pl.when(i == 0)
    def _():
        k_all[:reach] = kp_ref[...]
        k_all[reach:] = ko_ref[...]
        v_all[:reach] = vp_ref[...]
        v_all[reach:] = vo_ref[...]
        k_t[:, :reach] = kp_ref[...].T
        k_t[:, reach:] = ko_ref[...].T
        dk_sum[...] = jnp.zeros_like(dk_sum)
        dv_sum[...] = jnp.zeros_like(dv_sum)

    queries, grads, inner, logs = [], [], [], []
    for p in range(pairs):
        grad = g_ref[:, lanes(p)]
        queries += split_heads(q_ref[:, lanes(p)] * jnp.bfloat16(SCALE))
        grads += split_heads(grad)
        product = (grad.astype(jnp.float32) * o_ref[:, lanes(p)].astype(jnp.float32)).T
        for h in range(2):
            inner.append(jnp.sum(product[h * HEAD : (h + 1) * HEAD], axis=0, keepdims=True))
            logs.append(lse_ref[0, 0, 2 * p + h : 2 * p + h + 1])
    starts = start_ref[0]

    def step(masked, j, carried):
        rows = pl.ds(pl.multiple_of(j * TILE, TILE), TILE)
        if masked:
            allowed = tile_allowed(j, reach + i * TILE, starts)
        out = []
        for p in range(pairs):
            keys, values = k_all[rows, lanes(p)], v_all[rows, lanes(p)]
            dks, dvs = [], []
            for n in (2 * p, 2 * p + 1):
                s = contract_cols(keys, queries[n])
                d = contract_cols(values, grads[n])
                if masked:
                    s = jnp.where(allowed, s, NEG)
                shares = jnp.exp(s - logs[n])
                ds = (shares * (d - inner[n])).astype(jnp.bfloat16)
                dvs.append(matmul(shares.astype(jnp.bfloat16), grads[n]))
                dks.append(matmul(ds, queries[n]))
                out.append(carried[n] + matmul(k_t[n * HEAD : (n + 1) * HEAD, rows], ds))
            dv_sum[rows, lanes(p)] += dvs[0] + dvs[1]
            dk_sum[rows, lanes(p)] += dks[0] + dks[1]
        return tuple(out)

    state = over_tiles(bounds, i, step, (jnp.zeros((HEAD, TILE), jnp.float32),) * (2 * pairs))
    for p in range(pairs):
        turned = jnp.concatenate([state[2 * p], state[2 * p + 1]], axis=0).T
        dq_ref[:, lanes(p)] = (turned * SCALE).astype(dq_ref.dtype)

    @pl.when(i == pl.num_programs(1) - 1)
    def _():
        dkp_ref[...] = dk_sum[:reach].astype(dkp_ref.dtype)
        dvp_ref[...] = dv_sum[:reach].astype(dvp_ref.dtype)
        dko_ref[...] = dk_sum[reach:].astype(dko_ref.dtype)
        dvo_ref[...] = dv_sum[reach:].astype(dvo_ref.dtype)


def self_attend_back(q, grad, o, lse, kv_before, kv_own, starts):
    rows, width = q.shape
    reach = kv_before.shape[0]
    pairs, wide, grid, block, kv, logs, start_block = attend_specs(rows, reach, width)
    spec = pltpu.PrefetchScalarGridSpec(
        num_scalar_prefetch=1,
        grid=grid,
        in_specs=[block, block, block, logs, *kv, start_block],
        out_specs=[block, kv[0], kv[0], kv[2], kv[2]],
        scratch_shapes=[
            pltpu.VMEM((reach + rows, wide), jnp.bfloat16),
            pltpu.VMEM((reach + rows, wide), jnp.bfloat16),
            pltpu.VMEM((reach + rows, wide), jnp.float32),
            pltpu.VMEM((reach + rows, wide), jnp.float32),
            pltpu.VMEM((wide, reach + rows), jnp.bfloat16),
        ],
    )
    shape = lambda n: jax.ShapeDtypeStruct((n, width), jnp.bfloat16)
    return pl.pallas_call(
        functools.partial(attend_back_kernel, reach=reach, pairs=pairs),
        grid_spec=spec,
        out_shape=[shape(rows), shape(reach), shape(reach), shape(rows), shape(rows)],
        compiler_params=pltpu.CompilerParams(vmem_limit_bytes=VMEM_BYTES),
        cost_estimate=pl.CostEstimate(
            flops=40 * rows * rows * width,
            bytes_accessed=20 * rows * width,
            transcendentals=rows * rows * width // HEAD,
        ),
        name="self_attend_back",
    )(
        block_bounds(starts, reach), q, grad, o, lse, kv_before, kv_before, kv_own, kv_own,
        starts.reshape(-1, 1, TILE),
    )


def cross_kernel(q_ref, k_ref, v_ref, slot_ref, o_ref):
    lower = lax.broadcasted_iota(jnp.int32, (1, PAIR), 1) < HEAD
    zero = jnp.zeros((1, 1), jnp.bfloat16)
    scaled = q_ref[...] * jnp.bfloat16(SCALE)
    tokens, texts = q_ref.shape[0], k_ref.shape[0]
    allowed = slot_ref[:, :1] == lax.broadcasted_iota(jnp.int32, (tokens, texts), 1) // TXT
    results = []
    for h in range(2):
        half = jnp.where(lower, scaled, zero) if h == 0 else jnp.where(lower, zero, scaled)
        scores = jnp.where(allowed, contract_cols(half, k_ref[...]), NEG)
        weights = jnp.exp(scores - jnp.max(scores, axis=1, keepdims=True))
        shares = weights / jnp.sum(weights, axis=1, keepdims=True)
        results.append(matmul(shares.astype(jnp.bfloat16), v_ref[...]))
    o_ref[...] = jnp.where(lower, results[0], results[1]).astype(o_ref.dtype)


def cross_attend(q, k, v, slots_wide):
    tokens, width = q.shape
    texts = k.shape[0]
    column = lambda p: (0, p)
    return pl.pallas_call(
        cross_kernel,
        grid=(width // PAIR,),
        in_specs=[
            pl.BlockSpec((tokens, PAIR), column),
            pl.BlockSpec((texts, PAIR), column),
            pl.BlockSpec((texts, PAIR), column),
            pl.BlockSpec((tokens, PAIR), lambda p: (0, 0)),
        ],
        out_specs=pl.BlockSpec((tokens, PAIR), column),
        out_shape=jax.ShapeDtypeStruct(q.shape, jnp.bfloat16),
        compiler_params=pltpu.CompilerParams(vmem_limit_bytes=VMEM_BYTES),
        cost_estimate=pl.CostEstimate(
            flops=8 * tokens * texts * width,
            bytes_accessed=4 * tokens * width,
            transcendentals=tokens * texts * width // HEAD,
        ),
        name="cross_attend",
    )(q, k, v, slots_wide)


def cross_back_kernel(q_ref, g_ref, k_ref, v_ref, slot_ref, dq_ref, dk_ref, dv_ref):
    lower = lax.broadcasted_iota(jnp.int32, (1, PAIR), 1) < HEAD
    zero = jnp.zeros((1, 1), jnp.bfloat16)
    scaled = q_ref[...] * jnp.bfloat16(SCALE)
    grad = g_ref[...]
    keys = k_ref[...]
    tokens, texts = q_ref.shape[0], k_ref.shape[0]
    allowed = slot_ref[:, :1] == lax.broadcasted_iota(jnp.int32, (tokens, texts), 1) // TXT
    dqs, dks, dvs = [], [], []
    for h in range(2):
        q_half = jnp.where(lower, scaled, zero) if h == 0 else jnp.where(lower, zero, scaled)
        g_half = jnp.where(lower, grad, zero) if h == 0 else jnp.where(lower, zero, grad)
        scores = jnp.where(allowed, contract_cols(q_half, keys), NEG)
        weights = jnp.exp(scores - jnp.max(scores, axis=1, keepdims=True))
        shares = weights / jnp.sum(weights, axis=1, keepdims=True)
        grad_shares = contract_cols(g_half, v_ref[...])
        inner = jnp.sum(shares * grad_shares, axis=1, keepdims=True)
        grad_scores = (shares * (grad_shares - inner)).astype(jnp.bfloat16)
        dqs.append(matmul(grad_scores, keys))
        dks.append(contract_rows(grad_scores, q_half))
        dvs.append(contract_rows(shares.astype(jnp.bfloat16), g_half))
    dq_ref[...] = (jnp.where(lower, dqs[0], dqs[1]) * SCALE).astype(dq_ref.dtype)
    dk_ref[...] = dks[0] + dks[1]
    dv_ref[...] = dvs[0] + dvs[1]


def cross_attend_back(q, grad, k, v, slots_wide):
    tokens, width = q.shape
    texts = k.shape[0]
    column = lambda p: (0, p)
    return pl.pallas_call(
        cross_back_kernel,
        grid=(width // PAIR,),
        in_specs=[
            pl.BlockSpec((tokens, PAIR), column),
            pl.BlockSpec((tokens, PAIR), column),
            pl.BlockSpec((texts, PAIR), column),
            pl.BlockSpec((texts, PAIR), column),
            pl.BlockSpec((tokens, PAIR), lambda p: (0, 0)),
        ],
        out_specs=[
            pl.BlockSpec((tokens, PAIR), column),
            pl.BlockSpec((texts, PAIR), column),
            pl.BlockSpec((texts, PAIR), column),
        ],
        out_shape=[
            jax.ShapeDtypeStruct(q.shape, jnp.bfloat16),
            jax.ShapeDtypeStruct((texts, width), jnp.float32),
            jax.ShapeDtypeStruct((texts, width), jnp.float32),
        ],
        compiler_params=pltpu.CompilerParams(vmem_limit_bytes=VMEM_BYTES),
        cost_estimate=pl.CostEstimate(
            flops=20 * tokens * texts * width,
            bytes_accessed=6 * tokens * width,
            transcendentals=tokens * texts * width // HEAD,
        ),
        name="cross_attend_back",
    )(q, grad, k, v, slots_wide)


def swap(value, axis, bit):
    count = lax.axis_size(axis)
    return lax.ppermute(value, axis, [(i, i ^ bit) for i in range(count)])


def passed_along(value, axis, steps):
    count = lax.axis_size(axis)
    initial, last = (max(0, -steps), min(count, count - steps))
    return lax.ppermute(value, axis, [(source, source + steps) for source in range(initial, last)])


def in_order(mine, other, dim):
    second = lax.axis_index("seq") == 1
    return jnp.concatenate([jnp.where(second, other, mine), jnp.where(second, mine, other)], axis=dim)


def gathered(value, dim):
    if lax.axis_size("seq") == 2:
        return in_order(value, swap(value, "seq", 1), dim)
    return lax.all_gather(value, "seq", axis=dim, tiled=True)


def own_block(value, dim):
    size = value.shape[dim] // lax.axis_size("seq")
    return lax.dynamic_slice_in_dim(value, lax.axis_index("seq") * size, size, dim)


def other_block(value, dim):
    size = value.shape[dim] // 2
    return lax.dynamic_slice_in_dim(value, (1 - lax.axis_index("seq")) * size, size, dim)


def exchanged(value, split, concat):
    if lax.axis_size("seq") == 2:
        return in_order(own_block(value, split), swap(other_block(value, split), "seq", 1), concat)
    return lax.all_to_all(value, "seq", split_axis=split, concat_axis=concat, tiled=True)


def summed_block(value, dim):
    if lax.axis_size("seq") == 2:
        received = swap(other_block(value, dim).astype(jnp.bfloat16), "seq", 1)
        return own_block(value, dim) + received.astype(jnp.float32)
    return lax.psum_scatter(
        value.astype(jnp.bfloat16), "seq", scatter_dimension=dim, tiled=True
    ).astype(jnp.float32)


def paired(value):
    short = -value.shape[-1] % PAIR
    return jnp.pad(value, ((0, 0), (0, short))) if short else value


def normed(values):
    average = jnp.mean(values, axis=-1, keepdims=True)
    centred = values - average
    spread = jnp.mean(centred * centred, axis=-1, keepdims=True)
    root = lax.rsqrt(spread + EPS)
    return centred * root, root


def norm_back(grad, n, root, gain):
    a = grad * gain
    back = (a - jnp.mean(a, axis=-1, keepdims=True) - n * jnp.mean(a * n, axis=-1, keepdims=True)) * root
    return back, jnp.sum(grad * n, axis=0), jnp.sum(grad, axis=0)


def scattered(grad):
    return lax.psum_scatter(grad.astype(jnp.bfloat16), "fsdp", scatter_dimension=0, tiled=True)


def whole(part):
    if lax.axis_size("seq") == 2:
        return part.astype(jnp.float32) + swap(part, "seq", 1).astype(jnp.float32)
    return lax.psum(part, "seq").astype(jnp.float32)


def columns(part, blocks):
    split = part.reshape(part.shape[0], blocks, -1)
    return gathered(split, 2).reshape(part.shape[0], -1).astype(jnp.float32)


def everywhere(value):
    for axis in ("fsdp", "seq"):
        bit = 1
        while bit < lax.axis_size(axis):
            value = value + swap(value, axis, bit)
            bit *= 2
    return value


def clip_starts(segments, group_index, group_rows):
    padded = jnp.concatenate([jnp.full((SPAN,), -1, jnp.int32), segments])
    spans = lax.dynamic_slice_in_dim(padded, group_index * group_rows, SPAN + group_rows)
    spans = spans.reshape(-1, SPAN)
    ahead = jnp.sum((spans == spans[:, :1]).astype(jnp.int32), axis=1)
    firsts = ahead + jnp.arange(spans.shape[0], dtype=jnp.int32) * SPAN
    late = spans[1:] != spans[1:, :1]
    return jnp.where(late, firsts[1:, None], firsts[:-1, None]).reshape(group_rows), spans[1:].reshape(group_rows)


def shards(
    tokens,
    segments,
    text,
    qkv_weight,
    out_weight,
    cross_query_weight,
    cross_kv_weight,
    cross_out_weight,
    up_weight,
    down_weight,
    norm_gain,
    norm_bias,
    cotangent,
):
    group_index = lax.axis_index("fsdp")
    seq_index = lax.axis_index("seq")
    seq_count = lax.axis_size("seq")
    tok_rows, width = tokens.shape
    group_rows = tok_rows * seq_count
    head_cols = width // seq_count
    shard_rows = qkv_weight.shape[0]
    row_block = lambda value: lax.all_gather(value, "fsdp", axis=0, tiled=True)

    norms = jnp.pad(jnp.concatenate([norm_gain, norm_bias]).T, ((0, 0), (0, PAIR - 6)))
    qkv_mine = own_block(qkv_weight.reshape(shard_rows, 3, width), 2).reshape(shard_rows, 3 * head_cols)
    first = row_block(jnp.concatenate([qkv_mine, norms], axis=1))
    w_q, w_kv, w_qkv = first[:, :head_cols], first[:, head_cols : 3 * head_cols], first[:, : 3 * head_cols]
    norm_rows = first[:, 3 * head_cols : 3 * head_cols + 6].astype(jnp.float32).T
    gains, biases = norm_rows[:3], norm_rows[3:]

    ckv_mine = own_block(cross_kv_weight.reshape(shard_rows, 2, width), 2).reshape(shard_rows, 2 * head_cols)
    second = row_block(jnp.concatenate([out_weight, cross_query_weight, cross_out_weight, ckv_mine], axis=1))
    full_out, full_cq, full_cout = second[:, :width], second[:, width : 2 * width], second[:, 2 * width : 3 * width]
    w_ckv = second[:, 3 * width :]

    starts, seg_group = clip_starts(segments, group_index, group_rows)
    slots = own_block(seg_group, 0) - group_index * (group_rows // SPAN)
    slots_wide = jnp.broadcast_to(slots[:, None], (tok_rows, PAIR))

    inputs = tokens.astype(jnp.float32)
    n_group, _ = normed(gathered(tokens, 0).astype(jnp.float32))
    normed_one = (n_group * gains[0] + biases[0]).astype(jnp.bfloat16)
    kv_own = matmul(normed_one, w_kv).astype(jnp.bfloat16)
    kv_before = passed_along(kv_own[group_rows - SPAN :], "fsdp", 1)
    queries = matmul(normed_one, w_q).astype(jnp.bfloat16)
    if head_cols % PAIR:
        pad_kv = lambda kv: jnp.concatenate([paired(kv[:, :head_cols]), paired(kv[:, head_cols:])], axis=1)
        queries, kv_own, kv_before = paired(queries), pad_kv(kv_own), pad_kv(kv_before)
    heads_out, log_totals = self_attend(queries, kv_before, kv_own, starts)
    attended = exchanged(heads_out[:, :head_cols], 0, 1)
    hidden_one = inputs + matmul(attended, full_out)

    text_rows = text.reshape(-1, width)
    text_count = text_rows.shape[0]
    ckv_part = matmul(text_rows, w_ckv).astype(jnp.bfloat16).reshape(text_count, 2, head_cols)
    cross_kv = gathered(ckv_part, 2)
    cross_k, cross_v = cross_kv[:, 0], cross_kv[:, 1]
    n_two, root_two = normed(hidden_one)
    normed_two = (n_two * gains[1] + biases[1]).astype(jnp.bfloat16)
    cross_query = matmul(normed_two, full_cq).astype(jnp.bfloat16)
    cross_result = cross_attend(cross_query, cross_k, cross_v, slots_wide)
    hidden_two = hidden_one + matmul(cross_result, full_cout)

    full_up, full_down = row_block(up_weight), row_block(down_weight)
    n_three, root_three = normed(hidden_two)
    normed_three = (n_three * gains[2] + biases[2]).astype(jnp.bfloat16)
    upward = matmul(normed_three, full_up)
    below = 0.5 * (1.0 + lax.erf(upward * (0.5**0.5)))
    active = (upward * below).astype(jnp.bfloat16)
    slope = below + upward * (jnp.exp(-0.5 * upward * upward) * 0.3989422804014327)
    layer_out = (hidden_two + matmul(active, full_down)).astype(jnp.bfloat16)

    grad_down, slope = lax.optimization_barrier((contract_rows(active, cotangent).astype(jnp.bfloat16), slope))
    grad_down = scattered(grad_down)
    grad_upward = (contract_cols(cotangent, full_down) * slope).astype(jnp.bfloat16)
    grad_up, grad_upward = lax.optimization_barrier(
        (contract_rows(normed_three, grad_upward).astype(jnp.bfloat16), grad_upward)
    )
    grad_up = scattered(grad_up)
    back_h2, gain_three, bias_three = norm_back(contract_cols(grad_upward, full_up), n_three, root_three, gains[2])
    grad_two = cotangent.astype(jnp.float32) + back_h2
    grad_two_low = grad_two.astype(jnp.bfloat16)
    grad_cout = contract_rows(cross_result, grad_two_low)
    grad_result = contract_cols(grad_two_low, full_cout).astype(jnp.bfloat16)
    grad_query_c, grad_text_k, grad_text_v = cross_attend_back(cross_query, grad_result, cross_k, cross_v, slots_wide)
    grad_cq = contract_rows(normed_two, grad_query_c)
    grad_text_kv = summed_block(jnp.stack([grad_text_k, grad_text_v], axis=1), 2)
    grad_text_kv = grad_text_kv.astype(jnp.bfloat16).reshape(text_count, 2 * head_cols)
    grad_text = contract_cols(grad_text_kv, w_ckv)
    grad_ckv = contract_rows(text_rows, grad_text_kv)
    back_h1, gain_two, bias_two = norm_back(contract_cols(grad_query_c, full_cq), n_two, root_two, gains[1])
    grad_one = grad_two + back_h1

    grad_one_low = grad_one.astype(jnp.bfloat16)
    grad_attended = contract_cols(grad_one_low, full_out).astype(jnp.bfloat16)
    grad_heads = paired(exchanged(grad_attended, 1, 0))
    grad_wout = contract_rows(attended, grad_one_low)
    middle = scattered(
        jnp.concatenate([part.astype(jnp.bfloat16) for part in (grad_wout, grad_cq, grad_cout, grad_ckv)], axis=1)
    )
    grad_q, grad_k_before, grad_v_before, grad_k, grad_v = self_attend_back(
        queries, grad_heads, heads_out, log_totals, kv_before, kv_own, starts
    )
    late = group_rows - SPAN
    owned = [grad_q[:, :head_cols]]
    for part, before in ((grad_k, grad_k_before), (grad_v, grad_v_before)):
        returned = passed_along(before[:, :head_cols], "fsdp", -1).astype(jnp.float32)
        part = part[:, :head_cols].astype(jnp.float32)
        part = jnp.concatenate([part[:late], part[late:] + returned]) if late else part + returned
        owned.append(part.astype(jnp.bfloat16))
    grad_proj = jnp.concatenate(owned, axis=1)
    grad_wqkv = scattered(contract_rows(normed_one, grad_proj))
    grad_normed_one = summed_block(contract_cols(grad_proj, w_qkv), 0)
    n_one, root_one = normed(inputs)
    back_x, gain_one, bias_one = norm_back(grad_normed_one, n_one, root_one, gains[0])
    grad_tokens = (grad_one + back_x).astype(jnp.bfloat16)

    grad_ckv = columns(middle[:, 3 * width :], 2)
    middle = whole(middle[:, : 3 * width])

    norm_grads = everywhere(jnp.stack([gain_one, gain_two, gain_three, bias_one, bias_two, bias_three]))
    norm_grads = lax.dynamic_slice_in_dim(norm_grads, group_index * shard_rows, shard_rows, 1)
    return (
        layer_out,
        grad_tokens,
        whole(grad_text.astype(jnp.bfloat16)).reshape(text.shape),
        columns(grad_wqkv, 3),
        middle[:, :width],
        middle[:, width : 2 * width],
        grad_ckv,
        middle[:, 2 * width :],
        whole(grad_up),
        whole(grad_down),
        norm_grads[:3],
        norm_grads[3:],
    )


def solution(mesh):
    rows, shard, copied = P(("fsdp", "seq"), None), P("fsdp", None), P(None, "fsdp")
    groups = P("fsdp", None, None)
    in_specs = (rows, P(), groups, *[shard] * 7, copied, copied, rows)
    out_specs = (rows, rows, groups, *[shard] * 7, copied, copied)
    return jax.shard_map(shards, mesh=mesh, in_specs=in_specs, out_specs=out_specs, check_vma=False)
```

```python
import functools

import jax
import jax.numpy as jnp
from jax import lax
from jax.experimental import pallas as pl
from jax.experimental.pallas import tpu as pltpu
from jax.sharding import PartitionSpec as P

HEADS = 24
HEAD = 64
PAIR = 2 * HEAD
TXT = 64
SPAN = 1536
EPS = 1e-05
NEG = -1e30
SCALE = HEAD**-0.5
VMEM_BYTES = 56 * 2**20


def matmul(left_side, right_side):
    return jnp.dot(left_side, right_side, preferred_element_type=jnp.float32)


def contract_rows(left_side, right_side):
    return lax.dot_general(
        left_side, right_side, (((0,), (0,)), ((), ())), preferred_element_type=jnp.float32
    )


def contract_cols(left_side, right_side):
    return lax.dot_general(
        left_side, right_side, (((1,), (1,)), ((), ())), preferred_element_type=jnp.float32
    )


TILE = 384


def tile_bounds(starts, reach, base, kv_rows):
    count = kv_rows // TILE
    first, last = starts[::TILE] - base, starts[TILE - 1 :: TILE] - base
    row0 = reach - base + jnp.arange(first.shape[0], dtype=jnp.int32) * TILE
    low = jnp.clip(first // TILE, 0, count)
    high = jnp.clip((row0 + TILE - 1) // TILE + 1, low, count)
    free_low = jnp.clip((last + TILE - 1) // TILE, low, high)
    free_high = jnp.clip((row0 + 1) // TILE, free_low, high)
    return jnp.stack([low, free_low, free_high, high], axis=1)


def pairs_a_step(width):
    return 3 if width % (3 * PAIR) == 0 else 1


def split_heads(block):
    lower = lax.broadcasted_iota(jnp.int32, (1, PAIR), 1) < HEAD
    zero = jnp.zeros((1, 1), block.dtype)
    return [jnp.where(lower, block, zero), jnp.where(lower, zero, block)]


def lanes(p):
    return slice(p * PAIR, (p + 1) * PAIR)


def tile_allowed(col0, row0, starts):
    at = col0 + lax.broadcasted_iota(jnp.int32, (TILE, TILE), 0)
    row = row0 + lax.broadcasted_iota(jnp.int32, (TILE, TILE), 1)
    return (at >= starts) & (at <= row)


def over_tiles(bounds, i, step, state):
    low, free_low, free_high, high = (bounds[i, n] for n in range(4))
    state = lax.fori_loop(low, free_low, functools.partial(step, True), state)
    state = lax.fori_loop(free_low, free_high, functools.partial(step, False), state)
    return lax.fori_loop(free_high, high, functools.partial(step, True), state)


def attend_kernel(bounds, q_ref, k_ref, v_ref, start_ref, *refs, reach, base, pairs, ends):
    i = pl.program_id(1)
    if ends:
        before_ref, o_ref, lse_ref, v_t = refs
    else:
        after_ref, v_t = refs

    @pl.when(i == 0)
    def _():
        for p in range(pairs):
            turned = v_ref[:, lanes(p)].T
            for h in range(2):
                v_t[2 * p + h, :HEAD] = turned[h * HEAD : (h + 1) * HEAD]
                v_t[2 * p + h, HEAD:] = jnp.ones((16, turned.shape[1]), jnp.bfloat16)

    halves = []
    for p in range(pairs):
        halves += split_heads(q_ref[:, lanes(p)] * jnp.bfloat16(SCALE))
    starts = start_ref[0]

    def step(masked, j, carried):
        rows = pl.ds(pl.multiple_of(j * TILE, TILE), TILE)
        if masked:
            allowed = tile_allowed(base + j * TILE, reach + i * TILE, starts)
        scores = []
        for n in range(2 * pairs):
            s = contract_cols(k_ref[rows, lanes(n // 2)], halves[n])
            scores.append(jnp.where(allowed, s, NEG) if masked else s)
        out = []
        for n, (top, total) in enumerate(carried):
            new_top = jnp.maximum(top, jnp.max(scores[n], axis=0, keepdims=True))
            weights = jnp.exp(scores[n] - new_top).astype(jnp.bfloat16)
            total = total * jnp.exp(top - new_top) + matmul(v_t[n, :, rows], weights)
            out.append((new_top, total))
        return tuple(out)

    if ends:
        state = tuple((before_ref[0, 0, n, HEAD + 8 : HEAD + 9], before_ref[0, 0, n]) for n in range(2 * pairs))
    else:
        nothing = (jnp.full((1, TILE), NEG, jnp.float32), jnp.zeros((HEAD + 16, TILE), jnp.float32))
        state = (nothing,) * (2 * pairs)
    state = over_tiles(bounds, i, step, state)
    if not ends:
        for n, (top, total) in enumerate(state):
            after_ref[0, 0, n, : HEAD + 8] = total[: HEAD + 8]
            after_ref[0, 0, n, HEAD + 8 :] = jnp.broadcast_to(top, (8, TILE))
        return
    for p in range(pairs):
        outs = []
        for n in (2 * p, 2 * p + 1):
            top, total = state[n]
            count = total[HEAD : HEAD + 1]
            outs.append(total[:HEAD] / count)
            lse_ref[0, 0, n : n + 1, :] = top + jnp.log(count)
        o_ref[:, lanes(p)] = jnp.concatenate(outs, axis=0).T.astype(o_ref.dtype)


def attend_specs(rows, kv_rows, width):
    pairs = pairs_a_step(width)
    wide = pairs * PAIR
    steps = width // wide
    block = pl.BlockSpec((TILE, wide), lambda p, i, b: (i, p))
    keys = pl.BlockSpec((kv_rows, wide), lambda p, i, b: (0, p))
    values = pl.BlockSpec((kv_rows, wide), lambda p, i, b: (0, steps + p))
    by_tile = lambda *shape: pl.BlockSpec((1, 1, *shape, TILE), lambda p, i, b: (p, i, *[0] * len(shape), 0))
    starts = pl.BlockSpec((1, 1, TILE), lambda p, i, b: (i, 0, 0))
    return pairs, wide, (steps, rows // TILE), block, keys, values, by_tile, starts


def self_attend(q, kv, starts, reach, base, before=None):
    rows, width = q.shape
    kv_rows = kv.shape[0]
    ends = before is not None
    pairs, wide, grid, block, keys, values, by_tile, start_block = attend_specs(rows, kv_rows, width)
    state = by_tile(2 * pairs, HEAD + 16)
    state_shape = jax.ShapeDtypeStruct((*grid, 2 * pairs, HEAD + 16, TILE), jnp.float32)
    spec = pltpu.PrefetchScalarGridSpec(
        num_scalar_prefetch=1,
        grid=grid,
        in_specs=[block, keys, values, start_block] + [state] * ends,
        out_specs=[block, by_tile(8)] if ends else state,
        scratch_shapes=[pltpu.VMEM((2 * pairs, HEAD + 16, kv_rows), jnp.bfloat16)],
    )
    return pl.pallas_call(
        functools.partial(attend_kernel, reach=reach, base=base, pairs=pairs, ends=ends),
        grid_spec=spec,
        out_shape=[
            jax.ShapeDtypeStruct((rows, width), jnp.bfloat16),
            jax.ShapeDtypeStruct((*grid, 8, TILE), jnp.float32),
        ]
        if ends
        else state_shape,
        compiler_params=pltpu.CompilerParams(vmem_limit_bytes=VMEM_BYTES),
        cost_estimate=pl.CostEstimate(
            flops=10 * rows * kv_rows * width,
            bytes_accessed=16 * rows * width,
            transcendentals=rows * kv_rows * width // HEAD // 2,
        ),
        name="self_attend",
    )(tile_bounds(starts, reach, base, kv_rows), q, kv, kv, starts.reshape(-1, 1, TILE), *([before] if ends else []))


def attend_back_kernel(bounds, q_ref, g_ref, o_ref, lse_ref, k_ref, v_ref, start_ref, *refs, reach, base, pairs, ends):
    i = pl.program_id(1)
    if ends:
        before_ref, dq_ref, dk_ref, dv_ref, dk_sum, dv_sum, k_t = refs
    else:
        after_ref, dk_ref, dv_ref, dk_sum, dv_sum, k_t = refs

    @pl.when(i == 0)
    def _():
        k_t[...] = k_ref[...].T
        dk_sum[...] = jnp.zeros_like(dk_sum)
        dv_sum[...] = jnp.zeros_like(dv_sum)

    queries, grads, inner, logs = [], [], [], []
    for p in range(pairs):
        grad = g_ref[:, lanes(p)]
        queries += split_heads(q_ref[:, lanes(p)] * jnp.bfloat16(SCALE))
        grads += split_heads(grad)
        product = (grad.astype(jnp.float32) * o_ref[:, lanes(p)].astype(jnp.float32)).T
        for h in range(2):
            inner.append(jnp.sum(product[h * HEAD : (h + 1) * HEAD], axis=0, keepdims=True))
            logs.append(lse_ref[0, 0, 2 * p + h : 2 * p + h + 1])
    starts = start_ref[0]

    def step(masked, j, carried):
        rows = pl.ds(pl.multiple_of(j * TILE, TILE), TILE)
        if masked:
            allowed = tile_allowed(base + j * TILE, reach + i * TILE, starts)
        out = []
        for p in range(pairs):
            keys, values = k_ref[rows, lanes(p)], v_ref[rows, lanes(p)]
            dks, dvs = [], []
            for n in (2 * p, 2 * p + 1):
                s = contract_cols(keys, queries[n])
                d = contract_cols(values, grads[n])
                if masked:
                    s = jnp.where(allowed, s, NEG)
                shares = jnp.exp(s - logs[n])
                ds = (shares * (d - inner[n])).astype(jnp.bfloat16)
                dvs.append(matmul(shares.astype(jnp.bfloat16), grads[n]))
                dks.append(matmul(ds, queries[n]))
                out.append(carried[n] + matmul(k_t[n * HEAD : (n + 1) * HEAD, rows], ds))
            dv_sum[rows, lanes(p)] += dvs[0] + dvs[1]
            dk_sum[rows, lanes(p)] += dks[0] + dks[1]
        return tuple(out)

    if ends:
        state = tuple(before_ref[0, 0, n] for n in range(2 * pairs))
    else:
        state = (jnp.zeros((HEAD, TILE), jnp.float32),) * (2 * pairs)
    state = over_tiles(bounds, i, step, state)
    if ends:
        for p in range(pairs):
            turned = jnp.concatenate([state[2 * p], state[2 * p + 1]], axis=0).T
            dq_ref[:, lanes(p)] = (turned * SCALE).astype(dq_ref.dtype)
    else:
        for n in range(2 * pairs):
            after_ref[0, 0, n] = state[n]

    @pl.when(i == pl.num_programs(1) - 1)
    def _():
        dk_ref[...] = dk_sum[...].astype(dk_ref.dtype)
        dv_ref[...] = dv_sum[...].astype(dv_ref.dtype)


def self_attend_back(q, grad, o, lse, kv, starts, reach, base, before=None):
    rows, width = q.shape
    kv_rows = kv.shape[0]
    ends = before is not None
    pairs, wide, grid, block, keys, values, by_tile, start_block = attend_specs(rows, kv_rows, width)
    state = by_tile(2 * pairs, HEAD)
    shape = lambda n: jax.ShapeDtypeStruct((n, width), jnp.bfloat16)
    spec = pltpu.PrefetchScalarGridSpec(
        num_scalar_prefetch=1,
        grid=grid,
        in_specs=[block, block, block, by_tile(8), keys, values, start_block] + [state] * ends,
        out_specs=[block if ends else state, keys, keys],
        scratch_shapes=[
            pltpu.VMEM((kv_rows, wide), jnp.float32),
            pltpu.VMEM((kv_rows, wide), jnp.float32),
            pltpu.VMEM((wide, kv_rows), jnp.bfloat16),
        ],
    )
    return pl.pallas_call(
        functools.partial(attend_back_kernel, reach=reach, base=base, pairs=pairs, ends=ends),
        grid_spec=spec,
        out_shape=[
            shape(rows) if ends else jax.ShapeDtypeStruct((*grid, 2 * pairs, HEAD, TILE), jnp.float32),
            shape(kv_rows),
            shape(kv_rows),
        ],
        compiler_params=pltpu.CompilerParams(vmem_limit_bytes=VMEM_BYTES),
        cost_estimate=pl.CostEstimate(
            flops=20 * rows * kv_rows * width,
            bytes_accessed=20 * rows * width,
            transcendentals=rows * kv_rows * width // HEAD // 2,
        ),
        name="self_attend_back",
    )(
        tile_bounds(starts, reach, base, kv_rows), q, grad, o, lse, kv, kv, starts.reshape(-1, 1, TILE),
        *([before] if ends else []),
    )


def cross_kernel(q_ref, k_ref, v_ref, slot_ref, o_ref):
    lower = lax.broadcasted_iota(jnp.int32, (1, PAIR), 1) < HEAD
    zero = jnp.zeros((1, 1), jnp.bfloat16)
    scaled = q_ref[...] * jnp.bfloat16(SCALE)
    tokens, texts = q_ref.shape[0], k_ref.shape[0]
    allowed = slot_ref[:, :1] == lax.broadcasted_iota(jnp.int32, (tokens, texts), 1) // TXT
    results = []
    for h in range(2):
        half = jnp.where(lower, scaled, zero) if h == 0 else jnp.where(lower, zero, scaled)
        scores = jnp.where(allowed, contract_cols(half, k_ref[...]), NEG)
        weights = jnp.exp(scores - jnp.max(scores, axis=1, keepdims=True))
        shares = weights / jnp.sum(weights, axis=1, keepdims=True)
        results.append(matmul(shares.astype(jnp.bfloat16), v_ref[...]))
    o_ref[...] = jnp.where(lower, results[0], results[1]).astype(o_ref.dtype)


def cross_attend(q, k, v, slots_wide):
    tokens, width = q.shape
    texts = k.shape[0]
    column = lambda p: (0, p)
    return pl.pallas_call(
        cross_kernel,
        grid=(width // PAIR,),
        in_specs=[
            pl.BlockSpec((tokens, PAIR), column),
            pl.BlockSpec((texts, PAIR), column),
            pl.BlockSpec((texts, PAIR), column),
            pl.BlockSpec((tokens, PAIR), lambda p: (0, 0)),
        ],
        out_specs=pl.BlockSpec((tokens, PAIR), column),
        out_shape=jax.ShapeDtypeStruct(q.shape, jnp.bfloat16),
        compiler_params=pltpu.CompilerParams(vmem_limit_bytes=VMEM_BYTES),
        cost_estimate=pl.CostEstimate(
            flops=8 * tokens * texts * width,
            bytes_accessed=4 * tokens * width,
            transcendentals=tokens * texts * width // HEAD,
        ),
        name="cross_attend",
    )(q, k, v, slots_wide)


def cross_back_kernel(q_ref, g_ref, k_ref, v_ref, slot_ref, dq_ref, dk_ref, dv_ref):
    lower = lax.broadcasted_iota(jnp.int32, (1, PAIR), 1) < HEAD
    zero = jnp.zeros((1, 1), jnp.bfloat16)
    scaled = q_ref[...] * jnp.bfloat16(SCALE)
    grad = g_ref[...]
    keys = k_ref[...]
    tokens, texts = q_ref.shape[0], k_ref.shape[0]
    allowed = slot_ref[:, :1] == lax.broadcasted_iota(jnp.int32, (tokens, texts), 1) // TXT
    dqs, dks, dvs = [], [], []
    for h in range(2):
        q_half = jnp.where(lower, scaled, zero) if h == 0 else jnp.where(lower, zero, scaled)
        g_half = jnp.where(lower, grad, zero) if h == 0 else jnp.where(lower, zero, grad)
        scores = jnp.where(allowed, contract_cols(q_half, keys), NEG)
        weights = jnp.exp(scores - jnp.max(scores, axis=1, keepdims=True))
        shares = weights / jnp.sum(weights, axis=1, keepdims=True)
        grad_shares = contract_cols(g_half, v_ref[...])
        inner = jnp.sum(shares * grad_shares, axis=1, keepdims=True)
        grad_scores = (shares * (grad_shares - inner)).astype(jnp.bfloat16)
        dqs.append(matmul(grad_scores, keys))
        dks.append(contract_rows(grad_scores, q_half))
        dvs.append(contract_rows(shares.astype(jnp.bfloat16), g_half))
    dq_ref[...] = (jnp.where(lower, dqs[0], dqs[1]) * SCALE).astype(dq_ref.dtype)
    dk_ref[...] = dks[0] + dks[1]
    dv_ref[...] = dvs[0] + dvs[1]


def cross_attend_back(q, grad, k, v, slots_wide):
    tokens, width = q.shape
    texts = k.shape[0]
    column = lambda p: (0, p)
    return pl.pallas_call(
        cross_back_kernel,
        grid=(width // PAIR,),
        in_specs=[
            pl.BlockSpec((tokens, PAIR), column),
            pl.BlockSpec((tokens, PAIR), column),
            pl.BlockSpec((texts, PAIR), column),
            pl.BlockSpec((texts, PAIR), column),
            pl.BlockSpec((tokens, PAIR), lambda p: (0, 0)),
        ],
        out_specs=[
            pl.BlockSpec((tokens, PAIR), column),
            pl.BlockSpec((texts, PAIR), column),
            pl.BlockSpec((texts, PAIR), column),
        ],
        out_shape=[
            jax.ShapeDtypeStruct(q.shape, jnp.bfloat16),
            jax.ShapeDtypeStruct((texts, width), jnp.float32),
            jax.ShapeDtypeStruct((texts, width), jnp.float32),
        ],
        compiler_params=pltpu.CompilerParams(vmem_limit_bytes=VMEM_BYTES),
        cost_estimate=pl.CostEstimate(
            flops=20 * tokens * texts * width,
            bytes_accessed=6 * tokens * width,
            transcendentals=tokens * texts * width // HEAD,
        ),
        name="cross_attend_back",
    )(q, grad, k, v, slots_wide)


def swap(value, axis, bit):
    count = lax.axis_size(axis)
    return lax.ppermute(value, axis, [(i, i ^ bit) for i in range(count)])


def passed_along(value, axis, steps):
    count = lax.axis_size(axis)
    initial, last = (max(0, -steps), min(count, count - steps))
    return lax.ppermute(value, axis, [(source, source + steps) for source in range(initial, last)])


def in_order(mine, other, dim):
    second = lax.axis_index("seq") == 1
    return jnp.concatenate([jnp.where(second, other, mine), jnp.where(second, mine, other)], axis=dim)


def gathered(value, dim):
    if lax.axis_size("seq") == 2:
        return in_order(value, swap(value, "seq", 1), dim)
    return lax.all_gather(value, "seq", axis=dim, tiled=True)


def own_block(value, dim):
    size = value.shape[dim] // lax.axis_size("seq")
    return lax.dynamic_slice_in_dim(value, lax.axis_index("seq") * size, size, dim)


def other_block(value, dim):
    size = value.shape[dim] // 2
    return lax.dynamic_slice_in_dim(value, (1 - lax.axis_index("seq")) * size, size, dim)


def exchanged(value, split, concat):
    if lax.axis_size("seq") == 2:
        return in_order(own_block(value, split), swap(other_block(value, split), "seq", 1), concat)
    return lax.all_to_all(value, "seq", split_axis=split, concat_axis=concat, tiled=True)


def summed_block(value, dim):
    if lax.axis_size("seq") == 2:
        received = swap(other_block(value, dim).astype(jnp.bfloat16), "seq", 1)
        return own_block(value, dim) + received.astype(jnp.float32)
    return lax.psum_scatter(
        value.astype(jnp.bfloat16), "seq", scatter_dimension=dim, tiled=True
    ).astype(jnp.float32)


def paired(value):
    short = -value.shape[-1] % PAIR
    return jnp.pad(value, ((0, 0), (0, short))) if short else value


def normed(values):
    average = jnp.mean(values, axis=-1, keepdims=True)
    centred = values - average
    spread = jnp.mean(centred * centred, axis=-1, keepdims=True)
    root = lax.rsqrt(spread + EPS)
    return centred * root, root


def norm_back(grad, n, root, gain):
    a = grad * gain
    back = (a - jnp.mean(a, axis=-1, keepdims=True) - n * jnp.mean(a * n, axis=-1, keepdims=True)) * root
    return back, jnp.sum(grad * n, axis=0), jnp.sum(grad, axis=0)


def scattered(grad):
    return lax.psum_scatter(grad.astype(jnp.bfloat16), "fsdp", scatter_dimension=0, tiled=True)


def whole(part):
    if lax.axis_size("seq") == 2:
        return part.astype(jnp.float32) + swap(part, "seq", 1).astype(jnp.float32)
    return lax.psum(part, "seq").astype(jnp.float32)


def columns(part, blocks):
    split = part.reshape(part.shape[0], blocks, -1)
    return gathered(split, 2).reshape(part.shape[0], -1).astype(jnp.float32)


def four_sums(lefts, rights):
    chip, core = lax.axis_index("fsdp") // 2, lax.axis_index("fsdp") % 2
    seq_index, seq_count = lax.axis_index("seq"), lax.axis_size("seq")
    chips = lax.axis_size("fsdp") // 2
    if seq_count != 2:
        sums = [[scattered(contract_rows(a, b)) for a, b in zip(*each)] for each in zip(lefts, rights)]
        return [[whole(part) for part in each] for each in sums]

    def products(place):
        pick = lambda parts: jnp.stack([jnp.where(place == 0, a, b) for a, b in zip(*parts)])
        return jnp.einsum("kta,ktb->kab", pick(lefts), pick(rights), preferred_element_type=jnp.float32).astype(
            jnp.bfloat16
        )

    take = lambda value, place, dim=0: lax.dynamic_index_in_dim(value, place, dim, keepdims=False).astype(jnp.float32)
    sent = swap(products(1 - core), "fsdp", 1)
    kept = products(core)
    other = swap((take(kept, 1 - seq_index) + take(sent, 1 - seq_index)).astype(jnp.bfloat16), "seq", 1)
    total = take(kept, seq_index) + take(sent, seq_index) + other.astype(jnp.float32)
    bit, at = 2, chip
    total = total.reshape(chips, -1, total.shape[-1])
    while chips > 1:
        chips //= 2
        total = total.astype(jnp.bfloat16).reshape(chips, 2, *total.shape[1:])
        more = swap(take(total, 1 - at % 2, 1).astype(jnp.bfloat16), "fsdp", bit)
        total = take(total, at % 2, 1) + more.astype(jnp.float32)
        bit, at = bit * 2, at // 2
    total = total.astype(jnp.bfloat16).reshape(2, -1, total.shape[-1])
    mine = take(total, core).astype(jnp.bfloat16)
    theirs = swap(take(total, 1 - core).astype(jnp.bfloat16), "fsdp", 1)
    pair = jnp.stack([jnp.where(core == 0, mine, theirs), jnp.where(core == 0, theirs, mine)])
    beside = swap(pair, "seq", 1)
    by_seq = [jnp.where(seq_index == 0, pair, beside), jnp.where(seq_index == 0, beside, pair)]
    return [[by_seq[s][c].astype(jnp.float32) for s in range(2)] for c in range(2)]


def clip_starts(segments, group_index, group_rows):
    padded = jnp.concatenate([jnp.full((SPAN,), -1, jnp.int32), segments])
    spans = lax.dynamic_slice_in_dim(padded, group_index * group_rows, SPAN + group_rows)
    spans = spans.reshape(-1, SPAN)
    ahead = jnp.sum((spans == spans[:, :1]).astype(jnp.int32), axis=1)
    firsts = ahead + jnp.arange(spans.shape[0], dtype=jnp.int32) * SPAN
    late = spans[1:] != spans[1:, :1]
    return jnp.where(late, firsts[1:, None], firsts[:-1, None]).reshape(group_rows), spans[1:].reshape(group_rows)


def shards(
    tokens,
    segments,
    text,
    qkv_weight,
    out_weight,
    cross_query_weight,
    cross_kv_weight,
    cross_out_weight,
    up_weight,
    down_weight,
    norm_gain,
    norm_bias,
    cotangent,
):
    group_index = lax.axis_index("fsdp")
    seq_index = lax.axis_index("seq")
    seq_count = lax.axis_size("seq")
    tok_rows, width = tokens.shape
    group_rows = tok_rows * seq_count
    head_cols = width // seq_count
    shard_rows = qkv_weight.shape[0]
    row_block = lambda value: lax.all_gather(value, "fsdp", axis=0, tiled=True)

    norms = jnp.pad(jnp.concatenate([norm_gain, norm_bias]).T, ((0, 0), (0, PAIR - 6)))
    qkv_mine = own_block(qkv_weight.reshape(shard_rows, 3, width), 2).reshape(shard_rows, 3 * head_cols)
    first = row_block(jnp.concatenate([qkv_mine, norms], axis=1))
    w_q, w_kv, w_qkv = first[:, :head_cols], first[:, head_cols : 3 * head_cols], first[:, : 3 * head_cols]
    norm_rows = first[:, 3 * head_cols : 3 * head_cols + 6].astype(jnp.float32).T
    gains, biases = norm_rows[:3], norm_rows[3:]

    ckv_mine = own_block(cross_kv_weight.reshape(shard_rows, 2, width), 2).reshape(shard_rows, 2 * head_cols)
    second = row_block(jnp.concatenate([out_weight, cross_query_weight, cross_out_weight, ckv_mine], axis=1))
    full_out, full_cq, full_cout = second[:, :width], second[:, width : 2 * width], second[:, 2 * width : 3 * width]
    w_ckv = second[:, 3 * width :]

    starts, seg_group = clip_starts(segments, group_index, group_rows)
    slots = own_block(seg_group, 0) - group_index * (group_rows // SPAN)
    slots_wide = jnp.broadcast_to(slots[:, None], (tok_rows, PAIR))

    inputs = tokens.astype(jnp.float32)
    n_group, _ = normed(gathered(tokens, 0).astype(jnp.float32))
    normed_one = (n_group * gains[0] + biases[0]).astype(jnp.bfloat16)
    kv_own = matmul(normed_one, w_kv).astype(jnp.bfloat16)
    kv_before = passed_along(kv_own[group_rows - SPAN :], "fsdp", 1)
    queries = matmul(normed_one, w_q).astype(jnp.bfloat16)
    if head_cols % PAIR:
        pad_kv = lambda kv: jnp.concatenate([paired(kv[:, :head_cols]), paired(kv[:, head_cols:])], axis=1)
        queries, kv_own, kv_before = paired(queries), pad_kv(kv_own), pad_kv(kv_before)
    heads_state = self_attend(queries, kv_own, starts, SPAN, SPAN)
    heads_out, log_totals = self_attend(queries, kv_before, starts, SPAN, 0, heads_state)
    attended = exchanged(heads_out[:, :head_cols], 0, 1)
    hidden_one = inputs + matmul(attended, full_out)

    text_rows = text.reshape(-1, width)
    text_count = text_rows.shape[0]
    ckv_part = matmul(text_rows, w_ckv).astype(jnp.bfloat16).reshape(text_count, 2, head_cols)
    cross_kv = gathered(ckv_part, 2)
    cross_k, cross_v = cross_kv[:, 0], cross_kv[:, 1]
    n_two, root_two = normed(hidden_one)
    normed_two = (n_two * gains[1] + biases[1]).astype(jnp.bfloat16)
    cross_query = matmul(normed_two, full_cq).astype(jnp.bfloat16)
    cross_result = cross_attend(cross_query, cross_k, cross_v, slots_wide)
    hidden_two = hidden_one + matmul(cross_result, full_cout)

    full_up, full_down = row_block(up_weight), row_block(down_weight)
    n_three, root_three = normed(hidden_two)
    normed_three = (n_three * gains[2] + biases[2]).astype(jnp.bfloat16)
    upward = matmul(normed_three, full_up)
    below = 0.5 * (1.0 + lax.erf(upward * (0.5**0.5)))
    active = (upward * below).astype(jnp.bfloat16)
    slope = below + upward * (jnp.exp(-0.5 * upward * upward) * 0.3989422804014327)
    layer_out = (hidden_two + matmul(active, full_down)).astype(jnp.bfloat16)

    grad_down, slope = lax.optimization_barrier((contract_rows(active, cotangent).astype(jnp.bfloat16), slope))
    grad_down = scattered(grad_down)
    grad_upward = (contract_cols(cotangent, full_down) * slope).astype(jnp.bfloat16)
    grad_up, grad_upward = lax.optimization_barrier(
        (contract_rows(normed_three, grad_upward[:, :-width]).astype(jnp.bfloat16), grad_upward)
    )
    grad_up = scattered(lax.optimization_barrier((grad_up, grad_down))[0])
    back_h2, gain_three, bias_three = norm_back(contract_cols(grad_upward, full_up), n_three, root_three, gains[2])
    grad_two = cotangent.astype(jnp.float32) + back_h2
    grad_two_low = grad_two.astype(jnp.bfloat16)
    grad_result = contract_cols(grad_two_low, full_cout).astype(jnp.bfloat16)
    grad_query_c, grad_text_k, grad_text_v = cross_attend_back(cross_query, grad_result, cross_k, cross_v, slots_wide)
    grad_text_kv = summed_block(jnp.stack([grad_text_k, grad_text_v], axis=1), 2)
    grad_text_kv = grad_text_kv.astype(jnp.bfloat16).reshape(text_count, 2 * head_cols)
    grad_text = contract_cols(grad_text_kv, w_ckv)
    grad_ckv = contract_rows(text_rows, grad_text_kv).astype(jnp.bfloat16)
    grad_ckv = scattered(lax.optimization_barrier((grad_ckv, grad_up))[0])
    back_h1, gain_two, bias_two = norm_back(contract_cols(grad_query_c, full_cq), n_two, root_two, gains[1])
    grad_one = grad_two + back_h1

    grad_one_low = grad_one.astype(jnp.bfloat16)
    grad_attended = contract_cols(grad_one_low, full_out).astype(jnp.bfloat16)
    grad_heads = paired(exchanged(grad_attended, 1, 0))
    small = four_sums(
        ((attended, normed_two), (cross_result, normed_three)),
        ((grad_one_low, grad_query_c), (grad_two_low, grad_upward[:, -width:])),
    )
    back_args = (queries, grad_heads, heads_out, log_totals)
    query_state, *grad_before = self_attend_back(*back_args, kv_before, starts, SPAN, 0)
    returned = [passed_along(part[:, :head_cols], "fsdp", -1).astype(jnp.float32) for part in grad_before]
    grad_q, *grad_own = self_attend_back(*back_args, kv_own, starts, SPAN, SPAN, query_state)
    late = group_rows - SPAN
    owned = [grad_q[:, :head_cols]]
    for part, more in zip(grad_own, returned):
        part = part[:, :head_cols].astype(jnp.float32)
        part = jnp.concatenate([part[:late], part[late:] + more]) if late else part + more
        owned.append(part.astype(jnp.bfloat16))
    grad_proj = jnp.concatenate(owned, axis=1)
    grad_wqkv, grad_proj = lax.optimization_barrier(
        (contract_rows(normed_one, grad_proj).astype(jnp.bfloat16), grad_proj)
    )
    grad_wqkv = scattered(lax.optimization_barrier((grad_wqkv, grad_ckv))[0])
    grad_normed_one = summed_block(contract_cols(grad_proj, w_qkv), 0)
    n_one, root_one = normed(inputs)
    back_x, gain_one, bias_one = norm_back(grad_normed_one, n_one, root_one, gains[0])
    grad_tokens = (grad_one + back_x).astype(jnp.bfloat16)

    norm_grads = lax.psum(
        jnp.stack([gain_one, gain_two, gain_three, bias_one, bias_two, bias_three]), ("fsdp", "seq")
    )
    norm_grads = lax.dynamic_slice_in_dim(norm_grads, group_index * shard_rows, shard_rows, 1)
    return (
        layer_out,
        grad_tokens,
        whole(grad_text.astype(jnp.bfloat16)).reshape(text.shape),
        columns(grad_wqkv, 3),
        small[0][0],
        small[0][1],
        columns(grad_ckv, 2),
        small[1][0],
        jnp.concatenate([whole(grad_up), small[1][1]], axis=1),
        whole(grad_down),
        norm_grads[:3],
        norm_grads[3:],
    )


def solution(mesh):
    rows, shard, copied = P(("fsdp", "seq"), None), P("fsdp", None), P(None, "fsdp")
    groups = P("fsdp", None, None)
    in_specs = (rows, P(), groups, *[shard] * 7, copied, copied, rows)
    out_specs = (rows, rows, groups, *[shard] * 7, copied, copied)
    return jax.shard_map(shards, mesh=mesh, in_specs=in_specs, out_specs=out_specs, check_vma=False)
```

```python
import functools

import jax
import jax.numpy as jnp
from jax import lax
from jax.experimental import pallas as pl
from jax.experimental.pallas import tpu as pltpu
from jax.sharding import PartitionSpec as P

HEADS = 24
HEAD = 64
PAIR = 2 * HEAD
TXT = 64
SPAN = 1536
EPS = 1e-05
NEG = -1e30
SCALE = HEAD**-0.5
VMEM_BYTES = 56 * 2**20


def matmul(left_side, right_side):
    return jnp.dot(left_side, right_side, preferred_element_type=jnp.float32)


def contract_rows(left_side, right_side):
    return lax.dot_general(
        left_side, right_side, (((0,), (0,)), ((), ())), preferred_element_type=jnp.float32
    )


def contract_cols(left_side, right_side):
    return lax.dot_general(
        left_side, right_side, (((1,), (1,)), ((), ())), preferred_element_type=jnp.float32
    )


TILE = 384


def tile_bounds(starts, reach, base, kv_rows):
    count = kv_rows // TILE
    first, last = starts[::TILE] - base, starts[TILE - 1 :: TILE] - base
    row0 = reach - base + jnp.arange(first.shape[0], dtype=jnp.int32) * TILE
    low = jnp.clip(first // TILE, 0, count)
    high = jnp.clip((row0 + TILE - 1) // TILE + 1, low, count)
    free_low = jnp.clip((last + TILE - 1) // TILE, low, high)
    free_high = jnp.clip((row0 + 1) // TILE, free_low, high)
    return jnp.stack([low, free_low, free_high, high], axis=1)


def pairs_a_step(width):
    return 3 if width % (3 * PAIR) == 0 else 1


def split_heads(block):
    lower = lax.broadcasted_iota(jnp.int32, (1, PAIR), 1) < HEAD
    zero = jnp.zeros((1, 1), block.dtype)
    return [jnp.where(lower, block, zero), jnp.where(lower, zero, block)]


def lanes(p):
    return slice(p * PAIR, (p + 1) * PAIR)


def tile_allowed(col0, row0, starts):
    at = col0 + lax.broadcasted_iota(jnp.int32, (TILE, TILE), 0)
    row = row0 + lax.broadcasted_iota(jnp.int32, (TILE, TILE), 1)
    return (at >= starts) & (at <= row)


def over_tiles(bounds, i, step, state):
    low, free_low, free_high, high = (bounds[i, n] for n in range(4))
    state = lax.fori_loop(low, free_low, functools.partial(step, True), state)
    state = lax.fori_loop(free_low, free_high, functools.partial(step, False), state)
    return lax.fori_loop(free_high, high, functools.partial(step, True), state)


def attend_kernel(bounds, q_ref, k_ref, v_ref, start_ref, *refs, reach, base, pairs, ends):
    i = pl.program_id(1)
    if ends:
        before_ref, o_ref, lse_ref, v_t = refs
    else:
        after_ref, v_t = refs

    @pl.when(i == 0)
    def _():
        for p in range(pairs):
            turned = v_ref[:, lanes(p)].T
            for h in range(2):
                v_t[2 * p + h, :HEAD] = turned[h * HEAD : (h + 1) * HEAD]
                v_t[2 * p + h, HEAD:] = jnp.ones((16, turned.shape[1]), jnp.bfloat16)

    halves = []
    for p in range(pairs):
        halves += split_heads(q_ref[:, lanes(p)] * jnp.bfloat16(SCALE))
    starts = start_ref[0]

    def step(masked, j, carried):
        rows = pl.ds(pl.multiple_of(j * TILE, TILE), TILE)
        if masked:
            allowed = tile_allowed(base + j * TILE, reach + i * TILE, starts)
        scores = []
        for n in range(2 * pairs):
            s = contract_cols(k_ref[rows, lanes(n // 2)], halves[n])
            scores.append(jnp.where(allowed, s, NEG) if masked else s)
        out = []
        for n, (top, total) in enumerate(carried):
            new_top = jnp.maximum(top, jnp.max(scores[n], axis=0, keepdims=True))
            weights = jnp.exp(scores[n] - new_top).astype(jnp.bfloat16)
            total = total * jnp.exp(top - new_top) + matmul(v_t[n, :, rows], weights)
            out.append((new_top, total))
        return tuple(out)

    if ends:
        state = tuple((before_ref[0, 0, n, HEAD + 8 : HEAD + 9], before_ref[0, 0, n]) for n in range(2 * pairs))
    else:
        nothing = (jnp.full((1, TILE), NEG, jnp.float32), jnp.zeros((HEAD + 16, TILE), jnp.float32))
        state = (nothing,) * (2 * pairs)
    state = over_tiles(bounds, i, step, state)
    if not ends:
        for n, (top, total) in enumerate(state):
            after_ref[0, 0, n, : HEAD + 8] = total[: HEAD + 8]
            after_ref[0, 0, n, HEAD + 8 :] = jnp.broadcast_to(top, (8, TILE))
        return
    for p in range(pairs):
        outs = []
        for n in (2 * p, 2 * p + 1):
            top, total = state[n]
            count = total[HEAD : HEAD + 1]
            outs.append(total[:HEAD] / count)
            lse_ref[0, 0, n : n + 1, :] = top + jnp.log(count)
        o_ref[:, lanes(p)] = jnp.concatenate(outs, axis=0).T.astype(o_ref.dtype)


def attend_specs(rows, kv_rows, width):
    pairs = pairs_a_step(width)
    wide = pairs * PAIR
    steps = width // wide
    block = pl.BlockSpec((TILE, wide), lambda p, i, b: (i, p))
    keys = pl.BlockSpec((kv_rows, wide), lambda p, i, b: (0, p))
    values = pl.BlockSpec((kv_rows, wide), lambda p, i, b: (0, steps + p))
    by_tile = lambda *shape: pl.BlockSpec((1, 1, *shape, TILE), lambda p, i, b: (p, i, *[0] * len(shape), 0))
    starts = pl.BlockSpec((1, 1, TILE), lambda p, i, b: (i, 0, 0))
    return pairs, wide, (steps, rows // TILE), block, keys, values, by_tile, starts


def self_attend(q, kv, starts, reach, base, before=None):
    rows, width = q.shape
    kv_rows = kv.shape[0]
    ends = before is not None
    pairs, wide, grid, block, keys, values, by_tile, start_block = attend_specs(rows, kv_rows, width)
    state = by_tile(2 * pairs, HEAD + 16)
    state_shape = jax.ShapeDtypeStruct((*grid, 2 * pairs, HEAD + 16, TILE), jnp.float32)
    spec = pltpu.PrefetchScalarGridSpec(
        num_scalar_prefetch=1,
        grid=grid,
        in_specs=[block, keys, values, start_block] + [state] * ends,
        out_specs=[block, by_tile(8)] if ends else state,
        scratch_shapes=[pltpu.VMEM((2 * pairs, HEAD + 16, kv_rows), jnp.bfloat16)],
    )
    return pl.pallas_call(
        functools.partial(attend_kernel, reach=reach, base=base, pairs=pairs, ends=ends),
        grid_spec=spec,
        out_shape=[
            jax.ShapeDtypeStruct((rows, width), jnp.bfloat16),
            jax.ShapeDtypeStruct((*grid, 8, TILE), jnp.float32),
        ]
        if ends
        else state_shape,
        compiler_params=pltpu.CompilerParams(vmem_limit_bytes=VMEM_BYTES),
        cost_estimate=pl.CostEstimate(
            flops=rows * kv_rows * HEAD, bytes_accessed=rows * HEAD, transcendentals=0
        ),
        name="self_attend",
    )(tile_bounds(starts, reach, base, kv_rows), q, kv, kv, starts.reshape(-1, 1, TILE), *([before] if ends else []))


def attend_back_kernel(bounds, q_ref, g_ref, o_ref, lse_ref, k_ref, v_ref, start_ref, *refs, reach, base, pairs, ends):
    i = pl.program_id(1)
    if ends:
        before_ref, dq_ref, dk_ref, dv_ref, dk_sum, dv_sum, k_t = refs
    else:
        after_ref, dk_ref, dv_ref, dk_sum, dv_sum, k_t = refs

    @pl.when(i == 0)
    def _():
        k_t[...] = k_ref[...].T
        dk_sum[...] = jnp.zeros_like(dk_sum)
        dv_sum[...] = jnp.zeros_like(dv_sum)

    queries, grads, inner, logs = [], [], [], []
    for p in range(pairs):
        grad = g_ref[:, lanes(p)]
        queries += split_heads(q_ref[:, lanes(p)] * jnp.bfloat16(SCALE))
        grads += split_heads(grad)
        product = (grad.astype(jnp.float32) * o_ref[:, lanes(p)].astype(jnp.float32)).T
        for h in range(2):
            inner.append(jnp.sum(product[h * HEAD : (h + 1) * HEAD], axis=0, keepdims=True))
            logs.append(lse_ref[0, 0, 2 * p + h : 2 * p + h + 1])
    starts = start_ref[0]

    def step(masked, j, carried):
        rows = pl.ds(pl.multiple_of(j * TILE, TILE), TILE)
        if masked:
            allowed = tile_allowed(base + j * TILE, reach + i * TILE, starts)
        out = []
        for p in range(pairs):
            keys, values = k_ref[rows, lanes(p)], v_ref[rows, lanes(p)]
            dks, dvs = [], []
            for n in (2 * p, 2 * p + 1):
                s = contract_cols(keys, queries[n])
                d = contract_cols(values, grads[n])
                if masked:
                    s = jnp.where(allowed, s, NEG)
                shares = jnp.exp(s - logs[n])
                ds = (shares * (d - inner[n])).astype(jnp.bfloat16)
                dvs.append(matmul(shares.astype(jnp.bfloat16), grads[n]))
                dks.append(matmul(ds, queries[n]))
                out.append(carried[n] + matmul(k_t[n * HEAD : (n + 1) * HEAD, rows], ds))
            dv_sum[rows, lanes(p)] += dvs[0] + dvs[1]
            dk_sum[rows, lanes(p)] += dks[0] + dks[1]
        return tuple(out)

    if ends:
        state = tuple(before_ref[0, 0, n] for n in range(2 * pairs))
    else:
        state = (jnp.zeros((HEAD, TILE), jnp.float32),) * (2 * pairs)
    state = over_tiles(bounds, i, step, state)
    if ends:
        for p in range(pairs):
            turned = jnp.concatenate([state[2 * p], state[2 * p + 1]], axis=0).T
            dq_ref[:, lanes(p)] = (turned * SCALE).astype(dq_ref.dtype)
    else:
        for n in range(2 * pairs):
            after_ref[0, 0, n] = state[n]

    @pl.when(i == pl.num_programs(1) - 1)
    def _():
        dk_ref[...] = dk_sum[...].astype(dk_ref.dtype)
        dv_ref[...] = dv_sum[...].astype(dv_ref.dtype)


def self_attend_back(q, grad, o, lse, kv, starts, reach, base, before=None):
    rows, width = q.shape
    kv_rows = kv.shape[0]
    ends = before is not None
    pairs, wide, grid, block, keys, values, by_tile, start_block = attend_specs(rows, kv_rows, width)
    state = by_tile(2 * pairs, HEAD)
    shape = lambda n: jax.ShapeDtypeStruct((n, width), jnp.bfloat16)
    spec = pltpu.PrefetchScalarGridSpec(
        num_scalar_prefetch=1,
        grid=grid,
        in_specs=[block, block, block, by_tile(8), keys, values, start_block] + [state] * ends,
        out_specs=[block if ends else state, keys, keys],
        scratch_shapes=[
            pltpu.VMEM((kv_rows, wide), jnp.float32),
            pltpu.VMEM((kv_rows, wide), jnp.float32),
            pltpu.VMEM((wide, kv_rows), jnp.bfloat16),
        ],
    )
    return pl.pallas_call(
        functools.partial(attend_back_kernel, reach=reach, base=base, pairs=pairs, ends=ends),
        grid_spec=spec,
        out_shape=[
            shape(rows) if ends else jax.ShapeDtypeStruct((*grid, 2 * pairs, HEAD, TILE), jnp.float32),
            shape(kv_rows),
            shape(kv_rows),
        ],
        compiler_params=pltpu.CompilerParams(vmem_limit_bytes=VMEM_BYTES),
        cost_estimate=pl.CostEstimate(
            flops=rows * kv_rows * HEAD, bytes_accessed=rows * HEAD, transcendentals=0
        ),
        name="self_attend_back",
    )(
        tile_bounds(starts, reach, base, kv_rows), q, grad, o, lse, kv, kv, starts.reshape(-1, 1, TILE),
        *([before] if ends else []),
    )


def cross_kernel(q_ref, k_ref, v_ref, slot_ref, o_ref):
    lower = lax.broadcasted_iota(jnp.int32, (1, PAIR), 1) < HEAD
    zero = jnp.zeros((1, 1), jnp.bfloat16)
    scaled = q_ref[...] * jnp.bfloat16(SCALE)
    tokens, texts = q_ref.shape[0], k_ref.shape[0]
    allowed = slot_ref[:, :1] == lax.broadcasted_iota(jnp.int32, (tokens, texts), 1) // TXT
    results = []
    for h in range(2):
        half = jnp.where(lower, scaled, zero) if h == 0 else jnp.where(lower, zero, scaled)
        scores = jnp.where(allowed, contract_cols(half, k_ref[...]), NEG)
        weights = jnp.exp(scores - jnp.max(scores, axis=1, keepdims=True))
        shares = weights / jnp.sum(weights, axis=1, keepdims=True)
        results.append(matmul(shares.astype(jnp.bfloat16), v_ref[...]))
    o_ref[...] = jnp.where(lower, results[0], results[1]).astype(o_ref.dtype)


def cross_attend(q, k, v, slots_wide):
    tokens, width = q.shape
    texts = k.shape[0]
    column = lambda p: (0, p)
    return pl.pallas_call(
        cross_kernel,
        grid=(width // PAIR,),
        in_specs=[
            pl.BlockSpec((tokens, PAIR), column),
            pl.BlockSpec((texts, PAIR), column),
            pl.BlockSpec((texts, PAIR), column),
            pl.BlockSpec((tokens, PAIR), lambda p: (0, 0)),
        ],
        out_specs=pl.BlockSpec((tokens, PAIR), column),
        out_shape=jax.ShapeDtypeStruct(q.shape, jnp.bfloat16),
        compiler_params=pltpu.CompilerParams(vmem_limit_bytes=VMEM_BYTES),
        cost_estimate=pl.CostEstimate(
            flops=8 * tokens * texts * width,
            bytes_accessed=4 * tokens * width,
            transcendentals=tokens * texts * width // HEAD,
        ),
        name="cross_attend",
    )(q, k, v, slots_wide)


def cross_back_kernel(q_ref, g_ref, k_ref, v_ref, slot_ref, dq_ref, dk_ref, dv_ref):
    lower = lax.broadcasted_iota(jnp.int32, (1, PAIR), 1) < HEAD
    zero = jnp.zeros((1, 1), jnp.bfloat16)
    scaled = q_ref[...] * jnp.bfloat16(SCALE)
    grad = g_ref[...]
    keys = k_ref[...]
    tokens, texts = q_ref.shape[0], k_ref.shape[0]
    allowed = slot_ref[:, :1] == lax.broadcasted_iota(jnp.int32, (tokens, texts), 1) // TXT
    dqs, dks, dvs = [], [], []
    for h in range(2):
        q_half = jnp.where(lower, scaled, zero) if h == 0 else jnp.where(lower, zero, scaled)
        g_half = jnp.where(lower, grad, zero) if h == 0 else jnp.where(lower, zero, grad)
        scores = jnp.where(allowed, contract_cols(q_half, keys), NEG)
        weights = jnp.exp(scores - jnp.max(scores, axis=1, keepdims=True))
        shares = weights / jnp.sum(weights, axis=1, keepdims=True)
        grad_shares = contract_cols(g_half, v_ref[...])
        inner = jnp.sum(shares * grad_shares, axis=1, keepdims=True)
        grad_scores = (shares * (grad_shares - inner)).astype(jnp.bfloat16)
        dqs.append(matmul(grad_scores, keys))
        dks.append(contract_rows(grad_scores, q_half))
        dvs.append(contract_rows(shares.astype(jnp.bfloat16), g_half))
    dq_ref[...] = (jnp.where(lower, dqs[0], dqs[1]) * SCALE).astype(dq_ref.dtype)
    dk_ref[...] = dks[0] + dks[1]
    dv_ref[...] = dvs[0] + dvs[1]


def cross_attend_back(q, grad, k, v, slots_wide):
    tokens, width = q.shape
    texts = k.shape[0]
    column = lambda p: (0, p)
    return pl.pallas_call(
        cross_back_kernel,
        grid=(width // PAIR,),
        in_specs=[
            pl.BlockSpec((tokens, PAIR), column),
            pl.BlockSpec((tokens, PAIR), column),
            pl.BlockSpec((texts, PAIR), column),
            pl.BlockSpec((texts, PAIR), column),
            pl.BlockSpec((tokens, PAIR), lambda p: (0, 0)),
        ],
        out_specs=[
            pl.BlockSpec((tokens, PAIR), column),
            pl.BlockSpec((texts, PAIR), column),
            pl.BlockSpec((texts, PAIR), column),
        ],
        out_shape=[
            jax.ShapeDtypeStruct(q.shape, jnp.bfloat16),
            jax.ShapeDtypeStruct((texts, width), jnp.float32),
            jax.ShapeDtypeStruct((texts, width), jnp.float32),
        ],
        compiler_params=pltpu.CompilerParams(vmem_limit_bytes=VMEM_BYTES),
        cost_estimate=pl.CostEstimate(
            flops=20 * tokens * texts * width,
            bytes_accessed=6 * tokens * width,
            transcendentals=tokens * texts * width // HEAD,
        ),
        name="cross_attend_back",
    )(q, grad, k, v, slots_wide)


def swap(value, axis, bit):
    count = lax.axis_size(axis)
    return lax.ppermute(value, axis, [(i, i ^ bit) for i in range(count)])


def passed_along(value, axis, steps):
    count = lax.axis_size(axis)
    initial, last = (max(0, -steps), min(count, count - steps))
    return lax.ppermute(value, axis, [(source, source + steps) for source in range(initial, last)])


def in_order(mine, other, dim):
    second = lax.axis_index("seq") == 1
    return jnp.concatenate([jnp.where(second, other, mine), jnp.where(second, mine, other)], axis=dim)


def gathered(value, dim):
    if lax.axis_size("seq") == 2:
        return in_order(value, swap(value, "seq", 1), dim)
    return lax.all_gather(value, "seq", axis=dim, tiled=True)


def own_block(value, dim):
    size = value.shape[dim] // lax.axis_size("seq")
    return lax.dynamic_slice_in_dim(value, lax.axis_index("seq") * size, size, dim)


def other_block(value, dim):
    size = value.shape[dim] // 2
    return lax.dynamic_slice_in_dim(value, (1 - lax.axis_index("seq")) * size, size, dim)


def exchanged(value, split, concat):
    if lax.axis_size("seq") == 2:
        return in_order(own_block(value, split), swap(other_block(value, split), "seq", 1), concat)
    return lax.all_to_all(value, "seq", split_axis=split, concat_axis=concat, tiled=True)


def summed_block(value, dim):
    if lax.axis_size("seq") == 2:
        received = swap(other_block(value, dim).astype(jnp.bfloat16), "seq", 1)
        return own_block(value, dim) + received.astype(jnp.float32)
    return lax.psum_scatter(
        value.astype(jnp.bfloat16), "seq", scatter_dimension=dim, tiled=True
    ).astype(jnp.float32)


def paired(value):
    short = -value.shape[-1] % PAIR
    return jnp.pad(value, ((0, 0), (0, short))) if short else value


def normed(values):
    average = jnp.mean(values, axis=-1, keepdims=True)
    centred = values - average
    spread = jnp.mean(centred * centred, axis=-1, keepdims=True)
    root = lax.rsqrt(spread + EPS)
    return centred * root, root


def norm_back(grad, n, root, gain):
    a = grad * gain
    back = (a - jnp.mean(a, axis=-1, keepdims=True) - n * jnp.mean(a * n, axis=-1, keepdims=True)) * root
    return back, jnp.sum(grad * n, axis=0), jnp.sum(grad, axis=0)


def scattered(grad):
    return lax.psum_scatter(grad.astype(jnp.bfloat16), "fsdp", scatter_dimension=0, tiled=True)


def whole(part):
    if lax.axis_size("seq") == 2:
        return part.astype(jnp.float32) + swap(part, "seq", 1).astype(jnp.float32)
    return lax.psum(part, "seq").astype(jnp.float32)


def columns(part, blocks):
    split = part.reshape(part.shape[0], blocks, -1)
    return gathered(split, 2).reshape(part.shape[0], -1).astype(jnp.float32)


def core_products(left, right):
    size, core = right.shape[1] // 2, lax.axis_index("fsdp") % 2
    part = lambda place: contract_rows(left, lax.dynamic_slice_in_dim(right, place * size, size, 1)).astype(jnp.bfloat16)
    return part(core), part(1 - core)


def both(first, second):
    return (first.astype(jnp.float32) + second.astype(jnp.float32)).astype(jnp.bfloat16)


def half_rows(value, place):
    blocks = value.reshape(-1, 2, *value.shape[1:])
    return lax.dynamic_index_in_dim(blocks, place, 1, keepdims=False)


def own_rows(kept, came, at):
    value, bit = both(kept, came), 4
    while value.shape[0] > 1:
        at = at // 2
        value = both(half_rows(value, at % 2), swap(half_rows(value, 1 - at % 2), "fsdp", bit))
        bit *= 2
    core, second = lax.axis_index("fsdp") % 2, lax.axis_index("seq") == 1
    value = value.reshape(2, -1, value.shape[-1])
    take = lambda place: lax.dynamic_index_in_dim(value, place, 0, keepdims=False)
    mine, theirs = take(core), swap(take(1 - core), "fsdp", 1)
    pair = jnp.stack([jnp.where(core == 0, mine, theirs), jnp.where(core == 0, theirs, mine)])
    beside = swap(pair, "seq", 1)
    by_seq = jnp.where(second, beside, pair), jnp.where(second, pair, beside)
    return jnp.concatenate([by_seq[s][c] for c in range(2) for s in range(2)], axis=1).astype(jnp.float32)


def clip_starts(segments, group_index, group_rows):
    padded = jnp.concatenate([jnp.full((SPAN,), -1, jnp.int32), segments])
    spans = lax.dynamic_slice_in_dim(padded, group_index * group_rows, SPAN + group_rows)
    spans = spans.reshape(-1, SPAN)
    ahead = jnp.sum((spans == spans[:, :1]).astype(jnp.int32), axis=1)
    firsts = ahead + jnp.arange(spans.shape[0], dtype=jnp.int32) * SPAN
    late = spans[1:] != spans[1:, :1]
    return jnp.where(late, firsts[1:, None], firsts[:-1, None]).reshape(group_rows), spans[1:].reshape(group_rows)


def shards(
    tokens,
    segments,
    text,
    qkv_weight,
    out_weight,
    cross_query_weight,
    cross_kv_weight,
    cross_out_weight,
    up_weight,
    down_weight,
    norm_gain,
    norm_bias,
    cotangent,
):
    group_index = lax.axis_index("fsdp")
    seq_index = lax.axis_index("seq")
    seq_count = lax.axis_size("seq")
    tok_rows, width = tokens.shape
    group_rows = tok_rows * seq_count
    head_cols = width // seq_count
    shard_rows = qkv_weight.shape[0]
    row_block = lambda value: lax.all_gather(value, "fsdp", axis=0, tiled=True)

    norms = jnp.pad(jnp.concatenate([norm_gain, norm_bias]).T, ((0, 0), (0, PAIR - 6)))
    qkv_mine = own_block(qkv_weight.reshape(shard_rows, 3, width), 2).reshape(shard_rows, 3 * head_cols)
    first = row_block(jnp.concatenate([qkv_mine, norms], axis=1))
    w_q, w_kv, w_qkv = first[:, :head_cols], first[:, head_cols : 3 * head_cols], first[:, : 3 * head_cols]
    norm_rows = first[:, 3 * head_cols : 3 * head_cols + 6].astype(jnp.float32).T
    gains, biases = norm_rows[:3], norm_rows[3:]

    ckv_mine = own_block(cross_kv_weight.reshape(shard_rows, 2, width), 2).reshape(shard_rows, 2 * head_cols)
    second = row_block(jnp.concatenate([out_weight, cross_query_weight, cross_out_weight, ckv_mine], axis=1))
    full_out, full_cq, full_cout = second[:, :width], second[:, width : 2 * width], second[:, 2 * width : 3 * width]
    w_ckv = second[:, 3 * width :]

    starts, seg_group = clip_starts(segments, group_index, group_rows)
    slots = own_block(seg_group, 0) - group_index * (group_rows // SPAN)
    slots_wide = jnp.broadcast_to(slots[:, None], (tok_rows, PAIR))

    inputs = tokens.astype(jnp.float32)
    n_group, _ = normed(gathered(tokens, 0).astype(jnp.float32))
    normed_one = (n_group * gains[0] + biases[0]).astype(jnp.bfloat16)
    kv_own = matmul(normed_one, w_kv).astype(jnp.bfloat16)
    kv_before = passed_along(kv_own[group_rows - SPAN :], "fsdp", 1)
    queries = matmul(normed_one, w_q).astype(jnp.bfloat16)
    if head_cols % PAIR:
        pad_kv = lambda kv: jnp.concatenate([paired(kv[:, :head_cols]), paired(kv[:, head_cols:])], axis=1)
        queries, kv_own, kv_before = paired(queries), pad_kv(kv_own), pad_kv(kv_before)
    heads_state = self_attend(queries, kv_own, starts, SPAN, SPAN)
    heads_out, log_totals = self_attend(queries, kv_before, starts, SPAN, 0, heads_state)
    attended = exchanged(heads_out[:, :head_cols], 0, 1)
    hidden_one = inputs + matmul(attended, full_out)

    text_rows = text.reshape(-1, width)
    text_count = text_rows.shape[0]
    ckv_part = matmul(text_rows, w_ckv).astype(jnp.bfloat16).reshape(text_count, 2, head_cols)
    cross_kv = gathered(ckv_part, 2)
    cross_k, cross_v = cross_kv[:, 0], cross_kv[:, 1]
    n_two, root_two = normed(hidden_one)
    normed_two = (n_two * gains[1] + biases[1]).astype(jnp.bfloat16)
    cross_query = matmul(normed_two, full_cq).astype(jnp.bfloat16)
    cross_result = cross_attend(cross_query, cross_k, cross_v, slots_wide)
    hidden_two = hidden_one + matmul(cross_result, full_cout)

    full_up, full_down = row_block(up_weight), row_block(down_weight)
    n_three, root_three = normed(hidden_two)
    normed_three = (n_three * gains[2] + biases[2]).astype(jnp.bfloat16)
    upward = matmul(normed_three, full_up)
    below = 0.5 * (1.0 + lax.erf(upward * (0.5**0.5)))
    active = (upward * below).astype(jnp.bfloat16)
    slope = below + upward * (jnp.exp(-0.5 * upward * upward) * 0.3989422804014327)
    layer_out = (hidden_two + matmul(active, full_down)).astype(jnp.bfloat16)

    gate = lax.optimization_barrier
    by_steps = seq_count == 2
    chip = group_index // 2
    grad_down, slope = gate((contract_rows(active, cotangent).astype(jnp.bfloat16), slope))
    grad_down = scattered(grad_down)
    grad_upward = (contract_cols(cotangent, full_down) * slope).astype(jnp.bfloat16)
    if by_steps:
        up_kept, up_away, grad_upward = gate((*core_products(normed_three, grad_upward), grad_upward))
        up_came = swap(up_away, "fsdp", 1)
    else:
        grad_up = scattered(contract_rows(normed_three, grad_upward))
    back_h2, gain_three, bias_three = norm_back(contract_cols(grad_upward, full_up), n_three, root_three, gains[2])
    grad_two = cotangent.astype(jnp.float32) + back_h2
    grad_two_low = grad_two.astype(jnp.bfloat16)
    if by_steps:
        beside, grad_two_low = gate((both(other_block(up_kept, 1), other_block(up_came, 1)), grad_two_low))
        beside = swap(beside, "seq", 1)
    grad_result = contract_cols(grad_two_low, full_cout).astype(jnp.bfloat16)
    grad_query_c, grad_text_k, grad_text_v = cross_attend_back(cross_query, grad_result, cross_k, cross_v, slots_wide)
    grad_text_kv = summed_block(jnp.stack([grad_text_k, grad_text_v], axis=1), 2)
    grad_text_kv = grad_text_kv.astype(jnp.bfloat16).reshape(text_count, 2 * head_cols)
    grad_text = contract_cols(grad_text_kv, w_ckv)
    back_h1, gain_two, bias_two = norm_back(contract_cols(grad_query_c, full_cq), n_two, root_two, gains[1])
    grad_one = grad_two + back_h1

    grad_one_low = grad_one.astype(jnp.bfloat16)
    grad_attended = contract_cols(grad_one_low, full_out).astype(jnp.bfloat16)
    grad_heads = paired(exchanged(grad_attended, 1, 0))
    small = [
        contract_rows(left, right).astype(jnp.bfloat16)
        for left, right in (
            (cross_result, grad_two_low),
            (normed_two, grad_query_c),
            (attended, grad_one_low),
            (text_rows, grad_text_kv),
        )
    ]
    if by_steps:
        small = lax.psum_scatter(gate((jnp.stack(small), grad_down, grad_heads))[0], "fsdp", scatter_dimension=1, tiled=True)
    else:
        small = [scattered(part) for part in small]
    back_args = (queries, grad_heads, heads_out, log_totals)
    query_state, *grad_before = self_attend_back(*back_args, kv_before, starts, SPAN, 0)
    returned = [passed_along(part[:, :head_cols], "fsdp", -1).astype(jnp.float32) for part in grad_before]
    if by_steps:
        total = both(both(own_block(up_kept, 1), own_block(up_came, 1)), beside)
        total = total.reshape(-1, 2 * shard_rows, total.shape[1])
        first_away, grad_down, query_state = gate((half_rows(total, 1 - chip % 2), grad_down, query_state))
        down_beside = swap(grad_down, "seq", 1)
    grad_q, *grad_own = self_attend_back(*back_args, kv_own, starts, SPAN, SPAN, query_state)
    if by_steps:
        down_beside, first_came, grad_q = gate((down_beside, swap(first_away, "fsdp", 2), grad_q))
        grad_up = own_rows(half_rows(total, chip % 2), first_came, chip)
        grad_down = grad_down.astype(jnp.float32) + down_beside.astype(jnp.float32)
    else:
        grad_up, grad_down = whole(grad_up), whole(grad_down)
    late = group_rows - SPAN
    owned = [grad_q[:, :head_cols]]
    for part, more in zip(grad_own, returned):
        part = part[:, :head_cols].astype(jnp.float32)
        part = jnp.concatenate([part[:late], part[late:] + more]) if late else part + more
        owned.append(part.astype(jnp.bfloat16))
    grad_proj = jnp.concatenate(owned, axis=1)
    grad_wqkv, grad_proj = gate((contract_rows(normed_one, grad_proj).astype(jnp.bfloat16), grad_proj))
    grad_normed_one = contract_cols(grad_proj, w_qkv)
    grad_wqkv = scattered(gate((grad_wqkv, small, grad_normed_one))[0])
    grad_normed_one = summed_block(grad_normed_one, 0)
    n_one, root_one = normed(inputs)
    back_x, gain_one, bias_one = norm_back(grad_normed_one, n_one, root_one, gains[0])
    grad_tokens = (grad_one + back_x).astype(jnp.bfloat16)

    grad_cout, grad_cq, grad_wout = whole(small[:3]) if by_steps else [whole(part) for part in small[:3]]
    norm_grads = lax.psum(
        jnp.stack([gain_one, gain_two, gain_three, bias_one, bias_two, bias_three]), ("fsdp", "seq")
    )
    norm_grads = lax.dynamic_slice_in_dim(norm_grads, group_index * shard_rows, shard_rows, 1)
    return (
        layer_out,
        grad_tokens,
        whole(grad_text.astype(jnp.bfloat16)).reshape(text.shape),
        columns(grad_wqkv, 3),
        grad_wout,
        grad_cq,
        columns(small[3], 2),
        grad_cout,
        grad_up,
        grad_down,
        norm_grads[:3],
        norm_grads[3:],
    )


def solution(mesh):
    rows, shard, copied = P(("fsdp", "seq"), None), P("fsdp", None), P(None, "fsdp")
    groups = P("fsdp", None, None)
    in_specs = (rows, P(), groups, *[shard] * 7, copied, copied, rows)
    out_specs = (rows, rows, groups, *[shard] * 7, copied, copied)
    return jax.shard_map(shards, mesh=mesh, in_specs=in_specs, out_specs=out_specs, check_vma=False)
```

```python
import functools

import jax
import jax.numpy as jnp
from jax import lax
from jax.experimental import pallas as pl
from jax.experimental.pallas import tpu as pltpu
from jax.sharding import PartitionSpec as P

HEADS = 24
HEAD = 64
PAIR = 2 * HEAD
TXT = 64
SPAN = 1536
EPS = 1e-05
NEG = -1e30
SCALE = HEAD**-0.5
VMEM_BYTES = 56 * 2**20


def matmul(left_side, right_side):
    return jnp.dot(left_side, right_side, preferred_element_type=jnp.float32)


def contract_rows(left_side, right_side):
    return lax.dot_general(
        left_side, right_side, (((0,), (0,)), ((), ())), preferred_element_type=jnp.float32
    )


def contract_cols(left_side, right_side):
    return lax.dot_general(
        left_side, right_side, (((1,), (1,)), ((), ())), preferred_element_type=jnp.float32
    )


TILE = 384


def tile_bounds(starts, reach, base, kv_rows):
    count = kv_rows // TILE
    first, last = starts[::TILE] - base, starts[TILE - 1 :: TILE] - base
    row0 = reach - base + jnp.arange(first.shape[0], dtype=jnp.int32) * TILE
    low = jnp.clip(first // TILE, 0, count)
    high = jnp.clip((row0 + TILE - 1) // TILE + 1, low, count)
    free_low = jnp.clip((last + TILE - 1) // TILE, low, high)
    free_high = jnp.clip((row0 + 1) // TILE, free_low, high)
    return jnp.stack([low, free_low, free_high, high], axis=1)


def pairs_a_step(width):
    return 3 if width % (3 * PAIR) == 0 else 1


def split_heads(block):
    lower = lax.broadcasted_iota(jnp.int32, (1, PAIR), 1) < HEAD
    zero = jnp.zeros((1, 1), block.dtype)
    return [jnp.where(lower, block, zero), jnp.where(lower, zero, block)]


def lanes(p):
    return slice(p * PAIR, (p + 1) * PAIR)


def tile_allowed(col0, row0, starts):
    at = col0 + lax.broadcasted_iota(jnp.int32, (TILE, TILE), 0)
    row = row0 + lax.broadcasted_iota(jnp.int32, (TILE, TILE), 1)
    return (at >= starts) & (at <= row)


def over_tiles(bounds, i, step, state):
    low, free_low, free_high, high = (bounds[i, n] for n in range(4))
    state = lax.fori_loop(low, free_low, functools.partial(step, True), state)
    state = lax.fori_loop(free_low, free_high, functools.partial(step, False), state)
    return lax.fori_loop(free_high, high, functools.partial(step, True), state)


def attend_kernel(bounds, q_ref, k_ref, v_ref, start_ref, *refs, reach, base, pairs, ends):
    i = pl.program_id(1)
    if ends:
        before_ref, o_ref, lse_ref, v_t = refs
    else:
        after_ref, v_t = refs

    @pl.when(i == 0)
    def _():
        for p in range(pairs):
            turned = v_ref[:, lanes(p)].T
            for h in range(2):
                v_t[2 * p + h, :HEAD] = turned[h * HEAD : (h + 1) * HEAD]
                v_t[2 * p + h, HEAD:] = jnp.ones((16, turned.shape[1]), jnp.bfloat16)

    halves = []
    for p in range(pairs):
        halves += split_heads(q_ref[:, lanes(p)] * jnp.bfloat16(SCALE))
    starts = start_ref[0]

    def step(masked, j, carried):
        rows = pl.ds(pl.multiple_of(j * TILE, TILE), TILE)
        if masked:
            allowed = tile_allowed(base + j * TILE, reach + i * TILE, starts)
        scores = []
        for n in range(2 * pairs):
            s = contract_cols(k_ref[rows, lanes(n // 2)], halves[n])
            scores.append(jnp.where(allowed, s, NEG) if masked else s)
        out = []
        for n, (top, total) in enumerate(carried):
            new_top = jnp.maximum(top, jnp.max(scores[n], axis=0, keepdims=True))
            weights = jnp.exp(scores[n] - new_top).astype(jnp.bfloat16)
            total = total * jnp.exp(top - new_top) + matmul(v_t[n, :, rows], weights)
            out.append((new_top, total))
        return tuple(out)

    if ends:
        state = tuple((before_ref[0, 0, n, HEAD + 8 : HEAD + 9], before_ref[0, 0, n]) for n in range(2 * pairs))
    else:
        nothing = (jnp.full((1, TILE), NEG, jnp.float32), jnp.zeros((HEAD + 16, TILE), jnp.float32))
        state = (nothing,) * (2 * pairs)
    state = over_tiles(bounds, i, step, state)
    if not ends:
        for n, (top, total) in enumerate(state):
            after_ref[0, 0, n, : HEAD + 8] = total[: HEAD + 8]
            after_ref[0, 0, n, HEAD + 8 :] = jnp.broadcast_to(top, (8, TILE))
        return
    for p in range(pairs):
        outs = []
        for n in (2 * p, 2 * p + 1):
            top, total = state[n]
            count = total[HEAD : HEAD + 1]
            outs.append(total[:HEAD] / count)
            lse_ref[0, 0, n : n + 1, :] = top + jnp.log(count)
        o_ref[:, lanes(p)] = jnp.concatenate(outs, axis=0).T.astype(o_ref.dtype)


def attend_specs(rows, kv_rows, width):
    pairs = pairs_a_step(width)
    wide = pairs * PAIR
    steps = width // wide
    block = pl.BlockSpec((TILE, wide), lambda p, i, b: (i, p))
    keys = pl.BlockSpec((kv_rows, wide), lambda p, i, b: (0, p))
    values = pl.BlockSpec((kv_rows, wide), lambda p, i, b: (0, steps + p))
    by_tile = lambda *shape: pl.BlockSpec((1, 1, *shape, TILE), lambda p, i, b: (p, i, *[0] * len(shape), 0))
    starts = pl.BlockSpec((1, 1, TILE), lambda p, i, b: (i, 0, 0))
    return pairs, wide, (steps, rows // TILE), block, keys, values, by_tile, starts


def self_attend(q, kv, starts, reach, base, before=None):
    rows, width = q.shape
    kv_rows = kv.shape[0]
    ends = before is not None
    pairs, wide, grid, block, keys, values, by_tile, start_block = attend_specs(rows, kv_rows, width)
    state = by_tile(2 * pairs, HEAD + 16)
    state_shape = jax.ShapeDtypeStruct((*grid, 2 * pairs, HEAD + 16, TILE), jnp.float32)
    spec = pltpu.PrefetchScalarGridSpec(
        num_scalar_prefetch=1,
        grid=grid,
        in_specs=[block, keys, values, start_block] + [state] * ends,
        out_specs=[block, by_tile(8)] if ends else state,
        scratch_shapes=[pltpu.VMEM((2 * pairs, HEAD + 16, kv_rows), jnp.bfloat16)],
    )
    return pl.pallas_call(
        functools.partial(attend_kernel, reach=reach, base=base, pairs=pairs, ends=ends),
        grid_spec=spec,
        out_shape=[
            jax.ShapeDtypeStruct((rows, width), jnp.bfloat16),
            jax.ShapeDtypeStruct((*grid, 8, TILE), jnp.float32),
        ]
        if ends
        else state_shape,
        compiler_params=pltpu.CompilerParams(vmem_limit_bytes=VMEM_BYTES),
        cost_estimate=pl.CostEstimate(
            flops=rows * kv_rows * HEAD, bytes_accessed=rows * HEAD, transcendentals=0
        ),
        name="self_attend",
    )(tile_bounds(starts, reach, base, kv_rows), q, kv, kv, starts.reshape(-1, 1, TILE), *([before] if ends else []))


def attend_back_kernel(bounds, q_ref, g_ref, o_ref, lse_ref, k_ref, v_ref, start_ref, *refs, reach, base, pairs, ends):
    i = pl.program_id(1)
    if ends:
        before_ref, dq_ref, dk_ref, dv_ref, dk_sum, dv_sum, k_t = refs
    else:
        after_ref, dk_ref, dv_ref, dk_sum, dv_sum, k_t = refs

    @pl.when(i == 0)
    def _():
        k_t[...] = k_ref[...].T
        dk_sum[...] = jnp.zeros_like(dk_sum)
        dv_sum[...] = jnp.zeros_like(dv_sum)

    queries, grads, inner, logs = [], [], [], []
    for p in range(pairs):
        grad = g_ref[:, lanes(p)]
        queries += split_heads(q_ref[:, lanes(p)] * jnp.bfloat16(SCALE))
        grads += split_heads(grad)
        product = (grad.astype(jnp.float32) * o_ref[:, lanes(p)].astype(jnp.float32)).T
        for h in range(2):
            inner.append(jnp.sum(product[h * HEAD : (h + 1) * HEAD], axis=0, keepdims=True))
            logs.append(lse_ref[0, 0, 2 * p + h : 2 * p + h + 1])
    starts = start_ref[0]

    def step(masked, j, carried):
        rows = pl.ds(pl.multiple_of(j * TILE, TILE), TILE)
        if masked:
            allowed = tile_allowed(base + j * TILE, reach + i * TILE, starts)
        out = []
        for p in range(pairs):
            keys, values = k_ref[rows, lanes(p)], v_ref[rows, lanes(p)]
            dks, dvs = [], []
            for n in (2 * p, 2 * p + 1):
                s = contract_cols(keys, queries[n])
                d = contract_cols(values, grads[n])
                if masked:
                    s = jnp.where(allowed, s, NEG)
                shares = jnp.exp(s - logs[n])
                ds = (shares * (d - inner[n])).astype(jnp.bfloat16)
                dvs.append(matmul(shares.astype(jnp.bfloat16), grads[n]))
                dks.append(matmul(ds, queries[n]))
                out.append(carried[n] + matmul(k_t[n * HEAD : (n + 1) * HEAD, rows], ds))
            dv_sum[rows, lanes(p)] += dvs[0] + dvs[1]
            dk_sum[rows, lanes(p)] += dks[0] + dks[1]
        return tuple(out)

    if ends:
        state = tuple(before_ref[0, 0, n] for n in range(2 * pairs))
    else:
        state = (jnp.zeros((HEAD, TILE), jnp.float32),) * (2 * pairs)
    state = over_tiles(bounds, i, step, state)
    if ends:
        for p in range(pairs):
            turned = jnp.concatenate([state[2 * p], state[2 * p + 1]], axis=0).T
            dq_ref[:, lanes(p)] = (turned * SCALE).astype(dq_ref.dtype)
    else:
        for n in range(2 * pairs):
            after_ref[0, 0, n] = state[n]

    @pl.when(i == pl.num_programs(1) - 1)
    def _():
        dk_ref[...] = dk_sum[...].astype(dk_ref.dtype)
        dv_ref[...] = dv_sum[...].astype(dv_ref.dtype)


def self_attend_back(q, grad, o, lse, kv, starts, reach, base, before=None):
    rows, width = q.shape
    kv_rows = kv.shape[0]
    ends = before is not None
    pairs, wide, grid, block, keys, values, by_tile, start_block = attend_specs(rows, kv_rows, width)
    state = by_tile(2 * pairs, HEAD)
    shape = lambda n: jax.ShapeDtypeStruct((n, width), jnp.bfloat16)
    spec = pltpu.PrefetchScalarGridSpec(
        num_scalar_prefetch=1,
        grid=grid,
        in_specs=[block, block, block, by_tile(8), keys, values, start_block] + [state] * ends,
        out_specs=[block if ends else state, keys, keys],
        scratch_shapes=[
            pltpu.VMEM((kv_rows, wide), jnp.float32),
            pltpu.VMEM((kv_rows, wide), jnp.float32),
            pltpu.VMEM((wide, kv_rows), jnp.bfloat16),
        ],
    )
    return pl.pallas_call(
        functools.partial(attend_back_kernel, reach=reach, base=base, pairs=pairs, ends=ends),
        grid_spec=spec,
        out_shape=[
            shape(rows) if ends else jax.ShapeDtypeStruct((*grid, 2 * pairs, HEAD, TILE), jnp.float32),
            shape(kv_rows),
            shape(kv_rows),
        ],
        compiler_params=pltpu.CompilerParams(vmem_limit_bytes=VMEM_BYTES),
        cost_estimate=pl.CostEstimate(
            flops=rows * kv_rows * HEAD, bytes_accessed=rows * HEAD, transcendentals=0
        ),
        name="self_attend_back",
    )(
        tile_bounds(starts, reach, base, kv_rows), q, grad, o, lse, kv, kv, starts.reshape(-1, 1, TILE),
        *([before] if ends else []),
    )


def cross_kernel(q_ref, k_ref, v_ref, slot_ref, o_ref):
    lower = lax.broadcasted_iota(jnp.int32, (1, PAIR), 1) < HEAD
    zero = jnp.zeros((1, 1), jnp.bfloat16)
    scaled = q_ref[...] * jnp.bfloat16(SCALE)
    tokens, texts = q_ref.shape[0], k_ref.shape[0]
    allowed = slot_ref[:, :1] == lax.broadcasted_iota(jnp.int32, (tokens, texts), 1) // TXT
    results = []
    for h in range(2):
        half = jnp.where(lower, scaled, zero) if h == 0 else jnp.where(lower, zero, scaled)
        scores = jnp.where(allowed, contract_cols(half, k_ref[...]), NEG)
        weights = jnp.exp(scores - jnp.max(scores, axis=1, keepdims=True))
        shares = weights / jnp.sum(weights, axis=1, keepdims=True)
        results.append(matmul(shares.astype(jnp.bfloat16), v_ref[...]))
    o_ref[...] = jnp.where(lower, results[0], results[1]).astype(o_ref.dtype)


def cross_attend(q, k, v, slots_wide):
    tokens, width = q.shape
    texts = k.shape[0]
    column = lambda p: (0, p)
    return pl.pallas_call(
        cross_kernel,
        grid=(width // PAIR,),
        in_specs=[
            pl.BlockSpec((tokens, PAIR), column),
            pl.BlockSpec((texts, PAIR), column),
            pl.BlockSpec((texts, PAIR), column),
            pl.BlockSpec((tokens, PAIR), lambda p: (0, 0)),
        ],
        out_specs=pl.BlockSpec((tokens, PAIR), column),
        out_shape=jax.ShapeDtypeStruct(q.shape, jnp.bfloat16),
        compiler_params=pltpu.CompilerParams(vmem_limit_bytes=VMEM_BYTES),
        cost_estimate=pl.CostEstimate(
            flops=8 * tokens * texts * width,
            bytes_accessed=4 * tokens * width,
            transcendentals=tokens * texts * width // HEAD,
        ),
        name="cross_attend",
    )(q, k, v, slots_wide)


def cross_back_kernel(q_ref, g_ref, k_ref, v_ref, slot_ref, dq_ref, dk_ref, dv_ref):
    lower = lax.broadcasted_iota(jnp.int32, (1, PAIR), 1) < HEAD
    zero = jnp.zeros((1, 1), jnp.bfloat16)
    scaled = q_ref[...] * jnp.bfloat16(SCALE)
    grad = g_ref[...]
    keys = k_ref[...]
    tokens, texts = q_ref.shape[0], k_ref.shape[0]
    allowed = slot_ref[:, :1] == lax.broadcasted_iota(jnp.int32, (tokens, texts), 1) // TXT
    dqs, dks, dvs = [], [], []
    for h in range(2):
        q_half = jnp.where(lower, scaled, zero) if h == 0 else jnp.where(lower, zero, scaled)
        g_half = jnp.where(lower, grad, zero) if h == 0 else jnp.where(lower, zero, grad)
        scores = jnp.where(allowed, contract_cols(q_half, keys), NEG)
        weights = jnp.exp(scores - jnp.max(scores, axis=1, keepdims=True))
        shares = weights / jnp.sum(weights, axis=1, keepdims=True)
        grad_shares = contract_cols(g_half, v_ref[...])
        inner = jnp.sum(shares * grad_shares, axis=1, keepdims=True)
        grad_scores = (shares * (grad_shares - inner)).astype(jnp.bfloat16)
        dqs.append(matmul(grad_scores, keys))
        dks.append(contract_rows(grad_scores, q_half))
        dvs.append(contract_rows(shares.astype(jnp.bfloat16), g_half))
    dq_ref[...] = (jnp.where(lower, dqs[0], dqs[1]) * SCALE).astype(dq_ref.dtype)
    dk_ref[...] = dks[0] + dks[1]
    dv_ref[...] = dvs[0] + dvs[1]


def cross_attend_back(q, grad, k, v, slots_wide):
    tokens, width = q.shape
    texts = k.shape[0]
    column = lambda p: (0, p)
    return pl.pallas_call(
        cross_back_kernel,
        grid=(width // PAIR,),
        in_specs=[
            pl.BlockSpec((tokens, PAIR), column),
            pl.BlockSpec((tokens, PAIR), column),
            pl.BlockSpec((texts, PAIR), column),
            pl.BlockSpec((texts, PAIR), column),
            pl.BlockSpec((tokens, PAIR), lambda p: (0, 0)),
        ],
        out_specs=[
            pl.BlockSpec((tokens, PAIR), column),
            pl.BlockSpec((texts, PAIR), column),
            pl.BlockSpec((texts, PAIR), column),
        ],
        out_shape=[
            jax.ShapeDtypeStruct(q.shape, jnp.bfloat16),
            jax.ShapeDtypeStruct((texts, width), jnp.float32),
            jax.ShapeDtypeStruct((texts, width), jnp.float32),
        ],
        compiler_params=pltpu.CompilerParams(vmem_limit_bytes=VMEM_BYTES),
        cost_estimate=pl.CostEstimate(
            flops=20 * tokens * texts * width,
            bytes_accessed=6 * tokens * width,
            transcendentals=tokens * texts * width // HEAD,
        ),
        name="cross_attend_back",
    )(q, grad, k, v, slots_wide)


def swap(value, axis, bit):
    count = lax.axis_size(axis)
    return lax.ppermute(value, axis, [(i, i ^ bit) for i in range(count)])


def passed_along(value, axis, steps):
    count = lax.axis_size(axis)
    initial, last = (max(0, -steps), min(count, count - steps))
    return lax.ppermute(value, axis, [(source, source + steps) for source in range(initial, last)])


def in_order(mine, other, dim):
    second = lax.axis_index("seq") == 1
    return jnp.concatenate([jnp.where(second, other, mine), jnp.where(second, mine, other)], axis=dim)


def gathered(value, dim):
    if lax.axis_size("seq") == 2:
        return in_order(value, swap(value, "seq", 1), dim)
    return lax.all_gather(value, "seq", axis=dim, tiled=True)


def own_block(value, dim):
    size = value.shape[dim] // lax.axis_size("seq")
    return lax.dynamic_slice_in_dim(value, lax.axis_index("seq") * size, size, dim)


def other_block(value, dim):
    size = value.shape[dim] // 2
    return lax.dynamic_slice_in_dim(value, (1 - lax.axis_index("seq")) * size, size, dim)


def exchanged(value, split, concat):
    if lax.axis_size("seq") == 2:
        return in_order(own_block(value, split), swap(other_block(value, split), "seq", 1), concat)
    return lax.all_to_all(value, "seq", split_axis=split, concat_axis=concat, tiled=True)


def summed_block(value, dim):
    if lax.axis_size("seq") == 2:
        received = swap(other_block(value, dim).astype(jnp.bfloat16), "seq", 1)
        return own_block(value, dim) + received.astype(jnp.float32)
    return lax.psum_scatter(
        value.astype(jnp.bfloat16), "seq", scatter_dimension=dim, tiled=True
    ).astype(jnp.float32)


def paired(value):
    short = -value.shape[-1] % PAIR
    return jnp.pad(value, ((0, 0), (0, short))) if short else value


def normed(values):
    average = jnp.mean(values, axis=-1, keepdims=True)
    centred = values - average
    spread = jnp.mean(centred * centred, axis=-1, keepdims=True)
    root = lax.rsqrt(spread + EPS)
    return centred * root, root


def norm_back(grad, n, root, gain):
    a = grad * gain
    back = (a - jnp.mean(a, axis=-1, keepdims=True) - n * jnp.mean(a * n, axis=-1, keepdims=True)) * root
    return back, jnp.sum(grad * n, axis=0), jnp.sum(grad, axis=0)


def scattered(grad):
    return lax.psum_scatter(grad.astype(jnp.bfloat16), "fsdp", scatter_dimension=0, tiled=True)


def whole(part):
    if lax.axis_size("seq") == 2:
        return part.astype(jnp.float32) + swap(part, "seq", 1).astype(jnp.float32)
    return lax.psum(part, "seq").astype(jnp.float32)


def columns(part, blocks):
    split = part.reshape(part.shape[0], blocks, -1)
    return gathered(split, 2).reshape(part.shape[0], -1).astype(jnp.float32)


def core_products(left, right):
    size, core = right.shape[1] // 2, lax.axis_index("fsdp") % 2
    part = lambda place: contract_rows(left, lax.dynamic_slice_in_dim(right, place * size, size, 1)).astype(jnp.bfloat16)
    return part(core), part(1 - core)


def both(first, second):
    return (first.astype(jnp.float32) + second.astype(jnp.float32)).astype(jnp.bfloat16)


def half_rows(value, place):
    blocks = value.reshape(-1, 2, *value.shape[1:])
    return lax.dynamic_index_in_dim(blocks, place, 1, keepdims=False)


def own_rows(value, at, bit):
    while value.shape[0] > 1:
        at = at // 2
        value = both(half_rows(value, at % 2), swap(half_rows(value, 1 - at % 2), "fsdp", bit))
        bit *= 2
    core, second = lax.axis_index("fsdp") % 2, lax.axis_index("seq") == 1
    value = value.reshape(2, -1, value.shape[-1])
    take = lambda place: lax.dynamic_index_in_dim(value, place, 0, keepdims=False)
    mine, theirs = take(core), swap(take(1 - core), "fsdp", 1)
    pair = jnp.stack([jnp.where(core == 0, mine, theirs), jnp.where(core == 0, theirs, mine)])
    beside = swap(pair, "seq", 1)
    by_seq = jnp.where(second, beside, pair), jnp.where(second, pair, beside)
    return jnp.concatenate([by_seq[s][c] for c in range(2) for s in range(2)], axis=1).astype(jnp.float32)


def clip_starts(segments, group_index, group_rows):
    padded = jnp.concatenate([jnp.full((SPAN,), -1, jnp.int32), segments])
    spans = lax.dynamic_slice_in_dim(padded, group_index * group_rows, SPAN + group_rows)
    spans = spans.reshape(-1, SPAN)
    ahead = jnp.sum((spans == spans[:, :1]).astype(jnp.int32), axis=1)
    firsts = ahead + jnp.arange(spans.shape[0], dtype=jnp.int32) * SPAN
    late = spans[1:] != spans[1:, :1]
    return jnp.where(late, firsts[1:, None], firsts[:-1, None]).reshape(group_rows), spans[1:].reshape(group_rows)


def shards(
    tokens,
    segments,
    text,
    qkv_weight,
    out_weight,
    cross_query_weight,
    cross_kv_weight,
    cross_out_weight,
    up_weight,
    down_weight,
    norm_gain,
    norm_bias,
    cotangent,
):
    group_index = lax.axis_index("fsdp")
    seq_index = lax.axis_index("seq")
    seq_count = lax.axis_size("seq")
    tok_rows, width = tokens.shape
    group_rows = tok_rows * seq_count
    head_cols = width // seq_count
    shard_rows = qkv_weight.shape[0]
    row_block = lambda value: lax.all_gather(value, "fsdp", axis=0, tiled=True)

    norms = jnp.pad(jnp.concatenate([norm_gain, norm_bias]).T, ((0, 0), (0, PAIR - 6)))
    qkv_mine = own_block(qkv_weight.reshape(shard_rows, 3, width), 2).reshape(shard_rows, 3 * head_cols)
    first = row_block(jnp.concatenate([qkv_mine, norms], axis=1))
    w_q, w_kv, w_qkv = first[:, :head_cols], first[:, head_cols : 3 * head_cols], first[:, : 3 * head_cols]
    norm_rows = first[:, 3 * head_cols : 3 * head_cols + 6].astype(jnp.float32).T
    gains, biases = norm_rows[:3], norm_rows[3:]

    ckv_mine = own_block(cross_kv_weight.reshape(shard_rows, 2, width), 2).reshape(shard_rows, 2 * head_cols)
    second = row_block(jnp.concatenate([out_weight, cross_query_weight, cross_out_weight, ckv_mine], axis=1))
    full_out, full_cq, full_cout = second[:, :width], second[:, width : 2 * width], second[:, 2 * width : 3 * width]
    w_ckv = second[:, 3 * width :]

    starts, seg_group = clip_starts(segments, group_index, group_rows)
    slots = own_block(seg_group, 0) - group_index * (group_rows // SPAN)
    slots_wide = jnp.broadcast_to(slots[:, None], (tok_rows, PAIR))

    gate = lax.optimization_barrier
    by_steps = seq_count == 2 and group_rows == SPAN
    inputs = tokens.astype(jnp.float32)
    norm_one = lambda rows: (normed(rows.astype(jnp.float32))[0] * gains[0] + biases[0]).astype(jnp.bfloat16)
    normed_one = norm_one(gathered(tokens, 0))
    kv_own = matmul(normed_one, w_kv).astype(jnp.bfloat16)
    queries = matmul(normed_one, w_q).astype(jnp.bfloat16)
    if by_steps:
        before = passed_along(tokens, "fsdp", 1)
        before_other = swap(before, "seq", 1)
    else:
        kv_before = passed_along(kv_own[group_rows - SPAN :], "fsdp", 1)
    pad_kv = lambda kv: jnp.concatenate([paired(kv[:, :head_cols]), paired(kv[:, head_cols:])], axis=1)
    if head_cols % PAIR:
        queries, kv_own, kv_before = paired(queries), pad_kv(kv_own), pad_kv(kv_before)
    heads_state = self_attend(queries, kv_own, starts, SPAN, SPAN)
    if by_steps:
        before, before_other, heads_state = gate((before, before_other, heads_state))
        kv_before = matmul(norm_one(in_order(before, before_other, 0)), w_kv).astype(jnp.bfloat16)
    heads_out, log_totals = self_attend(queries, kv_before, starts, SPAN, 0, heads_state)
    attended = exchanged(heads_out[:, :head_cols], 0, 1)
    hidden_one = inputs + matmul(attended, full_out)

    text_rows = text.reshape(-1, width)
    text_count = text_rows.shape[0]
    ckv_part = matmul(text_rows, w_ckv).astype(jnp.bfloat16).reshape(text_count, 2, head_cols)
    cross_kv = gathered(ckv_part, 2)
    cross_k, cross_v = cross_kv[:, 0], cross_kv[:, 1]
    n_two, root_two = normed(hidden_one)
    normed_two = (n_two * gains[1] + biases[1]).astype(jnp.bfloat16)
    cross_query = matmul(normed_two, full_cq).astype(jnp.bfloat16)
    cross_result = cross_attend(cross_query, cross_k, cross_v, slots_wide)
    hidden_two = hidden_one + matmul(cross_result, full_cout)

    full_up, full_down = row_block(up_weight), row_block(down_weight)
    n_three, root_three = normed(hidden_two)
    normed_three = (n_three * gains[2] + biases[2]).astype(jnp.bfloat16)
    upward = matmul(normed_three, full_up)
    below = 0.5 * (1.0 + lax.erf(upward * (0.5**0.5)))
    active = (upward * below).astype(jnp.bfloat16)
    slope = below + upward * (jnp.exp(-0.5 * upward * upward) * 0.3989422804014327)
    layer_out = (hidden_two + matmul(active, full_down)).astype(jnp.bfloat16)

    chip = group_index // 2
    grad_down, slope = gate((contract_rows(active, cotangent).astype(jnp.bfloat16), slope))
    grad_down = scattered(grad_down)
    grad_upward = (contract_cols(cotangent, full_down) * slope).astype(jnp.bfloat16)
    if by_steps:
        up_kept, up_away, grad_upward = gate((*core_products(normed_three, grad_upward), grad_upward))
        up_came = swap(up_away, "fsdp", 1)
    else:
        grad_up = scattered(contract_rows(normed_three, grad_upward))
    back_h2, gain_three, bias_three = norm_back(contract_cols(grad_upward, full_up), n_three, root_three, gains[2])
    grad_two = cotangent.astype(jnp.float32) + back_h2
    grad_two_low = grad_two.astype(jnp.bfloat16)
    if by_steps:
        beside, grad_two_low = gate((both(other_block(up_kept, 1), other_block(up_came, 1)), grad_two_low))
        beside = swap(beside, "seq", 1)
    grad_result = contract_cols(grad_two_low, full_cout).astype(jnp.bfloat16)
    grad_query_c, grad_text_k, grad_text_v = cross_attend_back(cross_query, grad_result, cross_k, cross_v, slots_wide)
    grad_text_kv = summed_block(jnp.stack([grad_text_k, grad_text_v], axis=1), 2)
    grad_text_kv = grad_text_kv.astype(jnp.bfloat16).reshape(text_count, 2 * head_cols)
    grad_text = contract_cols(grad_text_kv, w_ckv)
    back_h1, gain_two, bias_two = norm_back(contract_cols(grad_query_c, full_cq), n_two, root_two, gains[1])
    grad_one = grad_two + back_h1

    grad_one_low = grad_one.astype(jnp.bfloat16)
    grad_attended = contract_cols(grad_one_low, full_out).astype(jnp.bfloat16)
    grad_heads = paired(exchanged(grad_attended, 1, 0))
    small = [
        contract_rows(left, right).astype(jnp.bfloat16)
        for left, right in (
            (cross_result, grad_two_low),
            (normed_two, grad_query_c),
            (attended, grad_one_low),
            (text_rows, grad_text_kv),
        )
    ]
    if by_steps:
        small = lax.psum_scatter(gate((jnp.stack(small), grad_down, grad_heads))[0], "fsdp", scatter_dimension=1, tiled=True)
    else:
        small = [scattered(part) for part in small]
    back_args = (queries, grad_heads, heads_out, log_totals)
    query_state, *grad_before = self_attend_back(*back_args, kv_before, starts, SPAN, 0)
    returned = [passed_along(part[:, :head_cols], "fsdp", -1).astype(jnp.float32) for part in grad_before]
    if by_steps:
        total = both(both(own_block(up_kept, 1), own_block(up_came, 1)), beside)
        total = total.reshape(-1, 2 * shard_rows, total.shape[1])
        first_away, grad_down, query_state = gate((half_rows(total, 1 - chip % 2), grad_down, query_state))
        down_beside = swap(grad_down, "seq", 1)
    grad_q, *grad_own = self_attend_back(*back_args, kv_own, starts, SPAN, SPAN, query_state)
    if by_steps:
        first_came = swap(first_away, "fsdp", 2)
        down_beside, grad_q = gate((down_beside, grad_q))
        grad_down = grad_down.astype(jnp.float32) + down_beside.astype(jnp.float32)
    else:
        grad_up, grad_down = whole(grad_up), whole(grad_down)
    late = group_rows - SPAN
    owned = [grad_q[:, :head_cols]]
    for part, more in zip(grad_own, returned):
        part = part[:, :head_cols].astype(jnp.float32)
        part = jnp.concatenate([part[:late], part[late:] + more]) if late else part + more
        owned.append(part.astype(jnp.bfloat16))
    grad_proj = jnp.concatenate(owned, axis=1)
    grad_wqkv, grad_proj = gate((contract_rows(normed_one, grad_proj).astype(jnp.bfloat16), grad_proj))
    grad_normed_one = contract_cols(grad_proj, w_qkv)
    grad_wqkv = scattered(gate((grad_wqkv, small, grad_normed_one))[0])
    grad_cout, grad_cq, grad_wout = whole(small[:3]) if by_steps else [whole(part) for part in small[:3]]
    grad_ckv = columns(small[3], 2)
    if by_steps:
        first_came, grad_normed_one = gate((first_came, grad_normed_one))
        up_rows = both(half_rows(total, chip % 2), first_came)
        second_came = swap(half_rows(up_rows, 1 - chip // 2 % 2), "fsdp", 4)
    grad_normed_one = summed_block(grad_normed_one, 0)
    n_one, root_one = normed(inputs)
    back_x, gain_one, bias_one = norm_back(grad_normed_one, n_one, root_one, gains[0])
    grad_tokens = (grad_one + back_x).astype(jnp.bfloat16)

    norm_grads = jnp.stack([gain_one, gain_two, gain_three, bias_one, bias_two, bias_three])
    norm_grads, grad_cout, grad_cq, grad_wout, grad_ckv = gate((norm_grads, grad_cout, grad_cq, grad_wout, grad_ckv))
    norm_grads = lax.psum(norm_grads, ("fsdp", "seq"))
    if by_steps:
        norm_grads, second_came = gate((norm_grads, second_came))
        grad_up = own_rows(both(half_rows(up_rows, chip // 2 % 2), second_came), chip // 2, 8)
    norm_grads = lax.dynamic_slice_in_dim(norm_grads, group_index * shard_rows, shard_rows, 1)
    return (
        layer_out,
        grad_tokens,
        whole(grad_text.astype(jnp.bfloat16)).reshape(text.shape),
        columns(grad_wqkv, 3),
        grad_wout,
        grad_cq,
        grad_ckv,
        grad_cout,
        grad_up,
        grad_down,
        norm_grads[:3],
        norm_grads[3:],
    )


def solution(mesh):
    rows, shard, copied = P(("fsdp", "seq"), None), P("fsdp", None), P(None, "fsdp")
    groups = P("fsdp", None, None)
    in_specs = (rows, P(), groups, *[shard] * 7, copied, copied, rows)
    out_specs = (rows, rows, groups, *[shard] * 7, copied, copied)
    return jax.shard_map(shards, mesh=mesh, in_specs=in_specs, out_specs=out_specs, check_vma=False)
```

```python
import functools

import jax
import jax.numpy as jnp
from jax import lax
from jax.experimental import pallas as pl
from jax.experimental.pallas import tpu as pltpu
from jax.sharding import PartitionSpec as P

HEADS = 24
HEAD = 64
PAIR = 2 * HEAD
TXT = 64
SPAN = 1536
EPS = 1e-05
NEG = -1e30
SCALE = HEAD**-0.5
VMEM_BYTES = 56 * 2**20


def matmul(left_side, right_side):
    return jnp.dot(left_side, right_side, preferred_element_type=jnp.float32)


def contract_rows(left_side, right_side):
    return lax.dot_general(
        left_side, right_side, (((0,), (0,)), ((), ())), preferred_element_type=jnp.float32
    )


def contract_cols(left_side, right_side):
    return lax.dot_general(
        left_side, right_side, (((1,), (1,)), ((), ())), preferred_element_type=jnp.float32
    )


TILE = 384


def tile_bounds(starts, reach, base, kv_rows):
    count = kv_rows // TILE
    first, last = starts[::TILE] - base, starts[TILE - 1 :: TILE] - base
    row0 = reach - base + jnp.arange(first.shape[0], dtype=jnp.int32) * TILE
    low = jnp.clip(first // TILE, 0, count)
    high = jnp.clip((row0 + TILE - 1) // TILE + 1, low, count)
    free_low = jnp.clip((last + TILE - 1) // TILE, low, high)
    free_high = jnp.clip((row0 + 1) // TILE, free_low, high)
    return jnp.stack([low, free_low, free_high, high], axis=1)


def pairs_a_step(width):
    return 3 if width % (3 * PAIR) == 0 else 1


def split_heads(block):
    lower = lax.broadcasted_iota(jnp.int32, (1, PAIR), 1) < HEAD
    zero = jnp.zeros((1, 1), block.dtype)
    return [jnp.where(lower, block, zero), jnp.where(lower, zero, block)]


def lanes(p):
    return slice(p * PAIR, (p + 1) * PAIR)


def tile_allowed(col0, row0, starts):
    at = col0 + lax.broadcasted_iota(jnp.int32, (TILE, TILE), 0)
    row = row0 + lax.broadcasted_iota(jnp.int32, (TILE, TILE), 1)
    return (at >= starts) & (at <= row)


def over_tiles(bounds, i, step, state):
    low, free_low, free_high, high = (bounds[i, n] for n in range(4))
    state = lax.fori_loop(low, free_low, functools.partial(step, True), state)
    state = lax.fori_loop(free_low, free_high, functools.partial(step, False), state)
    return lax.fori_loop(free_high, high, functools.partial(step, True), state)


def attend_kernel(bounds, q_ref, k_ref, v_ref, start_ref, *refs, reach, base, pairs, ends):
    i = pl.program_id(1)
    if ends:
        before_ref, o_ref, lse_ref, v_t = refs
    else:
        after_ref, v_t = refs

    @pl.when(i == 0)
    def _():
        for p in range(pairs):
            turned = v_ref[:, lanes(p)].T
            for h in range(2):
                v_t[2 * p + h, :HEAD] = turned[h * HEAD : (h + 1) * HEAD]
                v_t[2 * p + h, HEAD:] = jnp.ones((16, turned.shape[1]), jnp.bfloat16)

    halves = []
    for p in range(pairs):
        halves += split_heads(q_ref[:, lanes(p)] * jnp.bfloat16(SCALE))
    starts = start_ref[0]

    def step(masked, j, carried):
        rows = pl.ds(pl.multiple_of(j * TILE, TILE), TILE)
        if masked:
            allowed = tile_allowed(base + j * TILE, reach + i * TILE, starts)
        scores = []
        for n in range(2 * pairs):
            s = contract_cols(k_ref[rows, lanes(n // 2)], halves[n])
            scores.append(jnp.where(allowed, s, NEG) if masked else s)
        out = []
        for n, (top, total) in enumerate(carried):
            new_top = jnp.maximum(top, jnp.max(scores[n], axis=0, keepdims=True))
            weights = jnp.exp(scores[n] - new_top).astype(jnp.bfloat16)
            total = total * jnp.exp(top - new_top) + matmul(v_t[n, :, rows], weights)
            out.append((new_top, total))
        return tuple(out)

    if ends:
        state = tuple((before_ref[0, 0, n, HEAD + 8 : HEAD + 9], before_ref[0, 0, n]) for n in range(2 * pairs))
    else:
        nothing = (jnp.full((1, TILE), NEG, jnp.float32), jnp.zeros((HEAD + 16, TILE), jnp.float32))
        state = (nothing,) * (2 * pairs)
    state = over_tiles(bounds, i, step, state)
    if not ends:
        for n, (top, total) in enumerate(state):
            after_ref[0, 0, n, : HEAD + 8] = total[: HEAD + 8]
            after_ref[0, 0, n, HEAD + 8 :] = jnp.broadcast_to(top, (8, TILE))
        return
    for p in range(pairs):
        outs = []
        for n in (2 * p, 2 * p + 1):
            top, total = state[n]
            count = total[HEAD : HEAD + 1]
            outs.append(total[:HEAD] / count)
            lse_ref[0, 0, n : n + 1, :] = top + jnp.log(count)
        o_ref[:, lanes(p)] = jnp.concatenate(outs, axis=0).T.astype(o_ref.dtype)


def attend_specs(rows, kv_rows, width):
    pairs = pairs_a_step(width)
    wide = pairs * PAIR
    steps = width // wide
    block = pl.BlockSpec((TILE, wide), lambda p, i, b: (i, p))
    keys = pl.BlockSpec((kv_rows, wide), lambda p, i, b: (0, p))
    values = pl.BlockSpec((kv_rows, wide), lambda p, i, b: (0, steps + p))
    by_tile = lambda *shape: pl.BlockSpec((1, 1, *shape, TILE), lambda p, i, b: (p, i, *[0] * len(shape), 0))
    starts = pl.BlockSpec((1, 1, TILE), lambda p, i, b: (i, 0, 0))
    return pairs, wide, (steps, rows // TILE), block, keys, values, by_tile, starts


def self_attend(q, kv, starts, reach, base, before=None):
    rows, width = q.shape
    kv_rows = kv.shape[0]
    ends = before is not None
    pairs, wide, grid, block, keys, values, by_tile, start_block = attend_specs(rows, kv_rows, width)
    state = by_tile(2 * pairs, HEAD + 16)
    state_shape = jax.ShapeDtypeStruct((*grid, 2 * pairs, HEAD + 16, TILE), jnp.float32)
    spec = pltpu.PrefetchScalarGridSpec(
        num_scalar_prefetch=1,
        grid=grid,
        in_specs=[block, keys, values, start_block] + [state] * ends,
        out_specs=[block, by_tile(8)] if ends else state,
        scratch_shapes=[pltpu.VMEM((2 * pairs, HEAD + 16, kv_rows), jnp.bfloat16)],
    )
    return pl.pallas_call(
        functools.partial(attend_kernel, reach=reach, base=base, pairs=pairs, ends=ends),
        grid_spec=spec,
        out_shape=[
            jax.ShapeDtypeStruct((rows, width), jnp.bfloat16),
            jax.ShapeDtypeStruct((*grid, 8, TILE), jnp.float32),
        ]
        if ends
        else state_shape,
        compiler_params=pltpu.CompilerParams(vmem_limit_bytes=VMEM_BYTES),
        cost_estimate=pl.CostEstimate(
            flops=rows * kv_rows * HEAD, bytes_accessed=rows * HEAD, transcendentals=0
        ),
        name="self_attend",
    )(tile_bounds(starts, reach, base, kv_rows), q, kv, kv, starts.reshape(-1, 1, TILE), *([before] if ends else []))


def attend_back_kernel(bounds, q_ref, g_ref, o_ref, lse_ref, k_ref, v_ref, start_ref, *refs, reach, base, pairs, ends):
    i = pl.program_id(1)
    if ends:
        before_ref, dq_ref, dk_ref, dv_ref, dk_sum, dv_sum, k_t = refs
    else:
        after_ref, dk_ref, dv_ref, dk_sum, dv_sum, k_t = refs

    @pl.when(i == 0)
    def _():
        k_t[...] = k_ref[...].T
        dk_sum[...] = jnp.zeros_like(dk_sum)
        dv_sum[...] = jnp.zeros_like(dv_sum)

    queries, grads, inner, logs = [], [], [], []
    for p in range(pairs):
        grad = g_ref[:, lanes(p)]
        queries += split_heads(q_ref[:, lanes(p)] * jnp.bfloat16(SCALE))
        grads += split_heads(grad)
        product = (grad.astype(jnp.float32) * o_ref[:, lanes(p)].astype(jnp.float32)).T
        for h in range(2):
            inner.append(jnp.sum(product[h * HEAD : (h + 1) * HEAD], axis=0, keepdims=True))
            logs.append(lse_ref[0, 0, 2 * p + h : 2 * p + h + 1])
    starts = start_ref[0]

    def step(masked, j, carried):
        rows = pl.ds(pl.multiple_of(j * TILE, TILE), TILE)
        if masked:
            allowed = tile_allowed(base + j * TILE, reach + i * TILE, starts)
        out = []
        for p in range(pairs):
            keys, values = k_ref[rows, lanes(p)], v_ref[rows, lanes(p)]
            dks, dvs = [], []
            for n in (2 * p, 2 * p + 1):
                s = contract_cols(keys, queries[n])
                d = contract_cols(values, grads[n])
                if masked:
                    s = jnp.where(allowed, s, NEG)
                shares = jnp.exp(s - logs[n])
                ds = (shares * (d - inner[n])).astype(jnp.bfloat16)
                dvs.append(matmul(shares.astype(jnp.bfloat16), grads[n]))
                dks.append(matmul(ds, queries[n]))
                out.append(carried[n] + matmul(k_t[n * HEAD : (n + 1) * HEAD, rows], ds))
            dv_sum[rows, lanes(p)] += dvs[0] + dvs[1]
            dk_sum[rows, lanes(p)] += dks[0] + dks[1]
        return tuple(out)

    if ends:
        state = tuple(before_ref[0, 0, n] for n in range(2 * pairs))
    else:
        state = (jnp.zeros((HEAD, TILE), jnp.float32),) * (2 * pairs)
    state = over_tiles(bounds, i, step, state)
    if ends:
        for p in range(pairs):
            turned = jnp.concatenate([state[2 * p], state[2 * p + 1]], axis=0).T
            dq_ref[:, lanes(p)] = (turned * SCALE).astype(dq_ref.dtype)
    else:
        for n in range(2 * pairs):
            after_ref[0, 0, n] = state[n]

    @pl.when(i == pl.num_programs(1) - 1)
    def _():
        dk_ref[...] = dk_sum[...].astype(dk_ref.dtype)
        dv_ref[...] = dv_sum[...].astype(dv_ref.dtype)


def self_attend_back(q, grad, o, lse, kv, starts, reach, base, before=None):
    rows, width = q.shape
    kv_rows = kv.shape[0]
    ends = before is not None
    pairs, wide, grid, block, keys, values, by_tile, start_block = attend_specs(rows, kv_rows, width)
    state = by_tile(2 * pairs, HEAD)
    shape = lambda n: jax.ShapeDtypeStruct((n, width), jnp.bfloat16)
    spec = pltpu.PrefetchScalarGridSpec(
        num_scalar_prefetch=1,
        grid=grid,
        in_specs=[block, block, block, by_tile(8), keys, values, start_block] + [state] * ends,
        out_specs=[block if ends else state, keys, keys],
        scratch_shapes=[
            pltpu.VMEM((kv_rows, wide), jnp.float32),
            pltpu.VMEM((kv_rows, wide), jnp.float32),
            pltpu.VMEM((wide, kv_rows), jnp.bfloat16),
        ],
    )
    return pl.pallas_call(
        functools.partial(attend_back_kernel, reach=reach, base=base, pairs=pairs, ends=ends),
        grid_spec=spec,
        out_shape=[
            shape(rows) if ends else jax.ShapeDtypeStruct((*grid, 2 * pairs, HEAD, TILE), jnp.float32),
            shape(kv_rows),
            shape(kv_rows),
        ],
        compiler_params=pltpu.CompilerParams(vmem_limit_bytes=VMEM_BYTES),
        cost_estimate=pl.CostEstimate(
            flops=rows * kv_rows * HEAD, bytes_accessed=rows * HEAD, transcendentals=0
        ),
        name="self_attend_back",
    )(
        tile_bounds(starts, reach, base, kv_rows), q, grad, o, lse, kv, kv, starts.reshape(-1, 1, TILE),
        *([before] if ends else []),
    )


CROSS_PAIRS = 3


def cross_kernel(q_ref, k_ref, v_ref, slot_ref, o_ref):
    lower = lax.broadcasted_iota(jnp.int32, (1, PAIR), 1) < HEAD
    tokens, texts = q_ref.shape[0], k_ref.shape[0]
    allowed = slot_ref[:, :1] == lax.broadcasted_iota(jnp.int32, (tokens, texts), 1) // TXT
    for p in range(CROSS_PAIRS):
        results = []
        for half in split_heads(q_ref[:, lanes(p)] * jnp.bfloat16(SCALE)):
            scores = jnp.where(allowed, contract_cols(half, k_ref[:, lanes(p)]), NEG)
            weights = jnp.exp(scores - jnp.max(scores, axis=1, keepdims=True))
            shares = weights / jnp.sum(weights, axis=1, keepdims=True)
            results.append(matmul(shares.astype(jnp.bfloat16), v_ref[:, lanes(p)]))
        o_ref[:, lanes(p)] = jnp.where(lower, results[0], results[1]).astype(o_ref.dtype)


def cross_attend(q, k, v, slots_wide):
    tokens, width = q.shape
    texts = k.shape[0]
    column = lambda p: (0, p)
    return pl.pallas_call(
        cross_kernel,
        grid=(width // (CROSS_PAIRS * PAIR),),
        in_specs=[
            pl.BlockSpec((tokens, CROSS_PAIRS * PAIR), column),
            pl.BlockSpec((texts, CROSS_PAIRS * PAIR), column),
            pl.BlockSpec((texts, CROSS_PAIRS * PAIR), column),
            pl.BlockSpec((tokens, PAIR), lambda p: (0, 0)),
        ],
        out_specs=pl.BlockSpec((tokens, CROSS_PAIRS * PAIR), column),
        out_shape=jax.ShapeDtypeStruct(q.shape, jnp.bfloat16),
        compiler_params=pltpu.CompilerParams(vmem_limit_bytes=VMEM_BYTES),
        cost_estimate=pl.CostEstimate(
            flops=8 * tokens * texts * width,
            bytes_accessed=4 * tokens * width,
            transcendentals=tokens * texts * width // HEAD,
        ),
        name="cross_attend",
    )(q, k, v, slots_wide)


def cross_back_kernel(q_ref, g_ref, k_ref, v_ref, slot_ref, dq_ref, dk_ref, dv_ref):
    lower = lax.broadcasted_iota(jnp.int32, (1, PAIR), 1) < HEAD
    tokens, texts = q_ref.shape[0], k_ref.shape[0]
    allowed = slot_ref[:, :1] == lax.broadcasted_iota(jnp.int32, (tokens, texts), 1) // TXT
    for p in range(CROSS_PAIRS):
        keys, values = k_ref[:, lanes(p)], v_ref[:, lanes(p)]
        halves = zip(split_heads(q_ref[:, lanes(p)] * jnp.bfloat16(SCALE)), split_heads(g_ref[:, lanes(p)]))
        dqs, dks, dvs = [], [], []
        for q_half, g_half in halves:
            scores = jnp.where(allowed, contract_cols(q_half, keys), NEG)
            weights = jnp.exp(scores - jnp.max(scores, axis=1, keepdims=True))
            shares = weights / jnp.sum(weights, axis=1, keepdims=True)
            grad_shares = contract_cols(g_half, values)
            inner = jnp.sum(shares * grad_shares, axis=1, keepdims=True)
            grad_scores = (shares * (grad_shares - inner)).astype(jnp.bfloat16)
            dqs.append(matmul(grad_scores, keys))
            dks.append(contract_rows(grad_scores, q_half))
            dvs.append(contract_rows(shares.astype(jnp.bfloat16), g_half))
        dq_ref[:, lanes(p)] = (jnp.where(lower, dqs[0], dqs[1]) * SCALE).astype(dq_ref.dtype)
        dk_ref[:, lanes(p)] = dks[0] + dks[1]
        dv_ref[:, lanes(p)] = dvs[0] + dvs[1]


def cross_attend_back(q, grad, k, v, slots_wide):
    tokens, width = q.shape
    texts = k.shape[0]
    column = lambda p: (0, p)
    return pl.pallas_call(
        cross_back_kernel,
        grid=(width // (CROSS_PAIRS * PAIR),),
        in_specs=[
            pl.BlockSpec((tokens, CROSS_PAIRS * PAIR), column),
            pl.BlockSpec((tokens, CROSS_PAIRS * PAIR), column),
            pl.BlockSpec((texts, CROSS_PAIRS * PAIR), column),
            pl.BlockSpec((texts, CROSS_PAIRS * PAIR), column),
            pl.BlockSpec((tokens, PAIR), lambda p: (0, 0)),
        ],
        out_specs=[
            pl.BlockSpec((tokens, CROSS_PAIRS * PAIR), column),
            pl.BlockSpec((texts, CROSS_PAIRS * PAIR), column),
            pl.BlockSpec((texts, CROSS_PAIRS * PAIR), column),
        ],
        out_shape=[
            jax.ShapeDtypeStruct(q.shape, jnp.bfloat16),
            jax.ShapeDtypeStruct((texts, width), jnp.float32),
            jax.ShapeDtypeStruct((texts, width), jnp.float32),
        ],
        compiler_params=pltpu.CompilerParams(vmem_limit_bytes=VMEM_BYTES),
        cost_estimate=pl.CostEstimate(
            flops=20 * tokens * texts * width,
            bytes_accessed=6 * tokens * width,
            transcendentals=tokens * texts * width // HEAD,
        ),
        name="cross_attend_back",
    )(q, grad, k, v, slots_wide)


def swap(value, axis, bit):
    count = lax.axis_size(axis)
    return lax.ppermute(value, axis, [(i, i ^ bit) for i in range(count)])


def passed_along(value, axis, steps):
    count = lax.axis_size(axis)
    initial, last = (max(0, -steps), min(count, count - steps))
    return lax.ppermute(value, axis, [(source, source + steps) for source in range(initial, last)])


def in_order(mine, other, dim):
    second = lax.axis_index("seq") == 1
    return jnp.concatenate([jnp.where(second, other, mine), jnp.where(second, mine, other)], axis=dim)


def gathered(value, dim):
    if lax.axis_size("seq") == 2:
        return in_order(value, swap(value, "seq", 1), dim)
    return lax.all_gather(value, "seq", axis=dim, tiled=True)


def own_block(value, dim):
    size = value.shape[dim] // lax.axis_size("seq")
    return lax.dynamic_slice_in_dim(value, lax.axis_index("seq") * size, size, dim)


def other_block(value, dim):
    size = value.shape[dim] // 2
    return lax.dynamic_slice_in_dim(value, (1 - lax.axis_index("seq")) * size, size, dim)


def exchanged(value, split, concat):
    if lax.axis_size("seq") == 2:
        return in_order(own_block(value, split), swap(other_block(value, split), "seq", 1), concat)
    return lax.all_to_all(value, "seq", split_axis=split, concat_axis=concat, tiled=True)


def summed_block(value, dim):
    if lax.axis_size("seq") == 2:
        received = swap(other_block(value, dim).astype(jnp.bfloat16), "seq", 1)
        return own_block(value, dim) + received.astype(jnp.float32)
    return lax.psum_scatter(
        value.astype(jnp.bfloat16), "seq", scatter_dimension=dim, tiled=True
    ).astype(jnp.float32)


def paired(value):
    short = -value.shape[-1] % PAIR
    return jnp.pad(value, ((0, 0), (0, short))) if short else value


def normed(values):
    average = jnp.mean(values, axis=-1, keepdims=True)
    centred = values - average
    spread = jnp.mean(centred * centred, axis=-1, keepdims=True)
    root = lax.rsqrt(spread + EPS)
    return centred * root, root


def norm_back(grad, n, root, gain):
    a = grad * gain
    back = (a - jnp.mean(a, axis=-1, keepdims=True) - n * jnp.mean(a * n, axis=-1, keepdims=True)) * root
    return back, jnp.sum(grad * n, axis=0), jnp.sum(grad, axis=0)


def scattered(grad):
    return lax.psum_scatter(grad.astype(jnp.bfloat16), "fsdp", scatter_dimension=0, tiled=True)


def whole(part):
    if lax.axis_size("seq") == 2:
        return part.astype(jnp.float32) + swap(part, "seq", 1).astype(jnp.float32)
    return lax.psum(part, "seq").astype(jnp.float32)


def columns(part, blocks):
    split = part.reshape(part.shape[0], blocks, -1)
    return gathered(split, 2).reshape(part.shape[0], -1).astype(jnp.float32)


def core_products(left, right):
    size, core = right.shape[1] // 2, lax.axis_index("fsdp") % 2
    part = lambda place: contract_rows(left, lax.dynamic_slice_in_dim(right, place * size, size, 1)).astype(jnp.bfloat16)
    return part(core), part(1 - core)


def both(first, second):
    return (first.astype(jnp.float32) + second.astype(jnp.float32)).astype(jnp.bfloat16)


def half_rows(value, place):
    blocks = value.reshape(-1, 2, *value.shape[1:])
    return lax.dynamic_index_in_dim(blocks, place % 2, 1, keepdims=False)


def seq_away(kept, came):
    return both(other_block(kept, 1), other_block(came, 1))


def chip_blocks(kept, came, beside):
    value = both(both(own_block(kept, 1), own_block(came, 1)), beside)
    return value.reshape(lax.axis_size("fsdp") // 2, -1, value.shape[1])


def own_rows(value, at, bit):
    while value.shape[0] > 1:
        value = both(half_rows(value, at), swap(half_rows(value, at + 1), "fsdp", bit))
        at, bit = at // 2, bit * 2
    core, second = lax.axis_index("fsdp") % 2, lax.axis_index("seq") == 1
    value = value.reshape(2, -1, value.shape[-1])
    take = lambda place: lax.dynamic_index_in_dim(value, place, 0, keepdims=False)
    mine, theirs = take(core), swap(take(1 - core), "fsdp", 1)
    pair = jnp.stack([jnp.where(core == 0, mine, theirs), jnp.where(core == 0, theirs, mine)])
    beside = swap(pair, "seq", 1)
    by_seq = jnp.where(second, beside, pair), jnp.where(second, pair, beside)
    return jnp.concatenate([by_seq[s][c] for c in range(2) for s in range(2)], axis=1).astype(jnp.float32)


def clip_starts(segments, group_index, group_rows):
    padded = jnp.concatenate([jnp.full((SPAN,), -1, jnp.int32), segments])
    spans = lax.dynamic_slice_in_dim(padded, group_index * group_rows, SPAN + group_rows)
    spans = spans.reshape(-1, SPAN)
    ahead = jnp.sum((spans == spans[:, :1]).astype(jnp.int32), axis=1)
    firsts = ahead + jnp.arange(spans.shape[0], dtype=jnp.int32) * SPAN
    late = spans[1:] != spans[1:, :1]
    return jnp.where(late, firsts[1:, None], firsts[:-1, None]).reshape(group_rows), spans[1:].reshape(group_rows)


def shards(
    tokens,
    segments,
    text,
    qkv_weight,
    out_weight,
    cross_query_weight,
    cross_kv_weight,
    cross_out_weight,
    up_weight,
    down_weight,
    norm_gain,
    norm_bias,
    cotangent,
):
    group_index = lax.axis_index("fsdp")
    seq_index = lax.axis_index("seq")
    seq_count = lax.axis_size("seq")
    tok_rows, width = tokens.shape
    group_rows = tok_rows * seq_count
    head_cols = width // seq_count
    shard_rows = qkv_weight.shape[0]
    row_block = lambda value: lax.all_gather(value, "fsdp", axis=0, tiled=True)

    norms = jnp.pad(jnp.concatenate([norm_gain, norm_bias]).T, ((0, 0), (0, PAIR - 6)))
    qkv_mine = own_block(qkv_weight.reshape(shard_rows, 3, width), 2).reshape(shard_rows, 3 * head_cols)
    first = row_block(jnp.concatenate([qkv_mine, norms], axis=1))
    w_q, w_kv, w_qkv = first[:, :head_cols], first[:, head_cols : 3 * head_cols], first[:, : 3 * head_cols]
    norm_rows = first[:, 3 * head_cols : 3 * head_cols + 6].astype(jnp.float32).T
    gains, biases = norm_rows[:3], norm_rows[3:]

    ckv_mine = own_block(cross_kv_weight.reshape(shard_rows, 2, width), 2).reshape(shard_rows, 2 * head_cols)
    squares = (out_weight, cross_query_weight, cross_out_weight)
    gate = lax.optimization_barrier
    by_steps = seq_count == 2 and group_rows == SPAN
    second = row_block(jnp.concatenate([*squares, ckv_mine], axis=1))
    full_out, full_cq, full_cout = (second[:, i * width : (i + 1) * width] for i in range(3))
    w_ckv = second[:, 3 * width :]

    starts, seg_group = clip_starts(segments, group_index, group_rows)
    slots = own_block(seg_group, 0) - group_index * (group_rows // SPAN)
    slots_wide = jnp.broadcast_to(slots[:, None], (tok_rows, PAIR))

    inputs = tokens.astype(jnp.float32)
    norm_one = lambda rows: (normed(rows.astype(jnp.float32))[0] * gains[0] + biases[0]).astype(jnp.bfloat16)
    normed_one = norm_one(gathered(tokens, 0))
    kv_own = matmul(normed_one, w_kv).astype(jnp.bfloat16)
    queries = matmul(normed_one, w_q).astype(jnp.bfloat16)
    if by_steps:
        before = passed_along(tokens, "fsdp", 1)
        before_other = swap(before, "seq", 1)
    else:
        kv_before = passed_along(kv_own[group_rows - SPAN :], "fsdp", 1)
    pad_kv = lambda kv: jnp.concatenate([paired(kv[:, :head_cols]), paired(kv[:, head_cols:])], axis=1)
    if head_cols % PAIR:
        queries, kv_own, kv_before = paired(queries), pad_kv(kv_own), pad_kv(kv_before)
    heads_state = self_attend(queries, kv_own, starts, SPAN, SPAN)
    if by_steps:
        before, before_other, heads_state = gate((before, before_other, heads_state))
        kv_before = matmul(norm_one(in_order(before, before_other, 0)), w_kv).astype(jnp.bfloat16)
    heads_out, log_totals = self_attend(queries, kv_before, starts, SPAN, 0, heads_state)
    attended = exchanged(heads_out[:, :head_cols], 0, 1)
    hidden_one = inputs + matmul(attended, full_out)

    text_rows = text.reshape(-1, width)
    text_count = text_rows.shape[0]
    ckv_part = matmul(text_rows, w_ckv).astype(jnp.bfloat16).reshape(text_count, 2, head_cols)
    cross_kv = gathered(ckv_part, 2)
    cross_k, cross_v = cross_kv[:, 0], cross_kv[:, 1]
    n_two, root_two = normed(hidden_one)
    normed_two = (n_two * gains[1] + biases[1]).astype(jnp.bfloat16)
    cross_query = matmul(normed_two, full_cq).astype(jnp.bfloat16)
    cross_result = cross_attend(cross_query, cross_k, cross_v, slots_wide)
    hidden_two = hidden_one + matmul(cross_result, full_cout)

    full_up, full_down = row_block(up_weight), row_block(down_weight)
    n_three, root_three = normed(hidden_two)
    normed_three = (n_three * gains[2] + biases[2]).astype(jnp.bfloat16)
    upward = matmul(normed_three, full_up)
    below = 0.5 * (1.0 + lax.erf(upward * (0.5**0.5)))
    active = (upward * below).astype(jnp.bfloat16)
    slope = below + upward * (jnp.exp(-0.5 * upward * upward) * 0.3989422804014327)
    layer_out = (hidden_two + matmul(active, full_down)).astype(jnp.bfloat16)

    chip = group_index // 2
    grad_down, slope = gate((contract_rows(active, cotangent).astype(jnp.bfloat16), slope))
    grad_down = scattered(grad_down)
    grad_upward = (contract_cols(cotangent, full_down) * slope).astype(jnp.bfloat16)
    if by_steps:
        up_kept, up_away, grad_upward = gate((*core_products(normed_three, grad_upward), grad_upward))
        up_came = swap(up_away, "fsdp", 1)
    else:
        grad_up = scattered(contract_rows(normed_three, grad_upward))
    back_h2, gain_three, bias_three = norm_back(contract_cols(grad_upward, full_up), n_three, root_three, gains[2])
    grad_two = cotangent.astype(jnp.float32) + back_h2
    grad_two_low = grad_two.astype(jnp.bfloat16)
    if by_steps:
        up_beside, grad_two_low = gate((seq_away(up_kept, up_came), grad_two_low))
        up_beside = swap(up_beside, "seq", 1)
    grad_result = contract_cols(grad_two_low, full_cout).astype(jnp.bfloat16)
    grad_query_c, grad_text_k, grad_text_v = cross_attend_back(cross_query, grad_result, cross_k, cross_v, slots_wide)
    grad_text_kv = summed_block(jnp.stack([grad_text_k, grad_text_v], axis=1), 2)
    grad_text_kv = grad_text_kv.astype(jnp.bfloat16).reshape(text_count, 2 * head_cols)
    grad_text = contract_cols(grad_text_kv, w_ckv)
    back_h1, gain_two, bias_two = norm_back(contract_cols(grad_query_c, full_cq), n_two, root_two, gains[1])
    grad_one = grad_two + back_h1

    grad_one_low = grad_one.astype(jnp.bfloat16)
    grad_attended = contract_cols(grad_one_low, full_out).astype(jnp.bfloat16)
    grad_heads = paired(exchanged(grad_attended, 1, 0))
    small = [
        contract_rows(left, right).astype(jnp.bfloat16)
        for left, right in (
            (cross_result, grad_two_low),
            (normed_two, grad_query_c),
            (attended, grad_one_low),
            (text_rows, grad_text_kv),
        )
    ]
    if by_steps:
        small = lax.psum_scatter(gate((jnp.stack(small), grad_down, grad_heads))[0], "fsdp", scatter_dimension=1, tiled=True)
    else:
        small = [scattered(part) for part in small]
    back_args = (queries, grad_heads, heads_out, log_totals)
    query_state, *grad_before = self_attend_back(*back_args, kv_before, starts, SPAN, 0)
    returned = [passed_along(part[:, :head_cols], "fsdp", -1).astype(jnp.float32) for part in grad_before]
    if by_steps:
        up_rows = chip_blocks(up_kept, up_came, up_beside)
        up_away, grad_down, query_state = gate((half_rows(up_rows, chip + 1), grad_down, query_state))
        up_came, down_beside = swap(up_away, "fsdp", 2), swap(grad_down, "seq", 1)
    grad_q, *grad_own = self_attend_back(*back_args, kv_own, starts, SPAN, SPAN, query_state)
    if by_steps:
        down_beside, grad_q = gate((down_beside, grad_q))
        grad_down = grad_down.astype(jnp.float32) + down_beside.astype(jnp.float32)
    else:
        grad_up, grad_down = whole(grad_up), whole(grad_down)
    late = group_rows - SPAN
    owned = [grad_q[:, :head_cols]]
    for part, more in zip(grad_own, returned):
        part = part[:, :head_cols].astype(jnp.float32)
        part = jnp.concatenate([part[:late], part[late:] + more]) if late else part + more
        owned.append(part.astype(jnp.bfloat16))
    grad_proj = jnp.concatenate(owned, axis=1)
    grad_normed_one, grad_proj = gate((contract_cols(grad_proj, w_qkv), grad_proj))
    grad_wqkv = contract_rows(normed_one, grad_proj).astype(jnp.bfloat16)
    if by_steps:
        up_came, grad_normed_one = gate((up_came, grad_normed_one))
        up_rows = both(half_rows(up_rows, chip), up_came)
        up_came = swap(half_rows(up_rows, chip // 2 + 1), "fsdp", 4)
        normed_came = swap(other_block(grad_normed_one, 0).astype(jnp.bfloat16), "seq", 1)
        grad_wqkv = scattered(gate((grad_wqkv, small, normed_came))[0])
        grad_normed_one = own_block(grad_normed_one, 0) + normed_came.astype(jnp.float32)
        grad_cout, grad_cq, grad_wout = whole(small[:3])
    else:
        grad_wqkv, grad_normed_one = scattered(grad_wqkv), summed_block(grad_normed_one, 0)
        grad_cout, grad_cq, grad_wout = (whole(part) for part in small[:3])
    grad_ckv = columns(small[3], 2)
    n_one, root_one = normed(inputs)
    back_x, gain_one, bias_one = norm_back(grad_normed_one, n_one, root_one, gains[0])
    grad_tokens = (grad_one + back_x).astype(jnp.bfloat16)

    norm_grads = jnp.stack([gain_one, gain_two, gain_three, bias_one, bias_two, bias_three])
    norm_grads, grad_cout, grad_cq, grad_wout, grad_ckv = gate((norm_grads, grad_cout, grad_cq, grad_wout, grad_ckv))
    norm_grads = lax.psum(norm_grads, ("fsdp", "seq"))
    if by_steps:
        norm_grads, up_came = gate((norm_grads, up_came))
        grad_up = own_rows(both(half_rows(up_rows, chip // 2), up_came), chip // 4, 8)
    norm_grads = lax.dynamic_slice_in_dim(norm_grads, group_index * shard_rows, shard_rows, 1)
    return (
        layer_out,
        grad_tokens,
        whole(grad_text.astype(jnp.bfloat16)).reshape(text.shape),
        columns(grad_wqkv, 3),
        grad_wout,
        grad_cq,
        grad_ckv,
        grad_cout,
        grad_up,
        grad_down,
        norm_grads[:3],
        norm_grads[3:],
    )


def solution(mesh):
    rows, shard, copied = P(("fsdp", "seq"), None), P("fsdp", None), P(None, "fsdp")
    groups = P("fsdp", None, None)
    in_specs = (rows, P(), groups, *[shard] * 7, copied, copied, rows)
    out_specs = (rows, rows, groups, *[shard] * 7, copied, copied)
    return jax.shard_map(shards, mesh=mesh, in_specs=in_specs, out_specs=out_specs, check_vma=False)
```

```python
import functools

import jax
import jax.numpy as jnp
from jax import lax
from jax.experimental import pallas as pl
from jax.experimental.pallas import tpu as pltpu
from jax.sharding import PartitionSpec as P

HEADS = 24
HEAD = 64
PAIR = 2 * HEAD
TXT = 64
SPAN = 1536
EPS = 1e-05
NEG = -1e30
SCALE = HEAD**-0.5
VMEM_BYTES = 56 * 2**20


def matmul(left_side, right_side):
    return jnp.dot(left_side, right_side, preferred_element_type=jnp.float32)


def contract_rows(left_side, right_side):
    return lax.dot_general(
        left_side, right_side, (((0,), (0,)), ((), ())), preferred_element_type=jnp.float32
    )


def contract_cols(left_side, right_side):
    return lax.dot_general(
        left_side, right_side, (((1,), (1,)), ((), ())), preferred_element_type=jnp.float32
    )


TILE = 384


def tile_bounds(starts, reach, base, kv_rows):
    count = kv_rows // TILE
    first, last = starts[::TILE] - base, starts[TILE - 1 :: TILE] - base
    row0 = reach - base + jnp.arange(first.shape[0], dtype=jnp.int32) * TILE
    low = jnp.clip(first // TILE, 0, count)
    high = jnp.clip((row0 + TILE - 1) // TILE + 1, low, count)
    free_low = jnp.clip((last + TILE - 1) // TILE, low, high)
    free_high = jnp.clip((row0 + 1) // TILE, free_low, high)
    return jnp.stack([low, free_low, free_high, high], axis=1)


def pairs_a_step(width):
    return 3 if width % (3 * PAIR) == 0 else 1


def split_heads(block):
    lower = lax.broadcasted_iota(jnp.int32, (1, PAIR), 1) < HEAD
    zero = jnp.zeros((1, 1), block.dtype)
    return [jnp.where(lower, block, zero), jnp.where(lower, zero, block)]


def lanes(p):
    return slice(p * PAIR, (p + 1) * PAIR)


def tile_allowed(col0, row0, starts):
    at = col0 + lax.broadcasted_iota(jnp.int32, (TILE, TILE), 0)
    row = row0 + lax.broadcasted_iota(jnp.int32, (TILE, TILE), 1)
    return (at >= starts) & (at <= row)


def over_tiles(bounds, i, step, state):
    low, free_low, free_high, high = (bounds[i, n] for n in range(4))
    state = lax.fori_loop(low, free_low, functools.partial(step, True), state)
    state = lax.fori_loop(free_low, free_high, functools.partial(step, False), state)
    return lax.fori_loop(free_high, high, functools.partial(step, True), state)


def attend_kernel(bounds, q_ref, k_ref, v_ref, start_ref, *refs, reach, base, pairs, ends):
    i = pl.program_id(1)
    if ends:
        before_ref, o_ref, lse_ref, v_t = refs
    else:
        after_ref, v_t = refs

    @pl.when(i == 0)
    def _():
        for p in range(pairs):
            turned = v_ref[:, lanes(p)].T
            for h in range(2):
                v_t[2 * p + h, :HEAD] = turned[h * HEAD : (h + 1) * HEAD]
                v_t[2 * p + h, HEAD:] = jnp.ones((16, turned.shape[1]), jnp.bfloat16)

    halves = []
    for p in range(pairs):
        halves += split_heads(q_ref[:, lanes(p)] * jnp.bfloat16(SCALE))
    starts = start_ref[0]

    def step(masked, j, carried):
        rows = pl.ds(pl.multiple_of(j * TILE, TILE), TILE)
        if masked:
            allowed = tile_allowed(base + j * TILE, reach + i * TILE, starts)
        scores = []
        for n in range(2 * pairs):
            s = contract_cols(k_ref[rows, lanes(n // 2)], halves[n])
            scores.append(jnp.where(allowed, s, NEG) if masked else s)
        out = []
        for n, (top, total) in enumerate(carried):
            new_top = jnp.maximum(top, jnp.max(scores[n], axis=0, keepdims=True))
            weights = jnp.exp(scores[n] - new_top).astype(jnp.bfloat16)
            total = total * jnp.exp(top - new_top) + matmul(v_t[n, :, rows], weights)
            out.append((new_top, total))
        return tuple(out)

    if ends:
        state = tuple((before_ref[0, 0, n, HEAD + 8 : HEAD + 9], before_ref[0, 0, n]) for n in range(2 * pairs))
    else:
        nothing = (jnp.full((1, TILE), NEG, jnp.float32), jnp.zeros((HEAD + 16, TILE), jnp.float32))
        state = (nothing,) * (2 * pairs)
    state = over_tiles(bounds, i, step, state)
    if not ends:
        for n, (top, total) in enumerate(state):
            after_ref[0, 0, n, : HEAD + 8] = total[: HEAD + 8]
            after_ref[0, 0, n, HEAD + 8 :] = jnp.broadcast_to(top, (8, TILE))
        return
    for p in range(pairs):
        outs = []
        for n in (2 * p, 2 * p + 1):
            top, total = state[n]
            count = total[HEAD : HEAD + 1]
            outs.append(total[:HEAD] / count)
            lse_ref[0, 0, n : n + 1, :] = top + jnp.log(count)
        o_ref[:, lanes(p)] = jnp.concatenate(outs, axis=0).T.astype(o_ref.dtype)


def attend_specs(rows, kv_rows, width):
    pairs = pairs_a_step(width)
    wide = pairs * PAIR
    steps = width // wide
    block = pl.BlockSpec((TILE, wide), lambda p, i, b: (i, p))
    keys = pl.BlockSpec((kv_rows, wide), lambda p, i, b: (0, p))
    values = pl.BlockSpec((kv_rows, wide), lambda p, i, b: (0, steps + p))
    by_tile = lambda *shape: pl.BlockSpec((1, 1, *shape, TILE), lambda p, i, b: (p, i, *[0] * len(shape), 0))
    starts = pl.BlockSpec((1, 1, TILE), lambda p, i, b: (i, 0, 0))
    return pairs, wide, (steps, rows // TILE), block, keys, values, by_tile, starts


def self_attend(q, kv, starts, reach, base, before=None):
    rows, width = q.shape
    kv_rows = kv.shape[0]
    ends = before is not None
    pairs, wide, grid, block, keys, values, by_tile, start_block = attend_specs(rows, kv_rows, width)
    state = by_tile(2 * pairs, HEAD + 16)
    state_shape = jax.ShapeDtypeStruct((*grid, 2 * pairs, HEAD + 16, TILE), jnp.float32)
    spec = pltpu.PrefetchScalarGridSpec(
        num_scalar_prefetch=1,
        grid=grid,
        in_specs=[block, keys, values, start_block] + [state] * ends,
        out_specs=[block, by_tile(8)] if ends else state,
        scratch_shapes=[pltpu.VMEM((2 * pairs, HEAD + 16, kv_rows), jnp.bfloat16)],
    )
    return pl.pallas_call(
        functools.partial(attend_kernel, reach=reach, base=base, pairs=pairs, ends=ends),
        grid_spec=spec,
        out_shape=[
            jax.ShapeDtypeStruct((rows, width), jnp.bfloat16),
            jax.ShapeDtypeStruct((*grid, 8, TILE), jnp.float32),
        ]
        if ends
        else state_shape,
        compiler_params=pltpu.CompilerParams(vmem_limit_bytes=VMEM_BYTES),
        cost_estimate=pl.CostEstimate(
            flops=rows * kv_rows * HEAD, bytes_accessed=rows * HEAD, transcendentals=0
        ),
        name="self_attend",
    )(tile_bounds(starts, reach, base, kv_rows), q, kv, kv, starts.reshape(-1, 1, TILE), *([before] if ends else []))


def attend_back_kernel(bounds, q_ref, g_ref, o_ref, lse_ref, k_ref, v_ref, start_ref, *refs, reach, base, pairs, ends):
    i = pl.program_id(1)
    if ends:
        before_ref, dq_ref, dk_ref, dv_ref, dk_sum, dv_sum, k_t = refs
    else:
        after_ref, dk_ref, dv_ref, dk_sum, dv_sum, k_t = refs

    @pl.when(i == 0)
    def _():
        k_t[...] = k_ref[...].T
        dk_sum[...] = jnp.zeros_like(dk_sum)
        dv_sum[...] = jnp.zeros_like(dv_sum)

    queries, grads, inner, logs = [], [], [], []
    for p in range(pairs):
        grad = g_ref[:, lanes(p)]
        queries += split_heads(q_ref[:, lanes(p)] * jnp.bfloat16(SCALE))
        grads += split_heads(grad)
        product = (grad.astype(jnp.float32) * o_ref[:, lanes(p)].astype(jnp.float32)).T
        for h in range(2):
            inner.append(jnp.sum(product[h * HEAD : (h + 1) * HEAD], axis=0, keepdims=True))
            logs.append(lse_ref[0, 0, 2 * p + h : 2 * p + h + 1])
    starts = start_ref[0]

    def step(masked, j, carried):
        rows = pl.ds(pl.multiple_of(j * TILE, TILE), TILE)
        if masked:
            allowed = tile_allowed(base + j * TILE, reach + i * TILE, starts)
        out = []
        for p in range(pairs):
            keys, values = k_ref[rows, lanes(p)], v_ref[rows, lanes(p)]
            dks, dvs = [], []
            for n in (2 * p, 2 * p + 1):
                s = contract_cols(keys, queries[n])
                d = contract_cols(values, grads[n])
                if masked:
                    s = jnp.where(allowed, s, NEG)
                shares = jnp.exp(s - logs[n])
                ds = (shares * (d - inner[n])).astype(jnp.bfloat16)
                dvs.append(matmul(shares.astype(jnp.bfloat16), grads[n]))
                dks.append(matmul(ds, queries[n]))
                out.append(carried[n] + matmul(k_t[n * HEAD : (n + 1) * HEAD, rows], ds))
            dv_sum[rows, lanes(p)] += dvs[0] + dvs[1]
            dk_sum[rows, lanes(p)] += dks[0] + dks[1]
        return tuple(out)

    if ends:
        state = tuple(before_ref[0, 0, n] for n in range(2 * pairs))
    else:
        state = (jnp.zeros((HEAD, TILE), jnp.float32),) * (2 * pairs)
    state = over_tiles(bounds, i, step, state)
    if ends:
        for p in range(pairs):
            turned = jnp.concatenate([state[2 * p], state[2 * p + 1]], axis=0).T
            dq_ref[:, lanes(p)] = (turned * SCALE).astype(dq_ref.dtype)
    else:
        for n in range(2 * pairs):
            after_ref[0, 0, n] = state[n]

    @pl.when(i == pl.num_programs(1) - 1)
    def _():
        dk_ref[...] = dk_sum[...].astype(dk_ref.dtype)
        dv_ref[...] = dv_sum[...].astype(dv_ref.dtype)


def self_attend_back(q, grad, o, lse, kv, starts, reach, base, before=None):
    rows, width = q.shape
    kv_rows = kv.shape[0]
    ends = before is not None
    pairs, wide, grid, block, keys, values, by_tile, start_block = attend_specs(rows, kv_rows, width)
    state = by_tile(2 * pairs, HEAD)
    shape = lambda n: jax.ShapeDtypeStruct((n, width), jnp.bfloat16)
    spec = pltpu.PrefetchScalarGridSpec(
        num_scalar_prefetch=1,
        grid=grid,
        in_specs=[block, block, block, by_tile(8), keys, values, start_block] + [state] * ends,
        out_specs=[block if ends else state, keys, keys],
        scratch_shapes=[
            pltpu.VMEM((kv_rows, wide), jnp.float32),
            pltpu.VMEM((kv_rows, wide), jnp.float32),
            pltpu.VMEM((wide, kv_rows), jnp.bfloat16),
        ],
    )
    return pl.pallas_call(
        functools.partial(attend_back_kernel, reach=reach, base=base, pairs=pairs, ends=ends),
        grid_spec=spec,
        out_shape=[
            shape(rows) if ends else jax.ShapeDtypeStruct((*grid, 2 * pairs, HEAD, TILE), jnp.float32),
            shape(kv_rows),
            shape(kv_rows),
        ],
        compiler_params=pltpu.CompilerParams(vmem_limit_bytes=VMEM_BYTES),
        cost_estimate=pl.CostEstimate(
            flops=rows * kv_rows * HEAD, bytes_accessed=rows * HEAD, transcendentals=0
        ),
        name="self_attend_back",
    )(
        tile_bounds(starts, reach, base, kv_rows), q, grad, o, lse, kv, kv, starts.reshape(-1, 1, TILE),
        *([before] if ends else []),
    )


CROSS_PAIRS = 3


def cross_kernel(q_ref, k_ref, v_ref, slot_ref, o_ref):
    lower = lax.broadcasted_iota(jnp.int32, (1, PAIR), 1) < HEAD
    tokens, texts = q_ref.shape[0], k_ref.shape[0]
    allowed = slot_ref[:, :1] == lax.broadcasted_iota(jnp.int32, (tokens, texts), 1) // TXT
    for p in range(CROSS_PAIRS):
        results = []
        for half in split_heads(q_ref[:, lanes(p)] * jnp.bfloat16(SCALE)):
            scores = jnp.where(allowed, contract_cols(half, k_ref[:, lanes(p)]), NEG)
            weights = jnp.exp(scores - jnp.max(scores, axis=1, keepdims=True))
            shares = weights / jnp.sum(weights, axis=1, keepdims=True)
            results.append(matmul(shares.astype(jnp.bfloat16), v_ref[:, lanes(p)]))
        o_ref[:, lanes(p)] = jnp.where(lower, results[0], results[1]).astype(o_ref.dtype)


def cross_attend(q, k, v, slots_wide):
    tokens, width = q.shape
    texts = k.shape[0]
    column = lambda p: (0, p)
    return pl.pallas_call(
        cross_kernel,
        grid=(width // (CROSS_PAIRS * PAIR),),
        in_specs=[
            pl.BlockSpec((tokens, CROSS_PAIRS * PAIR), column),
            pl.BlockSpec((texts, CROSS_PAIRS * PAIR), column),
            pl.BlockSpec((texts, CROSS_PAIRS * PAIR), column),
            pl.BlockSpec((tokens, PAIR), lambda p: (0, 0)),
        ],
        out_specs=pl.BlockSpec((tokens, CROSS_PAIRS * PAIR), column),
        out_shape=jax.ShapeDtypeStruct(q.shape, jnp.bfloat16),
        compiler_params=pltpu.CompilerParams(vmem_limit_bytes=VMEM_BYTES),
        cost_estimate=pl.CostEstimate(
            flops=8 * tokens * texts * width,
            bytes_accessed=4 * tokens * width,
            transcendentals=tokens * texts * width // HEAD,
        ),
        name="cross_attend",
    )(q, k, v, slots_wide)


def cross_back_kernel(q_ref, g_ref, k_ref, v_ref, slot_ref, dq_ref, dk_ref, dv_ref):
    lower = lax.broadcasted_iota(jnp.int32, (1, PAIR), 1) < HEAD
    tokens, texts = q_ref.shape[0], k_ref.shape[0]
    allowed = slot_ref[:, :1] == lax.broadcasted_iota(jnp.int32, (tokens, texts), 1) // TXT
    for p in range(CROSS_PAIRS):
        keys, values = k_ref[:, lanes(p)], v_ref[:, lanes(p)]
        halves = zip(split_heads(q_ref[:, lanes(p)] * jnp.bfloat16(SCALE)), split_heads(g_ref[:, lanes(p)]))
        dqs, dks, dvs = [], [], []
        for q_half, g_half in halves:
            scores = jnp.where(allowed, contract_cols(q_half, keys), NEG)
            weights = jnp.exp(scores - jnp.max(scores, axis=1, keepdims=True))
            shares = weights / jnp.sum(weights, axis=1, keepdims=True)
            grad_shares = contract_cols(g_half, values)
            inner = jnp.sum(shares * grad_shares, axis=1, keepdims=True)
            grad_scores = (shares * (grad_shares - inner)).astype(jnp.bfloat16)
            dqs.append(matmul(grad_scores, keys))
            dks.append(contract_rows(grad_scores, q_half))
            dvs.append(contract_rows(shares.astype(jnp.bfloat16), g_half))
        dq_ref[:, lanes(p)] = (jnp.where(lower, dqs[0], dqs[1]) * SCALE).astype(dq_ref.dtype)
        dk_ref[:, lanes(p)] = dks[0] + dks[1]
        dv_ref[:, lanes(p)] = dvs[0] + dvs[1]


def cross_attend_back(q, grad, k, v, slots_wide):
    tokens, width = q.shape
    texts = k.shape[0]
    column = lambda p: (0, p)
    return pl.pallas_call(
        cross_back_kernel,
        grid=(width // (CROSS_PAIRS * PAIR),),
        in_specs=[
            pl.BlockSpec((tokens, CROSS_PAIRS * PAIR), column),
            pl.BlockSpec((tokens, CROSS_PAIRS * PAIR), column),
            pl.BlockSpec((texts, CROSS_PAIRS * PAIR), column),
            pl.BlockSpec((texts, CROSS_PAIRS * PAIR), column),
            pl.BlockSpec((tokens, PAIR), lambda p: (0, 0)),
        ],
        out_specs=[
            pl.BlockSpec((tokens, CROSS_PAIRS * PAIR), column),
            pl.BlockSpec((texts, CROSS_PAIRS * PAIR), column),
            pl.BlockSpec((texts, CROSS_PAIRS * PAIR), column),
        ],
        out_shape=[
            jax.ShapeDtypeStruct(q.shape, jnp.bfloat16),
            jax.ShapeDtypeStruct((texts, width), jnp.float32),
            jax.ShapeDtypeStruct((texts, width), jnp.float32),
        ],
        compiler_params=pltpu.CompilerParams(vmem_limit_bytes=VMEM_BYTES),
        cost_estimate=pl.CostEstimate(
            flops=20 * tokens * texts * width,
            bytes_accessed=6 * tokens * width,
            transcendentals=tokens * texts * width // HEAD,
        ),
        name="cross_attend_back",
    )(q, grad, k, v, slots_wide)


def swap(value, axis, bit):
    count = lax.axis_size(axis)
    return lax.ppermute(value, axis, [(i, i ^ bit) for i in range(count)])


def passed_along(value, axis, steps):
    count = lax.axis_size(axis)
    initial, last = (max(0, -steps), min(count, count - steps))
    return lax.ppermute(value, axis, [(source, source + steps) for source in range(initial, last)])


def in_order(mine, other, dim):
    second = lax.axis_index("seq") == 1
    return jnp.concatenate([jnp.where(second, other, mine), jnp.where(second, mine, other)], axis=dim)


def gathered(value, dim):
    if lax.axis_size("seq") == 2:
        return in_order(value, swap(value, "seq", 1), dim)
    return lax.all_gather(value, "seq", axis=dim, tiled=True)


def own_block(value, dim):
    size = value.shape[dim] // lax.axis_size("seq")
    return lax.dynamic_slice_in_dim(value, lax.axis_index("seq") * size, size, dim)


def other_block(value, dim):
    size = value.shape[dim] // 2
    return lax.dynamic_slice_in_dim(value, (1 - lax.axis_index("seq")) * size, size, dim)


def exchanged(value, split, concat):
    if lax.axis_size("seq") == 2:
        return in_order(own_block(value, split), swap(other_block(value, split), "seq", 1), concat)
    return lax.all_to_all(value, "seq", split_axis=split, concat_axis=concat, tiled=True)


def summed_block(value, dim):
    if lax.axis_size("seq") == 2:
        received = swap(other_block(value, dim).astype(jnp.bfloat16), "seq", 1)
        return own_block(value, dim) + received.astype(jnp.float32)
    return lax.psum_scatter(
        value.astype(jnp.bfloat16), "seq", scatter_dimension=dim, tiled=True
    ).astype(jnp.float32)


def paired(value):
    short = -value.shape[-1] % PAIR
    return jnp.pad(value, ((0, 0), (0, short))) if short else value


def normed(values):
    average = jnp.mean(values, axis=-1, keepdims=True)
    centred = values - average
    spread = jnp.mean(centred * centred, axis=-1, keepdims=True)
    root = lax.rsqrt(spread + EPS)
    return centred * root, root


def norm_back(grad, n, root, gain):
    a = grad * gain
    back = (a - jnp.mean(a, axis=-1, keepdims=True) - n * jnp.mean(a * n, axis=-1, keepdims=True)) * root
    return back, jnp.sum(grad * n, axis=0), jnp.sum(grad, axis=0)


def scattered(grad):
    return lax.psum_scatter(grad.astype(jnp.bfloat16), "fsdp", scatter_dimension=0, tiled=True)


def whole(part):
    if lax.axis_size("seq") == 2:
        return part.astype(jnp.float32) + swap(part, "seq", 1).astype(jnp.float32)
    return lax.psum(part, "seq").astype(jnp.float32)


def columns(part, blocks):
    split = part.reshape(part.shape[0], blocks, -1)
    return gathered(split, 2).reshape(part.shape[0], -1).astype(jnp.float32)


def core_products(left, right):
    size, core = right.shape[1] // 2, lax.axis_index("fsdp") % 2
    part = lambda place: contract_rows(left, lax.dynamic_slice_in_dim(right, place * size, size, 1)).astype(jnp.bfloat16)
    return part(core), part(1 - core)


def both(first, second):
    return (first.astype(jnp.float32) + second.astype(jnp.float32)).astype(jnp.bfloat16)


def half_rows(value, place):
    blocks = value.reshape(-1, 2, *value.shape[1:])
    return lax.dynamic_index_in_dim(blocks, place % 2, 1, keepdims=False)


def seq_away(kept, came):
    return both(other_block(kept, 1), other_block(came, 1))


def chip_blocks(kept, came, beside):
    value = both(both(own_block(kept, 1), own_block(came, 1)), beside)
    return value.reshape(lax.axis_size("fsdp") // 2, -1, value.shape[1])


def own_rows(value, at, bit):
    while value.shape[0] > 1:
        value = both(half_rows(value, at), swap(half_rows(value, at + 1), "fsdp", bit))
        at, bit = at // 2, bit * 2
    core, second = lax.axis_index("fsdp") % 2, lax.axis_index("seq") == 1
    value = value.reshape(2, -1, value.shape[-1])
    take = lambda place: lax.dynamic_index_in_dim(value, place, 0, keepdims=False)
    mine, theirs = take(core), swap(take(1 - core), "fsdp", 1)
    pair = jnp.stack([jnp.where(core == 0, mine, theirs), jnp.where(core == 0, theirs, mine)])
    beside = swap(pair, "seq", 1)
    by_seq = jnp.where(second, beside, pair), jnp.where(second, pair, beside)
    return jnp.concatenate([by_seq[s][c] for c in range(2) for s in range(2)], axis=1).astype(jnp.float32)


def clip_starts(segments, group_index, group_rows):
    padded = jnp.concatenate([jnp.full((SPAN,), -1, jnp.int32), segments])
    spans = lax.dynamic_slice_in_dim(padded, group_index * group_rows, SPAN + group_rows)
    spans = spans.reshape(-1, SPAN)
    ahead = jnp.sum((spans == spans[:, :1]).astype(jnp.int32), axis=1)
    firsts = ahead + jnp.arange(spans.shape[0], dtype=jnp.int32) * SPAN
    late = spans[1:] != spans[1:, :1]
    return jnp.where(late, firsts[1:, None], firsts[:-1, None]).reshape(group_rows), spans[1:].reshape(group_rows)


def shards(
    tokens,
    segments,
    text,
    qkv_weight,
    out_weight,
    cross_query_weight,
    cross_kv_weight,
    cross_out_weight,
    up_weight,
    down_weight,
    norm_gain,
    norm_bias,
    cotangent,
):
    group_index = lax.axis_index("fsdp")
    seq_index = lax.axis_index("seq")
    seq_count = lax.axis_size("seq")
    tok_rows, width = tokens.shape
    group_rows = tok_rows * seq_count
    head_cols = width // seq_count
    shard_rows = qkv_weight.shape[0]
    row_block = lambda value: lax.all_gather(value, "fsdp", axis=0, tiled=True)

    norms = jnp.pad(jnp.concatenate([norm_gain, norm_bias]).T, ((0, 0), (0, PAIR - 6)))
    qkv_mine = own_block(qkv_weight.reshape(shard_rows, 3, width), 2).reshape(shard_rows, 3 * head_cols)
    first = row_block(jnp.concatenate([qkv_mine, norms], axis=1))
    w_q, w_kv, w_qkv = first[:, :head_cols], first[:, head_cols : 3 * head_cols], first[:, : 3 * head_cols]
    norm_rows = first[:, 3 * head_cols : 3 * head_cols + 6].astype(jnp.float32).T
    gains, biases = norm_rows[:3], norm_rows[3:]

    ckv_mine = own_block(cross_kv_weight.reshape(shard_rows, 2, width), 2).reshape(shard_rows, 2 * head_cols)
    squares = (out_weight, cross_query_weight, cross_out_weight)
    gate = lax.optimization_barrier
    by_steps = seq_count == 2 and group_rows == SPAN
    second = row_block(jnp.concatenate([*squares, ckv_mine], axis=1))
    full_out, full_cq, full_cout = (second[:, i * width : (i + 1) * width] for i in range(3))
    w_ckv = second[:, 3 * width :]

    starts, seg_group = clip_starts(segments, group_index, group_rows)
    slots = own_block(seg_group, 0) - group_index * (group_rows // SPAN)
    slots_wide = jnp.broadcast_to(slots[:, None], (tok_rows, PAIR))

    inputs = tokens.astype(jnp.float32)
    norm_one = lambda rows: (normed(rows.astype(jnp.float32))[0] * gains[0] + biases[0]).astype(jnp.bfloat16)
    normed_one = norm_one(gathered(tokens, 0))
    kv_own = matmul(normed_one, w_kv).astype(jnp.bfloat16)
    queries = matmul(normed_one, w_q).astype(jnp.bfloat16)
    if by_steps:
        before = passed_along(tokens, "fsdp", 1)
        before_other = swap(before, "seq", 1)
    else:
        kv_before = passed_along(kv_own[group_rows - SPAN :], "fsdp", 1)
    pad_kv = lambda kv: jnp.concatenate([paired(kv[:, :head_cols]), paired(kv[:, head_cols:])], axis=1)
    if head_cols % PAIR:
        queries, kv_own, kv_before = paired(queries), pad_kv(kv_own), pad_kv(kv_before)
    heads_state = self_attend(queries, kv_own, starts, SPAN, SPAN)
    if by_steps:
        before, before_other, heads_state = gate((before, before_other, heads_state))
        kv_before = matmul(norm_one(in_order(before, before_other, 0)), w_kv).astype(jnp.bfloat16)
    heads_out, log_totals = self_attend(queries, kv_before, starts, SPAN, 0, heads_state)
    attended = exchanged(heads_out[:, :head_cols], 0, 1)
    hidden_one = inputs + matmul(attended, full_out)

    text_rows = text.reshape(-1, width)
    text_count = text_rows.shape[0]
    ckv_part = matmul(text_rows, w_ckv).astype(jnp.bfloat16).reshape(text_count, 2, head_cols)
    cross_kv = gathered(ckv_part, 2)
    cross_k, cross_v = cross_kv[:, 0], cross_kv[:, 1]
    n_two, root_two = normed(hidden_one)
    normed_two = (n_two * gains[1] + biases[1]).astype(jnp.bfloat16)
    cross_query = matmul(normed_two, full_cq).astype(jnp.bfloat16)
    cross_result = cross_attend(cross_query, cross_k, cross_v, slots_wide)
    hidden_two = hidden_one + matmul(cross_result, full_cout)

    full_up, full_down = row_block(up_weight), row_block(down_weight)
    n_three, root_three = normed(hidden_two)
    normed_three = (n_three * gains[2] + biases[2]).astype(jnp.bfloat16)
    upward = matmul(normed_three, full_up)
    below = 0.5 * (1.0 + lax.erf(upward * (0.5**0.5)))
    active = (upward * below).astype(jnp.bfloat16)
    slope = below + upward * (jnp.exp(-0.5 * upward * upward) * 0.3989422804014327)
    layer_out = (hidden_two + matmul(active, full_down)).astype(jnp.bfloat16)

    chip = group_index // 2
    grad_down, slope = gate((contract_rows(active, cotangent).astype(jnp.bfloat16), slope))
    grad_down = scattered(grad_down)
    grad_upward = (contract_cols(cotangent, full_down) * slope).astype(jnp.bfloat16)
    if by_steps:
        up_kept, up_away, grad_upward = gate((*core_products(normed_three, grad_upward), grad_upward))
        up_came = swap(up_away, "fsdp", 1)
    else:
        grad_up = scattered(contract_rows(normed_three, grad_upward))
    back_h2, gain_three, bias_three = norm_back(contract_cols(grad_upward, full_up), n_three, root_three, gains[2])
    grad_two = cotangent.astype(jnp.float32) + back_h2
    grad_two_low = grad_two.astype(jnp.bfloat16)
    if by_steps:
        up_beside, grad_two_low = gate((seq_away(up_kept, up_came), grad_two_low))
        up_beside = swap(up_beside, "seq", 1)
    grad_result = contract_cols(grad_two_low, full_cout).astype(jnp.bfloat16)
    grad_query_c, grad_text_k, grad_text_v = cross_attend_back(cross_query, grad_result, cross_k, cross_v, slots_wide)
    grad_text_kv = summed_block(jnp.stack([grad_text_k, grad_text_v], axis=1), 2)
    grad_text_kv = grad_text_kv.astype(jnp.bfloat16).reshape(text_count, 2 * head_cols)
    grad_text = contract_cols(grad_text_kv, w_ckv)
    back_h1, gain_two, bias_two = norm_back(contract_cols(grad_query_c, full_cq), n_two, root_two, gains[1])
    grad_one = grad_two + back_h1

    grad_one_low = grad_one.astype(jnp.bfloat16)
    grad_attended = contract_cols(grad_one_low, full_out).astype(jnp.bfloat16)
    grad_attended, grad_query_c, grad_two_low = gate((grad_attended, grad_query_c, grad_two_low))
    grad_heads = paired(exchanged(grad_attended, 1, 0))
    small = [
        contract_rows(left, right).astype(jnp.bfloat16)
        for left, right in (
            (cross_result, grad_two_low),
            (normed_two, grad_query_c),
            (attended, grad_one_low),
            (text_rows, grad_text_kv),
        )
    ]
    if by_steps:
        small = lax.psum_scatter(gate((jnp.stack(small), grad_down, grad_heads))[0], "fsdp", scatter_dimension=1, tiled=True)
    else:
        small = [scattered(part) for part in small]
    back_args = (queries, grad_heads, heads_out, log_totals)
    query_state, *grad_before = self_attend_back(*back_args, kv_before, starts, SPAN, 0)
    returned = [passed_along(part[:, :head_cols], "fsdp", -1).astype(jnp.float32) for part in grad_before]
    if by_steps:
        up_rows = chip_blocks(up_kept, up_came, up_beside)
        up_away, grad_down, query_state = gate((half_rows(up_rows, chip + 1), grad_down, query_state))
        up_came, down_beside = swap(up_away, "fsdp", 2), swap(grad_down, "seq", 1)
    grad_q, *grad_own = self_attend_back(*back_args, kv_own, starts, SPAN, SPAN, query_state)
    if by_steps:
        down_beside, grad_q = gate((down_beside, grad_q))
        grad_down = grad_down.astype(jnp.float32) + down_beside.astype(jnp.float32)
    else:
        grad_up, grad_down = whole(grad_up), whole(grad_down)
    late = group_rows - SPAN
    owned = [grad_q[:, :head_cols]]
    for part, more in zip(grad_own, returned):
        part = part[:, :head_cols].astype(jnp.float32)
        part = jnp.concatenate([part[:late], part[late:] + more]) if late else part + more
        owned.append(part.astype(jnp.bfloat16))
    grad_proj = jnp.concatenate(owned, axis=1)
    grad_normed_one, grad_proj = gate((contract_cols(grad_proj, w_qkv), grad_proj))
    grad_normed_one = summed_block(grad_normed_one, 0)
    grad_wqkv = contract_rows(normed_one, grad_proj).astype(jnp.bfloat16)
    n_one, root_one = normed(inputs)
    back_x, gain_one, bias_one = norm_back(grad_normed_one, n_one, root_one, gains[0])
    grad_tokens = (grad_one + back_x).astype(jnp.bfloat16)
    norm_grads = jnp.stack([gain_one, gain_two, gain_three, bias_one, bias_two, bias_three])
    norm_grads = jnp.pad(norm_grads.T.astype(jnp.bfloat16), ((0, 0), (0, PAIR - 6)))
    last, small = gate((jnp.concatenate([grad_wqkv, norm_grads], axis=1), small))
    if by_steps:
        up_came, last = gate((up_came, last))
    last = scattered(last)
    if by_steps:
        grad_cout, grad_cq, grad_wout = whole(small[:3])
        grad_up = own_rows(both(half_rows(up_rows, chip), up_came), chip // 2, 4)
    else:
        grad_cout, grad_cq, grad_wout = (whole(part) for part in small[:3])
    grad_ckv = columns(small[3], 2)
    last, grad_cout, grad_cq, grad_wout, grad_ckv, grad_up = gate(
        (last, grad_cout, grad_cq, grad_wout, grad_ckv, grad_up)
    )
    norm_grads = whole(last[:, -PAIR:]).T
    return (
        layer_out,
        grad_tokens,
        whole(grad_text.astype(jnp.bfloat16)).reshape(text.shape),
        columns(last[:, : 3 * head_cols], 3),
        grad_wout,
        grad_cq,
        grad_ckv,
        grad_cout,
        grad_up,
        grad_down,
        norm_grads[:3],
        norm_grads[3:6],
    )


def solution(mesh):
    rows, shard, copied = P(("fsdp", "seq"), None), P("fsdp", None), P(None, "fsdp")
    groups = P("fsdp", None, None)
    in_specs = (rows, P(), groups, *[shard] * 7, copied, copied, rows)
    out_specs = (rows, rows, groups, *[shard] * 7, copied, copied)
    return jax.shard_map(shards, mesh=mesh, in_specs=in_specs, out_specs=out_specs, check_vma=False)
```

```python
import functools

import jax
import jax.numpy as jnp
from jax import lax
from jax.experimental import pallas as pl
from jax.experimental.pallas import tpu as pltpu
from jax.sharding import PartitionSpec as P

HEADS = 24
HEAD = 64
PAIR = 2 * HEAD
TXT = 64
SPAN = 1536
EPS = 1e-05
NEG = -1e30
SCALE = HEAD**-0.5
VMEM_BYTES = 56 * 2**20


def matmul(left_side, right_side):
    return jnp.dot(left_side, right_side, preferred_element_type=jnp.float32)


def contract_rows(left_side, right_side):
    return lax.dot_general(
        left_side, right_side, (((0,), (0,)), ((), ())), preferred_element_type=jnp.float32
    )


def contract_cols(left_side, right_side):
    return lax.dot_general(
        left_side, right_side, (((1,), (1,)), ((), ())), preferred_element_type=jnp.float32
    )


TILE = 384


def tile_bounds(starts, reach, base, kv_rows):
    count = kv_rows // TILE
    first, last = starts[::TILE] - base, starts[TILE - 1 :: TILE] - base
    row0 = reach - base + jnp.arange(first.shape[0], dtype=jnp.int32) * TILE
    low = jnp.clip(first // TILE, 0, count)
    high = jnp.clip((row0 + TILE - 1) // TILE + 1, low, count)
    free_low = jnp.clip((last + TILE - 1) // TILE, low, high)
    free_high = jnp.clip((row0 + 1) // TILE, free_low, high)
    return jnp.stack([low, free_low, free_high, high], axis=1)


def pairs_a_step(width):
    return 3 if width % (3 * PAIR) == 0 else 1


def split_heads(block):
    lower = lax.broadcasted_iota(jnp.int32, (1, PAIR), 1) < HEAD
    zero = jnp.zeros((1, 1), block.dtype)
    return [jnp.where(lower, block, zero), jnp.where(lower, zero, block)]


def lanes(p):
    return slice(p * PAIR, (p + 1) * PAIR)


def tile_allowed(col0, row0, starts):
    at = col0 + lax.broadcasted_iota(jnp.int32, (TILE, TILE), 0)
    row = row0 + lax.broadcasted_iota(jnp.int32, (TILE, TILE), 1)
    return (at >= starts) & (at <= row)


def over_tiles(bounds, i, step, state):
    low, free_low, free_high, high = (bounds[i, n] for n in range(4))
    state = lax.fori_loop(low, free_low, functools.partial(step, True), state)
    state = lax.fori_loop(free_low, free_high, functools.partial(step, False), state)
    return lax.fori_loop(free_high, high, functools.partial(step, True), state)


def attend_kernel(bounds, q_ref, k_ref, v_ref, start_ref, *refs, reach, base, pairs, ends):
    i = pl.program_id(1)
    if ends:
        before_ref, o_ref, lse_ref, v_t = refs
    else:
        after_ref, v_t = refs

    @pl.when(i == 0)
    def _():
        for p in range(pairs):
            turned = v_ref[:, lanes(p)].T
            for h in range(2):
                v_t[2 * p + h, :HEAD] = turned[h * HEAD : (h + 1) * HEAD]
                v_t[2 * p + h, HEAD:] = jnp.ones((16, turned.shape[1]), jnp.bfloat16)

    halves = []
    for p in range(pairs):
        halves += split_heads(q_ref[:, lanes(p)] * jnp.bfloat16(SCALE))
    starts = start_ref[0]

    def step(masked, j, carried):
        rows = pl.ds(pl.multiple_of(j * TILE, TILE), TILE)
        if masked:
            allowed = tile_allowed(base + j * TILE, reach + i * TILE, starts)
        scores = []
        for n in range(2 * pairs):
            s = contract_cols(k_ref[rows, lanes(n // 2)], halves[n])
            scores.append(jnp.where(allowed, s, NEG) if masked else s)
        out = []
        for n, (top, total) in enumerate(carried):
            new_top = jnp.maximum(top, jnp.max(scores[n], axis=0, keepdims=True))
            weights = jnp.exp(scores[n] - new_top).astype(jnp.bfloat16)
            total = total * jnp.exp(top - new_top) + matmul(v_t[n, :, rows], weights)
            out.append((new_top, total))
        return tuple(out)

    if ends:
        state = tuple((before_ref[0, 0, n, HEAD + 8 : HEAD + 9], before_ref[0, 0, n]) for n in range(2 * pairs))
    else:
        nothing = (jnp.full((1, TILE), NEG, jnp.float32), jnp.zeros((HEAD + 16, TILE), jnp.float32))
        state = (nothing,) * (2 * pairs)
    state = over_tiles(bounds, i, step, state)
    if not ends:
        for n, (top, total) in enumerate(state):
            after_ref[0, 0, n, : HEAD + 8] = total[: HEAD + 8]
            after_ref[0, 0, n, HEAD + 8 :] = jnp.broadcast_to(top, (8, TILE))
        return
    for p in range(pairs):
        outs = []
        for n in (2 * p, 2 * p + 1):
            top, total = state[n]
            count = total[HEAD : HEAD + 1]
            outs.append(total[:HEAD] / count)
            lse_ref[0, 0, n : n + 1, :] = top + jnp.log(count)
        o_ref[:, lanes(p)] = jnp.concatenate(outs, axis=0).T.astype(o_ref.dtype)


def attend_specs(rows, kv_rows, width):
    pairs = pairs_a_step(width)
    wide = pairs * PAIR
    steps = width // wide
    block = pl.BlockSpec((TILE, wide), lambda p, i, b: (i, p))
    keys = pl.BlockSpec((kv_rows, wide), lambda p, i, b: (0, p))
    values = pl.BlockSpec((kv_rows, wide), lambda p, i, b: (0, steps + p))
    by_tile = lambda *shape: pl.BlockSpec((1, 1, *shape, TILE), lambda p, i, b: (p, i, *[0] * len(shape), 0))
    starts = pl.BlockSpec((1, 1, TILE), lambda p, i, b: (i, 0, 0))
    return pairs, wide, (steps, rows // TILE), block, keys, values, by_tile, starts


def self_attend(q, kv, starts, reach, base, before=None):
    rows, width = q.shape
    kv_rows = kv.shape[0]
    ends = before is not None
    pairs, wide, grid, block, keys, values, by_tile, start_block = attend_specs(rows, kv_rows, width)
    state = by_tile(2 * pairs, HEAD + 16)
    state_shape = jax.ShapeDtypeStruct((*grid, 2 * pairs, HEAD + 16, TILE), jnp.float32)
    spec = pltpu.PrefetchScalarGridSpec(
        num_scalar_prefetch=1,
        grid=grid,
        in_specs=[block, keys, values, start_block] + [state] * ends,
        out_specs=[block, by_tile(8)] if ends else state,
        scratch_shapes=[pltpu.VMEM((2 * pairs, HEAD + 16, kv_rows), jnp.bfloat16)],
    )
    return pl.pallas_call(
        functools.partial(attend_kernel, reach=reach, base=base, pairs=pairs, ends=ends),
        grid_spec=spec,
        out_shape=[
            jax.ShapeDtypeStruct((rows, width), jnp.bfloat16),
            jax.ShapeDtypeStruct((*grid, 8, TILE), jnp.float32),
        ]
        if ends
        else state_shape,
        compiler_params=pltpu.CompilerParams(vmem_limit_bytes=VMEM_BYTES),
        cost_estimate=pl.CostEstimate(
            flops=rows * kv_rows * HEAD, bytes_accessed=rows * HEAD, transcendentals=0
        ),
        name="self_attend",
    )(tile_bounds(starts, reach, base, kv_rows), q, kv, kv, starts.reshape(-1, 1, TILE), *([before] if ends else []))


def attend_back_kernel(bounds, q_ref, g_ref, o_ref, lse_ref, k_ref, v_ref, start_ref, *refs, reach, base, pairs, ends):
    i = pl.program_id(1)
    if ends:
        before_ref, dq_ref, dk_ref, dv_ref, dk_sum, dv_sum, k_t = refs
    else:
        after_ref, dk_ref, dv_ref, dk_sum, dv_sum, k_t = refs

    @pl.when(i == 0)
    def _():
        k_t[...] = k_ref[...].T
        dk_sum[...] = jnp.zeros_like(dk_sum)
        dv_sum[...] = jnp.zeros_like(dv_sum)

    queries, grads, inner, logs = [], [], [], []
    for p in range(pairs):
        grad = g_ref[:, lanes(p)]
        queries += split_heads(q_ref[:, lanes(p)] * jnp.bfloat16(SCALE))
        grads += split_heads(grad)
        product = (grad.astype(jnp.float32) * o_ref[:, lanes(p)].astype(jnp.float32)).T
        for h in range(2):
            inner.append(jnp.sum(product[h * HEAD : (h + 1) * HEAD], axis=0, keepdims=True))
            logs.append(lse_ref[0, 0, 2 * p + h : 2 * p + h + 1])
    starts = start_ref[0]

    def step(masked, j, carried):
        rows = pl.ds(pl.multiple_of(j * TILE, TILE), TILE)
        if masked:
            allowed = tile_allowed(base + j * TILE, reach + i * TILE, starts)
        out = []
        for p in range(pairs):
            keys, values = k_ref[rows, lanes(p)], v_ref[rows, lanes(p)]
            dks, dvs = [], []
            for n in (2 * p, 2 * p + 1):
                s = contract_cols(keys, queries[n])
                d = contract_cols(values, grads[n])
                if masked:
                    s = jnp.where(allowed, s, NEG)
                shares = jnp.exp(s - logs[n])
                ds = (shares * (d - inner[n])).astype(jnp.bfloat16)
                dvs.append(matmul(shares.astype(jnp.bfloat16), grads[n]))
                dks.append(matmul(ds, queries[n]))
                out.append(carried[n] + matmul(k_t[n * HEAD : (n + 1) * HEAD, rows], ds))
            dv_sum[rows, lanes(p)] += dvs[0] + dvs[1]
            dk_sum[rows, lanes(p)] += dks[0] + dks[1]
        return tuple(out)

    if ends:
        state = tuple(before_ref[0, 0, n] for n in range(2 * pairs))
    else:
        state = (jnp.zeros((HEAD, TILE), jnp.float32),) * (2 * pairs)
    state = over_tiles(bounds, i, step, state)
    if ends:
        for p in range(pairs):
            turned = jnp.concatenate([state[2 * p], state[2 * p + 1]], axis=0).T
            dq_ref[:, lanes(p)] = (turned * SCALE).astype(dq_ref.dtype)
    else:
        for n in range(2 * pairs):
            after_ref[0, 0, n] = state[n]

    @pl.when(i == pl.num_programs(1) - 1)
    def _():
        dk_ref[...] = dk_sum[...].astype(dk_ref.dtype)
        dv_ref[...] = dv_sum[...].astype(dv_ref.dtype)


def self_attend_back(q, grad, o, lse, kv, starts, reach, base, before=None):
    rows, width = q.shape
    kv_rows = kv.shape[0]
    ends = before is not None
    pairs, wide, grid, block, keys, values, by_tile, start_block = attend_specs(rows, kv_rows, width)
    state = by_tile(2 * pairs, HEAD)
    shape = lambda n: jax.ShapeDtypeStruct((n, width), jnp.bfloat16)
    spec = pltpu.PrefetchScalarGridSpec(
        num_scalar_prefetch=1,
        grid=grid,
        in_specs=[block, block, block, by_tile(8), keys, values, start_block] + [state] * ends,
        out_specs=[block if ends else state, keys, keys],
        scratch_shapes=[
            pltpu.VMEM((kv_rows, wide), jnp.float32),
            pltpu.VMEM((kv_rows, wide), jnp.float32),
            pltpu.VMEM((wide, kv_rows), jnp.bfloat16),
        ],
    )
    return pl.pallas_call(
        functools.partial(attend_back_kernel, reach=reach, base=base, pairs=pairs, ends=ends),
        grid_spec=spec,
        out_shape=[
            shape(rows) if ends else jax.ShapeDtypeStruct((*grid, 2 * pairs, HEAD, TILE), jnp.float32),
            shape(kv_rows),
            shape(kv_rows),
        ],
        compiler_params=pltpu.CompilerParams(vmem_limit_bytes=VMEM_BYTES),
        cost_estimate=pl.CostEstimate(
            flops=rows * kv_rows * HEAD, bytes_accessed=rows * HEAD, transcendentals=0
        ),
        name="self_attend_back",
    )(
        tile_bounds(starts, reach, base, kv_rows), q, grad, o, lse, kv, kv, starts.reshape(-1, 1, TILE),
        *([before] if ends else []),
    )


CROSS_PAIRS = 3


def cross_kernel(q_ref, k_ref, v_ref, slot_ref, o_ref):
    lower = lax.broadcasted_iota(jnp.int32, (1, PAIR), 1) < HEAD
    tokens, texts = q_ref.shape[0], k_ref.shape[0]
    allowed = slot_ref[:, :1] == lax.broadcasted_iota(jnp.int32, (tokens, texts), 1) // TXT
    for p in range(CROSS_PAIRS):
        results = []
        for half in split_heads(q_ref[:, lanes(p)] * jnp.bfloat16(SCALE)):
            scores = jnp.where(allowed, contract_cols(half, k_ref[:, lanes(p)]), NEG)
            weights = jnp.exp(scores - jnp.max(scores, axis=1, keepdims=True))
            shares = weights / jnp.sum(weights, axis=1, keepdims=True)
            results.append(matmul(shares.astype(jnp.bfloat16), v_ref[:, lanes(p)]))
        o_ref[:, lanes(p)] = jnp.where(lower, results[0], results[1]).astype(o_ref.dtype)


def cross_attend(q, k, v, slots_wide):
    tokens, width = q.shape
    texts = k.shape[0]
    column = lambda p: (0, p)
    return pl.pallas_call(
        cross_kernel,
        grid=(width // (CROSS_PAIRS * PAIR),),
        in_specs=[
            pl.BlockSpec((tokens, CROSS_PAIRS * PAIR), column),
            pl.BlockSpec((texts, CROSS_PAIRS * PAIR), column),
            pl.BlockSpec((texts, CROSS_PAIRS * PAIR), column),
            pl.BlockSpec((tokens, PAIR), lambda p: (0, 0)),
        ],
        out_specs=pl.BlockSpec((tokens, CROSS_PAIRS * PAIR), column),
        out_shape=jax.ShapeDtypeStruct(q.shape, jnp.bfloat16),
        compiler_params=pltpu.CompilerParams(vmem_limit_bytes=VMEM_BYTES),
        cost_estimate=pl.CostEstimate(
            flops=8 * tokens * texts * width,
            bytes_accessed=4 * tokens * width,
            transcendentals=tokens * texts * width // HEAD,
        ),
        name="cross_attend",
    )(q, k, v, slots_wide)


def cross_back_kernel(q_ref, g_ref, k_ref, v_ref, slot_ref, dq_ref, dk_ref, dv_ref):
    lower = lax.broadcasted_iota(jnp.int32, (1, PAIR), 1) < HEAD
    tokens, texts = q_ref.shape[0], k_ref.shape[0]
    allowed = slot_ref[:, :1] == lax.broadcasted_iota(jnp.int32, (tokens, texts), 1) // TXT
    for p in range(CROSS_PAIRS):
        keys, values = k_ref[:, lanes(p)], v_ref[:, lanes(p)]
        halves = zip(split_heads(q_ref[:, lanes(p)] * jnp.bfloat16(SCALE)), split_heads(g_ref[:, lanes(p)]))
        dqs, dks, dvs = [], [], []
        for q_half, g_half in halves:
            scores = jnp.where(allowed, contract_cols(q_half, keys), NEG)
            weights = jnp.exp(scores - jnp.max(scores, axis=1, keepdims=True))
            shares = weights / jnp.sum(weights, axis=1, keepdims=True)
            grad_shares = contract_cols(g_half, values)
            inner = jnp.sum(shares * grad_shares, axis=1, keepdims=True)
            grad_scores = (shares * (grad_shares - inner)).astype(jnp.bfloat16)
            dqs.append(matmul(grad_scores, keys))
            dks.append(contract_rows(grad_scores, q_half))
            dvs.append(contract_rows(shares.astype(jnp.bfloat16), g_half))
        dq_ref[:, lanes(p)] = (jnp.where(lower, dqs[0], dqs[1]) * SCALE).astype(dq_ref.dtype)
        dk_ref[:, lanes(p)] = dks[0] + dks[1]
        dv_ref[:, lanes(p)] = dvs[0] + dvs[1]


def cross_attend_back(q, grad, k, v, slots_wide):
    tokens, width = q.shape
    texts = k.shape[0]
    column = lambda p: (0, p)
    return pl.pallas_call(
        cross_back_kernel,
        grid=(width // (CROSS_PAIRS * PAIR),),
        in_specs=[
            pl.BlockSpec((tokens, CROSS_PAIRS * PAIR), column),
            pl.BlockSpec((tokens, CROSS_PAIRS * PAIR), column),
            pl.BlockSpec((texts, CROSS_PAIRS * PAIR), column),
            pl.BlockSpec((texts, CROSS_PAIRS * PAIR), column),
            pl.BlockSpec((tokens, PAIR), lambda p: (0, 0)),
        ],
        out_specs=[
            pl.BlockSpec((tokens, CROSS_PAIRS * PAIR), column),
            pl.BlockSpec((texts, CROSS_PAIRS * PAIR), column),
            pl.BlockSpec((texts, CROSS_PAIRS * PAIR), column),
        ],
        out_shape=[
            jax.ShapeDtypeStruct(q.shape, jnp.bfloat16),
            jax.ShapeDtypeStruct((texts, width), jnp.float32),
            jax.ShapeDtypeStruct((texts, width), jnp.float32),
        ],
        compiler_params=pltpu.CompilerParams(vmem_limit_bytes=VMEM_BYTES),
        cost_estimate=pl.CostEstimate(
            flops=20 * tokens * texts * width,
            bytes_accessed=6 * tokens * width,
            transcendentals=tokens * texts * width // HEAD,
        ),
        name="cross_attend_back",
    )(q, grad, k, v, slots_wide)


def swap(value, axis, bit):
    count = lax.axis_size(axis)
    return lax.ppermute(value, axis, [(i, i ^ bit) for i in range(count)])


def passed_along(value, axis, steps):
    count = lax.axis_size(axis)
    initial, last = (max(0, -steps), min(count, count - steps))
    return lax.ppermute(value, axis, [(source, source + steps) for source in range(initial, last)])


def in_order(mine, other, dim):
    second = lax.axis_index("seq") == 1
    return jnp.concatenate([jnp.where(second, other, mine), jnp.where(second, mine, other)], axis=dim)


def gathered(value, dim):
    if lax.axis_size("seq") == 2:
        return in_order(value, swap(value, "seq", 1), dim)
    return lax.all_gather(value, "seq", axis=dim, tiled=True)


def own_block(value, dim):
    size = value.shape[dim] // lax.axis_size("seq")
    return lax.dynamic_slice_in_dim(value, lax.axis_index("seq") * size, size, dim)


def other_block(value, dim):
    size = value.shape[dim] // 2
    return lax.dynamic_slice_in_dim(value, (1 - lax.axis_index("seq")) * size, size, dim)


def exchanged(value, split, concat):
    if lax.axis_size("seq") == 2:
        return in_order(own_block(value, split), swap(other_block(value, split), "seq", 1), concat)
    return lax.all_to_all(value, "seq", split_axis=split, concat_axis=concat, tiled=True)


def summed_block(value, dim):
    if lax.axis_size("seq") == 2:
        received = swap(other_block(value, dim).astype(jnp.bfloat16), "seq", 1)
        return own_block(value, dim) + received.astype(jnp.float32)
    return lax.psum_scatter(
        value.astype(jnp.bfloat16), "seq", scatter_dimension=dim, tiled=True
    ).astype(jnp.float32)


def paired(value):
    short = -value.shape[-1] % PAIR
    return jnp.pad(value, ((0, 0), (0, short))) if short else value


def normed(values):
    average = jnp.mean(values, axis=-1, keepdims=True)
    centred = values - average
    spread = jnp.mean(centred * centred, axis=-1, keepdims=True)
    root = lax.rsqrt(spread + EPS)
    return centred * root, root


def norm_back(grad, n, root, gain):
    a = grad * gain
    back = (a - jnp.mean(a, axis=-1, keepdims=True) - n * jnp.mean(a * n, axis=-1, keepdims=True)) * root
    return back, jnp.sum(grad * n, axis=0), jnp.sum(grad, axis=0)


def scattered(grad):
    return lax.psum_scatter(grad.astype(jnp.bfloat16), "fsdp", scatter_dimension=0, tiled=True)


def whole(part):
    if lax.axis_size("seq") == 2:
        return part.astype(jnp.float32) + swap(part, "seq", 1).astype(jnp.float32)
    return lax.psum(part, "seq").astype(jnp.float32)


def columns(part, blocks):
    split = part.reshape(part.shape[0], blocks, -1)
    return gathered(split, 2).reshape(part.shape[0], -1).astype(jnp.float32)


def core_products(left, right):
    size, core = right.shape[1] // 2, lax.axis_index("fsdp") % 2
    part = lambda place: contract_rows(left, lax.dynamic_slice_in_dim(right, place * size, size, 1)).astype(jnp.bfloat16)
    return part(core), part(1 - core)


def both(first, second):
    return (first.astype(jnp.float32) + second.astype(jnp.float32)).astype(jnp.bfloat16)


def half_rows(value, place):
    blocks = value.reshape(-1, 2, *value.shape[1:])
    return lax.dynamic_index_in_dim(blocks, place % 2, 1, keepdims=False)


def chip_sums(block, products):
    return jnp.concatenate([both(block(kept, 1), block(came, 1)) for kept, came in products], axis=1)


def chip_blocks(mine, beside):
    value = both(mine, beside)
    return value.reshape(lax.axis_size("fsdp") // 2, -1, value.shape[1])


def over_chips(value, at, bit):
    while value.shape[0] > 1:
        value = both(half_rows(value, at), swap(half_rows(value, at + 1), "fsdp", bit))
        at, bit = at // 2, bit * 2
    return value


def own_rows(value):
    core, second = lax.axis_index("fsdp") % 2, lax.axis_index("seq") == 1
    value = value.reshape(2, -1, value.shape[-1])
    take = lambda place: lax.dynamic_index_in_dim(value, place, 0, keepdims=False)
    mine, theirs = take(core), swap(take(1 - core), "fsdp", 1)
    pair = jnp.stack([jnp.where(core == 0, mine, theirs), jnp.where(core == 0, theirs, mine)])
    beside = swap(pair, "seq", 1)
    by_seq = jnp.where(second, beside, pair), jnp.where(second, pair, beside)
    return [by_seq[s][c].astype(jnp.float32) for c in range(2) for s in range(2)]


def clip_starts(segments, group_index, group_rows):
    padded = jnp.concatenate([jnp.full((SPAN,), -1, jnp.int32), segments])
    spans = lax.dynamic_slice_in_dim(padded, group_index * group_rows, SPAN + group_rows)
    spans = spans.reshape(-1, SPAN)
    ahead = jnp.sum((spans == spans[:, :1]).astype(jnp.int32), axis=1)
    firsts = ahead + jnp.arange(spans.shape[0], dtype=jnp.int32) * SPAN
    late = spans[1:] != spans[1:, :1]
    return jnp.where(late, firsts[1:, None], firsts[:-1, None]).reshape(group_rows), spans[1:].reshape(group_rows)


def shards(
    tokens,
    segments,
    text,
    qkv_weight,
    out_weight,
    cross_query_weight,
    cross_kv_weight,
    cross_out_weight,
    up_weight,
    down_weight,
    norm_gain,
    norm_bias,
    cotangent,
):
    group_index = lax.axis_index("fsdp")
    seq_index = lax.axis_index("seq")
    seq_count = lax.axis_size("seq")
    tok_rows, width = tokens.shape
    group_rows = tok_rows * seq_count
    head_cols = width // seq_count
    shard_rows = qkv_weight.shape[0]
    row_block = lambda value: lax.all_gather(value, "fsdp", axis=0, tiled=True)

    norms = jnp.pad(jnp.concatenate([norm_gain, norm_bias]).T, ((0, 0), (0, PAIR - 6)))
    qkv_mine = own_block(qkv_weight.reshape(shard_rows, 3, width), 2).reshape(shard_rows, 3 * head_cols)
    first = row_block(jnp.concatenate([qkv_mine, norms], axis=1))
    w_q, w_kv, w_qkv = first[:, :head_cols], first[:, head_cols : 3 * head_cols], first[:, : 3 * head_cols]
    norm_rows = first[:, 3 * head_cols : 3 * head_cols + 6].astype(jnp.float32).T
    gains, biases = norm_rows[:3], norm_rows[3:]

    ckv_mine = own_block(cross_kv_weight.reshape(shard_rows, 2, width), 2).reshape(shard_rows, 2 * head_cols)
    squares = (out_weight, cross_query_weight, cross_out_weight)
    gate = lax.optimization_barrier
    by_steps = seq_count == 2 and group_rows == SPAN and lax.axis_size("fsdp") == 16
    second = row_block(jnp.concatenate([*squares, ckv_mine], axis=1))
    full_out, full_cq, full_cout = (second[:, i * width : (i + 1) * width] for i in range(3))
    w_ckv = second[:, 3 * width :]

    starts, seg_group = clip_starts(segments, group_index, group_rows)
    slots = own_block(seg_group, 0) - group_index * (group_rows // SPAN)
    slots_wide = jnp.broadcast_to(slots[:, None], (tok_rows, PAIR))

    inputs = tokens.astype(jnp.float32)
    norm_one = lambda rows: (normed(rows.astype(jnp.float32))[0] * gains[0] + biases[0]).astype(jnp.bfloat16)
    normed_one = norm_one(gathered(tokens, 0))
    kv_own = matmul(normed_one, w_kv).astype(jnp.bfloat16)
    queries = matmul(normed_one, w_q).astype(jnp.bfloat16)
    if by_steps:
        before = passed_along(tokens, "fsdp", 1)
        before_other = swap(before, "seq", 1)
    else:
        kv_before = passed_along(kv_own[group_rows - SPAN :], "fsdp", 1)
    pad_kv = lambda kv: jnp.concatenate([paired(kv[:, :head_cols]), paired(kv[:, head_cols:])], axis=1)
    if head_cols % PAIR:
        queries, kv_own, kv_before = paired(queries), pad_kv(kv_own), pad_kv(kv_before)
    heads_state = self_attend(queries, kv_own, starts, SPAN, SPAN)
    if by_steps:
        before, before_other, heads_state = gate((before, before_other, heads_state))
        kv_before = matmul(norm_one(in_order(before, before_other, 0)), w_kv).astype(jnp.bfloat16)
    heads_out, log_totals = self_attend(queries, kv_before, starts, SPAN, 0, heads_state)
    attended = exchanged(heads_out[:, :head_cols], 0, 1)
    hidden_one = inputs + matmul(attended, full_out)

    text_rows = text.reshape(-1, width)
    text_count = text_rows.shape[0]
    ckv_part = matmul(text_rows, w_ckv).astype(jnp.bfloat16).reshape(text_count, 2, head_cols)
    cross_kv = gathered(ckv_part, 2)
    cross_k, cross_v = cross_kv[:, 0], cross_kv[:, 1]
    n_two, root_two = normed(hidden_one)
    normed_two = (n_two * gains[1] + biases[1]).astype(jnp.bfloat16)
    cross_query = matmul(normed_two, full_cq).astype(jnp.bfloat16)
    cross_result = cross_attend(cross_query, cross_k, cross_v, slots_wide)
    hidden_two = hidden_one + matmul(cross_result, full_cout)

    full_up, full_down = row_block(up_weight), row_block(down_weight)
    n_three, root_three = normed(hidden_two)
    normed_three = (n_three * gains[2] + biases[2]).astype(jnp.bfloat16)
    upward = matmul(normed_three, full_up)
    below = 0.5 * (1.0 + lax.erf(upward * (0.5**0.5)))
    active = (upward * below).astype(jnp.bfloat16)
    slope = below + upward * (jnp.exp(-0.5 * upward * upward) * 0.3989422804014327)
    layer_out = (hidden_two + matmul(active, full_down)).astype(jnp.bfloat16)

    chip = group_index // 2
    grad_down, slope = gate((contract_rows(active, cotangent).astype(jnp.bfloat16), slope))
    grad_down = scattered(grad_down)
    grad_upward = (contract_cols(cotangent, full_down) * slope).astype(jnp.bfloat16)
    if by_steps:
        up_kept, up_away, grad_upward = gate((*core_products(normed_three, grad_upward), grad_upward))
        up_came = swap(up_away, "fsdp", 1)
    else:
        grad_up = scattered(contract_rows(normed_three, grad_upward))
    back_h2, gain_three, bias_three = norm_back(contract_cols(grad_upward, full_up), n_three, root_three, gains[2])
    grad_two = cotangent.astype(jnp.float32) + back_h2
    grad_two_low = grad_two.astype(jnp.bfloat16)
    if by_steps:
        cout_kept, cout_away = core_products(cross_result, grad_two_low)
        tree = ((up_kept, up_came), (cout_kept, swap(cout_away, "fsdp", 1)))
    grad_result = contract_cols(grad_two_low, full_cout).astype(jnp.bfloat16)
    grad_query_c, grad_text_k, grad_text_v = cross_attend_back(cross_query, grad_result, cross_k, cross_v, slots_wide)
    grad_text_kv = jnp.stack([grad_text_k, grad_text_v], axis=1)
    if by_steps:
        text_came = swap(other_block(grad_text_kv, 2).astype(jnp.bfloat16), "seq", 1)
        text_came, grad_query_c = gate((text_came, grad_query_c))
        grad_text_kv = own_block(grad_text_kv, 2) + text_came.astype(jnp.float32)
    else:
        grad_text_kv = summed_block(grad_text_kv, 2)
    grad_text_kv = grad_text_kv.astype(jnp.bfloat16).reshape(text_count, 2 * head_cols)
    grad_text = contract_cols(grad_text_kv, w_ckv)
    back_h1, gain_two, bias_two = norm_back(contract_cols(grad_query_c, full_cq), n_two, root_two, gains[1])
    grad_one = grad_two + back_h1

    grad_one_low = grad_one.astype(jnp.bfloat16)
    grad_attended = contract_cols(grad_one_low, full_out).astype(jnp.bfloat16)
    grad_attended, grad_query_c, grad_two_low = gate((grad_attended, grad_query_c, grad_two_low))
    if by_steps:
        heads_came = swap(other_block(grad_attended, 1), "seq", 1)
    else:
        grad_heads = paired(exchanged(grad_attended, 1, 0))
    small = [
        contract_rows(left, right).astype(jnp.bfloat16)
        for left, right in ((normed_two, grad_query_c), (attended, grad_one_low), (text_rows, grad_text_kv))
    ]
    if by_steps:
        small, beside, heads_came = gate((jnp.stack(small), chip_sums(other_block, tree), heads_came))
        grad_heads = in_order(own_block(grad_attended, 1), heads_came, 0)
        small = lax.psum_scatter(small, "fsdp", scatter_dimension=1, tiled=True)
        beside = swap(beside, "seq", 1)
    else:
        small = [scattered(part) for part in small]
        grad_cout = scattered(contract_rows(cross_result, grad_two_low))
    back_args = (queries, grad_heads, heads_out, log_totals)
    query_state, *grad_before = self_attend_back(*back_args, kv_before, starts, SPAN, 0)
    returned = [passed_along(part[:, :head_cols], "fsdp", -1).astype(jnp.float32) for part in grad_before]
    if by_steps:
        up_rows = chip_blocks(chip_sums(own_block, tree), beside)
        up_away, grad_down, query_state = gate((half_rows(up_rows, chip + 1), grad_down, query_state))
        up_came, down_beside = swap(up_away, "fsdp", 2), swap(grad_down, "seq", 1)
    grad_q, *grad_own = self_attend_back(*back_args, kv_own, starts, SPAN, SPAN, query_state)
    if by_steps:
        down_beside, grad_q = gate((down_beside, grad_q))
        grad_down = grad_down.astype(jnp.float32) + down_beside.astype(jnp.float32)
    else:
        grad_up, grad_down = whole(grad_up), whole(grad_down)
    late = group_rows - SPAN
    owned = [grad_q[:, :head_cols]]
    for part, more in zip(grad_own, returned):
        part = part[:, :head_cols].astype(jnp.float32)
        part = jnp.concatenate([part[:late], part[late:] + more]) if late else part + more
        owned.append(part.astype(jnp.bfloat16))
    grad_proj = jnp.concatenate(owned, axis=1)
    grad_wqkv, grad_proj = gate((contract_rows(normed_one, grad_proj).astype(jnp.bfloat16), grad_proj))
    grad_normed_one = contract_cols(grad_proj, w_qkv)
    grad_wqkv, small, _ = gate((grad_wqkv, small, grad_normed_one))
    grad_wqkv = scattered(grad_wqkv)
    if by_steps:
        normed_came = swap(other_block(grad_normed_one, 0).astype(jnp.bfloat16), "seq", 1)
        up_came, grad_normed_one = gate((up_came, grad_normed_one))
        up_rows = both(half_rows(up_rows, chip), up_came)
        up_came, normed_came = gate((swap(half_rows(up_rows, chip // 2 + 1), "fsdp", 4), normed_came))
        up_rows = over_chips(both(half_rows(up_rows, chip // 2), up_came), chip // 4, 8)
        grad_normed_one = own_block(grad_normed_one, 0) + normed_came.astype(jnp.float32)
        grad_cq, grad_wout = whole(small[:2])
    else:
        grad_cq, grad_wout = (whole(part) for part in small[:2])
        grad_normed_one = summed_block(grad_normed_one, 0)
    grad_ckv = columns(small[2], 2)
    n_one, root_one = normed(inputs)
    back_x, gain_one, bias_one = norm_back(grad_normed_one, n_one, root_one, gains[0])
    grad_tokens = (grad_one + back_x).astype(jnp.bfloat16)
    norm_grads = lax.psum(
        jnp.stack([gain_one, gain_two, gain_three, bias_one, bias_two, bias_three]), ("fsdp", "seq")
    )
    if by_steps:
        norm_grads, up_rows = gate((norm_grads, up_rows))
        quarters = own_rows(up_rows)
        grad_up, grad_cout = (jnp.concatenate(parts, axis=1) for parts in zip(*((q[:, :width], q[:, width:]) for q in quarters)))
    else:
        grad_cout = whole(grad_cout)
    grad_wqkv, grad_cout, grad_cq, grad_wout, grad_ckv, grad_up = gate(
        (grad_wqkv, grad_cout, grad_cq, grad_wout, grad_ckv, grad_up)
    )
    norm_grads = lax.dynamic_slice_in_dim(norm_grads, group_index * shard_rows, shard_rows, 1)
    return (
        layer_out,
        grad_tokens,
        whole(grad_text.astype(jnp.bfloat16)).reshape(text.shape),
        columns(grad_wqkv, 3),
        grad_wout,
        grad_cq,
        grad_ckv,
        grad_cout,
        grad_up,
        grad_down,
        norm_grads[:3],
        norm_grads[3:],
    )


def solution(mesh):
    rows, shard, copied = P(("fsdp", "seq"), None), P("fsdp", None), P(None, "fsdp")
    groups = P("fsdp", None, None)
    in_specs = (rows, P(), groups, *[shard] * 7, copied, copied, rows)
    out_specs = (rows, rows, groups, *[shard] * 7, copied, copied)
    return jax.shard_map(shards, mesh=mesh, in_specs=in_specs, out_specs=out_specs, check_vma=False)
```

```python
import functools

import jax
import jax.numpy as jnp
from jax import lax
from jax.experimental import pallas as pl
from jax.experimental.pallas import tpu as pltpu
from jax.sharding import PartitionSpec as P

HEADS = 24
HEAD = 64
PAIR = 2 * HEAD
TXT = 64
SPAN = 1536
EPS = 1e-05
NEG = -1e30
SCALE = HEAD**-0.5
VMEM_BYTES = 56 * 2**20


def matmul(left_side, right_side):
    return jnp.dot(left_side, right_side, preferred_element_type=jnp.float32)


def contract_rows(left_side, right_side):
    return lax.dot_general(
        left_side, right_side, (((0,), (0,)), ((), ())), preferred_element_type=jnp.float32
    )


def contract_cols(left_side, right_side):
    return lax.dot_general(
        left_side, right_side, (((1,), (1,)), ((), ())), preferred_element_type=jnp.float32
    )


TILE = 384


def tile_bounds(starts, reach, base, kv_rows):
    count = kv_rows // TILE
    first, last = starts[::TILE] - base, starts[TILE - 1 :: TILE] - base
    row0 = reach - base + jnp.arange(first.shape[0], dtype=jnp.int32) * TILE
    low = jnp.clip(first // TILE, 0, count)
    high = jnp.clip((row0 + TILE - 1) // TILE + 1, low, count)
    free_low = jnp.clip((last + TILE - 1) // TILE, low, high)
    free_high = jnp.clip((row0 + 1) // TILE, free_low, high)
    return jnp.stack([low, free_low, free_high, high], axis=1)


def pairs_a_step(width):
    return 3 if width % (3 * PAIR) == 0 else 1


def split_heads(block):
    lower = lax.broadcasted_iota(jnp.int32, (1, PAIR), 1) < HEAD
    zero = jnp.zeros((1, 1), block.dtype)
    return [jnp.where(lower, block, zero), jnp.where(lower, zero, block)]


def lanes(p):
    return slice(p * PAIR, (p + 1) * PAIR)


def tile_allowed(col0, row0, starts):
    at = col0 + lax.broadcasted_iota(jnp.int32, (TILE, TILE), 0)
    row = row0 + lax.broadcasted_iota(jnp.int32, (TILE, TILE), 1)
    return (at >= starts) & (at <= row)


def over_tiles(bounds, i, step, state):
    low, free_low, free_high, high = (bounds[i, n] for n in range(4))
    state = lax.fori_loop(low, free_low, functools.partial(step, True), state)
    state = lax.fori_loop(free_low, free_high, functools.partial(step, False), state)
    return lax.fori_loop(free_high, high, functools.partial(step, True), state)


def attend_kernel(bounds, q_ref, k_ref, v_ref, start_ref, *refs, reach, base, pairs, ends):
    i = pl.program_id(1)
    if ends:
        before_ref, o_ref, lse_ref, v_t = refs
    else:
        after_ref, v_t = refs

    @pl.when(i == 0)
    def _():
        for p in range(pairs):
            turned = v_ref[:, lanes(p)].T
            for h in range(2):
                v_t[2 * p + h, :HEAD] = turned[h * HEAD : (h + 1) * HEAD]
                v_t[2 * p + h, HEAD:] = jnp.ones((16, turned.shape[1]), jnp.bfloat16)

    halves = []
    for p in range(pairs):
        halves += split_heads(q_ref[:, lanes(p)] * jnp.bfloat16(SCALE))
    starts = start_ref[0]

    def step(masked, j, carried):
        rows = pl.ds(pl.multiple_of(j * TILE, TILE), TILE)
        if masked:
            allowed = tile_allowed(base + j * TILE, reach + i * TILE, starts)
        scores = []
        for n in range(2 * pairs):
            s = contract_cols(k_ref[rows, lanes(n // 2)], halves[n])
            scores.append(jnp.where(allowed, s, NEG) if masked else s)
        out = []
        for n, (top, total) in enumerate(carried):
            new_top = jnp.maximum(top, jnp.max(scores[n], axis=0, keepdims=True))
            weights = jnp.exp(scores[n] - new_top).astype(jnp.bfloat16)
            total = total * jnp.exp(top - new_top) + matmul(v_t[n, :, rows], weights)
            out.append((new_top, total))
        return tuple(out)

    if ends:
        state = tuple((before_ref[0, 0, n, HEAD + 8 : HEAD + 9], before_ref[0, 0, n]) for n in range(2 * pairs))
    else:
        nothing = (jnp.full((1, TILE), NEG, jnp.float32), jnp.zeros((HEAD + 16, TILE), jnp.float32))
        state = (nothing,) * (2 * pairs)
    state = over_tiles(bounds, i, step, state)
    if not ends:
        for n, (top, total) in enumerate(state):
            after_ref[0, 0, n, : HEAD + 8] = total[: HEAD + 8]
            after_ref[0, 0, n, HEAD + 8 :] = jnp.broadcast_to(top, (8, TILE))
        return
    for p in range(pairs):
        outs = []
        for n in (2 * p, 2 * p + 1):
            top, total = state[n]
            count = total[HEAD : HEAD + 1]
            outs.append(total[:HEAD] / count)
            lse_ref[0, 0, n : n + 1, :] = top + jnp.log(count)
        o_ref[:, lanes(p)] = jnp.concatenate(outs, axis=0).T.astype(o_ref.dtype)


def attend_specs(rows, kv_rows, width):
    pairs = pairs_a_step(width)
    wide = pairs * PAIR
    steps = width // wide
    block = pl.BlockSpec((TILE, wide), lambda p, i, b: (i, p))
    keys = pl.BlockSpec((kv_rows, wide), lambda p, i, b: (0, p))
    values = pl.BlockSpec((kv_rows, wide), lambda p, i, b: (0, steps + p))
    by_tile = lambda *shape: pl.BlockSpec((1, 1, *shape, TILE), lambda p, i, b: (p, i, *[0] * len(shape), 0))
    starts = pl.BlockSpec((1, 1, TILE), lambda p, i, b: (i, 0, 0))
    return pairs, wide, (steps, rows // TILE), block, keys, values, by_tile, starts


def self_attend(q, kv, starts, reach, base, before=None):
    rows, width = q.shape
    kv_rows = kv.shape[0]
    ends = before is not None
    pairs, wide, grid, block, keys, values, by_tile, start_block = attend_specs(rows, kv_rows, width)
    state = by_tile(2 * pairs, HEAD + 16)
    state_shape = jax.ShapeDtypeStruct((*grid, 2 * pairs, HEAD + 16, TILE), jnp.float32)
    spec = pltpu.PrefetchScalarGridSpec(
        num_scalar_prefetch=1,
        grid=grid,
        in_specs=[block, keys, values, start_block] + [state] * ends,
        out_specs=[block, by_tile(8)] if ends else state,
        scratch_shapes=[pltpu.VMEM((2 * pairs, HEAD + 16, kv_rows), jnp.bfloat16)],
    )
    return pl.pallas_call(
        functools.partial(attend_kernel, reach=reach, base=base, pairs=pairs, ends=ends),
        grid_spec=spec,
        out_shape=[
            jax.ShapeDtypeStruct((rows, width), jnp.bfloat16),
            jax.ShapeDtypeStruct((*grid, 8, TILE), jnp.float32),
        ]
        if ends
        else state_shape,
        compiler_params=pltpu.CompilerParams(vmem_limit_bytes=VMEM_BYTES),
        cost_estimate=pl.CostEstimate(
            flops=rows * kv_rows * HEAD, bytes_accessed=rows * HEAD, transcendentals=0
        ),
        name="self_attend",
    )(tile_bounds(starts, reach, base, kv_rows), q, kv, kv, starts.reshape(-1, 1, TILE), *([before] if ends else []))


def attend_back_kernel(bounds, q_ref, g_ref, o_ref, lse_ref, k_ref, v_ref, start_ref, *refs, reach, base, pairs, ends):
    i = pl.program_id(1)
    if ends:
        before_ref, dq_ref, dk_ref, dv_ref, dk_sum, dv_sum, k_t = refs
    else:
        after_ref, dk_ref, dv_ref, dk_sum, dv_sum, k_t = refs

    @pl.when(i == 0)
    def _():
        k_t[...] = k_ref[...].T
        dk_sum[...] = jnp.zeros_like(dk_sum)
        dv_sum[...] = jnp.zeros_like(dv_sum)

    queries, grads, inner, logs = [], [], [], []
    for p in range(pairs):
        grad = g_ref[:, lanes(p)]
        queries += split_heads(q_ref[:, lanes(p)] * jnp.bfloat16(SCALE))
        grads += split_heads(grad)
        product = (grad.astype(jnp.float32) * o_ref[:, lanes(p)].astype(jnp.float32)).T
        for h in range(2):
            inner.append(jnp.sum(product[h * HEAD : (h + 1) * HEAD], axis=0, keepdims=True))
            logs.append(lse_ref[0, 0, 2 * p + h : 2 * p + h + 1])
    starts = start_ref[0]

    def step(masked, j, carried):
        rows = pl.ds(pl.multiple_of(j * TILE, TILE), TILE)
        if masked:
            allowed = tile_allowed(base + j * TILE, reach + i * TILE, starts)
        out = []
        for p in range(pairs):
            keys, values = k_ref[rows, lanes(p)], v_ref[rows, lanes(p)]
            dks, dvs = [], []
            for n in (2 * p, 2 * p + 1):
                s = contract_cols(keys, queries[n])
                d = contract_cols(values, grads[n])
                if masked:
                    s = jnp.where(allowed, s, NEG)
                shares = jnp.exp(s - logs[n])
                ds = (shares * (d - inner[n])).astype(jnp.bfloat16)
                dvs.append(matmul(shares.astype(jnp.bfloat16), grads[n]))
                dks.append(matmul(ds, queries[n]))
                out.append(carried[n] + matmul(k_t[n * HEAD : (n + 1) * HEAD, rows], ds))
            dv_sum[rows, lanes(p)] += dvs[0] + dvs[1]
            dk_sum[rows, lanes(p)] += dks[0] + dks[1]
        return tuple(out)

    if ends:
        state = tuple(before_ref[0, 0, n] for n in range(2 * pairs))
    else:
        state = (jnp.zeros((HEAD, TILE), jnp.float32),) * (2 * pairs)
    state = over_tiles(bounds, i, step, state)
    if ends:
        for p in range(pairs):
            turned = jnp.concatenate([state[2 * p], state[2 * p + 1]], axis=0).T
            dq_ref[:, lanes(p)] = (turned * SCALE).astype(dq_ref.dtype)
    else:
        for n in range(2 * pairs):
            after_ref[0, 0, n] = state[n]

    @pl.when(i == pl.num_programs(1) - 1)
    def _():
        dk_ref[...] = dk_sum[...].astype(dk_ref.dtype)
        dv_ref[...] = dv_sum[...].astype(dv_ref.dtype)


def self_attend_back(q, grad, o, lse, kv, starts, reach, base, before=None):
    rows, width = q.shape
    kv_rows = kv.shape[0]
    ends = before is not None
    pairs, wide, grid, block, keys, values, by_tile, start_block = attend_specs(rows, kv_rows, width)
    state = by_tile(2 * pairs, HEAD)
    shape = lambda n: jax.ShapeDtypeStruct((n, width), jnp.bfloat16)
    spec = pltpu.PrefetchScalarGridSpec(
        num_scalar_prefetch=1,
        grid=grid,
        in_specs=[block, block, block, by_tile(8), keys, values, start_block] + [state] * ends,
        out_specs=[block if ends else state, keys, keys],
        scratch_shapes=[
            pltpu.VMEM((kv_rows, wide), jnp.float32),
            pltpu.VMEM((kv_rows, wide), jnp.float32),
            pltpu.VMEM((wide, kv_rows), jnp.bfloat16),
        ],
    )
    return pl.pallas_call(
        functools.partial(attend_back_kernel, reach=reach, base=base, pairs=pairs, ends=ends),
        grid_spec=spec,
        out_shape=[
            shape(rows) if ends else jax.ShapeDtypeStruct((*grid, 2 * pairs, HEAD, TILE), jnp.float32),
            shape(kv_rows),
            shape(kv_rows),
        ],
        compiler_params=pltpu.CompilerParams(vmem_limit_bytes=VMEM_BYTES),
        cost_estimate=pl.CostEstimate(
            flops=rows * kv_rows * HEAD, bytes_accessed=rows * HEAD, transcendentals=0
        ),
        name="self_attend_back",
    )(
        tile_bounds(starts, reach, base, kv_rows), q, grad, o, lse, kv, kv, starts.reshape(-1, 1, TILE),
        *([before] if ends else []),
    )


CROSS_PAIRS = 3


def cross_kernel(q_ref, k_ref, v_ref, slot_ref, o_ref):
    lower = lax.broadcasted_iota(jnp.int32, (1, PAIR), 1) < HEAD
    tokens, texts = q_ref.shape[0], k_ref.shape[0]
    allowed = slot_ref[:, :1] == lax.broadcasted_iota(jnp.int32, (tokens, texts), 1) // TXT
    for p in range(CROSS_PAIRS):
        results = []
        for half in split_heads(q_ref[:, lanes(p)] * jnp.bfloat16(SCALE)):
            scores = jnp.where(allowed, contract_cols(half, k_ref[:, lanes(p)]), NEG)
            weights = jnp.exp(scores - jnp.max(scores, axis=1, keepdims=True))
            shares = weights / jnp.sum(weights, axis=1, keepdims=True)
            results.append(matmul(shares.astype(jnp.bfloat16), v_ref[:, lanes(p)]))
        o_ref[:, lanes(p)] = jnp.where(lower, results[0], results[1]).astype(o_ref.dtype)


def cross_attend(q, k, v, slots_wide):
    tokens, width = q.shape
    texts = k.shape[0]
    column = lambda p: (0, p)
    return pl.pallas_call(
        cross_kernel,
        grid=(width // (CROSS_PAIRS * PAIR),),
        in_specs=[
            pl.BlockSpec((tokens, CROSS_PAIRS * PAIR), column),
            pl.BlockSpec((texts, CROSS_PAIRS * PAIR), column),
            pl.BlockSpec((texts, CROSS_PAIRS * PAIR), column),
            pl.BlockSpec((tokens, PAIR), lambda p: (0, 0)),
        ],
        out_specs=pl.BlockSpec((tokens, CROSS_PAIRS * PAIR), column),
        out_shape=jax.ShapeDtypeStruct(q.shape, jnp.bfloat16),
        compiler_params=pltpu.CompilerParams(vmem_limit_bytes=VMEM_BYTES),
        cost_estimate=pl.CostEstimate(
            flops=8 * tokens * texts * width,
            bytes_accessed=4 * tokens * width,
            transcendentals=tokens * texts * width // HEAD,
        ),
        name="cross_attend",
    )(q, k, v, slots_wide)


def cross_back_kernel(q_ref, g_ref, k_ref, v_ref, slot_ref, dq_ref, dk_ref, dv_ref):
    lower = lax.broadcasted_iota(jnp.int32, (1, PAIR), 1) < HEAD
    tokens, texts = q_ref.shape[0], k_ref.shape[0]
    allowed = slot_ref[:, :1] == lax.broadcasted_iota(jnp.int32, (tokens, texts), 1) // TXT
    for p in range(CROSS_PAIRS):
        keys, values = k_ref[:, lanes(p)], v_ref[:, lanes(p)]
        halves = zip(split_heads(q_ref[:, lanes(p)] * jnp.bfloat16(SCALE)), split_heads(g_ref[:, lanes(p)]))
        dqs, dks, dvs = [], [], []
        for q_half, g_half in halves:
            scores = jnp.where(allowed, contract_cols(q_half, keys), NEG)
            weights = jnp.exp(scores - jnp.max(scores, axis=1, keepdims=True))
            shares = weights / jnp.sum(weights, axis=1, keepdims=True)
            grad_shares = contract_cols(g_half, values)
            inner = jnp.sum(shares * grad_shares, axis=1, keepdims=True)
            grad_scores = (shares * (grad_shares - inner)).astype(jnp.bfloat16)
            dqs.append(matmul(grad_scores, keys))
            dks.append(contract_rows(grad_scores, q_half))
            dvs.append(contract_rows(shares.astype(jnp.bfloat16), g_half))
        dq_ref[:, lanes(p)] = (jnp.where(lower, dqs[0], dqs[1]) * SCALE).astype(dq_ref.dtype)
        dk_ref[:, lanes(p)] = dks[0] + dks[1]
        dv_ref[:, lanes(p)] = dvs[0] + dvs[1]


def cross_attend_back(q, grad, k, v, slots_wide):
    tokens, width = q.shape
    texts = k.shape[0]
    column = lambda p: (0, p)
    return pl.pallas_call(
        cross_back_kernel,
        grid=(width // (CROSS_PAIRS * PAIR),),
        in_specs=[
            pl.BlockSpec((tokens, CROSS_PAIRS * PAIR), column),
            pl.BlockSpec((tokens, CROSS_PAIRS * PAIR), column),
            pl.BlockSpec((texts, CROSS_PAIRS * PAIR), column),
            pl.BlockSpec((texts, CROSS_PAIRS * PAIR), column),
            pl.BlockSpec((tokens, PAIR), lambda p: (0, 0)),
        ],
        out_specs=[
            pl.BlockSpec((tokens, CROSS_PAIRS * PAIR), column),
            pl.BlockSpec((texts, CROSS_PAIRS * PAIR), column),
            pl.BlockSpec((texts, CROSS_PAIRS * PAIR), column),
        ],
        out_shape=[
            jax.ShapeDtypeStruct(q.shape, jnp.bfloat16),
            jax.ShapeDtypeStruct((texts, width), jnp.float32),
            jax.ShapeDtypeStruct((texts, width), jnp.float32),
        ],
        compiler_params=pltpu.CompilerParams(vmem_limit_bytes=VMEM_BYTES),
        cost_estimate=pl.CostEstimate(
            flops=20 * tokens * texts * width,
            bytes_accessed=6 * tokens * width,
            transcendentals=tokens * texts * width // HEAD,
        ),
        name="cross_attend_back",
    )(q, grad, k, v, slots_wide)


def swap(value, axis, bit):
    count = lax.axis_size(axis)
    return lax.ppermute(value, axis, [(i, i ^ bit) for i in range(count)])


def passed_along(value, axis, steps):
    count = lax.axis_size(axis)
    initial, last = (max(0, -steps), min(count, count - steps))
    return lax.ppermute(value, axis, [(source, source + steps) for source in range(initial, last)])


def in_order(mine, other, dim):
    second = lax.axis_index("seq") == 1
    return jnp.concatenate([jnp.where(second, other, mine), jnp.where(second, mine, other)], axis=dim)


def gathered(value, dim):
    if lax.axis_size("seq") == 2:
        return in_order(value, swap(value, "seq", 1), dim)
    return lax.all_gather(value, "seq", axis=dim, tiled=True)


def own_block(value, dim):
    size = value.shape[dim] // lax.axis_size("seq")
    return lax.dynamic_slice_in_dim(value, lax.axis_index("seq") * size, size, dim)


def other_block(value, dim):
    size = value.shape[dim] // 2
    return lax.dynamic_slice_in_dim(value, (1 - lax.axis_index("seq")) * size, size, dim)


def exchanged(value, split, concat):
    if lax.axis_size("seq") == 2:
        return in_order(own_block(value, split), swap(other_block(value, split), "seq", 1), concat)
    return lax.all_to_all(value, "seq", split_axis=split, concat_axis=concat, tiled=True)


def summed_block(value, dim):
    if lax.axis_size("seq") == 2:
        received = swap(other_block(value, dim).astype(jnp.bfloat16), "seq", 1)
        return own_block(value, dim) + received.astype(jnp.float32)
    return lax.psum_scatter(
        value.astype(jnp.bfloat16), "seq", scatter_dimension=dim, tiled=True
    ).astype(jnp.float32)


def paired(value):
    short = -value.shape[-1] % PAIR
    return jnp.pad(value, ((0, 0), (0, short))) if short else value


def normed(values):
    average = jnp.mean(values, axis=-1, keepdims=True)
    centred = values - average
    spread = jnp.mean(centred * centred, axis=-1, keepdims=True)
    root = lax.rsqrt(spread + EPS)
    return centred * root, root


def norm_back(grad, n, root, gain):
    a = grad * gain
    back = (a - jnp.mean(a, axis=-1, keepdims=True) - n * jnp.mean(a * n, axis=-1, keepdims=True)) * root
    return back, jnp.sum(grad * n, axis=0), jnp.sum(grad, axis=0)


def scattered(grad):
    return lax.psum_scatter(grad.astype(jnp.bfloat16), "fsdp", scatter_dimension=0, tiled=True)


def whole(part):
    if lax.axis_size("seq") == 2:
        return part.astype(jnp.float32) + swap(part, "seq", 1).astype(jnp.float32)
    return lax.psum(part, "seq").astype(jnp.float32)


def columns(part, blocks):
    split = part.reshape(part.shape[0], blocks, -1)
    return gathered(split, 2).reshape(part.shape[0], -1).astype(jnp.float32)


def core_products(left, right):
    size, core = right.shape[1] // 2, lax.axis_index("fsdp") % 2
    part = lambda place: contract_rows(left, lax.dynamic_slice_in_dim(right, place * size, size, 1)).astype(jnp.bfloat16)
    return part(core), part(1 - core)


def both(first, second):
    return (first.astype(jnp.float32) + second.astype(jnp.float32)).astype(jnp.bfloat16)


def half_rows(value, place):
    blocks = value.reshape(-1, 2, *value.shape[1:])
    return lax.dynamic_index_in_dim(blocks, place % 2, 1, keepdims=False)


def chip_blocks(parts):
    value = jnp.concatenate([both(mine, beside) for mine, beside in parts], axis=1)
    return value.reshape(lax.axis_size("fsdp") // 2, -1, value.shape[1])


def over_chips(value, at, bit):
    while value.shape[0] > 1:
        value = both(half_rows(value, at), swap(half_rows(value, at + 1), "fsdp", bit))
        at, bit = at // 2, bit * 2
    return value


def own_rows(value):
    core, second = lax.axis_index("fsdp") % 2, lax.axis_index("seq") == 1
    value = value.reshape(2, -1, value.shape[-1])
    take = lambda place: lax.dynamic_index_in_dim(value, place, 0, keepdims=False)
    mine, theirs = take(core), swap(take(1 - core), "fsdp", 1)
    pair = jnp.stack([jnp.where(core == 0, mine, theirs), jnp.where(core == 0, theirs, mine)])
    beside = swap(pair, "seq", 1)
    by_seq = jnp.where(second, beside, pair), jnp.where(second, pair, beside)
    return [by_seq[s][c].astype(jnp.float32) for c in range(2) for s in range(2)]


def clip_starts(segments, group_index, group_rows):
    padded = jnp.concatenate([jnp.full((SPAN,), -1, jnp.int32), segments])
    spans = lax.dynamic_slice_in_dim(padded, group_index * group_rows, SPAN + group_rows)
    spans = spans.reshape(-1, SPAN)
    ahead = jnp.sum((spans == spans[:, :1]).astype(jnp.int32), axis=1)
    firsts = ahead + jnp.arange(spans.shape[0], dtype=jnp.int32) * SPAN
    late = spans[1:] != spans[1:, :1]
    return jnp.where(late, firsts[1:, None], firsts[:-1, None]).reshape(group_rows), spans[1:].reshape(group_rows)


def shards(
    tokens,
    segments,
    text,
    qkv_weight,
    out_weight,
    cross_query_weight,
    cross_kv_weight,
    cross_out_weight,
    up_weight,
    down_weight,
    norm_gain,
    norm_bias,
    cotangent,
):
    group_index = lax.axis_index("fsdp")
    seq_index = lax.axis_index("seq")
    seq_count = lax.axis_size("seq")
    tok_rows, width = tokens.shape
    group_rows = tok_rows * seq_count
    head_cols = width // seq_count
    shard_rows = qkv_weight.shape[0]
    row_block = lambda value: lax.all_gather(value, "fsdp", axis=0, tiled=True)

    norms = jnp.pad(jnp.concatenate([norm_gain, norm_bias]).T, ((0, 0), (0, PAIR - 6)))
    qkv_mine = own_block(qkv_weight.reshape(shard_rows, 3, width), 2).reshape(shard_rows, 3 * head_cols)
    first = row_block(jnp.concatenate([qkv_mine, norms], axis=1))
    w_q, w_kv, w_qkv = first[:, :head_cols], first[:, head_cols : 3 * head_cols], first[:, : 3 * head_cols]
    norm_rows = first[:, 3 * head_cols : 3 * head_cols + 6].astype(jnp.float32).T
    gains, biases = norm_rows[:3], norm_rows[3:]

    ckv_mine = own_block(cross_kv_weight.reshape(shard_rows, 2, width), 2).reshape(shard_rows, 2 * head_cols)
    squares = (out_weight, cross_query_weight, cross_out_weight)
    gate = lax.optimization_barrier
    by_steps = seq_count == 2 and group_rows == SPAN and lax.axis_size("fsdp") == 16
    second = row_block(jnp.concatenate([*squares, ckv_mine], axis=1))
    full_out, full_cq, full_cout = (second[:, i * width : (i + 1) * width] for i in range(3))
    w_ckv = second[:, 3 * width :]

    starts, seg_group = clip_starts(segments, group_index, group_rows)
    slots = own_block(seg_group, 0) - group_index * (group_rows // SPAN)
    slots_wide = jnp.broadcast_to(slots[:, None], (tok_rows, PAIR))

    inputs = tokens.astype(jnp.float32)
    norm_one = lambda rows: (normed(rows.astype(jnp.float32))[0] * gains[0] + biases[0]).astype(jnp.bfloat16)
    normed_one = norm_one(gathered(tokens, 0))
    kv_own = matmul(normed_one, w_kv).astype(jnp.bfloat16)
    queries = matmul(normed_one, w_q).astype(jnp.bfloat16)
    if by_steps:
        before = passed_along(tokens, "fsdp", 1)
        before_other = swap(before, "seq", 1)
    else:
        kv_before = passed_along(kv_own[group_rows - SPAN :], "fsdp", 1)
    pad_kv = lambda kv: jnp.concatenate([paired(kv[:, :head_cols]), paired(kv[:, head_cols:])], axis=1)
    if head_cols % PAIR:
        queries, kv_own, kv_before = paired(queries), pad_kv(kv_own), pad_kv(kv_before)
    heads_state = self_attend(queries, kv_own, starts, SPAN, SPAN)
    if by_steps:
        before, before_other, heads_state = gate((before, before_other, heads_state))
        kv_before = matmul(norm_one(in_order(before, before_other, 0)), w_kv).astype(jnp.bfloat16)
    heads_out, log_totals = self_attend(queries, kv_before, starts, SPAN, 0, heads_state)
    attended = exchanged(heads_out[:, :head_cols], 0, 1)
    hidden_one = inputs + matmul(attended, full_out)

    text_rows = text.reshape(-1, width)
    text_count = text_rows.shape[0]
    ckv_part = matmul(text_rows, w_ckv).astype(jnp.bfloat16).reshape(text_count, 2, head_cols)
    cross_kv = gathered(ckv_part, 2)
    cross_k, cross_v = cross_kv[:, 0], cross_kv[:, 1]
    n_two, root_two = normed(hidden_one)
    normed_two = (n_two * gains[1] + biases[1]).astype(jnp.bfloat16)
    cross_query = matmul(normed_two, full_cq).astype(jnp.bfloat16)
    cross_result = cross_attend(cross_query, cross_k, cross_v, slots_wide)
    hidden_two = hidden_one + matmul(cross_result, full_cout)

    full_up, full_down = row_block(up_weight), row_block(down_weight)
    n_three, root_three = normed(hidden_two)
    normed_three = (n_three * gains[2] + biases[2]).astype(jnp.bfloat16)
    upward = matmul(normed_three, full_up)
    below = 0.5 * (1.0 + lax.erf(upward * (0.5**0.5)))
    active = (upward * below).astype(jnp.bfloat16)
    slope = below + upward * (jnp.exp(-0.5 * upward * upward) * 0.3989422804014327)
    layer_out = (hidden_two + matmul(active, full_down)).astype(jnp.bfloat16)

    chip = group_index // 2
    grad_down, slope = gate((contract_rows(active, cotangent).astype(jnp.bfloat16), slope))
    grad_down = scattered(grad_down)
    grad_upward = (contract_cols(cotangent, full_down) * slope).astype(jnp.bfloat16)
    if by_steps:
        up_kept, up_away, grad_upward = gate((*core_products(normed_three, grad_upward), grad_upward))
        up_came = swap(up_away, "fsdp", 1)
    else:
        grad_up = scattered(contract_rows(normed_three, grad_upward))
    back_h2, gain_three, bias_three = norm_back(contract_cols(grad_upward, full_up), n_three, root_three, gains[2])
    grad_two = cotangent.astype(jnp.float32) + back_h2
    grad_two_low = grad_two.astype(jnp.bfloat16)
    if by_steps:
        up_beside, grad_two_low = gate((both(other_block(up_kept, 1), other_block(up_came, 1)), grad_two_low))
        half = up_beside.shape[1] // 2
        first_part, early, late_part = (up_beside[:, a * half // 2 : b * half // 2] for a, b in ((0, 1), (1, 2), (2, 4)))
        first_part, early = swap(first_part, "seq", 1), swap(early, "seq", 1)
        cout_kept, cout_away = core_products(cross_result, grad_two_low)
        cout_came = swap(cout_away, "fsdp", 1)
    grad_result = contract_cols(grad_two_low, full_cout).astype(jnp.bfloat16)
    grad_query_c, grad_text_k, grad_text_v = cross_attend_back(cross_query, grad_result, cross_k, cross_v, slots_wide)
    if by_steps:
        first_part, grad_query_c, grad_text_k, grad_text_v = gate((first_part, grad_query_c, grad_text_k, grad_text_v))
    grad_text_kv = jnp.stack([grad_text_k, grad_text_v], axis=1)
    if by_steps:
        text_came = swap(other_block(grad_text_kv, 2).astype(jnp.bfloat16), "seq", 1)
        text_came, grad_query_c = gate((text_came, grad_query_c))
        grad_text_kv = own_block(grad_text_kv, 2) + text_came.astype(jnp.float32)
    else:
        grad_text_kv = summed_block(grad_text_kv, 2)
    grad_text_kv = grad_text_kv.astype(jnp.bfloat16).reshape(text_count, 2 * head_cols)
    grad_text = contract_cols(grad_text_kv, w_ckv)
    back_h1, gain_two, bias_two = norm_back(contract_cols(grad_query_c, full_cq), n_two, root_two, gains[1])
    grad_one = grad_two + back_h1

    grad_one_low = grad_one.astype(jnp.bfloat16)
    if by_steps:
        early, grad_one_low = gate((early, grad_one_low))
    grad_attended = contract_cols(grad_one_low, full_out).astype(jnp.bfloat16)
    grad_attended, grad_query_c, grad_two_low = gate((grad_attended, grad_query_c, grad_two_low))
    if by_steps:
        heads_came = swap(other_block(grad_attended, 1), "seq", 1)
    else:
        grad_heads = paired(exchanged(grad_attended, 1, 0))
    small = [
        contract_rows(left, right).astype(jnp.bfloat16)
        for left, right in ((normed_two, grad_query_c), (attended, grad_one_low), (text_rows, grad_text_kv))
    ]
    if by_steps:
        cout_beside = both(other_block(cout_kept, 1), other_block(cout_came, 1))
        small, cout_beside, heads_came, late_part = gate((jnp.stack(small), cout_beside, heads_came, late_part))
        late_part = swap(late_part, "seq", 1)
        grad_heads = in_order(own_block(grad_attended, 1), heads_came, 0)
        small = lax.psum_scatter(small, "fsdp", scatter_dimension=1, tiled=True)
        cout_beside = swap(cout_beside, "seq", 1)
    else:
        small = [scattered(part) for part in small]
        grad_cout = scattered(contract_rows(cross_result, grad_two_low))
    back_args = (queries, grad_heads, heads_out, log_totals)
    query_state, *grad_before = self_attend_back(*back_args, kv_before, starts, SPAN, 0)
    returned = [passed_along(part[:, :head_cols], "fsdp", -1).astype(jnp.float32) for part in grad_before]
    if by_steps:
        up_mine = both(own_block(up_kept, 1), own_block(up_came, 1))
        cout_mine = both(own_block(cout_kept, 1), own_block(cout_came, 1))
        parts = ((0, half // 2, first_part), (half // 2, half, early), (half, 2 * half, late_part))
        up_rows = chip_blocks([(up_mine[:, a:b], part) for a, b, part in parts] + [(cout_mine, cout_beside)])
        up_away, grad_down, query_state = gate((half_rows(up_rows, chip + 1), grad_down, query_state))
        up_came, down_beside = swap(up_away, "fsdp", 2), swap(grad_down, "seq", 1)
    grad_q, *grad_own = self_attend_back(*back_args, kv_own, starts, SPAN, SPAN, query_state)
    if by_steps:
        down_beside, grad_q = gate((down_beside, grad_q))
        grad_down = grad_down.astype(jnp.float32) + down_beside.astype(jnp.float32)
    else:
        grad_up, grad_down = whole(grad_up), whole(grad_down)
    late = group_rows - SPAN
    owned = [grad_q[:, :head_cols]]
    for part, more in zip(grad_own, returned):
        part = part[:, :head_cols].astype(jnp.float32)
        part = jnp.concatenate([part[:late], part[late:] + more]) if late else part + more
        owned.append(part.astype(jnp.bfloat16))
    grad_proj = jnp.concatenate(owned, axis=1)
    grad_wqkv, grad_proj = gate((contract_rows(normed_one, grad_proj).astype(jnp.bfloat16), grad_proj))
    grad_normed_one = contract_cols(grad_proj, w_qkv)
    grad_wqkv, small, _ = gate((grad_wqkv, small, grad_normed_one))
    grad_wqkv = scattered(grad_wqkv)
    if by_steps:
        normed_came = swap(other_block(grad_normed_one, 0).astype(jnp.bfloat16), "seq", 1)
        up_came, grad_normed_one = gate((up_came, grad_normed_one))
        up_rows = both(half_rows(up_rows, chip), up_came)
        layer_out, normed_came = gate((layer_out, normed_came))
        up_rows = over_chips(up_rows, chip // 2, 4)
        grad_normed_one = own_block(grad_normed_one, 0) + normed_came.astype(jnp.float32)
    else:
        grad_normed_one = summed_block(grad_normed_one, 0)
    n_one, root_one = normed(inputs)
    back_x, gain_one, bias_one = norm_back(grad_normed_one, n_one, root_one, gains[0])
    grad_tokens = (grad_one + back_x).astype(jnp.bfloat16)
    norm_grads = lax.psum(
        jnp.stack([gain_one, gain_two, gain_three, bias_one, bias_two, bias_three]), ("fsdp", "seq")
    )
    if by_steps:
        norm_grads, up_rows, small = gate((norm_grads, up_rows, small))
        grad_cq, grad_wout = whole(small[:2])
        quarters = own_rows(up_rows)
        grad_up, grad_cout = (jnp.concatenate(parts, axis=1) for parts in zip(*((q[:, :width], q[:, width:]) for q in quarters)))
    else:
        grad_cout, grad_cq, grad_wout = whole(grad_cout), whole(small[0]), whole(small[1])
    grad_ckv = columns(small[2], 2)
    grad_wqkv, grad_cout, grad_cq, grad_wout, grad_ckv, grad_up = gate(
        (grad_wqkv, grad_cout, grad_cq, grad_wout, grad_ckv, grad_up)
    )
    norm_grads = lax.dynamic_slice_in_dim(norm_grads, group_index * shard_rows, shard_rows, 1)
    return (
        layer_out,
        grad_tokens,
        whole(grad_text.astype(jnp.bfloat16)).reshape(text.shape),
        columns(grad_wqkv, 3),
        grad_wout,
        grad_cq,
        grad_ckv,
        grad_cout,
        grad_up,
        grad_down,
        norm_grads[:3],
        norm_grads[3:],
    )


def solution(mesh):
    rows, shard, copied = P(("fsdp", "seq"), None), P("fsdp", None), P(None, "fsdp")
    groups = P("fsdp", None, None)
    in_specs = (rows, P(), groups, *[shard] * 7, copied, copied, rows)
    out_specs = (rows, rows, groups, *[shard] * 7, copied, copied)
    return jax.shard_map(shards, mesh=mesh, in_specs=in_specs, out_specs=out_specs, check_vma=False)
```

```python
import functools

import jax
import jax.numpy as jnp
from jax import lax
from jax.experimental import pallas as pl
from jax.experimental.pallas import tpu as pltpu
from jax.sharding import PartitionSpec as P

HEADS = 24
HEAD = 64
PAIR = 2 * HEAD
TXT = 64
SPAN = 1536
EPS = 1e-05
NEG = -1e30
SCALE = HEAD**-0.5
VMEM_BYTES = 56 * 2**20


def matmul(left_side, right_side):
    return jnp.dot(left_side, right_side, preferred_element_type=jnp.float32)


def contract_rows(left_side, right_side):
    return lax.dot_general(
        left_side, right_side, (((0,), (0,)), ((), ())), preferred_element_type=jnp.float32
    )


def contract_cols(left_side, right_side):
    return lax.dot_general(
        left_side, right_side, (((1,), (1,)), ((), ())), preferred_element_type=jnp.float32
    )


TILE = 384


def tile_bounds(starts, reach, base, kv_rows):
    count = kv_rows // TILE
    first, last = starts[::TILE] - base, starts[TILE - 1 :: TILE] - base
    row0 = reach - base + jnp.arange(first.shape[0], dtype=jnp.int32) * TILE
    low = jnp.clip(first // TILE, 0, count)
    high = jnp.clip((row0 + TILE - 1) // TILE + 1, low, count)
    free_low = jnp.clip((last + TILE - 1) // TILE, low, high)
    free_high = jnp.clip((row0 + 1) // TILE, free_low, high)
    return jnp.stack([low, free_low, free_high, high], axis=1)


def pairs_a_step(width):
    return 3 if width % (3 * PAIR) == 0 else 1


def split_heads(block):
    lower = lax.broadcasted_iota(jnp.int32, (1, PAIR), 1) < HEAD
    zero = jnp.zeros((1, 1), block.dtype)
    return [jnp.where(lower, block, zero), jnp.where(lower, zero, block)]


def lanes(p):
    return slice(p * PAIR, (p + 1) * PAIR)


def tile_allowed(col0, row0, starts):
    at = col0 + lax.broadcasted_iota(jnp.int32, (TILE, TILE), 0)
    row = row0 + lax.broadcasted_iota(jnp.int32, (TILE, TILE), 1)
    return (at >= starts) & (at <= row)


def over_tiles(bounds, i, step, state):
    low, free_low, free_high, high = (bounds[i, n] for n in range(4))
    state = lax.fori_loop(low, free_low, functools.partial(step, True), state)
    state = lax.fori_loop(free_low, free_high, functools.partial(step, False), state)
    return lax.fori_loop(free_high, high, functools.partial(step, True), state)


def attend_kernel(bounds, q_ref, k_ref, v_ref, start_ref, *refs, reach, base, pairs, ends):
    i = pl.program_id(1)
    if ends:
        before_ref, o_ref, lse_ref, v_t = refs
    else:
        after_ref, v_t = refs

    @pl.when(i == 0)
    def _():
        for p in range(pairs):
            turned = v_ref[:, lanes(p)].T
            for h in range(2):
                v_t[2 * p + h, :HEAD] = turned[h * HEAD : (h + 1) * HEAD]
                v_t[2 * p + h, HEAD:] = jnp.ones((16, turned.shape[1]), jnp.bfloat16)

    halves = []
    for p in range(pairs):
        halves += split_heads(q_ref[:, lanes(p)] * jnp.bfloat16(SCALE))
    starts = start_ref[0]

    def step(masked, j, carried):
        rows = pl.ds(pl.multiple_of(j * TILE, TILE), TILE)
        if masked:
            allowed = tile_allowed(base + j * TILE, reach + i * TILE, starts)
        scores = []
        for n in range(2 * pairs):
            s = contract_cols(k_ref[rows, lanes(n // 2)], halves[n])
            scores.append(jnp.where(allowed, s, NEG) if masked else s)
        out = []
        for n, (top, total) in enumerate(carried):
            new_top = jnp.maximum(top, jnp.max(scores[n], axis=0, keepdims=True))
            weights = jnp.exp(scores[n] - new_top).astype(jnp.bfloat16)
            total = total * jnp.exp(top - new_top) + matmul(v_t[n, :, rows], weights)
            out.append((new_top, total))
        return tuple(out)

    if ends:
        state = tuple((before_ref[0, 0, n, HEAD + 8 : HEAD + 9], before_ref[0, 0, n]) for n in range(2 * pairs))
    else:
        nothing = (jnp.full((1, TILE), NEG, jnp.float32), jnp.zeros((HEAD + 16, TILE), jnp.float32))
        state = (nothing,) * (2 * pairs)
    state = over_tiles(bounds, i, step, state)
    if not ends:
        for n, (top, total) in enumerate(state):
            after_ref[0, 0, n, : HEAD + 8] = total[: HEAD + 8]
            after_ref[0, 0, n, HEAD + 8 :] = jnp.broadcast_to(top, (8, TILE))
        return
    for p in range(pairs):
        outs = []
        for n in (2 * p, 2 * p + 1):
            top, total = state[n]
            count = total[HEAD : HEAD + 1]
            outs.append(total[:HEAD] / count)
            lse_ref[0, 0, n : n + 1, :] = top + jnp.log(count)
        o_ref[:, lanes(p)] = jnp.concatenate(outs, axis=0).T.astype(o_ref.dtype)


def attend_specs(rows, kv_rows, width):
    pairs = pairs_a_step(width)
    wide = pairs * PAIR
    steps = width // wide
    block = pl.BlockSpec((TILE, wide), lambda p, i, b: (i, p))
    keys = pl.BlockSpec((kv_rows, wide), lambda p, i, b: (0, p))
    values = pl.BlockSpec((kv_rows, wide), lambda p, i, b: (0, steps + p))
    by_tile = lambda *shape: pl.BlockSpec((1, 1, *shape, TILE), lambda p, i, b: (p, i, *[0] * len(shape), 0))
    starts = pl.BlockSpec((1, 1, TILE), lambda p, i, b: (i, 0, 0))
    return pairs, wide, (steps, rows // TILE), block, keys, values, by_tile, starts


def self_attend(q, kv, starts, reach, base, before=None):
    rows, width = q.shape
    kv_rows = kv.shape[0]
    ends = before is not None
    pairs, wide, grid, block, keys, values, by_tile, start_block = attend_specs(rows, kv_rows, width)
    state = by_tile(2 * pairs, HEAD + 16)
    state_shape = jax.ShapeDtypeStruct((*grid, 2 * pairs, HEAD + 16, TILE), jnp.float32)
    spec = pltpu.PrefetchScalarGridSpec(
        num_scalar_prefetch=1,
        grid=grid,
        in_specs=[block, keys, values, start_block] + [state] * ends,
        out_specs=[block, by_tile(8)] if ends else state,
        scratch_shapes=[pltpu.VMEM((2 * pairs, HEAD + 16, kv_rows), jnp.bfloat16)],
    )
    return pl.pallas_call(
        functools.partial(attend_kernel, reach=reach, base=base, pairs=pairs, ends=ends),
        grid_spec=spec,
        out_shape=[
            jax.ShapeDtypeStruct((rows, width), jnp.bfloat16),
            jax.ShapeDtypeStruct((*grid, 8, TILE), jnp.float32),
        ]
        if ends
        else state_shape,
        compiler_params=pltpu.CompilerParams(vmem_limit_bytes=VMEM_BYTES),
        cost_estimate=pl.CostEstimate(
            flops=rows * kv_rows * HEAD, bytes_accessed=rows * HEAD, transcendentals=0
        ),
        name="self_attend",
    )(tile_bounds(starts, reach, base, kv_rows), q, kv, kv, starts.reshape(-1, 1, TILE), *([before] if ends else []))


def attend_back_kernel(bounds, q_ref, g_ref, o_ref, lse_ref, k_ref, v_ref, start_ref, *refs, reach, base, pairs, ends):
    i = pl.program_id(1)
    if ends:
        before_ref, dq_ref, dk_ref, dv_ref, dk_sum, dv_sum, k_t = refs
    else:
        after_ref, dk_ref, dv_ref, dk_sum, dv_sum, k_t = refs

    @pl.when(i == 0)
    def _():
        k_t[...] = k_ref[...].T
        dk_sum[...] = jnp.zeros_like(dk_sum)
        dv_sum[...] = jnp.zeros_like(dv_sum)

    queries, grads, inner, logs = [], [], [], []
    for p in range(pairs):
        grad = g_ref[:, lanes(p)]
        queries += split_heads(q_ref[:, lanes(p)] * jnp.bfloat16(SCALE))
        grads += split_heads(grad)
        product = (grad.astype(jnp.float32) * o_ref[:, lanes(p)].astype(jnp.float32)).T
        for h in range(2):
            inner.append(jnp.sum(product[h * HEAD : (h + 1) * HEAD], axis=0, keepdims=True))
            logs.append(lse_ref[0, 0, 2 * p + h : 2 * p + h + 1])
    starts = start_ref[0]

    def step(masked, j, carried):
        rows = pl.ds(pl.multiple_of(j * TILE, TILE), TILE)
        if masked:
            allowed = tile_allowed(base + j * TILE, reach + i * TILE, starts)
        out = []
        for p in range(pairs):
            keys, values = k_ref[rows, lanes(p)], v_ref[rows, lanes(p)]
            dks, dvs = [], []
            for n in (2 * p, 2 * p + 1):
                s = contract_cols(keys, queries[n])
                d = contract_cols(values, grads[n])
                if masked:
                    s = jnp.where(allowed, s, NEG)
                shares = jnp.exp(s - logs[n])
                ds = (shares * (d - inner[n])).astype(jnp.bfloat16)
                dvs.append(matmul(shares.astype(jnp.bfloat16), grads[n]))
                dks.append(matmul(ds, queries[n]))
                out.append(carried[n] + matmul(k_t[n * HEAD : (n + 1) * HEAD, rows], ds))
            dv_sum[rows, lanes(p)] += dvs[0] + dvs[1]
            dk_sum[rows, lanes(p)] += dks[0] + dks[1]
        return tuple(out)

    if ends:
        state = tuple(before_ref[0, 0, n] for n in range(2 * pairs))
    else:
        state = (jnp.zeros((HEAD, TILE), jnp.float32),) * (2 * pairs)
    state = over_tiles(bounds, i, step, state)
    if ends:
        for p in range(pairs):
            turned = jnp.concatenate([state[2 * p], state[2 * p + 1]], axis=0).T
            dq_ref[:, lanes(p)] = (turned * SCALE).astype(dq_ref.dtype)
    else:
        for n in range(2 * pairs):
            after_ref[0, 0, n] = state[n]

    @pl.when(i == pl.num_programs(1) - 1)
    def _():
        dk_ref[...] = dk_sum[...].astype(dk_ref.dtype)
        dv_ref[...] = dv_sum[...].astype(dv_ref.dtype)


def self_attend_back(q, grad, o, lse, kv, starts, reach, base, before=None):
    rows, width = q.shape
    kv_rows = kv.shape[0]
    ends = before is not None
    pairs, wide, grid, block, keys, values, by_tile, start_block = attend_specs(rows, kv_rows, width)
    state = by_tile(2 * pairs, HEAD)
    shape = lambda n: jax.ShapeDtypeStruct((n, width), jnp.bfloat16)
    spec = pltpu.PrefetchScalarGridSpec(
        num_scalar_prefetch=1,
        grid=grid,
        in_specs=[block, block, block, by_tile(8), keys, values, start_block] + [state] * ends,
        out_specs=[block if ends else state, keys, keys],
        scratch_shapes=[
            pltpu.VMEM((kv_rows, wide), jnp.float32),
            pltpu.VMEM((kv_rows, wide), jnp.float32),
            pltpu.VMEM((wide, kv_rows), jnp.bfloat16),
        ],
    )
    return pl.pallas_call(
        functools.partial(attend_back_kernel, reach=reach, base=base, pairs=pairs, ends=ends),
        grid_spec=spec,
        out_shape=[
            shape(rows) if ends else jax.ShapeDtypeStruct((*grid, 2 * pairs, HEAD, TILE), jnp.float32),
            shape(kv_rows),
            shape(kv_rows),
        ],
        compiler_params=pltpu.CompilerParams(vmem_limit_bytes=VMEM_BYTES),
        cost_estimate=pl.CostEstimate(
            flops=rows * kv_rows * HEAD, bytes_accessed=rows * HEAD, transcendentals=0
        ),
        name="self_attend_back",
    )(
        tile_bounds(starts, reach, base, kv_rows), q, grad, o, lse, kv, kv, starts.reshape(-1, 1, TILE),
        *([before] if ends else []),
    )


CROSS_PAIRS = 3


def cross_kernel(q_ref, k_ref, v_ref, slot_ref, o_ref):
    lower = lax.broadcasted_iota(jnp.int32, (1, PAIR), 1) < HEAD
    tokens, texts = q_ref.shape[0], k_ref.shape[0]
    allowed = slot_ref[:, :1] == lax.broadcasted_iota(jnp.int32, (tokens, texts), 1) // TXT
    for p in range(CROSS_PAIRS):
        results = []
        for half in split_heads(q_ref[:, lanes(p)] * jnp.bfloat16(SCALE)):
            scores = jnp.where(allowed, contract_cols(half, k_ref[:, lanes(p)]), NEG)
            weights = jnp.exp(scores - jnp.max(scores, axis=1, keepdims=True))
            shares = weights / jnp.sum(weights, axis=1, keepdims=True)
            results.append(matmul(shares.astype(jnp.bfloat16), v_ref[:, lanes(p)]))
        o_ref[:, lanes(p)] = jnp.where(lower, results[0], results[1]).astype(o_ref.dtype)


def cross_attend(q, k, v, slots_wide):
    tokens, width = q.shape
    texts = k.shape[0]
    column = lambda p: (0, p)
    return pl.pallas_call(
        cross_kernel,
        grid=(width // (CROSS_PAIRS * PAIR),),
        in_specs=[
            pl.BlockSpec((tokens, CROSS_PAIRS * PAIR), column),
            pl.BlockSpec((texts, CROSS_PAIRS * PAIR), column),
            pl.BlockSpec((texts, CROSS_PAIRS * PAIR), column),
            pl.BlockSpec((tokens, PAIR), lambda p: (0, 0)),
        ],
        out_specs=pl.BlockSpec((tokens, CROSS_PAIRS * PAIR), column),
        out_shape=jax.ShapeDtypeStruct(q.shape, jnp.bfloat16),
        compiler_params=pltpu.CompilerParams(vmem_limit_bytes=VMEM_BYTES),
        cost_estimate=pl.CostEstimate(
            flops=8 * tokens * texts * width,
            bytes_accessed=4 * tokens * width,
            transcendentals=tokens * texts * width // HEAD,
        ),
        name="cross_attend",
    )(q, k, v, slots_wide)


def cross_back_kernel(q_ref, g_ref, k_ref, v_ref, slot_ref, dq_ref, dk_ref, dv_ref):
    lower = lax.broadcasted_iota(jnp.int32, (1, PAIR), 1) < HEAD
    tokens, texts = q_ref.shape[0], k_ref.shape[0]
    allowed = slot_ref[:, :1] == lax.broadcasted_iota(jnp.int32, (tokens, texts), 1) // TXT
    for p in range(CROSS_PAIRS):
        keys, values = k_ref[:, lanes(p)], v_ref[:, lanes(p)]
        halves = zip(split_heads(q_ref[:, lanes(p)] * jnp.bfloat16(SCALE)), split_heads(g_ref[:, lanes(p)]))
        dqs, dks, dvs = [], [], []
        for q_half, g_half in halves:
            scores = jnp.where(allowed, contract_cols(q_half, keys), NEG)
            weights = jnp.exp(scores - jnp.max(scores, axis=1, keepdims=True))
            shares = weights / jnp.sum(weights, axis=1, keepdims=True)
            grad_shares = contract_cols(g_half, values)
            inner = jnp.sum(shares * grad_shares, axis=1, keepdims=True)
            grad_scores = (shares * (grad_shares - inner)).astype(jnp.bfloat16)
            dqs.append(matmul(grad_scores, keys))
            dks.append(contract_rows(grad_scores, q_half))
            dvs.append(contract_rows(shares.astype(jnp.bfloat16), g_half))
        dq_ref[:, lanes(p)] = (jnp.where(lower, dqs[0], dqs[1]) * SCALE).astype(dq_ref.dtype)
        dk_ref[:, lanes(p)] = dks[0] + dks[1]
        dv_ref[:, lanes(p)] = dvs[0] + dvs[1]


def cross_attend_back(q, grad, k, v, slots_wide):
    tokens, width = q.shape
    texts = k.shape[0]
    column = lambda p: (0, p)
    return pl.pallas_call(
        cross_back_kernel,
        grid=(width // (CROSS_PAIRS * PAIR),),
        in_specs=[
            pl.BlockSpec((tokens, CROSS_PAIRS * PAIR), column),
            pl.BlockSpec((tokens, CROSS_PAIRS * PAIR), column),
            pl.BlockSpec((texts, CROSS_PAIRS * PAIR), column),
            pl.BlockSpec((texts, CROSS_PAIRS * PAIR), column),
            pl.BlockSpec((tokens, PAIR), lambda p: (0, 0)),
        ],
        out_specs=[
            pl.BlockSpec((tokens, CROSS_PAIRS * PAIR), column),
            pl.BlockSpec((texts, CROSS_PAIRS * PAIR), column),
            pl.BlockSpec((texts, CROSS_PAIRS * PAIR), column),
        ],
        out_shape=[
            jax.ShapeDtypeStruct(q.shape, jnp.bfloat16),
            jax.ShapeDtypeStruct((texts, width), jnp.float32),
            jax.ShapeDtypeStruct((texts, width), jnp.float32),
        ],
        compiler_params=pltpu.CompilerParams(vmem_limit_bytes=VMEM_BYTES),
        cost_estimate=pl.CostEstimate(
            flops=20 * tokens * texts * width,
            bytes_accessed=6 * tokens * width,
            transcendentals=tokens * texts * width // HEAD,
        ),
        name="cross_attend_back",
    )(q, grad, k, v, slots_wide)


def swap(value, axis, bit):
    count = lax.axis_size(axis)
    return lax.ppermute(value, axis, [(i, i ^ bit) for i in range(count)])


def passed_along(value, axis, steps):
    count = lax.axis_size(axis)
    initial, last = (max(0, -steps), min(count, count - steps))
    return lax.ppermute(value, axis, [(source, source + steps) for source in range(initial, last)])


def in_order(mine, other, dim):
    second = lax.axis_index("seq") == 1
    return jnp.concatenate([jnp.where(second, other, mine), jnp.where(second, mine, other)], axis=dim)


def gathered(value, dim):
    if lax.axis_size("seq") == 2:
        return in_order(value, swap(value, "seq", 1), dim)
    return lax.all_gather(value, "seq", axis=dim, tiled=True)


def own_block(value, dim):
    size = value.shape[dim] // lax.axis_size("seq")
    return lax.dynamic_slice_in_dim(value, lax.axis_index("seq") * size, size, dim)


def other_block(value, dim):
    size = value.shape[dim] // 2
    return lax.dynamic_slice_in_dim(value, (1 - lax.axis_index("seq")) * size, size, dim)


def exchanged(value, split, concat):
    if lax.axis_size("seq") == 2:
        return in_order(own_block(value, split), swap(other_block(value, split), "seq", 1), concat)
    return lax.all_to_all(value, "seq", split_axis=split, concat_axis=concat, tiled=True)


def summed_block(value, dim):
    if lax.axis_size("seq") == 2:
        received = swap(other_block(value, dim).astype(jnp.bfloat16), "seq", 1)
        return own_block(value, dim) + received.astype(jnp.float32)
    return lax.psum_scatter(
        value.astype(jnp.bfloat16), "seq", scatter_dimension=dim, tiled=True
    ).astype(jnp.float32)


def paired(value):
    short = -value.shape[-1] % PAIR
    return jnp.pad(value, ((0, 0), (0, short))) if short else value


def normed(values):
    average = jnp.mean(values, axis=-1, keepdims=True)
    centred = values - average
    spread = jnp.mean(centred * centred, axis=-1, keepdims=True)
    root = lax.rsqrt(spread + EPS)
    return centred * root, root


def norm_back(grad, n, root, gain):
    a = grad * gain
    back = (a - jnp.mean(a, axis=-1, keepdims=True) - n * jnp.mean(a * n, axis=-1, keepdims=True)) * root
    return back, jnp.sum(grad * n, axis=0), jnp.sum(grad, axis=0)


def scattered(grad):
    return lax.psum_scatter(grad.astype(jnp.bfloat16), "fsdp", scatter_dimension=0, tiled=True)


def whole(part):
    if lax.axis_size("seq") == 2:
        return part.astype(jnp.float32) + swap(part, "seq", 1).astype(jnp.float32)
    return lax.psum(part, "seq").astype(jnp.float32)


def columns(part, blocks):
    split = part.reshape(part.shape[0], blocks, -1)
    return gathered(split, 2).reshape(part.shape[0], -1).astype(jnp.float32)


def core_products(left, right):
    size, core = right.shape[1] // 2, lax.axis_index("fsdp") % 2
    part = lambda place: contract_rows(left, lax.dynamic_slice_in_dim(right, place * size, size, 1)).astype(jnp.bfloat16)
    return part(core), part(1 - core)


def both(first, second):
    return (first.astype(jnp.float32) + second.astype(jnp.float32)).astype(jnp.bfloat16)


def half_rows(value, place):
    blocks = value.reshape(-1, 2, *value.shape[1:])
    return lax.dynamic_index_in_dim(blocks, place % 2, 1, keepdims=False)


def seq_away(kept, came):
    return both(other_block(kept, 1), other_block(came, 1))


def chip_blocks(kept, came, beside):
    value = both(both(own_block(kept, 1), own_block(came, 1)), beside)
    return value.reshape(lax.axis_size("fsdp") // 2, -1, value.shape[1])


def own_rows(value, at, bit):
    while value.shape[0] > 1:
        value = both(half_rows(value, at), swap(half_rows(value, at + 1), "fsdp", bit))
        at, bit = at // 2, bit * 2
    core, second = lax.axis_index("fsdp") % 2, lax.axis_index("seq") == 1
    value = value.reshape(2, -1, value.shape[-1])
    take = lambda place: lax.dynamic_index_in_dim(value, place, 0, keepdims=False)
    mine, theirs = take(core), swap(take(1 - core), "fsdp", 1)
    pair = jnp.stack([jnp.where(core == 0, mine, theirs), jnp.where(core == 0, theirs, mine)])
    beside = swap(pair, "seq", 1)
    by_seq = jnp.where(second, beside, pair), jnp.where(second, pair, beside)
    return jnp.concatenate([by_seq[s][c] for c in range(2) for s in range(2)], axis=1).astype(jnp.float32)


def clip_starts(segments, group_index, group_rows):
    padded = jnp.concatenate([jnp.full((SPAN,), -1, jnp.int32), segments])
    spans = lax.dynamic_slice_in_dim(padded, group_index * group_rows, SPAN + group_rows)
    spans = spans.reshape(-1, SPAN)
    ahead = jnp.sum((spans == spans[:, :1]).astype(jnp.int32), axis=1)
    firsts = ahead + jnp.arange(spans.shape[0], dtype=jnp.int32) * SPAN
    late = spans[1:] != spans[1:, :1]
    return jnp.where(late, firsts[1:, None], firsts[:-1, None]).reshape(group_rows), spans[1:].reshape(group_rows)


def shards(
    tokens,
    segments,
    text,
    qkv_weight,
    out_weight,
    cross_query_weight,
    cross_kv_weight,
    cross_out_weight,
    up_weight,
    down_weight,
    norm_gain,
    norm_bias,
    cotangent,
):
    group_index = lax.axis_index("fsdp")
    seq_index = lax.axis_index("seq")
    seq_count = lax.axis_size("seq")
    tok_rows, width = tokens.shape
    group_rows = tok_rows * seq_count
    head_cols = width // seq_count
    shard_rows = qkv_weight.shape[0]
    row_block = lambda value: lax.all_gather(value, "fsdp", axis=0, tiled=True)

    norms = jnp.pad(jnp.concatenate([norm_gain, norm_bias]).T, ((0, 0), (0, PAIR - 6)))
    qkv_mine = own_block(qkv_weight.reshape(shard_rows, 3, width), 2).reshape(shard_rows, 3 * head_cols)
    first = row_block(jnp.concatenate([qkv_mine, norms], axis=1))
    w_q, w_kv, w_qkv = first[:, :head_cols], first[:, head_cols : 3 * head_cols], first[:, : 3 * head_cols]
    norm_rows = first[:, 3 * head_cols : 3 * head_cols + 6].astype(jnp.float32).T
    gains, biases = norm_rows[:3], norm_rows[3:]

    ckv_mine = own_block(cross_kv_weight.reshape(shard_rows, 2, width), 2).reshape(shard_rows, 2 * head_cols)
    squares = (out_weight, cross_query_weight, cross_out_weight)
    gate = lax.optimization_barrier
    by_steps = seq_count == 2 and group_rows == SPAN
    second = row_block(jnp.concatenate([*squares, ckv_mine], axis=1))
    full_out, full_cq, full_cout = (second[:, i * width : (i + 1) * width] for i in range(3))
    w_ckv = second[:, 3 * width :]

    starts, seg_group = clip_starts(segments, group_index, group_rows)
    slots = own_block(seg_group, 0) - group_index * (group_rows // SPAN)
    slots_wide = jnp.broadcast_to(slots[:, None], (tok_rows, PAIR))

    inputs = tokens.astype(jnp.float32)
    norm_one = lambda rows: (normed(rows.astype(jnp.float32))[0] * gains[0] + biases[0]).astype(jnp.bfloat16)
    normed_one = norm_one(gathered(tokens, 0))
    kv_own = matmul(normed_one, w_kv).astype(jnp.bfloat16)
    queries = matmul(normed_one, w_q).astype(jnp.bfloat16)
    if by_steps:
        before = passed_along(gate((tokens, first))[0], "fsdp", 1)
        before_other = swap(before, "seq", 1)
    else:
        kv_before = passed_along(kv_own[group_rows - SPAN :], "fsdp", 1)
    pad_kv = lambda kv: jnp.concatenate([paired(kv[:, :head_cols]), paired(kv[:, head_cols:])], axis=1)
    if head_cols % PAIR:
        queries, kv_own, kv_before = paired(queries), pad_kv(kv_own), pad_kv(kv_before)
    heads_state = self_attend(queries, kv_own, starts, SPAN, SPAN)
    if by_steps:
        before, before_other, heads_state = gate((before, before_other, heads_state))
        kv_before = matmul(norm_one(in_order(before, before_other, 0)), w_kv).astype(jnp.bfloat16)
    heads_out, log_totals = self_attend(queries, kv_before, starts, SPAN, 0, heads_state)
    attended = exchanged(heads_out[:, :head_cols], 0, 1)
    hidden_one = inputs + matmul(attended, full_out)

    text_rows = text.reshape(-1, width)
    text_count = text_rows.shape[0]
    ckv_part = matmul(text_rows, w_ckv).astype(jnp.bfloat16).reshape(text_count, 2, head_cols)
    cross_kv = gathered(ckv_part, 2)
    cross_k, cross_v = cross_kv[:, 0], cross_kv[:, 1]
    n_two, root_two = normed(hidden_one)
    normed_two = (n_two * gains[1] + biases[1]).astype(jnp.bfloat16)
    cross_query = matmul(normed_two, full_cq).astype(jnp.bfloat16)
    cross_result = cross_attend(cross_query, cross_k, cross_v, slots_wide)
    hidden_two = hidden_one + matmul(cross_result, full_cout)

    full_up, full_down = row_block(up_weight), row_block(down_weight)
    n_three, root_three = normed(hidden_two)
    normed_three = (n_three * gains[2] + biases[2]).astype(jnp.bfloat16)
    upward = matmul(normed_three, full_up)
    below = 0.5 * (1.0 + lax.erf(upward * (0.5**0.5)))
    active = (upward * below).astype(jnp.bfloat16)
    slope = below + upward * (jnp.exp(-0.5 * upward * upward) * 0.3989422804014327)
    layer_out = (hidden_two + matmul(active, full_down)).astype(jnp.bfloat16)

    chip = group_index // 2
    grad_down, slope = gate((contract_rows(active, cotangent).astype(jnp.bfloat16), slope))
    grad_down = scattered(grad_down)
    grad_upward = (contract_cols(cotangent, full_down) * slope).astype(jnp.bfloat16)
    if by_steps:
        up_kept, up_away, grad_upward = gate((*core_products(normed_three, grad_upward), grad_upward))
        up_came = swap(up_away, "fsdp", 1)
    else:
        grad_up = scattered(contract_rows(normed_three, grad_upward))
    back_h2, gain_three, bias_three = norm_back(contract_cols(grad_upward, full_up), n_three, root_three, gains[2])
    grad_two = cotangent.astype(jnp.float32) + back_h2
    grad_two_low = grad_two.astype(jnp.bfloat16)
    if by_steps:
        up_beside, grad_two_low = gate((seq_away(up_kept, up_came), grad_two_low))
    grad_result = contract_cols(grad_two_low, full_cout).astype(jnp.bfloat16)
    grad_query_c, grad_text_k, grad_text_v = cross_attend_back(cross_query, grad_result, cross_k, cross_v, slots_wide)
    grad_text_kv = jnp.stack([grad_text_k, grad_text_v], axis=1)
    if by_steps:
        text_came = swap(other_block(grad_text_kv, 2).astype(jnp.bfloat16), "seq", 1)
    else:
        grad_text_kv = summed_block(grad_text_kv, 2)
    back_h1, gain_two, bias_two = norm_back(contract_cols(grad_query_c, full_cq), n_two, root_two, gains[1])
    grad_one = grad_two + back_h1

    grad_one_low = grad_one.astype(jnp.bfloat16)
    if by_steps:
        text_came, grad_one_low = gate((text_came, grad_one_low))
        grad_text_kv = own_block(grad_text_kv, 2) + text_came.astype(jnp.float32)
    grad_text_kv = grad_text_kv.astype(jnp.bfloat16).reshape(text_count, 2 * head_cols)
    grad_text = contract_cols(grad_text_kv, w_ckv)
    grad_attended = contract_cols(grad_one_low, full_out).astype(jnp.bfloat16)
    grad_attended, grad_query_c, grad_two_low = gate((grad_attended, grad_query_c, grad_two_low))
    if by_steps:
        heads_came = swap(other_block(grad_attended, 1), "seq", 1)
    else:
        grad_heads = paired(exchanged(grad_attended, 1, 0))
    small = [
        contract_rows(left, right).astype(jnp.bfloat16)
        for left, right in (
            (cross_result, grad_two_low),
            (normed_two, grad_query_c),
            (attended, grad_one_low),
            (text_rows, grad_text_kv),
        )
    ]
    if by_steps:
        small, up_beside, heads_came = gate((jnp.stack(small), up_beside, heads_came))
        small = lax.psum_scatter(small, "fsdp", scatter_dimension=1, tiled=True)
        up_beside = swap(up_beside, "seq", 1)
        grad_heads = in_order(own_block(grad_attended, 1), heads_came, 0)
    else:
        small = [scattered(part) for part in small]
    back_args = (queries, grad_heads, heads_out, log_totals)
    query_state, *grad_before = self_attend_back(*back_args, kv_before, starts, SPAN, 0)
    returned = [passed_along(part[:, :head_cols], "fsdp", -1).astype(jnp.float32) for part in grad_before]
    if by_steps:
        up_rows = chip_blocks(up_kept, up_came, up_beside)
        up_away, grad_down, query_state = gate((half_rows(up_rows, chip + 1), grad_down, query_state))
        up_came, down_beside = swap(up_away, "fsdp", 2), swap(grad_down, "seq", 1)
    grad_q, *grad_own = self_attend_back(*back_args, kv_own, starts, SPAN, SPAN, query_state)
    if by_steps:
        down_beside, grad_q = gate((down_beside, grad_q))
        grad_down = grad_down.astype(jnp.float32) + down_beside.astype(jnp.float32)
    else:
        grad_up, grad_down = whole(grad_up), whole(grad_down)
    late = group_rows - SPAN
    owned = [grad_q[:, :head_cols]]
    for part, more in zip(grad_own, returned):
        part = part[:, :head_cols].astype(jnp.float32)
        part = jnp.concatenate([part[:late], part[late:] + more]) if late else part + more
        owned.append(part.astype(jnp.bfloat16))
    grad_proj = jnp.concatenate(owned, axis=1)
    if by_steps:
        away = contract_cols(other_block(grad_proj, 0), w_qkv).astype(jnp.bfloat16)
        away, grad_proj = gate((away, grad_proj))
        grad_normed_one = swap(away, "seq", 1).astype(jnp.float32) + contract_cols(own_block(grad_proj, 0), w_qkv)
    else:
        grad_normed_one = summed_block(contract_cols(grad_proj, w_qkv), 0)
    grad_wqkv = contract_rows(normed_one, grad_proj).astype(jnp.bfloat16)
    n_one, root_one = normed(inputs)
    back_x, gain_one, bias_one = norm_back(grad_normed_one, n_one, root_one, gains[0])
    grad_tokens = (grad_one + back_x).astype(jnp.bfloat16)
    norm_grads = jnp.stack([gain_one, gain_two, gain_three, bias_one, bias_two, bias_three])
    norm_grads = jnp.pad(norm_grads.T.astype(jnp.bfloat16), ((0, 0), (0, PAIR - 6)))
    last, small = gate((jnp.concatenate([grad_wqkv, norm_grads], axis=1), small))
    if by_steps:
        up_came, last = gate((up_came, last))
    last = scattered(last)
    if by_steps:
        grad_cout, grad_cq, grad_wout = whole(small[:3])
        grad_up = own_rows(both(half_rows(up_rows, chip), up_came), chip // 2, 4)
    else:
        grad_cout, grad_cq, grad_wout = (whole(part) for part in small[:3])
    grad_ckv = columns(small[3], 2)
    last, grad_cout, grad_cq, grad_wout, grad_ckv, grad_up = gate(
        (last, grad_cout, grad_cq, grad_wout, grad_ckv, grad_up)
    )
    norm_grads = whole(last[:, -PAIR:]).T
    return (
        layer_out,
        grad_tokens,
        whole(grad_text.astype(jnp.bfloat16)).reshape(text.shape),
        columns(last[:, : 3 * head_cols], 3),
        grad_wout,
        grad_cq,
        grad_ckv,
        grad_cout,
        grad_up,
        grad_down,
        norm_grads[:3],
        norm_grads[3:6],
    )


def solution(mesh):
    rows, shard, copied = P(("fsdp", "seq"), None), P("fsdp", None), P(None, "fsdp")
    groups = P("fsdp", None, None)
    in_specs = (rows, P(), groups, *[shard] * 7, copied, copied, rows)
    out_specs = (rows, rows, groups, *[shard] * 7, copied, copied)
    return jax.shard_map(shards, mesh=mesh, in_specs=in_specs, out_specs=out_specs, check_vma=False)
```

```python
import functools

import jax
import jax.numpy as jnp
from jax import lax
from jax.experimental import pallas as pl
from jax.experimental.pallas import tpu as pltpu
from jax.sharding import PartitionSpec as P

HEADS = 24
HEAD = 64
PAIR = 2 * HEAD
TXT = 64
SPAN = 1536
EPS = 1e-05
NEG = -1e30
SCALE = HEAD**-0.5
VMEM_BYTES = 56 * 2**20


def matmul(left_side, right_side):
    return jnp.dot(left_side, right_side, preferred_element_type=jnp.float32)


def contract_rows(left_side, right_side):
    return lax.dot_general(
        left_side, right_side, (((0,), (0,)), ((), ())), preferred_element_type=jnp.float32
    )


def contract_cols(left_side, right_side):
    return lax.dot_general(
        left_side, right_side, (((1,), (1,)), ((), ())), preferred_element_type=jnp.float32
    )


TILE = 384


def tile_bounds(starts, reach, base, kv_rows):
    count = kv_rows // TILE
    first, last = starts[::TILE] - base, starts[TILE - 1 :: TILE] - base
    row0 = reach - base + jnp.arange(first.shape[0], dtype=jnp.int32) * TILE
    low = jnp.clip(first // TILE, 0, count)
    high = jnp.clip((row0 + TILE - 1) // TILE + 1, low, count)
    free_low = jnp.clip((last + TILE - 1) // TILE, low, high)
    free_high = jnp.clip((row0 + 1) // TILE, free_low, high)
    return jnp.stack([low, free_low, free_high, high], axis=1)


def pairs_a_step(width):
    return 3 if width % (3 * PAIR) == 0 else 1


def split_heads(block):
    lower = lax.broadcasted_iota(jnp.int32, (1, PAIR), 1) < HEAD
    zero = jnp.zeros((1, 1), block.dtype)
    return [jnp.where(lower, block, zero), jnp.where(lower, zero, block)]


def lanes(p):
    return slice(p * PAIR, (p + 1) * PAIR)


def tile_allowed(col0, row0, starts):
    at = col0 + lax.broadcasted_iota(jnp.int32, (TILE, TILE), 0)
    row = row0 + lax.broadcasted_iota(jnp.int32, (TILE, TILE), 1)
    return (at >= starts) & (at <= row)


def over_tiles(bounds, i, step, state):
    low, free_low, free_high, high = (bounds[i, n] for n in range(4))
    state = lax.fori_loop(low, free_low, functools.partial(step, True), state)
    state = lax.fori_loop(free_low, free_high, functools.partial(step, False), state)
    return lax.fori_loop(free_high, high, functools.partial(step, True), state)


def attend_kernel(bounds, q_ref, k_ref, v_ref, start_ref, *refs, reach, base, pairs, ends):
    i = pl.program_id(1)
    if ends:
        before_ref, o_ref, lse_ref, v_t = refs
    else:
        after_ref, v_t = refs

    @pl.when(i == 0)
    def _():
        for p in range(pairs):
            turned = v_ref[:, lanes(p)].T
            for h in range(2):
                v_t[2 * p + h, :HEAD] = turned[h * HEAD : (h + 1) * HEAD]
                v_t[2 * p + h, HEAD:] = jnp.ones((16, turned.shape[1]), jnp.bfloat16)

    halves = []
    for p in range(pairs):
        halves += split_heads(q_ref[:, lanes(p)] * jnp.bfloat16(SCALE))
    starts = start_ref[0]

    def step(masked, j, carried):
        rows = pl.ds(pl.multiple_of(j * TILE, TILE), TILE)
        if masked:
            allowed = tile_allowed(base + j * TILE, reach + i * TILE, starts)
        scores = []
        for n in range(2 * pairs):
            s = contract_cols(k_ref[rows, lanes(n // 2)], halves[n])
            scores.append(jnp.where(allowed, s, NEG) if masked else s)
        out = []
        for n, (top, total) in enumerate(carried):
            new_top = jnp.maximum(top, jnp.max(scores[n], axis=0, keepdims=True))
            weights = jnp.exp(scores[n] - new_top).astype(jnp.bfloat16)
            total = total * jnp.exp(top - new_top) + matmul(v_t[n, :, rows], weights)
            out.append((new_top, total))
        return tuple(out)

    if ends:
        state = tuple((before_ref[0, 0, n, HEAD + 8 : HEAD + 9], before_ref[0, 0, n]) for n in range(2 * pairs))
    else:
        nothing = (jnp.full((1, TILE), NEG, jnp.float32), jnp.zeros((HEAD + 16, TILE), jnp.float32))
        state = (nothing,) * (2 * pairs)
    state = over_tiles(bounds, i, step, state)
    if not ends:
        for n, (top, total) in enumerate(state):
            after_ref[0, 0, n, : HEAD + 8] = total[: HEAD + 8]
            after_ref[0, 0, n, HEAD + 8 :] = jnp.broadcast_to(top, (8, TILE))
        return
    for p in range(pairs):
        outs = []
        for n in (2 * p, 2 * p + 1):
            top, total = state[n]
            count = total[HEAD : HEAD + 1]
            outs.append(total[:HEAD] / count)
            lse_ref[0, 0, n : n + 1, :] = top + jnp.log(count)
        o_ref[:, lanes(p)] = jnp.concatenate(outs, axis=0).T.astype(o_ref.dtype)


def attend_specs(rows, kv_rows, width):
    pairs = pairs_a_step(width)
    wide = pairs * PAIR
    steps = width // wide
    block = pl.BlockSpec((TILE, wide), lambda p, i, b: (i, p))
    keys = pl.BlockSpec((kv_rows, wide), lambda p, i, b: (0, p))
    values = pl.BlockSpec((kv_rows, wide), lambda p, i, b: (0, steps + p))
    by_tile = lambda *shape: pl.BlockSpec((1, 1, *shape, TILE), lambda p, i, b: (p, i, *[0] * len(shape), 0))
    starts = pl.BlockSpec((1, 1, TILE), lambda p, i, b: (i, 0, 0))
    return pairs, wide, (steps, rows // TILE), block, keys, values, by_tile, starts


def self_attend(q, kv, starts, reach, base, before=None):
    rows, width = q.shape
    kv_rows = kv.shape[0]
    ends = before is not None
    pairs, wide, grid, block, keys, values, by_tile, start_block = attend_specs(rows, kv_rows, width)
    state = by_tile(2 * pairs, HEAD + 16)
    state_shape = jax.ShapeDtypeStruct((*grid, 2 * pairs, HEAD + 16, TILE), jnp.float32)
    spec = pltpu.PrefetchScalarGridSpec(
        num_scalar_prefetch=1,
        grid=grid,
        in_specs=[block, keys, values, start_block] + [state] * ends,
        out_specs=[block, by_tile(8)] if ends else state,
        scratch_shapes=[pltpu.VMEM((2 * pairs, HEAD + 16, kv_rows), jnp.bfloat16)],
    )
    return pl.pallas_call(
        functools.partial(attend_kernel, reach=reach, base=base, pairs=pairs, ends=ends),
        grid_spec=spec,
        out_shape=[
            jax.ShapeDtypeStruct((rows, width), jnp.bfloat16),
            jax.ShapeDtypeStruct((*grid, 8, TILE), jnp.float32),
        ]
        if ends
        else state_shape,
        compiler_params=pltpu.CompilerParams(vmem_limit_bytes=VMEM_BYTES),
        cost_estimate=pl.CostEstimate(
            flops=rows * kv_rows * HEAD, bytes_accessed=rows * HEAD, transcendentals=0
        ),
        name="self_attend",
    )(tile_bounds(starts, reach, base, kv_rows), q, kv, kv, starts.reshape(-1, 1, TILE), *([before] if ends else []))


def attend_back_kernel(bounds, q_ref, g_ref, o_ref, lse_ref, k_ref, v_ref, start_ref, *refs, reach, base, pairs, ends):
    i = pl.program_id(1)
    if ends:
        before_ref, dq_ref, dk_ref, dv_ref, dk_sum, dv_sum, k_t = refs
    else:
        after_ref, dk_ref, dv_ref, dk_sum, dv_sum, k_t = refs

    @pl.when(i == 0)
    def _():
        k_t[...] = k_ref[...].T
        dk_sum[...] = jnp.zeros_like(dk_sum)
        dv_sum[...] = jnp.zeros_like(dv_sum)

    queries, grads, inner, logs = [], [], [], []
    for p in range(pairs):
        grad = g_ref[:, lanes(p)]
        queries += split_heads(q_ref[:, lanes(p)] * jnp.bfloat16(SCALE))
        grads += split_heads(grad)
        product = (grad.astype(jnp.float32) * o_ref[:, lanes(p)].astype(jnp.float32)).T
        for h in range(2):
            inner.append(jnp.sum(product[h * HEAD : (h + 1) * HEAD], axis=0, keepdims=True))
            logs.append(lse_ref[0, 0, 2 * p + h : 2 * p + h + 1])
    starts = start_ref[0]

    def step(masked, j, carried):
        rows = pl.ds(pl.multiple_of(j * TILE, TILE), TILE)
        if masked:
            allowed = tile_allowed(base + j * TILE, reach + i * TILE, starts)
        out = []
        for p in range(pairs):
            keys, values = k_ref[rows, lanes(p)], v_ref[rows, lanes(p)]
            dks, dvs = [], []
            for n in (2 * p, 2 * p + 1):
                s = contract_cols(keys, queries[n])
                d = contract_cols(values, grads[n])
                if masked:
                    s = jnp.where(allowed, s, NEG)
                shares = jnp.exp(s - logs[n])
                ds = (shares * (d - inner[n])).astype(jnp.bfloat16)
                dvs.append(matmul(shares.astype(jnp.bfloat16), grads[n]))
                dks.append(matmul(ds, queries[n]))
                out.append(carried[n] + matmul(k_t[n * HEAD : (n + 1) * HEAD, rows], ds))
            dv_sum[rows, lanes(p)] += dvs[0] + dvs[1]
            dk_sum[rows, lanes(p)] += dks[0] + dks[1]
        return tuple(out)

    if ends:
        state = tuple(before_ref[0, 0, n] for n in range(2 * pairs))
    else:
        state = (jnp.zeros((HEAD, TILE), jnp.float32),) * (2 * pairs)
    state = over_tiles(bounds, i, step, state)
    if ends:
        for p in range(pairs):
            turned = jnp.concatenate([state[2 * p], state[2 * p + 1]], axis=0).T
            dq_ref[:, lanes(p)] = (turned * SCALE).astype(dq_ref.dtype)
    else:
        for n in range(2 * pairs):
            after_ref[0, 0, n] = state[n]

    @pl.when(i == pl.num_programs(1) - 1)
    def _():
        dk_ref[...] = dk_sum[...].astype(dk_ref.dtype)
        dv_ref[...] = dv_sum[...].astype(dv_ref.dtype)


def self_attend_back(q, grad, o, lse, kv, starts, reach, base, before=None):
    rows, width = q.shape
    kv_rows = kv.shape[0]
    ends = before is not None
    pairs, wide, grid, block, keys, values, by_tile, start_block = attend_specs(rows, kv_rows, width)
    state = by_tile(2 * pairs, HEAD)
    shape = lambda n: jax.ShapeDtypeStruct((n, width), jnp.bfloat16)
    spec = pltpu.PrefetchScalarGridSpec(
        num_scalar_prefetch=1,
        grid=grid,
        in_specs=[block, block, block, by_tile(8), keys, values, start_block] + [state] * ends,
        out_specs=[block if ends else state, keys, keys],
        scratch_shapes=[
            pltpu.VMEM((kv_rows, wide), jnp.float32),
            pltpu.VMEM((kv_rows, wide), jnp.float32),
            pltpu.VMEM((wide, kv_rows), jnp.bfloat16),
        ],
    )
    return pl.pallas_call(
        functools.partial(attend_back_kernel, reach=reach, base=base, pairs=pairs, ends=ends),
        grid_spec=spec,
        out_shape=[
            shape(rows) if ends else jax.ShapeDtypeStruct((*grid, 2 * pairs, HEAD, TILE), jnp.float32),
            shape(kv_rows),
            shape(kv_rows),
        ],
        compiler_params=pltpu.CompilerParams(vmem_limit_bytes=VMEM_BYTES),
        cost_estimate=pl.CostEstimate(
            flops=rows * kv_rows * HEAD, bytes_accessed=rows * HEAD, transcendentals=0
        ),
        name="self_attend_back",
    )(
        tile_bounds(starts, reach, base, kv_rows), q, grad, o, lse, kv, kv, starts.reshape(-1, 1, TILE),
        *([before] if ends else []),
    )


CROSS_PAIRS = 3


def cross_kernel(q_ref, k_ref, v_ref, slot_ref, o_ref):
    lower = lax.broadcasted_iota(jnp.int32, (1, PAIR), 1) < HEAD
    tokens, texts = q_ref.shape[0], k_ref.shape[0]
    allowed = slot_ref[:, :1] == lax.broadcasted_iota(jnp.int32, (tokens, texts), 1) // TXT
    for p in range(CROSS_PAIRS):
        results = []
        for half in split_heads(q_ref[:, lanes(p)] * jnp.bfloat16(SCALE)):
            scores = jnp.where(allowed, contract_cols(half, k_ref[:, lanes(p)]), NEG)
            weights = jnp.exp(scores - jnp.max(scores, axis=1, keepdims=True))
            shares = weights / jnp.sum(weights, axis=1, keepdims=True)
            results.append(matmul(shares.astype(jnp.bfloat16), v_ref[:, lanes(p)]))
        o_ref[:, lanes(p)] = jnp.where(lower, results[0], results[1]).astype(o_ref.dtype)


def cross_attend(q, k, v, slots_wide):
    tokens, width = q.shape
    texts = k.shape[0]
    column = lambda p: (0, p)
    return pl.pallas_call(
        cross_kernel,
        grid=(width // (CROSS_PAIRS * PAIR),),
        in_specs=[
            pl.BlockSpec((tokens, CROSS_PAIRS * PAIR), column),
            pl.BlockSpec((texts, CROSS_PAIRS * PAIR), column),
            pl.BlockSpec((texts, CROSS_PAIRS * PAIR), column),
            pl.BlockSpec((tokens, PAIR), lambda p: (0, 0)),
        ],
        out_specs=pl.BlockSpec((tokens, CROSS_PAIRS * PAIR), column),
        out_shape=jax.ShapeDtypeStruct(q.shape, jnp.bfloat16),
        compiler_params=pltpu.CompilerParams(vmem_limit_bytes=VMEM_BYTES),
        cost_estimate=pl.CostEstimate(
            flops=8 * tokens * texts * width,
            bytes_accessed=4 * tokens * width,
            transcendentals=tokens * texts * width // HEAD,
        ),
        name="cross_attend",
    )(q, k, v, slots_wide)


def cross_back_kernel(q_ref, g_ref, k_ref, v_ref, slot_ref, dq_ref, dk_ref, dv_ref):
    lower = lax.broadcasted_iota(jnp.int32, (1, PAIR), 1) < HEAD
    tokens, texts = q_ref.shape[0], k_ref.shape[0]
    allowed = slot_ref[:, :1] == lax.broadcasted_iota(jnp.int32, (tokens, texts), 1) // TXT
    for p in range(CROSS_PAIRS):
        keys, values = k_ref[:, lanes(p)], v_ref[:, lanes(p)]
        halves = zip(split_heads(q_ref[:, lanes(p)] * jnp.bfloat16(SCALE)), split_heads(g_ref[:, lanes(p)]))
        dqs, dks, dvs = [], [], []
        for q_half, g_half in halves:
            scores = jnp.where(allowed, contract_cols(q_half, keys), NEG)
            weights = jnp.exp(scores - jnp.max(scores, axis=1, keepdims=True))
            shares = weights / jnp.sum(weights, axis=1, keepdims=True)
            grad_shares = contract_cols(g_half, values)
            inner = jnp.sum(shares * grad_shares, axis=1, keepdims=True)
            grad_scores = (shares * (grad_shares - inner)).astype(jnp.bfloat16)
            dqs.append(matmul(grad_scores, keys))
            dks.append(contract_rows(grad_scores, q_half))
            dvs.append(contract_rows(shares.astype(jnp.bfloat16), g_half))
        dq_ref[:, lanes(p)] = (jnp.where(lower, dqs[0], dqs[1]) * SCALE).astype(dq_ref.dtype)
        dk_ref[:, lanes(p)] = dks[0] + dks[1]
        dv_ref[:, lanes(p)] = dvs[0] + dvs[1]


def cross_attend_back(q, grad, k, v, slots_wide):
    tokens, width = q.shape
    texts = k.shape[0]
    column = lambda p: (0, p)
    return pl.pallas_call(
        cross_back_kernel,
        grid=(width // (CROSS_PAIRS * PAIR),),
        in_specs=[
            pl.BlockSpec((tokens, CROSS_PAIRS * PAIR), column),
            pl.BlockSpec((tokens, CROSS_PAIRS * PAIR), column),
            pl.BlockSpec((texts, CROSS_PAIRS * PAIR), column),
            pl.BlockSpec((texts, CROSS_PAIRS * PAIR), column),
            pl.BlockSpec((tokens, PAIR), lambda p: (0, 0)),
        ],
        out_specs=[
            pl.BlockSpec((tokens, CROSS_PAIRS * PAIR), column),
            pl.BlockSpec((texts, CROSS_PAIRS * PAIR), column),
            pl.BlockSpec((texts, CROSS_PAIRS * PAIR), column),
        ],
        out_shape=[
            jax.ShapeDtypeStruct(q.shape, jnp.bfloat16),
            jax.ShapeDtypeStruct((texts, width), jnp.float32),
            jax.ShapeDtypeStruct((texts, width), jnp.float32),
        ],
        compiler_params=pltpu.CompilerParams(vmem_limit_bytes=VMEM_BYTES),
        cost_estimate=pl.CostEstimate(
            flops=20 * tokens * texts * width,
            bytes_accessed=6 * tokens * width,
            transcendentals=tokens * texts * width // HEAD,
        ),
        name="cross_attend_back",
    )(q, grad, k, v, slots_wide)


def swap(value, axis, bit):
    count = lax.axis_size(axis)
    return lax.ppermute(value, axis, [(i, i ^ bit) for i in range(count)])


def passed_along(value, axis, steps):
    count = lax.axis_size(axis)
    initial, last = (max(0, -steps), min(count, count - steps))
    return lax.ppermute(value, axis, [(source, source + steps) for source in range(initial, last)])


def in_order(mine, other, dim):
    second = lax.axis_index("seq") == 1
    return jnp.concatenate([jnp.where(second, other, mine), jnp.where(second, mine, other)], axis=dim)


def gathered(value, dim):
    if lax.axis_size("seq") == 2:
        return in_order(value, swap(value, "seq", 1), dim)
    return lax.all_gather(value, "seq", axis=dim, tiled=True)


def own_block(value, dim):
    size = value.shape[dim] // lax.axis_size("seq")
    return lax.dynamic_slice_in_dim(value, lax.axis_index("seq") * size, size, dim)


def other_block(value, dim):
    size = value.shape[dim] // 2
    return lax.dynamic_slice_in_dim(value, (1 - lax.axis_index("seq")) * size, size, dim)


def exchanged(value, split, concat):
    if lax.axis_size("seq") == 2:
        return in_order(own_block(value, split), swap(other_block(value, split), "seq", 1), concat)
    return lax.all_to_all(value, "seq", split_axis=split, concat_axis=concat, tiled=True)


def summed_block(value, dim):
    if lax.axis_size("seq") == 2:
        received = swap(other_block(value, dim).astype(jnp.bfloat16), "seq", 1)
        return own_block(value, dim) + received.astype(jnp.float32)
    return lax.psum_scatter(
        value.astype(jnp.bfloat16), "seq", scatter_dimension=dim, tiled=True
    ).astype(jnp.float32)


def paired(value):
    short = -value.shape[-1] % PAIR
    return jnp.pad(value, ((0, 0), (0, short))) if short else value


def normed(values):
    average = jnp.mean(values, axis=-1, keepdims=True)
    centred = values - average
    spread = jnp.mean(centred * centred, axis=-1, keepdims=True)
    root = lax.rsqrt(spread + EPS)
    return centred * root, root


def norm_back(grad, n, root, gain):
    a = grad * gain
    back = (a - jnp.mean(a, axis=-1, keepdims=True) - n * jnp.mean(a * n, axis=-1, keepdims=True)) * root
    return back, jnp.sum(grad * n, axis=0), jnp.sum(grad, axis=0)


def scattered(grad):
    return lax.psum_scatter(grad.astype(jnp.bfloat16), "fsdp", scatter_dimension=0, tiled=True)


def whole(part):
    if lax.axis_size("seq") == 2:
        return part.astype(jnp.float32) + swap(part, "seq", 1).astype(jnp.float32)
    return lax.psum(part, "seq").astype(jnp.float32)


def columns(part, blocks):
    split = part.reshape(part.shape[0], blocks, -1)
    return gathered(split, 2).reshape(part.shape[0], -1).astype(jnp.float32)


def core_products(left, right):
    size, core = right.shape[1] // 2, lax.axis_index("fsdp") % 2
    part = lambda place: contract_rows(left, lax.dynamic_slice_in_dim(right, place * size, size, 1)).astype(jnp.bfloat16)
    return part(core), part(1 - core)


def both(first, second):
    return (first.astype(jnp.float32) + second.astype(jnp.float32)).astype(jnp.bfloat16)


def half_rows(value, place):
    blocks = value.reshape(-1, 2, *value.shape[1:])
    return lax.dynamic_index_in_dim(blocks, place % 2, 1, keepdims=False)


def seq_away(kept, came):
    return both(other_block(kept, 1), other_block(came, 1))


def chip_blocks(kept, came, beside):
    value = both(both(own_block(kept, 1), own_block(came, 1)), beside)
    return value.reshape(lax.axis_size("fsdp") // 2, -1, value.shape[1])


def own_rows(value, at, bit):
    while value.shape[0] > 1:
        value = both(half_rows(value, at), swap(half_rows(value, at + 1), "fsdp", bit))
        at, bit = at // 2, bit * 2
    core, second = lax.axis_index("fsdp") % 2, lax.axis_index("seq") == 1
    value = value.reshape(2, -1, value.shape[-1])
    take = lambda place: lax.dynamic_index_in_dim(value, place, 0, keepdims=False)
    mine, theirs = take(core), swap(take(1 - core), "fsdp", 1)
    pair = jnp.stack([jnp.where(core == 0, mine, theirs), jnp.where(core == 0, theirs, mine)])
    beside = swap(pair, "seq", 1)
    by_seq = jnp.where(second, beside, pair), jnp.where(second, pair, beside)
    return jnp.concatenate([by_seq[s][c] for c in range(2) for s in range(2)], axis=1).astype(jnp.float32)


def clip_starts(segments, group_index, group_rows):
    padded = jnp.concatenate([jnp.full((SPAN,), -1, jnp.int32), segments])
    spans = lax.dynamic_slice_in_dim(padded, group_index * group_rows, SPAN + group_rows)
    spans = spans.reshape(-1, SPAN)
    ahead = jnp.sum((spans == spans[:, :1]).astype(jnp.int32), axis=1)
    firsts = ahead + jnp.arange(spans.shape[0], dtype=jnp.int32) * SPAN
    late = spans[1:] != spans[1:, :1]
    return jnp.where(late, firsts[1:, None], firsts[:-1, None]).reshape(group_rows), spans[1:].reshape(group_rows)


def shards(
    tokens,
    segments,
    text,
    qkv_weight,
    out_weight,
    cross_query_weight,
    cross_kv_weight,
    cross_out_weight,
    up_weight,
    down_weight,
    norm_gain,
    norm_bias,
    cotangent,
):
    group_index = lax.axis_index("fsdp")
    seq_index = lax.axis_index("seq")
    seq_count = lax.axis_size("seq")
    tok_rows, width = tokens.shape
    group_rows = tok_rows * seq_count
    head_cols = width // seq_count
    shard_rows = qkv_weight.shape[0]
    row_block = lambda value: lax.all_gather(value, "fsdp", axis=0, tiled=True)

    norms = jnp.pad(jnp.concatenate([norm_gain, norm_bias]).T, ((0, 0), (0, PAIR - 6)))
    qkv_mine = own_block(qkv_weight.reshape(shard_rows, 3, width), 2).reshape(shard_rows, 3 * head_cols)
    first = row_block(jnp.concatenate([qkv_mine, norms], axis=1))
    w_q, w_kv, w_qkv = first[:, :head_cols], first[:, head_cols : 3 * head_cols], first[:, : 3 * head_cols]
    norm_rows = first[:, 3 * head_cols : 3 * head_cols + 6].astype(jnp.float32).T
    gains, biases = norm_rows[:3], norm_rows[3:]

    ckv_mine = own_block(cross_kv_weight.reshape(shard_rows, 2, width), 2).reshape(shard_rows, 2 * head_cols)
    squares = (out_weight, cross_query_weight, cross_out_weight)
    gate = lax.optimization_barrier
    by_steps = seq_count == 2 and group_rows == SPAN
    second = row_block(jnp.concatenate([*squares, ckv_mine], axis=1))
    full_out, full_cq, full_cout = (second[:, i * width : (i + 1) * width] for i in range(3))
    w_ckv = second[:, 3 * width :]

    starts, seg_group = clip_starts(segments, group_index, group_rows)
    slots = own_block(seg_group, 0) - group_index * (group_rows // SPAN)
    slots_wide = jnp.broadcast_to(slots[:, None], (tok_rows, PAIR))

    inputs = tokens.astype(jnp.float32)
    norm_one = lambda rows: (normed(rows.astype(jnp.float32))[0] * gains[0] + biases[0]).astype(jnp.bfloat16)
    normed_one = norm_one(gathered(tokens, 0))
    kv_own = matmul(normed_one, w_kv).astype(jnp.bfloat16)
    queries = matmul(normed_one, w_q).astype(jnp.bfloat16)
    if by_steps:
        before = passed_along(tokens, "fsdp", 1)
        before_other = swap(before, "seq", 1)
    else:
        kv_before = passed_along(kv_own[group_rows - SPAN :], "fsdp", 1)
    pad_kv = lambda kv: jnp.concatenate([paired(kv[:, :head_cols]), paired(kv[:, head_cols:])], axis=1)
    if head_cols % PAIR:
        queries, kv_own, kv_before = paired(queries), pad_kv(kv_own), pad_kv(kv_before)
    heads_state = self_attend(queries, kv_own, starts, SPAN, SPAN)
    if by_steps:
        before, before_other, heads_state = gate((before, before_other, heads_state))
        kv_before = matmul(norm_one(in_order(before, before_other, 0)), w_kv).astype(jnp.bfloat16)
    heads_out, log_totals = self_attend(queries, kv_before, starts, SPAN, 0, heads_state)
    attended = exchanged(heads_out[:, :head_cols], 0, 1)
    hidden_one = inputs + matmul(attended, full_out)

    text_rows = text.reshape(-1, width)
    text_count = text_rows.shape[0]
    ckv_part = matmul(text_rows, w_ckv).astype(jnp.bfloat16).reshape(text_count, 2, head_cols)
    cross_kv = gathered(ckv_part, 2)
    cross_k, cross_v = cross_kv[:, 0], cross_kv[:, 1]
    n_two, root_two = normed(hidden_one)
    normed_two = (n_two * gains[1] + biases[1]).astype(jnp.bfloat16)
    cross_query = matmul(normed_two, full_cq).astype(jnp.bfloat16)
    cross_result = cross_attend(cross_query, cross_k, cross_v, slots_wide)
    hidden_two = hidden_one + matmul(cross_result, full_cout)

    full_up, full_down = row_block(up_weight), row_block(down_weight)
    n_three, root_three = normed(hidden_two)
    normed_three = (n_three * gains[2] + biases[2]).astype(jnp.bfloat16)
    upward = matmul(normed_three, full_up)
    below = 0.5 * (1.0 + lax.erf(upward * (0.5**0.5)))
    active = (upward * below).astype(jnp.bfloat16)
    slope = below + upward * (jnp.exp(-0.5 * upward * upward) * 0.3989422804014327)
    layer_out = (hidden_two + matmul(active, full_down)).astype(jnp.bfloat16)

    chip = group_index // 2
    grad_down, slope = gate((contract_rows(active, cotangent).astype(jnp.bfloat16), slope))
    grad_down = scattered(grad_down)
    grad_upward = (contract_cols(cotangent, full_down) * slope).astype(jnp.bfloat16)
    if by_steps:
        up_kept, up_away, grad_upward = gate((*core_products(normed_three, grad_upward), grad_upward))
        up_came = swap(up_away, "fsdp", 1)
    else:
        grad_up = scattered(contract_rows(normed_three, grad_upward))
    back_h2, gain_three, bias_three = norm_back(contract_cols(grad_upward, full_up), n_three, root_three, gains[2])
    grad_two = cotangent.astype(jnp.float32) + back_h2
    grad_two_low = grad_two.astype(jnp.bfloat16)
    if by_steps:
        up_beside, grad_two_low = gate((seq_away(up_kept, up_came), grad_two_low))
    grad_result = contract_cols(grad_two_low, full_cout).astype(jnp.bfloat16)
    grad_query_c, grad_text_k, grad_text_v = cross_attend_back(cross_query, grad_result, cross_k, cross_v, slots_wide)
    grad_text_kv = jnp.stack([grad_text_k, grad_text_v], axis=1)
    if by_steps:
        text_came = swap(other_block(grad_text_kv, 2).astype(jnp.bfloat16), "seq", 1)
    else:
        grad_text_kv = summed_block(grad_text_kv, 2)
    back_h1, gain_two, bias_two = norm_back(contract_cols(grad_query_c, full_cq), n_two, root_two, gains[1])
    grad_one = grad_two + back_h1

    grad_one_low = grad_one.astype(jnp.bfloat16)
    if by_steps:
        text_came, grad_one_low = gate((text_came, grad_one_low))
        grad_text_kv = own_block(grad_text_kv, 2) + text_came.astype(jnp.float32)
    grad_text_kv = grad_text_kv.astype(jnp.bfloat16).reshape(text_count, 2 * head_cols)
    grad_text = contract_cols(grad_text_kv, w_ckv)
    grad_attended = contract_cols(grad_one_low, full_out).astype(jnp.bfloat16)
    grad_attended, grad_query_c, grad_two_low = gate((grad_attended, grad_query_c, grad_two_low))
    if by_steps:
        heads_came = swap(other_block(grad_attended, 1), "seq", 1)
    else:
        grad_heads = paired(exchanged(grad_attended, 1, 0))
    small = [
        contract_rows(left, right).astype(jnp.bfloat16)
        for left, right in (
            (cross_result, grad_two_low),
            (normed_two, grad_query_c),
            (attended, grad_one_low),
            (text_rows, grad_text_kv),
        )
    ]
    if by_steps:
        small, up_beside, heads_came = gate((jnp.stack(small), up_beside, heads_came))
        small = lax.psum_scatter(small, "fsdp", scatter_dimension=1, tiled=True)
        up_beside = swap(up_beside, "seq", 1)
        grad_heads = in_order(own_block(grad_attended, 1), heads_came, 0)
    else:
        small = [scattered(part) for part in small]
    back_args = (queries, grad_heads, heads_out, log_totals)
    query_state, *grad_before = self_attend_back(*back_args, kv_before, starts, SPAN, 0)
    returned = [passed_along(part[:, :head_cols], "fsdp", -1).astype(jnp.float32) for part in grad_before]
    if by_steps:
        up_rows = chip_blocks(up_kept, up_came, up_beside)
        up_away, grad_down, query_state = gate((half_rows(up_rows, chip + 1), grad_down, query_state))
        up_came, down_beside = swap(up_away, "fsdp", 2), swap(grad_down, "seq", 1)
    grad_q, *grad_own = self_attend_back(*back_args, kv_own, starts, SPAN, SPAN, query_state)
    if by_steps:
        down_beside, grad_q = gate((down_beside, grad_q))
        grad_down = grad_down.astype(jnp.float32) + down_beside.astype(jnp.float32)
    else:
        grad_up, grad_down = whole(grad_up), whole(grad_down)
    late = group_rows - SPAN
    owned = [grad_q[:, :head_cols]]
    for part, more in zip(grad_own, returned):
        part = part[:, :head_cols].astype(jnp.float32)
        part = jnp.concatenate([part[:late], part[late:] + more]) if late else part + more
        owned.append(part.astype(jnp.bfloat16))
    grad_proj = jnp.concatenate(owned, axis=1)
    if by_steps:
        away = contract_cols(other_block(grad_proj, 0), w_qkv).astype(jnp.bfloat16)
        away, grad_proj = gate((away, grad_proj))
        grad_normed_one = swap(away, "seq", 1).astype(jnp.float32) + contract_cols(own_block(grad_proj, 0), w_qkv)
    else:
        grad_normed_one = summed_block(contract_cols(grad_proj, w_qkv), 0)
    grad_wqkv = contract_rows(normed_one, grad_proj).astype(jnp.bfloat16)
    n_one, root_one = normed(inputs)
    back_x, gain_one, bias_one = norm_back(grad_normed_one, n_one, root_one, gains[0])
    grad_tokens = (grad_one + back_x).astype(jnp.bfloat16)
    norm_grads = jnp.stack([gain_one, gain_two, gain_three, bias_one, bias_two, bias_three])
    norm_grads = jnp.pad(norm_grads.T.astype(jnp.bfloat16), ((0, 0), (0, PAIR - 6)))
    last, small = gate((jnp.concatenate([grad_wqkv, norm_grads], axis=1), small))
    if by_steps:
        up_came, last = gate((up_came, last))
    last = scattered(last)
    if by_steps:
        grad_cout, grad_cq, grad_wout = whole(small[:3])
        grad_up = own_rows(both(half_rows(up_rows, chip), up_came), chip // 2, 4)
    else:
        grad_cout, grad_cq, grad_wout = (whole(part) for part in small[:3])
    grad_ckv = columns(small[3], 2)
    last, grad_cout, grad_cq, grad_wout, grad_ckv, grad_up, grad_tokens = gate(
        (last, grad_cout, grad_cq, grad_wout, grad_ckv, grad_up, grad_tokens)
    )
    norm_grads = whole(last[:, -PAIR:]).T
    return (
        layer_out,
        grad_tokens,
        whole(grad_text.astype(jnp.bfloat16)).reshape(text.shape),
        columns(last[:, : 3 * head_cols], 3),
        grad_wout,
        grad_cq,
        grad_ckv,
        grad_cout,
        grad_up,
        grad_down,
        norm_grads[:3],
        norm_grads[3:6],
    )


def solution(mesh):
    rows, shard, copied = P(("fsdp", "seq"), None), P("fsdp", None), P(None, "fsdp")
    groups = P("fsdp", None, None)
    in_specs = (rows, P(), groups, *[shard] * 7, copied, copied, rows)
    out_specs = (rows, rows, groups, *[shard] * 7, copied, copied)
    return jax.shard_map(shards, mesh=mesh, in_specs=in_specs, out_specs=out_specs, check_vma=False)
```

```python
import functools

import jax
import jax.numpy as jnp
from jax import lax
from jax.experimental import pallas as pl
from jax.experimental.pallas import tpu as pltpu
from jax.sharding import PartitionSpec as P

HEADS = 24
HEAD = 64
PAIR = 2 * HEAD
TXT = 64
SPAN = 1536
EPS = 1e-05
NEG = -1e30
SCALE = HEAD**-0.5
VMEM_BYTES = 56 * 2**20


def matmul(left_side, right_side):
    return jnp.dot(left_side, right_side, preferred_element_type=jnp.float32)


def contract_rows(left_side, right_side):
    return lax.dot_general(
        left_side, right_side, (((0,), (0,)), ((), ())), preferred_element_type=jnp.float32
    )


def contract_cols(left_side, right_side):
    return lax.dot_general(
        left_side, right_side, (((1,), (1,)), ((), ())), preferred_element_type=jnp.float32
    )


TILE = 384


def tile_bounds(starts, reach, base, kv_rows):
    count = kv_rows // TILE
    first, last = starts[::TILE] - base, starts[TILE - 1 :: TILE] - base
    row0 = reach - base + jnp.arange(first.shape[0], dtype=jnp.int32) * TILE
    low = jnp.clip(first // TILE, 0, count)
    high = jnp.clip((row0 + TILE - 1) // TILE + 1, low, count)
    free_low = jnp.clip((last + TILE - 1) // TILE, low, high)
    free_high = jnp.clip((row0 + 1) // TILE, free_low, high)
    return jnp.stack([low, free_low, free_high, high], axis=1)


def pairs_a_step(width):
    return 3 if width % (3 * PAIR) == 0 else 1


def split_heads(block):
    lower = lax.broadcasted_iota(jnp.int32, (1, PAIR), 1) < HEAD
    zero = jnp.zeros((1, 1), block.dtype)
    return [jnp.where(lower, block, zero), jnp.where(lower, zero, block)]


def lanes(p):
    return slice(p * PAIR, (p + 1) * PAIR)


def tile_allowed(col0, row0, starts):
    at = col0 + lax.broadcasted_iota(jnp.int32, (TILE, TILE), 0)
    row = row0 + lax.broadcasted_iota(jnp.int32, (TILE, TILE), 1)
    return (at >= starts) & (at <= row)


def over_tiles(bounds, i, step, state):
    low, free_low, free_high, high = (bounds[i, n] for n in range(4))
    state = lax.fori_loop(low, free_low, functools.partial(step, True), state)
    state = lax.fori_loop(free_low, free_high, functools.partial(step, False), state)
    return lax.fori_loop(free_high, high, functools.partial(step, True), state)


def attend_kernel(bounds, q_ref, k_ref, v_ref, start_ref, *refs, reach, base, pairs, ends):
    i = pl.program_id(1)
    if ends:
        before_ref, o_ref, lse_ref, v_t = refs
    else:
        after_ref, v_t = refs

    @pl.when(i == 0)
    def _():
        for p in range(pairs):
            turned = v_ref[:, lanes(p)].T
            for h in range(2):
                v_t[2 * p + h, :HEAD] = turned[h * HEAD : (h + 1) * HEAD]
                v_t[2 * p + h, HEAD:] = jnp.ones((16, turned.shape[1]), jnp.bfloat16)

    halves = []
    for p in range(pairs):
        halves += split_heads(q_ref[:, lanes(p)] * jnp.bfloat16(SCALE))
    starts = start_ref[0]

    def step(masked, j, carried):
        rows = pl.ds(pl.multiple_of(j * TILE, TILE), TILE)
        if masked:
            allowed = tile_allowed(base + j * TILE, reach + i * TILE, starts)
        scores = []
        for n in range(2 * pairs):
            s = contract_cols(k_ref[rows, lanes(n // 2)], halves[n])
            scores.append(jnp.where(allowed, s, NEG) if masked else s)
        out = []
        for n, (top, total) in enumerate(carried):
            new_top = jnp.maximum(top, jnp.max(scores[n], axis=0, keepdims=True))
            weights = jnp.exp(scores[n] - new_top).astype(jnp.bfloat16)
            total = total * jnp.exp(top - new_top) + matmul(v_t[n, :, rows], weights)
            out.append((new_top, total))
        return tuple(out)

    if ends:
        state = tuple((before_ref[0, 0, n, HEAD + 8 : HEAD + 9], before_ref[0, 0, n]) for n in range(2 * pairs))
    else:
        nothing = (jnp.full((1, TILE), NEG, jnp.float32), jnp.zeros((HEAD + 16, TILE), jnp.float32))
        state = (nothing,) * (2 * pairs)
    state = over_tiles(bounds, i, step, state)
    if not ends:
        for n, (top, total) in enumerate(state):
            after_ref[0, 0, n, : HEAD + 8] = total[: HEAD + 8]
            after_ref[0, 0, n, HEAD + 8 :] = jnp.broadcast_to(top, (8, TILE))
        return
    for p in range(pairs):
        outs = []
        for n in (2 * p, 2 * p + 1):
            top, total = state[n]
            count = total[HEAD : HEAD + 1]
            outs.append(total[:HEAD] / count)
            lse_ref[0, 0, n : n + 1, :] = top + jnp.log(count)
        o_ref[:, lanes(p)] = jnp.concatenate(outs, axis=0).T.astype(o_ref.dtype)


def attend_specs(rows, kv_rows, width):
    pairs = pairs_a_step(width)
    wide = pairs * PAIR
    steps = width // wide
    block = pl.BlockSpec((TILE, wide), lambda p, i, b: (i, p))
    keys = pl.BlockSpec((kv_rows, wide), lambda p, i, b: (0, p))
    values = pl.BlockSpec((kv_rows, wide), lambda p, i, b: (0, steps + p))
    by_tile = lambda *shape: pl.BlockSpec((1, 1, *shape, TILE), lambda p, i, b: (p, i, *[0] * len(shape), 0))
    starts = pl.BlockSpec((1, 1, TILE), lambda p, i, b: (i, 0, 0))
    return pairs, wide, (steps, rows // TILE), block, keys, values, by_tile, starts


def self_attend(q, kv, starts, reach, base, before=None):
    rows, width = q.shape
    kv_rows = kv.shape[0]
    ends = before is not None
    pairs, wide, grid, block, keys, values, by_tile, start_block = attend_specs(rows, kv_rows, width)
    state = by_tile(2 * pairs, HEAD + 16)
    state_shape = jax.ShapeDtypeStruct((*grid, 2 * pairs, HEAD + 16, TILE), jnp.float32)
    spec = pltpu.PrefetchScalarGridSpec(
        num_scalar_prefetch=1,
        grid=grid,
        in_specs=[block, keys, values, start_block] + [state] * ends,
        out_specs=[block, by_tile(8)] if ends else state,
        scratch_shapes=[pltpu.VMEM((2 * pairs, HEAD + 16, kv_rows), jnp.bfloat16)],
    )
    return pl.pallas_call(
        functools.partial(attend_kernel, reach=reach, base=base, pairs=pairs, ends=ends),
        grid_spec=spec,
        out_shape=[
            jax.ShapeDtypeStruct((rows, width), jnp.bfloat16),
            jax.ShapeDtypeStruct((*grid, 8, TILE), jnp.float32),
        ]
        if ends
        else state_shape,
        compiler_params=pltpu.CompilerParams(vmem_limit_bytes=VMEM_BYTES),
        cost_estimate=pl.CostEstimate(
            flops=rows * kv_rows * HEAD, bytes_accessed=rows * HEAD, transcendentals=0
        ),
        name="self_attend",
    )(tile_bounds(starts, reach, base, kv_rows), q, kv, kv, starts.reshape(-1, 1, TILE), *([before] if ends else []))


def attend_back_kernel(bounds, q_ref, g_ref, o_ref, lse_ref, k_ref, v_ref, start_ref, *refs, reach, base, pairs, ends):
    i = pl.program_id(1)
    if ends:
        before_ref, dq_ref, dk_ref, dv_ref, dk_sum, dv_sum, k_t = refs
    else:
        after_ref, dk_ref, dv_ref, dk_sum, dv_sum, k_t = refs

    @pl.when(i == 0)
    def _():
        k_t[...] = k_ref[...].T
        dk_sum[...] = jnp.zeros_like(dk_sum)
        dv_sum[...] = jnp.zeros_like(dv_sum)

    queries, grads, inner, logs = [], [], [], []
    for p in range(pairs):
        grad = g_ref[:, lanes(p)]
        queries += split_heads(q_ref[:, lanes(p)] * jnp.bfloat16(SCALE))
        grads += split_heads(grad)
        product = (grad.astype(jnp.float32) * o_ref[:, lanes(p)].astype(jnp.float32)).T
        for h in range(2):
            inner.append(jnp.sum(product[h * HEAD : (h + 1) * HEAD], axis=0, keepdims=True))
            logs.append(lse_ref[0, 0, 2 * p + h : 2 * p + h + 1])
    starts = start_ref[0]

    def step(masked, j, carried):
        rows = pl.ds(pl.multiple_of(j * TILE, TILE), TILE)
        if masked:
            allowed = tile_allowed(base + j * TILE, reach + i * TILE, starts)
        out = []
        for p in range(pairs):
            keys, values = k_ref[rows, lanes(p)], v_ref[rows, lanes(p)]
            dks, dvs = [], []
            for n in (2 * p, 2 * p + 1):
                s = contract_cols(keys, queries[n])
                d = contract_cols(values, grads[n])
                if masked:
                    s = jnp.where(allowed, s, NEG)
                shares = jnp.exp(s - logs[n])
                ds = (shares * (d - inner[n])).astype(jnp.bfloat16)
                dvs.append(matmul(shares.astype(jnp.bfloat16), grads[n]))
                dks.append(matmul(ds, queries[n]))
                out.append(carried[n] + matmul(k_t[n * HEAD : (n + 1) * HEAD, rows], ds))
            dv_sum[rows, lanes(p)] += dvs[0] + dvs[1]
            dk_sum[rows, lanes(p)] += dks[0] + dks[1]
        return tuple(out)

    if ends:
        state = tuple(before_ref[0, 0, n] for n in range(2 * pairs))
    else:
        state = (jnp.zeros((HEAD, TILE), jnp.float32),) * (2 * pairs)
    state = over_tiles(bounds, i, step, state)
    if ends:
        for p in range(pairs):
            turned = jnp.concatenate([state[2 * p], state[2 * p + 1]], axis=0).T
            dq_ref[:, lanes(p)] = (turned * SCALE).astype(dq_ref.dtype)
    else:
        for n in range(2 * pairs):
            after_ref[0, 0, n] = state[n]

    @pl.when(i == pl.num_programs(1) - 1)
    def _():
        dk_ref[...] = dk_sum[...].astype(dk_ref.dtype)
        dv_ref[...] = dv_sum[...].astype(dv_ref.dtype)


def self_attend_back(q, grad, o, lse, kv, starts, reach, base, before=None):
    rows, width = q.shape
    kv_rows = kv.shape[0]
    ends = before is not None
    pairs, wide, grid, block, keys, values, by_tile, start_block = attend_specs(rows, kv_rows, width)
    state = by_tile(2 * pairs, HEAD)
    shape = lambda n: jax.ShapeDtypeStruct((n, width), jnp.bfloat16)
    spec = pltpu.PrefetchScalarGridSpec(
        num_scalar_prefetch=1,
        grid=grid,
        in_specs=[block, block, block, by_tile(8), keys, values, start_block] + [state] * ends,
        out_specs=[block if ends else state, keys, keys],
        scratch_shapes=[
            pltpu.VMEM((kv_rows, wide), jnp.float32),
            pltpu.VMEM((kv_rows, wide), jnp.float32),
            pltpu.VMEM((wide, kv_rows), jnp.bfloat16),
        ],
    )
    return pl.pallas_call(
        functools.partial(attend_back_kernel, reach=reach, base=base, pairs=pairs, ends=ends),
        grid_spec=spec,
        out_shape=[
            shape(rows) if ends else jax.ShapeDtypeStruct((*grid, 2 * pairs, HEAD, TILE), jnp.float32),
            shape(kv_rows),
            shape(kv_rows),
        ],
        compiler_params=pltpu.CompilerParams(vmem_limit_bytes=VMEM_BYTES),
        cost_estimate=pl.CostEstimate(
            flops=rows * kv_rows * HEAD, bytes_accessed=rows * HEAD, transcendentals=0
        ),
        name="self_attend_back",
    )(
        tile_bounds(starts, reach, base, kv_rows), q, grad, o, lse, kv, kv, starts.reshape(-1, 1, TILE),
        *([before] if ends else []),
    )


CROSS_PAIRS = 3


def cross_kernel(q_ref, k_ref, v_ref, slot_ref, o_ref):
    lower = lax.broadcasted_iota(jnp.int32, (1, PAIR), 1) < HEAD
    tokens, texts = q_ref.shape[0], k_ref.shape[0]
    allowed = slot_ref[:, :1] == lax.broadcasted_iota(jnp.int32, (tokens, texts), 1) // TXT
    for p in range(CROSS_PAIRS):
        results = []
        for half in split_heads(q_ref[:, lanes(p)] * jnp.bfloat16(SCALE)):
            scores = jnp.where(allowed, contract_cols(half, k_ref[:, lanes(p)]), NEG)
            weights = jnp.exp(scores - jnp.max(scores, axis=1, keepdims=True))
            shares = weights / jnp.sum(weights, axis=1, keepdims=True)
            results.append(matmul(shares.astype(jnp.bfloat16), v_ref[:, lanes(p)]))
        o_ref[:, lanes(p)] = jnp.where(lower, results[0], results[1]).astype(o_ref.dtype)


def cross_attend(q, k, v, slots_wide):
    tokens, width = q.shape
    texts = k.shape[0]
    column = lambda p: (0, p)
    return pl.pallas_call(
        cross_kernel,
        grid=(width // (CROSS_PAIRS * PAIR),),
        in_specs=[
            pl.BlockSpec((tokens, CROSS_PAIRS * PAIR), column),
            pl.BlockSpec((texts, CROSS_PAIRS * PAIR), column),
            pl.BlockSpec((texts, CROSS_PAIRS * PAIR), column),
            pl.BlockSpec((tokens, PAIR), lambda p: (0, 0)),
        ],
        out_specs=pl.BlockSpec((tokens, CROSS_PAIRS * PAIR), column),
        out_shape=jax.ShapeDtypeStruct(q.shape, jnp.bfloat16),
        compiler_params=pltpu.CompilerParams(vmem_limit_bytes=VMEM_BYTES),
        cost_estimate=pl.CostEstimate(
            flops=8 * tokens * texts * width,
            bytes_accessed=4 * tokens * width,
            transcendentals=tokens * texts * width // HEAD,
        ),
        name="cross_attend",
    )(q, k, v, slots_wide)


def cross_back_kernel(q_ref, g_ref, k_ref, v_ref, slot_ref, dq_ref, dk_ref, dv_ref):
    lower = lax.broadcasted_iota(jnp.int32, (1, PAIR), 1) < HEAD
    tokens, texts = q_ref.shape[0], k_ref.shape[0]
    allowed = slot_ref[:, :1] == lax.broadcasted_iota(jnp.int32, (tokens, texts), 1) // TXT
    for p in range(CROSS_PAIRS):
        keys, values = k_ref[:, lanes(p)], v_ref[:, lanes(p)]
        halves = zip(split_heads(q_ref[:, lanes(p)] * jnp.bfloat16(SCALE)), split_heads(g_ref[:, lanes(p)]))
        dqs, dks, dvs = [], [], []
        for q_half, g_half in halves:
            scores = jnp.where(allowed, contract_cols(q_half, keys), NEG)
            weights = jnp.exp(scores - jnp.max(scores, axis=1, keepdims=True))
            shares = weights / jnp.sum(weights, axis=1, keepdims=True)
            grad_shares = contract_cols(g_half, values)
            inner = jnp.sum(shares * grad_shares, axis=1, keepdims=True)
            grad_scores = (shares * (grad_shares - inner)).astype(jnp.bfloat16)
            dqs.append(matmul(grad_scores, keys))
            dks.append(contract_rows(grad_scores, q_half))
            dvs.append(contract_rows(shares.astype(jnp.bfloat16), g_half))
        dq_ref[:, lanes(p)] = (jnp.where(lower, dqs[0], dqs[1]) * SCALE).astype(dq_ref.dtype)
        dk_ref[:, lanes(p)] = dks[0] + dks[1]
        dv_ref[:, lanes(p)] = dvs[0] + dvs[1]


def cross_attend_back(q, grad, k, v, slots_wide):
    tokens, width = q.shape
    texts = k.shape[0]
    column = lambda p: (0, p)
    return pl.pallas_call(
        cross_back_kernel,
        grid=(width // (CROSS_PAIRS * PAIR),),
        in_specs=[
            pl.BlockSpec((tokens, CROSS_PAIRS * PAIR), column),
            pl.BlockSpec((tokens, CROSS_PAIRS * PAIR), column),
            pl.BlockSpec((texts, CROSS_PAIRS * PAIR), column),
            pl.BlockSpec((texts, CROSS_PAIRS * PAIR), column),
            pl.BlockSpec((tokens, PAIR), lambda p: (0, 0)),
        ],
        out_specs=[
            pl.BlockSpec((tokens, CROSS_PAIRS * PAIR), column),
            pl.BlockSpec((texts, CROSS_PAIRS * PAIR), column),
            pl.BlockSpec((texts, CROSS_PAIRS * PAIR), column),
        ],
        out_shape=[
            jax.ShapeDtypeStruct(q.shape, jnp.bfloat16),
            jax.ShapeDtypeStruct((texts, width), jnp.float32),
            jax.ShapeDtypeStruct((texts, width), jnp.float32),
        ],
        compiler_params=pltpu.CompilerParams(vmem_limit_bytes=VMEM_BYTES),
        cost_estimate=pl.CostEstimate(
            flops=20 * tokens * texts * width,
            bytes_accessed=6 * tokens * width,
            transcendentals=tokens * texts * width // HEAD,
        ),
        name="cross_attend_back",
    )(q, grad, k, v, slots_wide)


def swap(value, axis, bit):
    count = lax.axis_size(axis)
    return lax.ppermute(value, axis, [(i, i ^ bit) for i in range(count)])


def passed_along(value, axis, steps):
    count = lax.axis_size(axis)
    initial, last = (max(0, -steps), min(count, count - steps))
    return lax.ppermute(value, axis, [(source, source + steps) for source in range(initial, last)])


def in_order(mine, other, dim):
    second = lax.axis_index("seq") == 1
    return jnp.concatenate([jnp.where(second, other, mine), jnp.where(second, mine, other)], axis=dim)


def gathered(value, dim):
    if lax.axis_size("seq") == 2:
        return in_order(value, swap(value, "seq", 1), dim)
    return lax.all_gather(value, "seq", axis=dim, tiled=True)


def own_block(value, dim):
    size = value.shape[dim] // lax.axis_size("seq")
    return lax.dynamic_slice_in_dim(value, lax.axis_index("seq") * size, size, dim)


def other_block(value, dim):
    size = value.shape[dim] // 2
    return lax.dynamic_slice_in_dim(value, (1 - lax.axis_index("seq")) * size, size, dim)


def exchanged(value, split, concat):
    if lax.axis_size("seq") == 2:
        return in_order(own_block(value, split), swap(other_block(value, split), "seq", 1), concat)
    return lax.all_to_all(value, "seq", split_axis=split, concat_axis=concat, tiled=True)


def summed_block(value, dim):
    if lax.axis_size("seq") == 2:
        received = swap(other_block(value, dim).astype(jnp.bfloat16), "seq", 1)
        return own_block(value, dim) + received.astype(jnp.float32)
    return lax.psum_scatter(
        value.astype(jnp.bfloat16), "seq", scatter_dimension=dim, tiled=True
    ).astype(jnp.float32)


def paired(value):
    short = -value.shape[-1] % PAIR
    return jnp.pad(value, ((0, 0), (0, short))) if short else value


def normed(values):
    average = jnp.mean(values, axis=-1, keepdims=True)
    centred = values - average
    spread = jnp.mean(centred * centred, axis=-1, keepdims=True)
    root = lax.rsqrt(spread + EPS)
    return centred * root, root


def norm_back(grad, n, root, gain):
    a = grad * gain
    back = (a - jnp.mean(a, axis=-1, keepdims=True) - n * jnp.mean(a * n, axis=-1, keepdims=True)) * root
    return back, jnp.sum(grad * n, axis=0), jnp.sum(grad, axis=0)


def scattered(grad):
    return lax.psum_scatter(grad.astype(jnp.bfloat16), "fsdp", scatter_dimension=0, tiled=True)


def whole(part):
    if lax.axis_size("seq") == 2:
        return part.astype(jnp.float32) + swap(part, "seq", 1).astype(jnp.float32)
    return lax.psum(part, "seq").astype(jnp.float32)


def columns(part, blocks):
    split = part.reshape(part.shape[0], blocks, -1)
    return gathered(split, 2).reshape(part.shape[0], -1).astype(jnp.float32)


def core_products(left, right):
    size, core = right.shape[1] // 2, lax.axis_index("fsdp") % 2
    part = lambda place: contract_rows(left, lax.dynamic_slice_in_dim(right, place * size, size, 1)).astype(jnp.bfloat16)
    return part(core), part(1 - core)


def both(first, second):
    return (first.astype(jnp.float32) + second.astype(jnp.float32)).astype(jnp.bfloat16)


def half_rows(value, place):
    blocks = value.reshape(-1, 2, *value.shape[1:])
    return lax.dynamic_index_in_dim(blocks, place % 2, 1, keepdims=False)


def seq_away(kept, came):
    return both(other_block(kept, 1), other_block(came, 1))


def chip_blocks(kept, came, beside):
    value = both(both(own_block(kept, 1), own_block(came, 1)), beside)
    return value.reshape(lax.axis_size("fsdp") // 2, -1, value.shape[1])


def own_rows(value, at, bit):
    while value.shape[0] > 1:
        value = both(half_rows(value, at), swap(half_rows(value, at + 1), "fsdp", bit))
        at, bit = at // 2, bit * 2
    core, second = lax.axis_index("fsdp") % 2, lax.axis_index("seq") == 1
    value = value.reshape(2, -1, value.shape[-1])
    take = lambda place: lax.dynamic_index_in_dim(value, place, 0, keepdims=False)
    mine, theirs = take(core), swap(take(1 - core), "fsdp", 1)
    pair = jnp.stack([jnp.where(core == 0, mine, theirs), jnp.where(core == 0, theirs, mine)])
    beside = swap(pair, "seq", 1)
    by_seq = jnp.where(second, beside, pair), jnp.where(second, pair, beside)
    return jnp.concatenate([by_seq[s][c] for c in range(2) for s in range(2)], axis=1).astype(jnp.float32)


def clip_starts(segments, group_index, group_rows):
    padded = jnp.concatenate([jnp.full((SPAN,), -1, jnp.int32), segments])
    spans = lax.dynamic_slice_in_dim(padded, group_index * group_rows, SPAN + group_rows)
    spans = spans.reshape(-1, SPAN)
    ahead = jnp.sum((spans == spans[:, :1]).astype(jnp.int32), axis=1)
    firsts = ahead + jnp.arange(spans.shape[0], dtype=jnp.int32) * SPAN
    late = spans[1:] != spans[1:, :1]
    return jnp.where(late, firsts[1:, None], firsts[:-1, None]).reshape(group_rows), spans[1:].reshape(group_rows)


def shards(
    tokens,
    segments,
    text,
    qkv_weight,
    out_weight,
    cross_query_weight,
    cross_kv_weight,
    cross_out_weight,
    up_weight,
    down_weight,
    norm_gain,
    norm_bias,
    cotangent,
):
    group_index = lax.axis_index("fsdp")
    seq_index = lax.axis_index("seq")
    seq_count = lax.axis_size("seq")
    tok_rows, width = tokens.shape
    group_rows = tok_rows * seq_count
    head_cols = width // seq_count
    shard_rows = qkv_weight.shape[0]
    row_block = lambda value: lax.all_gather(value, "fsdp", axis=0, tiled=True)

    norms = jnp.pad(jnp.concatenate([norm_gain, norm_bias]).T, ((0, 0), (0, PAIR - 6)))
    qkv_mine = [own_block(qkv_weight[:, i * width : (i + 1) * width], 1) for i in range(3)]
    first = row_block(jnp.concatenate([*qkv_mine, norms], axis=1))
    w_q, w_kv, w_qkv = first[:, :head_cols], first[:, head_cols : 3 * head_cols], first[:, : 3 * head_cols]
    norm_rows = first[:, 3 * head_cols : 3 * head_cols + 6].astype(jnp.float32).T
    gains, biases = norm_rows[:3], norm_rows[3:]

    ckv_mine = own_block(cross_kv_weight.reshape(shard_rows, 2, width), 2).reshape(shard_rows, 2 * head_cols)
    squares = (out_weight, cross_query_weight, cross_out_weight)
    gate = lax.optimization_barrier
    by_steps = seq_count == 2 and group_rows == SPAN
    second = row_block(jnp.concatenate([*squares, ckv_mine], axis=1))
    full_out, full_cq, full_cout = (second[:, i * width : (i + 1) * width] for i in range(3))
    w_ckv = second[:, 3 * width :]

    starts, seg_group = clip_starts(segments, group_index, group_rows)
    slots = own_block(seg_group, 0) - group_index * (group_rows // SPAN)
    slots_wide = jnp.broadcast_to(slots[:, None], (tok_rows, PAIR))

    inputs = tokens.astype(jnp.float32)
    norm_one = lambda rows: (normed(rows.astype(jnp.float32))[0] * gains[0] + biases[0]).astype(jnp.bfloat16)
    normed_one = norm_one(gathered(tokens, 0))
    kv_own = matmul(normed_one, w_kv).astype(jnp.bfloat16)
    queries = matmul(normed_one, w_q).astype(jnp.bfloat16)
    if by_steps:
        before = passed_along(tokens, "fsdp", 1)
        before_other = swap(before, "seq", 1)
    else:
        kv_before = passed_along(kv_own[group_rows - SPAN :], "fsdp", 1)
    pad_kv = lambda kv: jnp.concatenate([paired(kv[:, :head_cols]), paired(kv[:, head_cols:])], axis=1)
    if head_cols % PAIR:
        queries, kv_own, kv_before = paired(queries), pad_kv(kv_own), pad_kv(kv_before)
    heads_state = self_attend(queries, kv_own, starts, SPAN, SPAN)
    if by_steps:
        before, before_other, heads_state = gate((before, before_other, heads_state))
        kv_before = matmul(norm_one(in_order(before, before_other, 0)), w_kv).astype(jnp.bfloat16)
    heads_out, log_totals = self_attend(queries, kv_before, starts, SPAN, 0, heads_state)
    attended = exchanged(heads_out[:, :head_cols], 0, 1)
    hidden_one = inputs + matmul(attended, full_out)

    text_rows = text.reshape(-1, width)
    text_count = text_rows.shape[0]
    ckv_part = matmul(text_rows, w_ckv).astype(jnp.bfloat16).reshape(text_count, 2, head_cols)
    cross_kv = gathered(ckv_part, 2)
    cross_k, cross_v = cross_kv[:, 0], cross_kv[:, 1]
    n_two, root_two = normed(hidden_one)
    normed_two = (n_two * gains[1] + biases[1]).astype(jnp.bfloat16)
    cross_query = matmul(normed_two, full_cq).astype(jnp.bfloat16)
    cross_result = cross_attend(cross_query, cross_k, cross_v, slots_wide)
    hidden_two = hidden_one + matmul(cross_result, full_cout)

    full_up, full_down = row_block(up_weight), row_block(down_weight)
    n_three, root_three = normed(hidden_two)
    normed_three = (n_three * gains[2] + biases[2]).astype(jnp.bfloat16)
    upward = matmul(normed_three, full_up)
    below = 0.5 * (1.0 + lax.erf(upward * (0.5**0.5)))
    active = (upward * below).astype(jnp.bfloat16)
    slope = below + upward * (jnp.exp(-0.5 * upward * upward) * 0.3989422804014327)
    layer_out = (hidden_two + matmul(active, full_down)).astype(jnp.bfloat16)

    chip = group_index // 2
    grad_down, slope = gate((contract_rows(active, cotangent).astype(jnp.bfloat16), slope))
    grad_down = scattered(grad_down)
    grad_upward = (contract_cols(cotangent, full_down) * slope).astype(jnp.bfloat16)
    if by_steps:
        up_kept, up_away, grad_upward = gate((*core_products(normed_three, grad_upward), grad_upward))
        up_came = swap(up_away, "fsdp", 1)
    else:
        grad_up = scattered(contract_rows(normed_three, grad_upward))
    back_h2, gain_three, bias_three = norm_back(contract_cols(grad_upward, full_up), n_three, root_three, gains[2])
    grad_two = cotangent.astype(jnp.float32) + back_h2
    grad_two_low = grad_two.astype(jnp.bfloat16)
    if by_steps:
        up_beside, grad_two_low = gate((seq_away(up_kept, up_came), grad_two_low))
    grad_result = contract_cols(grad_two_low, full_cout).astype(jnp.bfloat16)
    grad_query_c, grad_text_k, grad_text_v = cross_attend_back(cross_query, grad_result, cross_k, cross_v, slots_wide)
    grad_text_kv = jnp.stack([grad_text_k, grad_text_v], axis=1)
    if by_steps:
        text_came = swap(other_block(grad_text_kv, 2).astype(jnp.bfloat16), "seq", 1)
    else:
        grad_text_kv = summed_block(grad_text_kv, 2)
    back_h1, gain_two, bias_two = norm_back(contract_cols(grad_query_c, full_cq), n_two, root_two, gains[1])
    grad_one = grad_two + back_h1

    grad_one_low = grad_one.astype(jnp.bfloat16)
    if by_steps:
        text_came, grad_one_low = gate((text_came, grad_one_low))
        grad_text_kv = own_block(grad_text_kv, 2) + text_came.astype(jnp.float32)
    grad_text_kv = grad_text_kv.astype(jnp.bfloat16).reshape(text_count, 2 * head_cols)
    grad_text = contract_cols(grad_text_kv, w_ckv)
    grad_attended = contract_cols(grad_one_low, full_out).astype(jnp.bfloat16)
    grad_attended, grad_query_c, grad_two_low = gate((grad_attended, grad_query_c, grad_two_low))
    if by_steps:
        heads_came = swap(other_block(grad_attended, 1), "seq", 1)
    else:
        grad_heads = paired(exchanged(grad_attended, 1, 0))
    small = [
        contract_rows(left, right).astype(jnp.bfloat16)
        for left, right in (
            (cross_result, grad_two_low),
            (normed_two, grad_query_c),
            (attended, grad_one_low),
            (text_rows, grad_text_kv),
        )
    ]
    if by_steps:
        small, up_beside, heads_came = gate((jnp.stack(small), up_beside, heads_came))
        small = lax.psum_scatter(small, "fsdp", scatter_dimension=1, tiled=True)
        up_beside = swap(up_beside, "seq", 1)
        grad_heads = in_order(own_block(grad_attended, 1), heads_came, 0)
    else:
        small = [scattered(part) for part in small]
    back_args = (queries, grad_heads, heads_out, log_totals)
    query_state, *grad_before = self_attend_back(*back_args, kv_before, starts, SPAN, 0)
    returned = [passed_along(part[:, :head_cols], "fsdp", -1).astype(jnp.float32) for part in grad_before]
    if by_steps:
        up_rows = chip_blocks(up_kept, up_came, up_beside)
        up_away, grad_down, query_state = gate((half_rows(up_rows, chip + 1), grad_down, query_state))
        up_came, down_beside = swap(up_away, "fsdp", 2), swap(grad_down, "seq", 1)
    grad_q, *grad_own = self_attend_back(*back_args, kv_own, starts, SPAN, SPAN, query_state)
    if by_steps:
        down_beside, grad_q = gate((down_beside, grad_q))
        grad_down = grad_down.astype(jnp.float32) + down_beside.astype(jnp.float32)
    else:
        grad_up, grad_down = whole(grad_up), whole(grad_down)
    late = group_rows - SPAN
    owned = [grad_q[:, :head_cols]]
    for part, more in zip(grad_own, returned):
        part = part[:, :head_cols].astype(jnp.float32)
        part = jnp.concatenate([part[:late], part[late:] + more]) if late else part + more
        owned.append(part.astype(jnp.bfloat16))
    grad_proj = jnp.concatenate(owned, axis=1)
    if by_steps:
        away = contract_cols(other_block(grad_proj, 0), w_qkv).astype(jnp.bfloat16)
        away, grad_proj = gate((away, grad_proj))
        grad_normed_one = swap(away, "seq", 1).astype(jnp.float32) + contract_cols(own_block(grad_proj, 0), w_qkv)
    else:
        grad_normed_one = summed_block(contract_cols(grad_proj, w_qkv), 0)
    grad_wqkv = contract_rows(normed_one, grad_proj).astype(jnp.bfloat16)
    n_one, root_one = normed(inputs)
    back_x, gain_one, bias_one = norm_back(grad_normed_one, n_one, root_one, gains[0])
    grad_tokens = (grad_one + back_x).astype(jnp.bfloat16)
    norm_grads = jnp.stack([gain_one, gain_two, gain_three, bias_one, bias_two, bias_three])
    norm_grads = jnp.pad(norm_grads.T.astype(jnp.bfloat16), ((0, 0), (0, PAIR - 6)))
    last, small = gate((jnp.concatenate([grad_wqkv, norm_grads], axis=1), small))
    if by_steps:
        up_came, last = gate((up_came, last))
    last = scattered(last)
    if by_steps:
        grad_cout, grad_cq, grad_wout = whole(small[:3])
        grad_up = own_rows(both(half_rows(up_rows, chip), up_came), chip // 2, 4)
    else:
        grad_cout, grad_cq, grad_wout = (whole(part) for part in small[:3])
    grad_ckv = columns(small[3], 2)
    last, grad_cout, grad_cq, grad_wout, grad_ckv, grad_up, grad_tokens = gate(
        (last, grad_cout, grad_cq, grad_wout, grad_ckv, grad_up, grad_tokens)
    )
    norm_grads = whole(last[:, -PAIR:]).T
    return (
        layer_out,
        grad_tokens,
        whole(grad_text.astype(jnp.bfloat16)).reshape(text.shape),
        columns(last[:, : 3 * head_cols], 3),
        grad_wout,
        grad_cq,
        grad_ckv,
        grad_cout,
        grad_up,
        grad_down,
        norm_grads[:3],
        norm_grads[3:6],
    )


def solution(mesh):
    rows, shard, copied = P(("fsdp", "seq"), None), P("fsdp", None), P(None, "fsdp")
    groups = P("fsdp", None, None)
    in_specs = (rows, P(), groups, *[shard] * 7, copied, copied, rows)
    out_specs = (rows, rows, groups, *[shard] * 7, copied, copied)
    return jax.shard_map(shards, mesh=mesh, in_specs=in_specs, out_specs=out_specs, check_vma=False)
```
